32 devices in a mesh: dp: 8 (over z, x), seq: 4 (over y, core).
Axes of the slice: x: 2, y: 2, z: 4, core: 2. Of those that a mesh axis runs over, the one named last changes fastest.
Arguments:
- query: bfloat16 [8, 1024, 2048], P('dp', 'seq'), may hold values from -6 to 6
- keys: bfloat16 [8, 1024, 256], P('dp', 'seq'), may hold values from -6 to 6
- values: bfloat16 [8, 1024, 256], P('dp', 'seq'), may hold values from -6 to 6
- grad_out: bfloat16 [8, 1024, 2048], P('dp', 'seq'), may hold values from -6 to 6
- layer_input: bfloat16 [8, 1024, 1536], P('dp', 'seq'), may hold values from -6 to 6
- sinks: float32 [32], replicated, may hold values from 1 to 5
- segments: int32 [8, 1024], P('dp', 'seq'), may hold values from 0 to 255, as said below
- positions: int32 [8, 1024], P('dp', 'seq'), may hold values from 0 to 8191, as said below
Outputs:
- grad_query: bfloat16 [8, 1024, 2048], P('dp', 'seq')
- weight_grads: float32 [1536, 256], P('dp')
The draws below stay inside these ranges and needn't reach their ends.
Inputs may be any that keep to these rules, and one draw needn't show every extreme that they name: `segments`: segment ids never fall along a span. positions rise by one inside a document.
All inputs are finite; a program needn't handle non-finite values.
Results may differ from the reference program's by a relative error of at most 0.0086.
Values may be sent and summed in bfloat16 or wider, within the bound.
No kernel may reach another device: no remote copies, remote signals or barrier semaphores. Data moves between devices by JAX's collectives and lax.ppermute only.
A program may use at most 64 MiB of HBM per device.

```python
import jax
import jax.numpy as jnp
from jax import lax

QHEADS = 32
KVHEADS = 4
HEADDIM = 64
WINDOW = 128
FEATURES = 1536
SEQ = 1024
SPANS = 8


def document_layout(key):
    starts_key, offset_key = jax.random.split(jax.random.fold_in(key, 5))
    marks = jax.random.randint(starts_key, (SPANS, SEQ), 0, 192) == 0
    marks = marks.at[:, 0].set(True)
    marks = marks.at[0, SEQ // 2].set(True)
    raw_ids = jnp.cumsum(marks.astype(jnp.int32), axis=1) - 1
    capped = jnp.minimum(raw_ids, 254)
    last_doc = capped[:, SEQ - 1:SEQ]
    seg_ids = jnp.where(capped == last_doc, 255, capped)
    index = jnp.broadcast_to(jnp.arange(SEQ, dtype=jnp.int32), (SPANS, SEQ))
    begin = lax.cummax(jnp.where(marks, index, 0), axis=1)
    offsets = jax.random.randint(offset_key, (SPANS, SEQ), 0, 8192 - SEQ)
    first_len = jnp.sum((raw_ids[0] == 0).astype(jnp.int32))
    offsets = offsets.at[0, 0].set(8192 - first_len)
    offsets = offsets.at[SPANS - 1, 0].set(0)
    doc_offset = jnp.take_along_axis(offsets, raw_ids, axis=1)
    return (seg_ids, doc_offset + index - begin)


def draw_segments(key, part):
    return document_layout(key)[0]


def draw_positions(key, part):
    return document_layout(key)[1]


def query_key_pair(key):
    qkey, kkey = jax.random.split(jax.random.fold_in(key, 9), 2)
    qshape = (SPANS, SEQ, QHEADS * HEADDIM)
    kshape = (SPANS, SEQ, KVHEADS * HEADDIM)
    q_vals = jnp.clip(jax.random.normal(qkey, qshape, jnp.float32), -6.0, 6.0)
    k_vals = jnp.clip(jax.random.normal(kkey, kshape, jnp.float32), -6.0, 6.0)
    return (q_vals, k_vals)


def draw_query(key, part):
    return query_key_pair(key)[0].astype(jnp.bfloat16)


def draw_keys(key, part):
    return query_key_pair(key)[1].astype(jnp.bfloat16)


def with_spikes(result, key, source, target, shards_of, factor):
    owner, partner = [(jnp.arange(result.shape[position]) // (result.shape[position] // shards_of)).reshape([-1 if axis == position else 1 for axis in range(result.ndim)]) for position in (source, target)]
    chosen = jax.random.permutation(key, shards_of)[partner]
    strong = (owner == chosen) | (owner == (partner + shards_of // 2) % shards_of)
    return jnp.where(strong, factor * result, result)


def steps_of(stream_key, shape, pieces, smallest, largest):
    def one(position, parts):
        heights = jax.random.uniform(jax.random.fold_in(jax.random.fold_in(stream_key, 6), position), (parts,), jnp.float32, smallest / len(pieces), largest / len(pieces))
        return jnp.repeat(jnp.exp(heights), shape[position] // parts).reshape((-1,) + (1,) * (len(shape) - position - 1))

    loudness = one(*pieces[0])
    for cut in pieces[1:]:
        loudness = loudness * one(*cut)
    return loudness


def normal_values(own_key, dims, scale, limit, shards=(), kind=jnp.bfloat16):
    level = steps_of(own_key, dims, shards, -0.22, 0.18) if shards else 1.0
    result = jax.random.normal(own_key, dims, jnp.float32) * scale * level
    return jnp.minimum(jnp.maximum(result, -limit), limit).astype(kind)


def noise_with(key, shape, spread, reach, pieces, heavy, kind=jnp.bfloat16):
    result = spread * jax.random.normal(key, shape, jnp.float32)
    if pieces:
        result = result * steps_of(key, shape, pieces, -0.22, 0.18)
    return jnp.clip(with_spikes(result, jax.random.fold_in(key, 3), *heavy), -reach, reach).astype(kind)


def setup_inputs(seed: int = 0) -> dict:
    streams_of = jax.random.split(jax.random.key(seed), 9)
    query = draw_query(jax.random.fold_in(streams_of[8], 71), 0)
    keys = draw_keys(jax.random.fold_in(streams_of[8], 71), 0)
    values = normal_values(streams_of[2], (SPANS, SEQ, KVHEADS * HEADDIM), 1.0, 6.0, ((0, 8), (1, 4)))
    grad_out = normal_values(streams_of[3], (SPANS, SEQ, QHEADS * HEADDIM), 1.0, 6.0, ((0, 8), (1, 4)))
    layer_input = noise_with(streams_of[4], (SPANS, SEQ, FEATURES), 1.0, 6.0, ((0, 8), (1, 4)), (0, 2, 8, 2.0))
    sinks = jnp.clip(jax.random.uniform(streams_of[5], (QHEADS,), jnp.float32, 1.0, 5.0), 1.0, 5.0)
    segments = draw_segments(jax.random.fold_in(streams_of[8], 71), 0)
    positions = draw_positions(jax.random.fold_in(streams_of[8], 71), 0)
    return dict(query=query, keys=keys, values=values, grad_out=grad_out, layer_input=layer_input, sinks=sinks, segments=segments, positions=positions)


theta_base = 150000.0


def rotate_back(grads, token_pos):
    half_dim = grads.shape[-1] // 2
    frequency = theta_base ** (-(jnp.arange(half_dim, dtype=jnp.float32) * 2.0 / grads.shape[-1]))
    angles = token_pos.astype(jnp.float32)[:, None] * frequency[None, :]
    cosine = jnp.cos(angles)[:, None, :]
    sine_val = jnp.sin(angles)[:, None, :]
    lower_half = grads[..., :half_dim]
    upper_half = grads[..., half_dim:]
    return jnp.concatenate([lower_half * cosine + upper_half * sine_val, upper_half * cosine - lower_half * sine_val], axis=-1)


def span_grads(query, keys, values, grad_out, segments, positions, sinks):
    width = WINDOW
    blocks = SEQ // width
    group = QHEADS // KVHEADS
    scale = 1.0 / (HEADDIM ** 0.5)
    q_blk = query.astype(jnp.float32).reshape(blocks, width, KVHEADS, group, HEADDIM)
    g_blk = grad_out.astype(jnp.float32).reshape(blocks, width, KVHEADS, group, HEADDIM)
    zero_rows = jnp.zeros((width, KVHEADS * HEADDIM), jnp.float32)
    k_pad = jnp.concatenate([zero_rows, keys.astype(jnp.float32)], 0).reshape(blocks + 1, width, KVHEADS, HEADDIM)
    v_pad = jnp.concatenate([zero_rows, values.astype(jnp.float32)], 0).reshape(blocks + 1, width, KVHEADS, HEADDIM)
    k_win = jnp.concatenate([k_pad[:-1], k_pad[1:]], axis=1)
    v_win = jnp.concatenate([v_pad[:-1], v_pad[1:]], axis=1)
    s_pad = jnp.concatenate([jnp.full((width,), -1, jnp.int32), segments.astype(jnp.int32)]).reshape(blocks + 1, width)
    s_win = jnp.concatenate([s_pad[:-1], s_pad[1:]], axis=1)
    s_query = segments.astype(jnp.int32).reshape(blocks, width)
    offset = jnp.arange(width)[:, None] + width - jnp.arange(2 * width)[None, :]
    allowed = (offset >= 0) & (offset < width)
    allowed = allowed[None] & (s_query[:, :, None] == s_win[:, None, :])
    allowed = allowed[:, None, None]
    scores = jnp.einsum("bqgzd,bkgd->bgzqk", q_blk, k_win) * scale
    sink_col = sinks.reshape(KVHEADS, group)[None, :, :, None, None]
    masked = jnp.where(allowed, scores, -jnp.inf)
    peak = jnp.maximum(jnp.max(masked, axis=-1, keepdims=True), sink_col)
    expo = jnp.where(allowed, jnp.exp(masked - peak), 0.0)
    total = jnp.sum(expo, axis=-1, keepdims=True) + jnp.exp(sink_col - peak)
    probs = expo / total
    grad_probs = jnp.einsum("bqgzd,bkgd->bgzqk", g_blk, v_win)
    delta = jnp.sum(probs * grad_probs, axis=-1, keepdims=True)
    grad_scores = probs * (grad_probs - delta)
    grad_b = lax.optimization_barrier(grad_scores.astype(jnp.bfloat16)).astype(jnp.float32)
    grad_q = jnp.einsum("bgzqk,bkgd->bqgzd", grad_b, k_win) * scale
    grad_q = grad_q.reshape(SEQ, QHEADS * HEADDIM).astype(jnp.bfloat16)
    key_win = jnp.einsum("bgzqk,bqgzd->bkgd", grad_b, q_blk) * scale
    zero_pad = jnp.zeros((blocks + 1, width, KVHEADS, HEADDIM), jnp.float32)
    key_grad = zero_pad.at[:-1].add(key_win[:, :width]).at[1:].add(key_win[:, width:])[1:]
    key_grad = rotate_back(key_grad.reshape(SEQ, KVHEADS, HEADDIM), positions)
    return grad_q, key_grad.reshape(SEQ, KVHEADS * HEADDIM).astype(jnp.bfloat16)


def reference(query, keys, values, grad_out, layer_input, sinks, segments, positions):
    def step(carry, items):
        q_one, k_one, v_one, g_one, x_one, s_one, p_one = items
        grad_q, k_grads = span_grads(q_one, k_one, v_one, g_one, s_one, p_one, sinks)
        carry = carry + jnp.dot(x_one.T, k_grads, preferred_element_type=jnp.float32)
        return carry, grad_q

    start = jnp.zeros((FEATURES, KVHEADS * HEADDIM), jnp.float32)
    weight_grads, grad_query = lax.scan(step, start, (query, keys, values, grad_out, layer_input, segments, positions))
    return grad_query, weight_grads
```

```python
import jax
import jax.numpy as jnp
import numpy as np
from jax import lax
from jax.experimental import pallas as pl
from jax.experimental.pallas import tpu as pltpu
from jax.sharding import PartitionSpec as P

HEADDIM = 64
WINDOW = 128
THETA = 150000.0
LOW = -1e30

F32 = jnp.float32
BF16 = jnp.bfloat16


def dot(a, b, ca, cb):
    return lax.dot_general(a, b, (((ca,), (cb,)), ((), ())), preferred_element_type=F32)


def iota(shape, dim):
    return lax.broadcasted_iota(jnp.int32, shape, dim)


def sin_cos(angle):
    turns = jnp.floor(angle * np.float32(2.0 / np.pi) + np.float32(0.5))
    rest = angle - turns * np.float32(1.5703125)
    rest = rest - turns * np.float32(4.837512969970703125e-4)
    rest = rest - turns * np.float32(7.54978995489188216e-8)
    sq = rest * rest
    sin_part = np.float32(-1.9515295891e-4) * sq + np.float32(8.3321608736e-3)
    sin_part = (sin_part * sq + np.float32(-1.6666654611e-1)) * sq * rest + rest
    cos_part = np.float32(2.443315711809948e-5) * sq + np.float32(-1.388731625493765e-3)
    cos_part = (cos_part * sq + np.float32(4.166664568298827e-2)) * sq * sq
    cos_part = cos_part - np.float32(0.5) * sq + np.float32(1.0)
    quadrant = turns.astype(jnp.int32)
    odd = (quadrant & 1) == 1
    sine = jnp.where(odd, cos_part, sin_part)
    cosine = jnp.where(odd, sin_part, cos_part)
    sine = jnp.where((quadrant & 2) == 2, -sine, sine)
    cosine = jnp.where(((quadrant + 1) & 2) == 2, -cosine, cosine)
    return sine, cosine


def as_column(row):
    return jnp.broadcast_to(row, (row.shape[1], row.shape[1])).T


def attention_kernel(
    group, n_kv, sinks_ref, first_ref, query_ref, grad_ref, keys_ref, values_ref,
    rim_keys_ref, rim_values_ref, rim_aux_ref, segs_ref, pos_ref, freq_ref,
    dq_ref, dk_ref, keys2, values2, keys_t, bias, acc, dk_all,
):
    kv = pl.program_id(0)
    w = WINDOW
    rows = query_ref.shape[0]
    blocks = rows // w
    lanes = 2 * HEADDIM
    lower = iota((w, lanes), 1) < HEADDIM
    tri = iota((w, w), 0) <= iota((w, w), 1)

    @pl.when(kv == 0)
    def _():
        rim_segs = rim_aux_ref[0:1, rim_aux_ref.shape[1] - w :].astype(F32)
        rim_segs = jnp.where(first_ref[0] == 0, np.float32(-1.0), rim_segs)
        segs = [rim_segs]
        for b in range(blocks):
            segs.append(segs_ref[0:1, b * w : (b + 1) * w].astype(F32))
        columns = [as_column(s) for s in segs]
        for b in range(blocks):
            key_segs = jnp.where(tri, columns[b + 1], columns[b])
            bias[b] = jnp.where(key_segs == segs[b + 1], np.float32(0.0), np.float32(LOW))

    own_half = (iota((w, lanes), 1) < HEADDIM) == ((kv % 2) == 0)
    for b in range(blocks + 1):
        if b == 0:
            k_tile, v_tile = rim_keys_ref[...], rim_values_ref[...]
        else:
            k_tile = keys_ref[(b - 1) * w : b * w, :]
            v_tile = values_ref[(b - 1) * w : b * w, :]
        k_tile = k_tile.astype(F32) * np.float32(HEADDIM**-0.5)
        v_tile = v_tile.astype(F32)
        k_tile = jnp.where(own_half, k_tile, pltpu.roll(k_tile, HEADDIM, 1))
        v_tile = jnp.where(own_half, v_tile, pltpu.roll(v_tile, HEADDIM, 1))
        keys2[b * w : (b + 1) * w, :] = k_tile.astype(BF16)
        values2[b * w : (b + 1) * w, :] = v_tile.astype(BF16)
        keys_t[:, b * w : (b + 1) * w] = k_tile.T[:HEADDIM].astype(BF16)

    tri2 = jnp.concatenate([tri, tri], axis=1)
    left = iota((1, 2 * w), 1) < w
    zero = jnp.zeros((), BF16)
    for b in range(blocks):
        key_win = keys2[b * w : (b + 2) * w, :]
        value_win = values2[b * w : (b + 2) * w, :]
        keyt_win = keys_t[:, b * w : (b + 2) * w]
        bias2 = jnp.concatenate([bias[b], bias[b]], axis=1)
        total_dk = None
        for pair in range(group // 2):
            q_tile = query_ref[b * w : (b + 1) * w, pair * lanes : (pair + 1) * lanes]
            g_tile = grad_ref[b * w : (b + 1) * w, pair * lanes : (pair + 1) * lanes]
            q2 = jnp.concatenate([jnp.where(lower, q_tile, zero), jnp.where(lower, zero, q_tile)], 0)
            g2 = jnp.concatenate([jnp.where(lower, g_tile, zero), jnp.where(lower, zero, g_tile)], 0)
            scores = dot(key_win, q2, 1, 1)
            scores = jnp.where(tri2, scores[w:], scores[:w]) + bias2
            head = kv * group + 2 * pair
            sink = jnp.where(left, sinks_ref[head], sinks_ref[head + 1])
            peak = jnp.maximum(jnp.max(scores, axis=0, keepdims=True), sink)
            expo = jnp.exp(scores - peak)
            total = jnp.sum(expo, axis=0, keepdims=True) + jnp.exp(sink - peak)
            probs = expo * (np.float32(1.0) / total)
            grad_probs = dot(value_win, g2, 1, 1)
            grad_probs = jnp.where(tri2, grad_probs[w:], grad_probs[:w])
            delta = jnp.sum(probs * grad_probs, axis=0, keepdims=True)
            ds = probs * (grad_probs - delta)
            ds_prev = jnp.where(tri2, np.float32(0.0), ds).astype(BF16)
            ds_cur = jnp.where(tri2, ds, np.float32(0.0)).astype(BF16)
            ds_win = jnp.concatenate([ds_prev, ds_cur], axis=0)
            part = dot(ds_win, q2, 1, 0)
            total_dk = part if total_dk is None else total_dk + part
            dq_t = dot(keyt_win, ds_win, 1, 0)
            dq_t = jnp.concatenate([dq_t[:, :w], dq_t[:, w:]], axis=0)
            dq_ref[b * w : (b + 1) * w, pair * lanes : (pair + 1) * lanes] = dq_t.T.astype(BF16)
        if b == 0:
            acc[0 : 2 * w, :] = total_dk
        else:
            acc[b * w : (b + 1) * w, :] += total_dk[:w]
            acc[(b + 1) * w : (b + 2) * w, :] = total_dk[w:]

    for tile in range(n_kv // 2):
        for odd in range(2):

            @pl.when(kv == 2 * tile + odd)
            def _(tile=tile, odd=odd):
                both = acc[...]
                both = (both + pltpu.roll(both, HEADDIM, 1)) * np.float32(HEADDIM**-0.5)
                cols = slice(tile * lanes, (tile + 1) * lanes)
                if odd == 0:
                    dk_all[:, cols] = both
                else:
                    low = iota(both.shape, 1) < HEADDIM
                    dk_all[:, cols] = jnp.where(low, dk_all[:, cols], both)

    @pl.when(kv == n_kv - 1)
    def _():
        half = HEADDIM // 2
        low = (iota((w, lanes), 1) % HEADDIM) < half
        for b in range(blocks + 1):
            if b == 0:
                pos = (
                    rim_aux_ref[1:2, rim_aux_ref.shape[1] - w :].astype(F32) * np.float32(256.0)
                    + rim_aux_ref[2:3, rim_aux_ref.shape[1] - w :].astype(F32)
                )
            else:
                pos = pos_ref[0:1, (b - 1) * w : b * w].astype(F32)
            sine, cosine = sin_cos(as_column(pos) * freq_ref[...])
            sine = jnp.where(low, sine, -sine)
            for tile in range(n_kv // 2):
                cols = slice(tile * lanes, (tile + 1) * lanes)
                dk = dk_all[b * w : (b + 1) * w, cols]
                other = jnp.where(low, pltpu.roll(dk, lanes - half, 1), pltpu.roll(dk, half, 1))
                dk_ref[b * w : (b + 1) * w, cols] = (dk * cosine + other * sine).astype(BF16)


def attention_grads(query, grad_out, keys, values, rim, segments, positions, sinks, first):
    rows, width = query.shape
    kv_width = keys.shape[1]
    n_kv = kv_width // HEADDIM
    n_heads = width // HEADDIM
    group = n_heads // n_kv
    w = WINDOW
    lanes = 2 * HEADDIM
    step = group * HEADDIM
    index = np.arange(lanes) % (HEADDIM // 2)
    freq = jnp.asarray((THETA ** (-2.0 * index / HEADDIM)).astype(np.float32)[None, :])
    return pl.pallas_call(
        lambda *refs: attention_kernel(group, n_kv, *refs),
        name="attention_grads",
        grid=(n_kv,),
        in_specs=[
            pl.BlockSpec(memory_space=pltpu.SMEM),
            pl.BlockSpec(memory_space=pltpu.SMEM),
            pl.BlockSpec((rows, step), lambda g: (0, g)),
            pl.BlockSpec((rows, step), lambda g: (0, g)),
            pl.BlockSpec((rows, lanes), lambda g: (0, g // 2)),
            pl.BlockSpec((rows, lanes), lambda g: (0, g // 2)),
            pl.BlockSpec((w, lanes), lambda g: (0, g // 2)),
            pl.BlockSpec((w, lanes), lambda g: (1, g // 2)),
            pl.BlockSpec((16, kv_width), lambda g: (2 * w // 16, 0)),
            pl.BlockSpec((1, rows), lambda g: (0, 0)),
            pl.BlockSpec((1, rows), lambda g: (0, 0)),
            pl.BlockSpec((1, lanes), lambda g: (0, 0)),
        ],
        out_specs=[
            pl.BlockSpec((rows, step), lambda g: (0, g)),
            pl.BlockSpec((rows + w, kv_width), lambda g: (0, 0)),
        ],
        out_shape=[
            jax.ShapeDtypeStruct((rows, width), BF16),
            jax.ShapeDtypeStruct((rows + w, kv_width), BF16),
        ],
        scratch_shapes=[
            pltpu.VMEM((rows + w, lanes), BF16),
            pltpu.VMEM((rows + w, lanes), BF16),
            pltpu.VMEM((HEADDIM, rows + w), BF16),
            pltpu.VMEM((rows // w, w, w), F32),
            pltpu.VMEM((rows + w, lanes), F32),
            pltpu.VMEM((rows + w, kv_width), F32),
        ],
        cost_estimate=pl.CostEstimate(
            flops=10 * rows * 2 * w * width, bytes_accessed=6 * rows * width, transcendentals=rows * w * n_heads
        ),
    )(sinks, first, query, grad_out, keys, values, rim, rim, rim, segments, positions, freq)


def bit_reversed(n):
    bits = n.bit_length() - 1
    return [int(format(i, "b").zfill(bits)[::-1], 2) if bits else 0 for i in range(n)]


def weight_kernel(n_dp, place_ref, inputs_ref, rim_ref, dk_ref, out_ref, scratch):
    rows = inputs_ref.shape[0]
    w = rim_ref.shape[0]
    scratch[...] = dot(inputs_ref[...], dk_ref[w : w + rows, :], 0, 0) + dot(
        rim_ref[...], dk_ref[0:w, :], 0, 0
    )
    piece = scratch.shape[0] // (2 * n_dp)
    for half in range(2):
        for j, relative in enumerate(bit_reversed(n_dp)):
            block = (place_ref[0] ^ relative) * 2 + (place_ref[1] ^ half)
            start = pl.multiple_of(block * piece, piece)
            out_ref[half, j * piece : (j + 1) * piece, :] = scratch[pl.ds(start, piece), :].astype(BF16)


def weight_plain_kernel(inputs_ref, rim_ref, dk_ref, out_ref):
    rows = inputs_ref.shape[0]
    w = rim_ref.shape[0]
    total = dot(inputs_ref[...], dk_ref[w : w + rows, :], 0, 0)
    out_ref[...] = (total + dot(rim_ref[...], dk_ref[0:w, :], 0, 0)).astype(BF16)


def weight_parts(layer_input, rim_input, dk, n_dp, dp_index, core):
    features = layer_input.shape[1]
    kv_width = dk.shape[1]
    piece = features // (2 * n_dp)
    if piece % 16 == 0:
        place = jnp.stack([dp_index, core]).astype(jnp.int32)
        vmem = pl.BlockSpec(memory_space=pltpu.VMEM)
        return pl.pallas_call(
            lambda *refs: weight_kernel(n_dp, *refs),
            name="weight_parts",
            in_specs=[pl.BlockSpec(memory_space=pltpu.SMEM), vmem, vmem, vmem],
            out_specs=vmem,
            out_shape=jax.ShapeDtypeStruct((2, features // 2, kv_width), BF16),
            scratch_shapes=[pltpu.VMEM((features, kv_width), F32)],
            cost_estimate=pl.CostEstimate(
                flops=2 * features * dk.shape[0] * kv_width,
                bytes_accessed=4 * features * kv_width,
                transcendentals=0,
            ),
        )(place, layer_input, rim_input, dk)
    plain = pl.pallas_call(
        weight_plain_kernel,
        name="weight_plain",
        out_shape=jax.ShapeDtypeStruct((features, kv_width), BF16),
    )(layer_input, rim_input, dk)
    plain = plain.reshape(n_dp, 2, piece, kv_width)
    order = jnp.asarray(bit_reversed(n_dp), jnp.int32) ^ dp_index
    plain = jnp.take(plain, order, axis=0)
    halves = [jnp.take(plain, core ^ half, axis=1) for half in range(2)]
    return jnp.stack(halves).reshape(2, features // 2, kv_width)


def exchange(part, axis, by):
    count = lax.axis_size(axis)
    return lax.ppermute(part, axis, [(i, i ^ by) for i in range(count)])


def forward_one(part, axis):
    count = lax.axis_size(axis)
    return lax.ppermute(part, axis, [(i, i + 1) for i in range(count - 1)])


def body(query, keys, values, grad_out, layer_input, sinks, segments, positions):
    rows = query.shape[1]
    w = WINDOW
    n_dp = lax.axis_size("dp")
    n_seq = lax.axis_size("seq")
    dp_index = lax.axis_index("dp")
    seq_index = lax.axis_index("seq")
    core = seq_index % 2

    kv_width = keys.shape[2]
    line = lax.broadcasted_iota(jnp.int32, (16, kv_width), 0)
    seg_row = segments[:, rows - kv_width :]
    pos_row = positions[:, rows - kv_width :]
    aux = jnp.where(line == 0, seg_row, jnp.where(line == 1, pos_row >> 8, pos_row & 255))
    tail = jnp.concatenate([keys[0, rows - w :], values[0, rows - w :], aux.astype(BF16)], axis=0)
    rim = forward_one(tail, "seq")
    rim_input = forward_one(layer_input[0, rows - w :], "seq")

    dq, dk = attention_grads(
        query[0], grad_out[0], keys[0], values[0], rim, segments, positions, sinks, seq_index[None]
    )
    parts = weight_parts(layer_input[0], rim_input, dk, n_dp, dp_index, core)
    total = parts[0].astype(F32) + exchange(parts[1], "seq", 1).astype(F32)
    by = 1
    while by < n_dp:
        half = total.shape[0] // 2
        got = exchange(total[half:].astype(BF16), "dp", by)
        total = total[:half] + got.astype(F32)
        by *= 2
    by = 2
    while by < n_seq:
        mine = total.astype(BF16)
        total = mine.astype(F32) + exchange(mine, "seq", by).astype(F32)
        by *= 2
    other = exchange(total, "seq", 1)
    pair = jnp.where(core == 0, jnp.stack([total, other]), jnp.stack([other, total]))
    return (dq[None], pair.reshape(-1, kv_width))


def solution(mesh):
    return jax.shard_map(
        body,
        mesh=mesh,
        in_specs=(
            P("dp", "seq", None),
            P("dp", "seq", None),
            P("dp", "seq", None),
            P("dp", "seq", None),
            P("dp", "seq", None),
            P(),
            P("dp", "seq"),
            P("dp", "seq"),
        ),
        out_specs=(P("dp", "seq", None), P("dp", None)),
        check_vma=False,
    )
```

```python
import jax
import jax.numpy as jnp
import numpy as np
from jax import lax
from jax.experimental import pallas as pl
from jax.experimental.pallas import tpu as pltpu
from jax.sharding import PartitionSpec as P

HEADDIM = 64
WINDOW = 128
THETA = 150000.0
LOW = -1e30

F32 = jnp.float32
BF16 = jnp.bfloat16


def dot(a, b, ca, cb):
    return lax.dot_general(a, b, (((ca,), (cb,)), ((), ())), preferred_element_type=F32)


def iota(shape, dim):
    return lax.broadcasted_iota(jnp.int32, shape, dim)


def sin_cos(angle):
    turns = jnp.floor(angle * np.float32(2.0 / np.pi) + np.float32(0.5))
    rest = angle - turns * np.float32(1.5703125)
    rest = rest - turns * np.float32(4.837512969970703125e-4)
    rest = rest - turns * np.float32(7.54978995489188216e-8)
    sq = rest * rest
    sin_part = np.float32(-1.9515295891e-4) * sq + np.float32(8.3321608736e-3)
    sin_part = (sin_part * sq + np.float32(-1.6666654611e-1)) * sq * rest + rest
    cos_part = np.float32(2.443315711809948e-5) * sq + np.float32(-1.388731625493765e-3)
    cos_part = (cos_part * sq + np.float32(4.166664568298827e-2)) * sq * sq
    cos_part = cos_part - np.float32(0.5) * sq + np.float32(1.0)
    quadrant = turns.astype(jnp.int32)
    odd = (quadrant & 1) == 1
    sine = jnp.where(odd, cos_part, sin_part)
    cosine = jnp.where(odd, sin_part, cos_part)
    sine = jnp.where((quadrant & 2) == 2, -sine, sine)
    cosine = jnp.where(((quadrant + 1) & 2) == 2, -cosine, cosine)
    return sine, cosine


def as_column(row):
    return jnp.broadcast_to(row, (row.shape[1], row.shape[1])).T


def load(copies):
    for copy in copies:
        copy.start()
    return copies


def prepare_keys(kv, blocks, keys2, values2, keys_t):
    w = WINDOW
    lanes = 2 * HEADDIM
    own_half = (iota((w, lanes), 1) < HEADDIM) == (kv % 2 == 0)
    cols = slice(kv // 2 * lanes, (kv // 2 + 1) * lanes)
    for b, (k_ref, v_ref, first_row) in enumerate(blocks):
        k_tile = k_ref[first_row : first_row + w, cols].astype(F32) * np.float32(HEADDIM**-0.5)
        v_tile = v_ref[first_row : first_row + w, cols].astype(F32)
        k_tile = jnp.where(own_half, k_tile, pltpu.roll(k_tile, HEADDIM, 1))
        v_tile = jnp.where(own_half, v_tile, pltpu.roll(v_tile, HEADDIM, 1))
        keys2[kv, b * w : (b + 1) * w, :] = k_tile.astype(BF16)
        values2[kv, b * w : (b + 1) * w, :] = v_tile.astype(BF16)
        keys_t[kv, :, b * w : (b + 1) * w] = k_tile.T[:HEADDIM].astype(BF16)


def attend(n_kv, group, row_blocks, wait_kv, done_kv, sinks_ref, query, grad, dq, bias, scratch, add_dk):
    keys2, values2, keys_t, scores_s, grads_s, q2_s, ds_s = scratch
    w = WINDOW
    lanes = 2 * HEADDIM
    pairs = group // 2
    lower = iota((w, lanes), 1) < HEADDIM
    tri = iota((w, w), 0) <= iota((w, w), 1)
    tri2 = jnp.concatenate([tri, tri], axis=1)
    zero = jnp.zeros((), BF16)
    items = [(b, kv, pair) for kv in range(n_kv) for b in range(row_blocks) for pair in range(pairs)]

    def to_scores(n):
        b, kv, pair = items[n]
        if b == 0 and pair == 0:
            wait_kv(kv)
        unit = (n // pairs) % 2
        rows = slice(b * w, (b + 1) * w)
        cols = slice((kv * pairs + pair) * lanes, (kv * pairs + pair + 1) * lanes)
        window = slice(b * w, (b + 2) * w)
        q_tile = query[rows, cols]
        g_tile = grad[rows, cols]
        q2 = jnp.concatenate([jnp.where(lower, q_tile, zero), jnp.where(lower, zero, q_tile)], 0)
        g2 = jnp.concatenate([jnp.where(lower, g_tile, zero), jnp.where(lower, zero, g_tile)], 0)
        q2_s[unit, pair * 2 * w : (pair + 1) * 2 * w, :] = q2
        scores = dot(keys2[kv, window, :], q2, 1, 1)
        bias2 = jnp.concatenate([bias[b], bias[b]], axis=1)
        scores_s[n % 2] = jnp.where(tri2, scores[w:], scores[:w]) + bias2
        grads = dot(values2[kv, window, :], g2, 1, 1)
        grads_s[n % 2] = jnp.where(tri2, grads[w:], grads[:w])

    def to_ds(n):
        b, kv, pair = items[n]
        unit = (n // pairs) % 2
        for one in range(2):
            cols = slice(one * w, (one + 1) * w)
            sink = sinks_ref[kv * group + 2 * pair + one]
            scores = scores_s[n % 2, :, cols]
            peak = jnp.maximum(jnp.max(scores, axis=0, keepdims=True), sink)
            expo = jnp.exp(scores - peak)
            total = jnp.sum(expo, axis=0, keepdims=True) + jnp.exp(sink - peak)
            probs = expo * (np.float32(1.0) / total)
            grads = grads_s[n % 2, :, cols]
            delta = jnp.sum(probs * grads, axis=0, keepdims=True)
            ds = probs * (grads - delta)
            out_cols = slice(pair * 2 * w + one * w, pair * 2 * w + (one + 1) * w)
            ds_s[unit, 0:w, out_cols] = jnp.where(tri, np.float32(0.0), ds).astype(BF16)
            ds_s[unit, w : 2 * w, out_cols] = jnp.where(tri, ds, np.float32(0.0)).astype(BF16)

    def to_grads(n):
        b, kv, pair = items[n]
        unit = (n // pairs) % 2
        rows = slice(b * w, (b + 1) * w)
        cols = slice((kv * pairs + pair) * lanes, (kv * pairs + pair + 1) * lanes)
        ds = ds_s[unit, :, pair * 2 * w : (pair + 1) * 2 * w]
        dq_t = dot(keys_t[kv, :, b * w : (b + 2) * w], ds, 1, 0)
        dq_t = jnp.concatenate([dq_t[:, :w], dq_t[:, w:]], axis=0)
        dq[rows, cols] = dq_t.T.astype(BF16)
        if pair == pairs - 1:
            add_dk(b, kv, dot(ds_s[unit], q2_s[unit], 1, 0))
            if b == row_blocks - 1:
                done_kv(kv)

    for n in range(len(items) + 2):
        if n < len(items):
            to_scores(n)
        if 0 <= n - 1 < len(items):
            to_ds(n - 1)
        if n >= 2:
            to_grads(n - 2)


def attend_scratch(n_kv, group, row_blocks):
    w = WINDOW
    lanes = 2 * HEADDIM
    return [
        pltpu.VMEM((n_kv, (row_blocks + 1) * w, lanes), BF16),
        pltpu.VMEM((n_kv, (row_blocks + 1) * w, lanes), BF16),
        pltpu.VMEM((n_kv, HEADDIM, (row_blocks + 1) * w), BF16),
        pltpu.VMEM((2, w, 2 * w), F32),
        pltpu.VMEM((2, w, 2 * w), F32),
        pltpu.VMEM((2, group * w, lanes), BF16),
        pltpu.VMEM((2, 2 * w, group * w), BF16),
    ]


def window_bias(bias, b, prev_segs, own_segs):
    tri = iota((WINDOW, WINDOW), 0) <= iota((WINDOW, WINDOW), 1)
    key_segs = jnp.where(tri, as_column(own_segs), as_column(prev_segs))
    bias[b] = jnp.where(key_segs == own_segs, np.float32(0.0), np.float32(LOW))


def store_dk(dk_part, dk_all, first_block, b, kv, part, seen):
    w = WINDOW
    lanes = 2 * HEADDIM
    if kv % 2 == 0:
        dk_part[b] = part
        return
    even = dk_part[b]
    low = iota(part.shape, 1) < HEADDIM
    both = jnp.where(low, even, part) + pltpu.roll(jnp.where(low, part, even), HEADDIM, 1)
    cols = slice(kv // 2 * lanes, (kv // 2 + 1) * lanes)
    for k in range(2):
        rows = slice((first_block + b + k) * w, (first_block + b + k + 1) * w)
        piece = both[k * w : (k + 1) * w]
        if (first_block + b + k, kv) in seen:
            piece = piece + dk_all[rows, cols]
        seen.add((first_block + b + k, kv))
        dk_all[rows, cols] = piece


def rotate(dk, sine, cosine):
    half = HEADDIM // 2
    lanes = dk.shape[1]
    low = (iota(dk.shape, 1) % HEADDIM) < half
    other = jnp.where(low, pltpu.roll(dk, lanes - half, 1), pltpu.roll(dk, half, 1))
    return (dk * cosine + other * sine) * np.float32(HEADDIM**-0.5)


def turn_table(pos, freq):
    sine, cosine = sin_cos(as_column(pos.astype(F32)) * freq)
    low = (iota(sine.shape, 1) % HEADDIM) < HEADDIM // 2
    return jnp.where(low, sine, -sine), cosine


def local_kernel(
    n_kv, group, sinks_ref, segs_ref, pos_ref, freq_ref, query_hbm, grad_hbm, keys_hbm, values_hbm,
    dq_hbm, dk_ref, own_ref, table_ref,
    query, grad, dq, keys, values, bias, dk_part, dk_all, key_sem, in_sem, out_sem, *scratch,
):
    w = WINDOW
    lanes = 2 * HEADDIM
    rows = keys.shape[0]
    row_blocks = rows // w - 1
    step = group * HEADDIM
    key_copies = load(
        [
            pltpu.make_async_copy(keys_hbm, keys, key_sem.at[0]),
            pltpu.make_async_copy(values_hbm, values, key_sem.at[1]),
        ]
    )

    def ins(kv):
        cols = slice(kv * step, (kv + 1) * step)
        return [
            pltpu.make_async_copy(query_hbm.at[w:, cols], query.at[:, cols], in_sem.at[0, kv]),
            pltpu.make_async_copy(grad_hbm.at[w:, cols], grad.at[:, cols], in_sem.at[1, kv]),
        ]

    def out(kv):
        cols = slice(kv * step, (kv + 1) * step)
        return pltpu.make_async_copy(dq.at[:, cols], dq_hbm.at[w:, cols], out_sem.at[kv])

    in_copies = [load(ins(kv)) for kv in range(n_kv)]
    segs = [segs_ref[0:1, b * w : (b + 1) * w].astype(F32) for b in range(row_blocks + 1)]
    for b in range(row_blocks):
        window_bias(bias, b, segs[b], segs[b + 1])
    tables = []
    for b in range(row_blocks + 1):
        sine, cosine = turn_table(pos_ref[0:1, b * w : (b + 1) * w], freq_ref[...])
        table_ref[2 * b] = sine
        table_ref[2 * b + 1] = cosine
    for copy in key_copies:
        copy.wait()
    seen = set()

    def wait_kv(kv):
        prepare_keys(kv, [(keys, values, b * w) for b in range(row_blocks + 1)], *scratch[:3])
        for copy in in_copies[kv]:
            copy.wait()

    attend(
        n_kv, group, row_blocks, wait_kv, lambda kv: out(kv).start(), sinks_ref, query, grad, dq, bias, scratch,
        lambda b, kv, part: store_dk(dk_part, dk_all, 0, b, kv, part, seen),
    )
    for b in range(row_blocks + 1):
        for tile in range(n_kv // 2):
            cols = slice(tile * lanes, (tile + 1) * lanes)
            turned = rotate(dk_all[b * w : (b + 1) * w, cols], table_ref[2 * b], table_ref[2 * b + 1])
            if b == 0:
                own_ref[:, cols] = turned
            else:
                dk_ref[(b - 1) * w : b * w, cols] = turned.astype(BF16)
    for kv in range(n_kv):
        out(kv).wait()


def rim_kernel(
    n_kv, group, n_dp, place_ref, sinks_ref, segs_ref, freq_ref, dk_ref, own_ref, table_ref,
    query_hbm, grad_hbm, keys_hbm, values_hbm, inputs_hbm, rim_hbm, dq_in,
    dq_hbm, send_ref, keep_ref,
    query, grad, dq, keys, values, inputs, rim, bias, dk_part, dk_all, dk16, sums, key_sem, in_sem, out_sem,
    *scratch,
):
    w = WINDOW
    lanes = 2 * HEADDIM
    step = group * HEADDIM
    features = inputs.shape[1]
    kv_width = n_kv * HEADDIM
    rows = inputs.shape[0]
    key_copies = load(
        [
            pltpu.make_async_copy(keys_hbm.at[0:w], keys, key_sem.at[0]),
            pltpu.make_async_copy(values_hbm.at[0:w], values, key_sem.at[1]),
            pltpu.make_async_copy(rim_hbm, rim, key_sem.at[2]),
        ]
    )

    def ins(kv):
        cols = slice(kv * step, (kv + 1) * step)
        return [
            pltpu.make_async_copy(query_hbm.at[0:w, cols], query.at[:, cols], in_sem.at[0, kv]),
            pltpu.make_async_copy(grad_hbm.at[0:w, cols], grad.at[:, cols], in_sem.at[1, kv]),
        ]

    def out(kv):
        cols = slice(kv * step, (kv + 1) * step)
        return pltpu.make_async_copy(dq.at[:, cols], dq_hbm.at[0:w, cols], out_sem.at[kv])

    in_copies = [load(ins(kv)) for kv in range(n_kv)]
    inputs_copy = pltpu.make_async_copy(inputs_hbm, inputs, key_sem.at[3])
    inputs_copy.start()
    for copy in key_copies:
        copy.wait()
    rim_keys = rim.at[:, features : features + kv_width]
    rim_values = rim.at[:, features + kv_width : features + 2 * kv_width]
    aux = rim[0:16, features + 2 * kv_width :].astype(F32)
    rim_segs = jnp.where(place_ref[2] == 0, np.float32(-1.0), aux[0:1])
    window_bias(bias, 0, rim_segs, segs_ref[0:1, 0:w].astype(F32))
    rim_sine, rim_cosine = turn_table(aux[1:2] * np.float32(256.0) + aux[2:3], freq_ref[...])
    seen = set()

    def wait_kv(kv):
        prepare_keys(kv, [(rim_keys, rim_values, 0), (keys, values, 0)], *scratch[:3])
        for copy in in_copies[kv]:
            copy.wait()

    attend(
        n_kv, group, 1, wait_kv, lambda kv: out(kv).start(), sinks_ref, query, grad, dq, bias, scratch,
        lambda b, kv, part: store_dk(dk_part, dk_all, 0, b, kv, part, seen),
    )
    for tile in range(n_kv // 2):
        cols = slice(tile * lanes, (tile + 1) * lanes)
        dk16[0:w, cols] = rotate(dk_all[0:w, cols], rim_sine, rim_cosine).astype(BF16)
        own = rotate(dk_all[w : 2 * w, cols], table_ref[0], table_ref[1]) + own_ref[:, cols]
        dk16[w : 2 * w, cols] = own.astype(BF16)
    if rows > w:
        dk16[2 * w :, :] = dk_ref[...]
    inputs_copy.wait()
    sums[...] = dot(inputs[...], dk16[w:, :], 0, 0) + dot(rim[:, 0:features], dk16[0:w, :], 0, 0)
    piece = features // (2 * n_dp)
    for half, ref in enumerate([keep_ref, send_ref]):
        for j, relative in enumerate(bit_reversed(n_dp)):
            if piece % 16 == 0:
                block = (place_ref[0] ^ relative) * 2 + (place_ref[1] ^ half)
                start = pl.multiple_of(block * piece, piece)
                ref[j * piece : (j + 1) * piece, :] = sums[pl.ds(start, piece), :].astype(BF16)
    if piece % 16:
        keep_ref[...] = sums[0 : features // 2, :].astype(BF16)
        send_ref[...] = sums[features // 2 :, :].astype(BF16)
    for kv in range(n_kv):
        out(kv).wait()


ANY = pl.BlockSpec(memory_space=pl.ANY)
HBM = pl.BlockSpec(memory_space=pltpu.HBM)
VMEM = pl.BlockSpec(memory_space=pltpu.VMEM)
SMEM = pl.BlockSpec(memory_space=pltpu.SMEM)
LIMIT = 24 * 2**20


def rotation_rates():
    index = np.arange(2 * HEADDIM) % (HEADDIM // 2)
    return jnp.asarray((THETA ** (-2.0 * index / HEADDIM)).astype(np.float32)[None, :])


def shared_scratch(n_kv, group, row_blocks):
    w = WINDOW
    width = n_kv * group * HEADDIM
    lanes = 2 * HEADDIM
    wide = pltpu.VMEM((row_blocks * w, width), BF16)
    return [wide, wide, wide]


def estimate(row_blocks, width, extra_flops, extra_bytes):
    w = WINDOW
    return pl.CostEstimate(
        flops=10 * row_blocks * w * 2 * w * width + extra_flops,
        bytes_accessed=6 * row_blocks * w * width + extra_bytes,
        transcendentals=row_blocks * w * w * width // HEADDIM,
    )


def local_grads(query, grad_out, keys, values, segments, positions, sinks):
    rows, width = query.shape
    kv_width = keys.shape[1]
    n_kv = kv_width // HEADDIM
    group = width // kv_width
    w = WINDOW
    lanes = 2 * HEADDIM
    row_blocks = rows // w - 1
    return pl.pallas_call(
        lambda *refs: local_kernel(n_kv, group, *refs),
        name="local_grads",
        in_specs=[SMEM, VMEM, VMEM, VMEM, HBM, HBM, HBM, HBM],
        out_specs=[HBM, VMEM, VMEM, VMEM],
        out_shape=[
            jax.ShapeDtypeStruct((rows, width), BF16),
            jax.ShapeDtypeStruct((rows - w, kv_width), BF16),
            jax.ShapeDtypeStruct((w, kv_width), F32),
            jax.ShapeDtypeStruct((2 * (row_blocks + 1), w, lanes), F32),
        ],
        scratch_shapes=shared_scratch(n_kv, group, row_blocks)
        + [
            pltpu.VMEM((rows, kv_width), BF16),
            pltpu.VMEM((rows, kv_width), BF16),
            pltpu.VMEM((row_blocks, w, w), F32),
            pltpu.VMEM((row_blocks, 2 * w, lanes), F32),
            pltpu.VMEM((rows, kv_width), F32),
            pltpu.SemaphoreType.DMA((2,)),
            pltpu.SemaphoreType.DMA((2, n_kv)),
            pltpu.SemaphoreType.DMA((n_kv,)),
        ]
        + attend_scratch(n_kv, group, row_blocks),
        compiler_params=pltpu.CompilerParams(vmem_limit_bytes=LIMIT),
        cost_estimate=estimate(row_blocks, width, 0, 0),
    )(sinks, segments, positions, rotation_rates(), query, grad_out, keys, values)


def rim_grads(local, query, grad_out, keys, values, layer_input, rim, segments, sinks, place, n_dp):
    dq, dk, own, table = local
    rows, width = query.shape
    kv_width = keys.shape[1]
    features = layer_input.shape[1]
    n_kv = kv_width // HEADDIM
    group = width // kv_width
    w = WINDOW
    lanes = 2 * HEADDIM
    return pl.pallas_call(
        lambda *refs: rim_kernel(n_kv, group, n_dp, *refs),
        name="rim_grads",
        in_specs=[SMEM, SMEM] + [VMEM] * 5 + [HBM] * 5 + [ANY, HBM],
        out_specs=[HBM, VMEM, VMEM],
        out_shape=[
            jax.ShapeDtypeStruct((rows, width), BF16),
            jax.ShapeDtypeStruct((features // 2, kv_width), BF16),
            jax.ShapeDtypeStruct((features // 2, kv_width), BF16),
        ],
        input_output_aliases={13: 0},
        scratch_shapes=shared_scratch(n_kv, group, 1)
        + [
            pltpu.VMEM((w, kv_width), BF16),
            pltpu.VMEM((w, kv_width), BF16),
            pltpu.VMEM((rows, features), BF16),
            pltpu.VMEM(rim.shape, BF16),
            pltpu.VMEM((1, w, w), F32),
            pltpu.VMEM((1, 2 * w, lanes), F32),
            pltpu.VMEM((2 * w, kv_width), F32),
            pltpu.VMEM((rows + w, kv_width), BF16),
            pltpu.VMEM((features, kv_width), F32),
            pltpu.SemaphoreType.DMA((4,)),
            pltpu.SemaphoreType.DMA((2, n_kv)),
            pltpu.SemaphoreType.DMA((n_kv,)),
        ]
        + attend_scratch(n_kv, group, 1),
        compiler_params=pltpu.CompilerParams(vmem_limit_bytes=LIMIT),
        cost_estimate=estimate(1, width, 2 * features * kv_width * (rows + w), 8 * features * kv_width),
    )(place, sinks, segments, rotation_rates(), dk, own, table, query, grad_out, keys, values, layer_input, rim, dq)


def tail_kernel(segs_ref, pos_ref, inputs_hbm, keys_hbm, values_hbm, out_ref, sem):
    w = WINDOW
    rows, features = inputs_hbm.shape
    kv_width = keys_hbm.shape[1]
    copies = load(
        [
            pltpu.make_async_copy(inputs_hbm.at[rows - w :], out_ref.at[:, 0:features], sem.at[0]),
            pltpu.make_async_copy(
                keys_hbm.at[rows - w :], out_ref.at[:, features : features + kv_width], sem.at[1]
            ),
            pltpu.make_async_copy(
                values_hbm.at[rows - w :],
                out_ref.at[:, features + kv_width : features + 2 * kv_width],
                sem.at[2],
            ),
        ]
    )
    line = iota((16, w), 0)
    segs = segs_ref[0:1, rows - w :]
    pos = pos_ref[0:1, rows - w :]
    aux = jnp.where(line == 0, segs, jnp.where(line == 1, pos >> 8, pos & 255))
    out_ref[0:16, features + 2 * kv_width :] = aux.astype(F32).astype(BF16)
    out_ref[16:, features + 2 * kv_width :] = jnp.zeros((w - 16, w), BF16)
    for copy in copies:
        copy.wait()


def last_tokens(layer_input, keys, values, segments, positions):
    width = layer_input.shape[1] + 2 * keys.shape[1] + WINDOW
    return pl.pallas_call(
        tail_kernel,
        name="last_tokens",
        in_specs=[VMEM, VMEM, HBM, HBM, HBM],
        out_specs=VMEM,
        out_shape=jax.ShapeDtypeStruct((WINDOW, width), BF16),
        scratch_shapes=[pltpu.SemaphoreType.DMA((3,))],
        compiler_params=pltpu.CompilerParams(vmem_limit_bytes=LIMIT),
    )(segments, positions, layer_input, keys, values)


def bit_reversed(n):
    bits = n.bit_length() - 1
    return [int(format(i, "b").zfill(bits)[::-1], 2) if bits else 0 for i in range(n)]


def exchange(part, axis, by):
    count = lax.axis_size(axis)
    return lax.ppermute(part, axis, [(i, i ^ by) for i in range(count)])


def forward_one(part, axis):
    count = lax.axis_size(axis)
    return lax.ppermute(part, axis, [(i, i + 1) for i in range(count - 1)])


def body(query, keys, values, grad_out, layer_input, sinks, segments, positions):
    n_dp = lax.axis_size("dp")
    n_seq = lax.axis_size("seq")
    dp_index = lax.axis_index("dp")
    seq_index = lax.axis_index("seq")
    core = seq_index & 1
    kv_width = keys.shape[2]
    features = layer_input.shape[2]
    piece = features // (2 * n_dp)

    tail = last_tokens(layer_input[0], keys[0], values[0], segments, positions)
    rim = forward_one(tail, "seq")
    local = local_grads(query[0], grad_out[0], keys[0], values[0], segments, positions, sinks)
    place = jnp.stack([dp_index, core, seq_index]).astype(jnp.int32)
    dq, send, keep = rim_grads(
        local, query[0], grad_out[0], keys[0], values[0], layer_input[0], rim, segments, sinks, place, n_dp
    )
    if piece % 16:
        plain = jnp.concatenate([keep, send], axis=0).reshape(n_dp, 2, piece, kv_width)
        plain = jnp.take(plain, jnp.asarray(bit_reversed(n_dp), jnp.int32) ^ dp_index, axis=0)
        keep = jnp.take(plain, core, axis=1).reshape(-1, kv_width)
        send = jnp.take(plain, core ^ 1, axis=1).reshape(-1, kv_width)
    total = keep.astype(F32) + exchange(send, "seq", 1).astype(F32)
    by = 1
    while by < n_dp:
        half = total.shape[0] // 2
        got = exchange(total[half:].astype(BF16), "dp", by)
        total = total[:half] + got.astype(F32)
        by *= 2
    by = 2
    while by < n_seq:
        mine = total.astype(BF16)
        total = mine.astype(F32) + exchange(mine, "seq", by).astype(F32)
        by *= 2
    other = exchange(total, "seq", 1)
    pair = jnp.where(core == 0, jnp.stack([total, other]), jnp.stack([other, total]))
    return (dq[None], pair.reshape(-1, kv_width))


def solution(mesh):
    return jax.shard_map(
        body,
        mesh=mesh,
        in_specs=(
            P("dp", "seq", None),
            P("dp", "seq", None),
            P("dp", "seq", None),
            P("dp", "seq", None),
            P("dp", "seq", None),
            P(),
            P("dp", "seq"),
            P("dp", "seq"),
        ),
        out_specs=(P("dp", "seq", None), P("dp", None)),
        check_vma=False,
    )
```

```python
import jax
import jax.numpy as jnp
import numpy as np
from jax import lax
from jax.experimental import pallas as pl
from jax.experimental.pallas import tpu as pltpu
from jax.sharding import PartitionSpec as P

HEADDIM = 64
WINDOW = 128
THETA = 150000.0
LOW = -1e30

F32 = jnp.float32
BF16 = jnp.bfloat16


def dot(a, b, ca, cb):
    return lax.dot_general(a, b, (((ca,), (cb,)), ((), ())), preferred_element_type=F32)


def iota(shape, dim):
    return lax.broadcasted_iota(jnp.int32, shape, dim)


def sin_cos(angle):
    turns = jnp.floor(angle * np.float32(2.0 / np.pi) + np.float32(0.5))
    rest = angle - turns * np.float32(1.5703125)
    rest = rest - turns * np.float32(4.837512969970703125e-4)
    rest = rest - turns * np.float32(7.54978995489188216e-8)
    sq = rest * rest
    sin_part = np.float32(-1.9515295891e-4) * sq + np.float32(8.3321608736e-3)
    sin_part = (sin_part * sq + np.float32(-1.6666654611e-1)) * sq * rest + rest
    cos_part = np.float32(2.443315711809948e-5) * sq + np.float32(-1.388731625493765e-3)
    cos_part = (cos_part * sq + np.float32(4.166664568298827e-2)) * sq * sq
    cos_part = cos_part - np.float32(0.5) * sq + np.float32(1.0)
    quadrant = turns.astype(jnp.int32)
    odd = (quadrant & 1) == 1
    sine = jnp.where(odd, cos_part, sin_part)
    cosine = jnp.where(odd, sin_part, cos_part)
    sine = jnp.where((quadrant & 2) == 2, -sine, sine)
    cosine = jnp.where(((quadrant + 1) & 2) == 2, -cosine, cosine)
    return sine, cosine


def as_column(row):
    return jnp.broadcast_to(row, (row.shape[1], row.shape[1])).T


def load(copies):
    for copy in copies:
        copy.start()
    return copies


def prepare_keys(kv, blocks, keys2, values2, keys_t):
    w = WINDOW
    lanes = 2 * HEADDIM
    own_half = (iota((w, lanes), 1) < HEADDIM) == (kv % 2 == 0)
    cols = slice(kv // 2 * lanes, (kv // 2 + 1) * lanes)
    for b, (k_ref, v_ref, first_row) in enumerate(blocks):
        k_tile = k_ref[first_row : first_row + w, cols].astype(F32) * np.float32(HEADDIM**-0.5)
        v_tile = v_ref[first_row : first_row + w, cols].astype(F32)
        k_tile = jnp.where(own_half, k_tile, pltpu.roll(k_tile, HEADDIM, 1))
        v_tile = jnp.where(own_half, v_tile, pltpu.roll(v_tile, HEADDIM, 1))
        keys2[kv, b * w : (b + 1) * w, :] = k_tile.astype(BF16)
        values2[kv, b * w : (b + 1) * w, :] = v_tile.astype(BF16)
        keys_t[kv, :, b * w : (b + 1) * w] = k_tile.T[:HEADDIM].astype(BF16)


def attend(n_kv, group, row_blocks, wait_kv, done_kv, sinks_ref, query, grad, dq, bias, scratch, add_dk):
    keys2, values2, keys_t, scores_s, grads_s, q2_s, ds_s = scratch
    w = WINDOW
    lanes = 2 * HEADDIM
    pairs = group // 2
    lower = iota((w, lanes), 1) < HEADDIM
    tri = iota((w, w), 0) <= iota((w, w), 1)
    tri2 = jnp.concatenate([tri, tri], axis=1)
    zero = jnp.zeros((), BF16)
    items = [(b, kv, pair) for kv in range(n_kv) for b in range(row_blocks) for pair in range(pairs)]

    def to_scores(n):
        b, kv, pair = items[n]
        if b == 0 and pair == 0:
            wait_kv(kv)
        unit = (n // pairs) % 2
        rows = slice(b * w, (b + 1) * w)
        cols = slice((kv * pairs + pair) * lanes, (kv * pairs + pair + 1) * lanes)
        window = slice(b * w, (b + 2) * w)
        q_tile = query[rows, cols]
        g_tile = grad[rows, cols]
        q2 = jnp.concatenate([jnp.where(lower, q_tile, zero), jnp.where(lower, zero, q_tile)], 0)
        g2 = jnp.concatenate([jnp.where(lower, g_tile, zero), jnp.where(lower, zero, g_tile)], 0)
        q2_s[unit, pair * 2 * w : (pair + 1) * 2 * w, :] = q2
        scores = dot(keys2[kv, window, :], q2, 1, 1)
        bias2 = jnp.concatenate([bias[b], bias[b]], axis=1)
        scores_s[n % 2] = jnp.where(tri2, scores[w:], scores[:w]) + bias2
        grads = dot(values2[kv, window, :], g2, 1, 1)
        grads_s[n % 2] = jnp.where(tri2, grads[w:], grads[:w])

    def to_ds(n):
        b, kv, pair = items[n]
        unit = (n // pairs) % 2
        for one in range(2):
            cols = slice(one * w, (one + 1) * w)
            sink = sinks_ref[kv * group + 2 * pair + one]
            scores = scores_s[n % 2, :, cols]
            peak = jnp.maximum(jnp.max(scores, axis=0, keepdims=True), sink)
            expo = jnp.exp(scores - peak)
            total = jnp.sum(expo, axis=0, keepdims=True) + jnp.exp(sink - peak)
            probs = expo * (np.float32(1.0) / total)
            grads = grads_s[n % 2, :, cols]
            delta = jnp.sum(probs * grads, axis=0, keepdims=True)
            ds = probs * (grads - delta)
            out_cols = slice(pair * 2 * w + one * w, pair * 2 * w + (one + 1) * w)
            ds_s[unit, 0:w, out_cols] = jnp.where(tri, np.float32(0.0), ds).astype(BF16)
            ds_s[unit, w : 2 * w, out_cols] = jnp.where(tri, ds, np.float32(0.0)).astype(BF16)

    def to_grads(n):
        b, kv, pair = items[n]
        unit = (n // pairs) % 2
        rows = slice(b * w, (b + 1) * w)
        cols = slice((kv * pairs + pair) * lanes, (kv * pairs + pair + 1) * lanes)
        ds = ds_s[unit, :, pair * 2 * w : (pair + 1) * 2 * w]
        dq_t = dot(keys_t[kv, :, b * w : (b + 2) * w], ds, 1, 0)
        dq_t = jnp.concatenate([dq_t[:, :w], dq_t[:, w:]], axis=0)
        dq[rows, cols] = dq_t.T.astype(BF16)
        if pair == pairs - 1:
            add_dk(b, kv, dot(ds_s[unit], q2_s[unit], 1, 0))
            if b == row_blocks - 1:
                done_kv(kv)

    for n in range(len(items) + 2):
        if n < len(items):
            to_scores(n)
        if 0 <= n - 1 < len(items):
            to_ds(n - 1)
        if n >= 2:
            to_grads(n - 2)


def attend_scratch(n_kv, group, row_blocks):
    w = WINDOW
    lanes = 2 * HEADDIM
    return [
        pltpu.VMEM((n_kv, (row_blocks + 1) * w, lanes), BF16),
        pltpu.VMEM((n_kv, (row_blocks + 1) * w, lanes), BF16),
        pltpu.VMEM((n_kv, HEADDIM, (row_blocks + 1) * w), BF16),
        pltpu.VMEM((2, w, 2 * w), F32),
        pltpu.VMEM((2, w, 2 * w), F32),
        pltpu.VMEM((2, group * w, lanes), BF16),
        pltpu.VMEM((2, 2 * w, group * w), BF16),
    ]


def window_bias(bias, b, prev_segs, own_segs):
    tri = iota((WINDOW, WINDOW), 0) <= iota((WINDOW, WINDOW), 1)
    key_segs = jnp.where(tri, as_column(own_segs), as_column(prev_segs))
    bias[b] = jnp.where(key_segs == own_segs, np.float32(0.0), np.float32(LOW))


def store_dk(dk_part, dk_all, first_block, b, kv, part, seen):
    w = WINDOW
    lanes = 2 * HEADDIM
    if kv % 2 == 0:
        dk_part[b] = part
        return
    even = dk_part[b]
    low = iota(part.shape, 1) < HEADDIM
    both = jnp.where(low, even, part) + pltpu.roll(jnp.where(low, part, even), HEADDIM, 1)
    cols = slice(kv // 2 * lanes, (kv // 2 + 1) * lanes)
    for k in range(2):
        rows = slice((first_block + b + k) * w, (first_block + b + k + 1) * w)
        piece = both[k * w : (k + 1) * w]
        if (first_block + b + k, kv) in seen:
            piece = piece + dk_all[rows, cols]
        seen.add((first_block + b + k, kv))
        dk_all[rows, cols] = piece


def rotate(dk, sine, cosine):
    half = HEADDIM // 2
    lanes = dk.shape[1]
    low = (iota(dk.shape, 1) % HEADDIM) < half
    other = jnp.where(low, pltpu.roll(dk, lanes - half, 1), pltpu.roll(dk, half, 1))
    return (dk * cosine + other * sine) * np.float32(HEADDIM**-0.5)


def turn_table(pos):
    half = HEADDIM // 2
    index = iota((1, 2 * HEADDIM), 1) % half
    rates = (THETA ** (-2.0 * np.arange(half) / HEADDIM)).astype(np.float32)
    freq = jnp.zeros((1, 2 * HEADDIM), F32)
    for t in range(half):
        freq = jnp.where(index == t, rates[t], freq)
    sine, cosine = sin_cos(as_column(pos.astype(F32)) * freq)
    low = (iota(sine.shape, 1) % HEADDIM) < HEADDIM // 2
    return jnp.where(low, sine, -sine), cosine


def local_kernel(
    n_kv, group, sinks_hbm, segs_hbm, pos_hbm, query_hbm, grad_hbm, keys_hbm, values_hbm,
    dq_hbm, dk_ref, own_ref, table_ref,
    query, grad, dq, sinks_ref, segs_ref, pos_ref, keys, values, bias, dk_part, dk_all,
    key_sem, in_sem, out_sem, *scratch,
):
    w = WINDOW
    lanes = 2 * HEADDIM
    rows = keys.shape[0]
    row_blocks = rows // w - 1
    step = group * HEADDIM
    ids = load(
        [
            pltpu.make_async_copy(segs_hbm, segs_ref, key_sem.at[2]),
            pltpu.make_async_copy(pos_hbm, pos_ref, key_sem.at[3]),
            pltpu.make_async_copy(sinks_hbm, sinks_ref, key_sem.at[4]),
        ]
    )
    key_copies = load(
        [
            pltpu.make_async_copy(keys_hbm, keys, key_sem.at[0]),
            pltpu.make_async_copy(values_hbm, values, key_sem.at[1]),
        ]
    )

    def ins(kv):
        cols = slice(kv * step, (kv + 1) * step)
        return [
            pltpu.make_async_copy(query_hbm.at[w:, cols], query.at[:, cols], in_sem.at[0, kv]),
            pltpu.make_async_copy(grad_hbm.at[w:, cols], grad.at[:, cols], in_sem.at[1, kv]),
        ]

    def out(kv):
        cols = slice(kv * step, (kv + 1) * step)
        return pltpu.make_async_copy(dq.at[:, cols], dq_hbm.at[w:, cols], out_sem.at[kv])

    in_copies = [load(ins(kv)) for kv in range(n_kv)]
    for copy in ids:
        copy.wait()
    segs = [segs_ref[0:1, b * w : (b + 1) * w].astype(F32) for b in range(row_blocks + 1)]
    for b in range(row_blocks):
        window_bias(bias, b, segs[b], segs[b + 1])
    tables = []
    for b in range(row_blocks + 1):
        sine, cosine = turn_table(pos_ref[0:1, b * w : (b + 1) * w])
        table_ref[2 * b] = sine
        table_ref[2 * b + 1] = cosine
    for copy in key_copies:
        copy.wait()
    seen = set()

    def wait_kv(kv):
        prepare_keys(kv, [(keys, values, b * w) for b in range(row_blocks + 1)], *scratch[:3])
        for copy in in_copies[kv]:
            copy.wait()

    attend(
        n_kv, group, row_blocks, wait_kv, lambda kv: out(kv).start(), sinks_ref, query, grad, dq, bias, scratch,
        lambda b, kv, part: store_dk(dk_part, dk_all, 0, b, kv, part, seen),
    )
    for b in range(row_blocks + 1):
        for tile in range(n_kv // 2):
            cols = slice(tile * lanes, (tile + 1) * lanes)
            turned = rotate(dk_all[b * w : (b + 1) * w, cols], table_ref[2 * b], table_ref[2 * b + 1])
            if b == 0:
                own_ref[:, cols] = turned
            else:
                dk_ref[(b - 1) * w : b * w, cols] = turned.astype(BF16)
    for kv in range(n_kv):
        out(kv).wait()


def rim_kernel(
    n_kv, group, n_dp, dk_ref, own_ref, table_ref, sinks_hbm, segs_hbm,
    query_hbm, grad_hbm, keys_hbm, values_hbm, inputs_hbm, rim_hbm, dq_in,
    dq_hbm, send_ref, keep_ref,
    query, grad, dq, sinks_ref, segs_ref, keys, values, inputs, rim, bias, dk_part, dk_all, dk16, sums,
    key_sem, in_sem, out_sem, *scratch,
):
    w = WINDOW
    lanes = 2 * HEADDIM
    step = group * HEADDIM
    features = inputs.shape[1]
    kv_width = n_kv * HEADDIM
    rows = inputs.shape[0]
    key_copies = load(
        [
            pltpu.make_async_copy(keys_hbm.at[0:w], keys, key_sem.at[0]),
            pltpu.make_async_copy(values_hbm.at[0:w], values, key_sem.at[1]),
            pltpu.make_async_copy(rim_hbm, rim, key_sem.at[2]),
            pltpu.make_async_copy(sinks_hbm, sinks_ref, key_sem.at[4]),
            pltpu.make_async_copy(segs_hbm, segs_ref, key_sem.at[5]),
        ]
    )

    def ins(kv):
        cols = slice(kv * step, (kv + 1) * step)
        return [
            pltpu.make_async_copy(query_hbm.at[0:w, cols], query.at[:, cols], in_sem.at[0, kv]),
            pltpu.make_async_copy(grad_hbm.at[0:w, cols], grad.at[:, cols], in_sem.at[1, kv]),
        ]

    def out(kv):
        cols = slice(kv * step, (kv + 1) * step)
        return pltpu.make_async_copy(dq.at[:, cols], dq_hbm.at[0:w, cols], out_sem.at[kv])

    in_copies = [load(ins(kv)) for kv in range(n_kv)]
    inputs_copy = pltpu.make_async_copy(inputs_hbm, inputs, key_sem.at[3])
    inputs_copy.start()
    for copy in key_copies:
        copy.wait()
    rim_keys = rim.at[:, features : features + kv_width]
    rim_values = rim.at[:, features + kv_width : features + 2 * kv_width]
    aux = rim[0:16, features + 2 * kv_width :].astype(F32)
    rim_segs = jnp.where(lax.axis_index("seq") == 0, np.float32(-1.0), aux[0:1])
    window_bias(bias, 0, rim_segs, segs_ref[0:1, 0:w].astype(F32))
    rim_sine, rim_cosine = turn_table(aux[1:2] * np.float32(256.0) + aux[2:3])
    seen = set()

    def wait_kv(kv):
        prepare_keys(kv, [(rim_keys, rim_values, 0), (keys, values, 0)], *scratch[:3])
        for copy in in_copies[kv]:
            copy.wait()

    attend(
        n_kv, group, 1, wait_kv, lambda kv: out(kv).start(), sinks_ref, query, grad, dq, bias, scratch,
        lambda b, kv, part: store_dk(dk_part, dk_all, 0, b, kv, part, seen),
    )
    for tile in range(n_kv // 2):
        cols = slice(tile * lanes, (tile + 1) * lanes)
        dk16[0:w, cols] = rotate(dk_all[0:w, cols], rim_sine, rim_cosine).astype(BF16)
        own = rotate(dk_all[w : 2 * w, cols], table_ref[0], table_ref[1]) + own_ref[:, cols]
        dk16[w : 2 * w, cols] = own.astype(BF16)
    if rows > w:
        dk16[2 * w :, :] = dk_ref[...]
    inputs_copy.wait()
    sums[...] = dot(inputs[...], dk16[w:, :], 0, 0) + dot(rim[:, 0:features], dk16[0:w, :], 0, 0)
    piece = features // (2 * n_dp)
    dp_index = lax.axis_index("dp")
    core = lax.axis_index("seq") & 1
    for half, ref in enumerate([keep_ref, send_ref]):
        for j, relative in enumerate(bit_reversed(n_dp)):
            if piece % 16 == 0:
                block = (dp_index ^ relative) * 2 + (core ^ half)
                start = pl.multiple_of(block * piece, piece)
                ref[j * piece : (j + 1) * piece, :] = sums[pl.ds(start, piece), :].astype(BF16)
    if piece % 16:
        keep_ref[...] = sums[0 : features // 2, :].astype(BF16)
        send_ref[...] = sums[features // 2 :, :].astype(BF16)
    for kv in range(n_kv):
        out(kv).wait()


ANY = pl.BlockSpec(memory_space=pl.ANY)
HBM = pl.BlockSpec(memory_space=pltpu.HBM)
VMEM = pl.BlockSpec(memory_space=pltpu.VMEM)
SMEM = pl.BlockSpec(memory_space=pltpu.SMEM)
LIMIT = 24 * 2**20


def shared_scratch(n_kv, group, row_blocks):
    w = WINDOW
    width = n_kv * group * HEADDIM
    lanes = 2 * HEADDIM
    wide = pltpu.VMEM((row_blocks * w, width), BF16)
    return [wide, wide, wide]


def estimate(row_blocks, width, extra_flops, extra_bytes):
    w = WINDOW
    return pl.CostEstimate(
        flops=10 * row_blocks * w * 2 * w * width + extra_flops,
        bytes_accessed=6 * row_blocks * w * width + extra_bytes,
        transcendentals=row_blocks * w * w * width // HEADDIM,
    )


def local_grads(query, grad_out, keys, values, segments, positions, sinks):
    rows, width = query.shape
    kv_width = keys.shape[1]
    n_kv = kv_width // HEADDIM
    group = width // kv_width
    w = WINDOW
    lanes = 2 * HEADDIM
    row_blocks = rows // w - 1
    return pl.pallas_call(
        lambda *refs: local_kernel(n_kv, group, *refs),
        name="local_grads",
        in_specs=[HBM] * 7,
        out_specs=[HBM, VMEM, VMEM, VMEM],
        out_shape=[
            jax.ShapeDtypeStruct((rows, width), BF16),
            jax.ShapeDtypeStruct((rows - w, kv_width), BF16),
            jax.ShapeDtypeStruct((w, kv_width), F32),
            jax.ShapeDtypeStruct((2 * (row_blocks + 1), w, lanes), F32),
        ],
        scratch_shapes=shared_scratch(n_kv, group, row_blocks)
        + [
            pltpu.SMEM(sinks.shape, F32),
            pltpu.VMEM(segments.shape, jnp.int32),
            pltpu.VMEM(segments.shape, jnp.int32),
            pltpu.VMEM((rows, kv_width), BF16),
            pltpu.VMEM((rows, kv_width), BF16),
            pltpu.VMEM((row_blocks, w, w), F32),
            pltpu.VMEM((row_blocks, 2 * w, lanes), F32),
            pltpu.VMEM((rows, kv_width), F32),
            pltpu.SemaphoreType.DMA((5,)),
            pltpu.SemaphoreType.DMA((2, n_kv)),
            pltpu.SemaphoreType.DMA((n_kv,)),
        ]
        + attend_scratch(n_kv, group, row_blocks),
        compiler_params=pltpu.CompilerParams(vmem_limit_bytes=LIMIT),
        cost_estimate=estimate(row_blocks, width, 0, 0),
    )(sinks, segments, positions, query, grad_out, keys, values)


def rim_grads(local, query, grad_out, keys, values, layer_input, rim, segments, sinks, n_dp):
    dq, dk, own, table = local
    rows, width = query.shape
    kv_width = keys.shape[1]
    features = layer_input.shape[1]
    n_kv = kv_width // HEADDIM
    group = width // kv_width
    w = WINDOW
    lanes = 2 * HEADDIM
    return pl.pallas_call(
        lambda *refs: rim_kernel(n_kv, group, n_dp, *refs),
        name="rim_grads",
        in_specs=[VMEM] * 3 + [HBM] * 7 + [ANY, HBM],
        out_specs=[HBM, VMEM, VMEM],
        out_shape=[
            jax.ShapeDtypeStruct((rows, width), BF16),
            jax.ShapeDtypeStruct((features // 2, kv_width), BF16),
            jax.ShapeDtypeStruct((features // 2, kv_width), BF16),
        ],
        input_output_aliases={11: 0},
        scratch_shapes=shared_scratch(n_kv, group, 1)
        + [
            pltpu.SMEM(sinks.shape, F32),
            pltpu.VMEM(segments.shape, jnp.int32),
            pltpu.VMEM((w, kv_width), BF16),
            pltpu.VMEM((w, kv_width), BF16),
            pltpu.VMEM((rows, features), BF16),
            pltpu.VMEM(rim.shape, BF16),
            pltpu.VMEM((1, w, w), F32),
            pltpu.VMEM((1, 2 * w, lanes), F32),
            pltpu.VMEM((2 * w, kv_width), F32),
            pltpu.VMEM((rows + w, kv_width), BF16),
            pltpu.VMEM((features, kv_width), F32),
            pltpu.SemaphoreType.DMA((6,)),
            pltpu.SemaphoreType.DMA((2, n_kv)),
            pltpu.SemaphoreType.DMA((n_kv,)),
        ]
        + attend_scratch(n_kv, group, 1),
        compiler_params=pltpu.CompilerParams(vmem_limit_bytes=LIMIT),
        cost_estimate=estimate(1, width, 2 * features * kv_width * (rows + w), 8 * features * kv_width),
    )(dk, own, table, sinks, segments, query, grad_out, keys, values, layer_input, rim, dq)


def tail_kernel(segs_hbm, pos_hbm, inputs_hbm, keys_hbm, values_hbm, out_ref, segs_ref, pos_ref, sem):
    w = WINDOW
    ids = load(
        [
            pltpu.make_async_copy(segs_hbm, segs_ref, sem.at[3]),
            pltpu.make_async_copy(pos_hbm, pos_ref, sem.at[4]),
        ]
    )
    rows, features = inputs_hbm.shape
    kv_width = keys_hbm.shape[1]
    copies = load(
        [
            pltpu.make_async_copy(inputs_hbm.at[rows - w :], out_ref.at[:, 0:features], sem.at[0]),
            pltpu.make_async_copy(
                keys_hbm.at[rows - w :], out_ref.at[:, features : features + kv_width], sem.at[1]
            ),
            pltpu.make_async_copy(
                values_hbm.at[rows - w :],
                out_ref.at[:, features + kv_width : features + 2 * kv_width],
                sem.at[2],
            ),
        ]
    )
    for copy in ids:
        copy.wait()
    line = iota((16, w), 0)
    segs = segs_ref[0:1, rows - w :]
    pos = pos_ref[0:1, rows - w :]
    aux = jnp.where(line == 0, segs, jnp.where(line == 1, pos >> 8, pos & 255))
    out_ref[0:16, features + 2 * kv_width :] = aux.astype(F32).astype(BF16)
    out_ref[16:, features + 2 * kv_width :] = jnp.zeros((w - 16, w), BF16)
    for copy in copies:
        copy.wait()


def last_tokens(layer_input, keys, values, segments, positions):
    width = layer_input.shape[1] + 2 * keys.shape[1] + WINDOW
    return pl.pallas_call(
        tail_kernel,
        name="last_tokens",
        in_specs=[HBM] * 5,
        out_specs=VMEM,
        out_shape=jax.ShapeDtypeStruct((WINDOW, width), BF16),
        scratch_shapes=[
            pltpu.VMEM(segments.shape, jnp.int32),
            pltpu.VMEM(segments.shape, jnp.int32),
            pltpu.SemaphoreType.DMA((5,)),
        ],
        compiler_params=pltpu.CompilerParams(vmem_limit_bytes=LIMIT),
    )(segments, positions, layer_input, keys, values)


def bit_reversed(n):
    bits = n.bit_length() - 1
    return [int(format(i, "b").zfill(bits)[::-1], 2) if bits else 0 for i in range(n)]


def exchange(part, axis, by):
    count = lax.axis_size(axis)
    return lax.ppermute(part, axis, [(i, i ^ by) for i in range(count)])


def share(total, axis, by, ways):
    rows = total.shape[0] // ways
    parts = [total[k * rows : (k + 1) * rows] for k in range(ways)]
    sends = [part.astype(BF16) for part in parts[1:]]
    got = {}
    for k in reversed(range(1, ways)):
        relative = bit_reversed(ways)[k] * by
        got[k] = exchange(sends[k - 1], axis, relative)
    total = parts[0]
    for k in range(1, ways):
        total = total + got[k].astype(F32)
    return total


def forward_one(part, axis):
    count = lax.axis_size(axis)
    return lax.ppermute(part, axis, [(i, i + 1) for i in range(count - 1)])


def body(query, keys, values, grad_out, layer_input, sinks, segments, positions):
    n_dp = lax.axis_size("dp")
    n_seq = lax.axis_size("seq")
    dp_index = lax.axis_index("dp")
    seq_index = lax.axis_index("seq")
    core = seq_index & 1
    kv_width = keys.shape[2]
    features = layer_input.shape[2]
    piece = features // (2 * n_dp)
    query, grad_out, layer_input, keys, values = [
        pltpu.with_memory_space_constraint(x[0], pltpu.HBM) for x in (query, grad_out, layer_input, keys, values)
    ]
    sinks, segments, positions = [
        pltpu.with_memory_space_constraint(x, pltpu.HBM) for x in (sinks, segments, positions)
    ]
    tail = last_tokens(layer_input, keys, values, segments, positions)
    rim = forward_one(tail, "seq")
    local = local_grads(query, grad_out, keys, values, segments, positions, sinks)
    dq, send, keep = rim_grads(
        local, query, grad_out, keys, values, layer_input, rim, segments, sinks, n_dp
    )
    if piece % 16:
        plain = jnp.concatenate([keep, send], axis=0).reshape(n_dp, 2, piece, kv_width)
        plain = jnp.take(plain, jnp.asarray(bit_reversed(n_dp), jnp.int32) ^ dp_index, axis=0)
        keep = jnp.take(plain, core, axis=1).reshape(-1, kv_width)
        send = jnp.take(plain, core ^ 1, axis=1).reshape(-1, kv_width)
    total = keep.astype(F32) + exchange(send, "seq", 1).astype(F32)
    by = 1
    while by < n_dp:
        ways = 4 if 4 * by <= n_dp else 2
        total = share(total, "dp", by, ways)
        by *= ways
    by = 2
    while by < n_seq:
        mine = total.astype(BF16)
        total = mine.astype(F32) + exchange(mine, "seq", by).astype(F32)
        by *= 2
    other = exchange(total, "seq", 1)
    pair = jnp.where(core == 0, jnp.stack([total, other]), jnp.stack([other, total]))
    return (dq[None], pair.reshape(-1, kv_width))


def solution(mesh):
    return jax.shard_map(
        body,
        mesh=mesh,
        in_specs=(
            P("dp", "seq", None),
            P("dp", "seq", None),
            P("dp", "seq", None),
            P("dp", "seq", None),
            P("dp", "seq", None),
            P(),
            P("dp", "seq"),
            P("dp", "seq"),
        ),
        out_specs=(P("dp", "seq", None), P("dp", None)),
        check_vma=False,
    )
```

```python
import jax
import jax.numpy as jnp
import numpy as np
from jax import lax
from jax.experimental import pallas as pl
from jax.experimental.pallas import tpu as pltpu
from jax.sharding import PartitionSpec as P

HEADDIM = 64
WINDOW = 128
THETA = 150000.0
LOW = -1e30

F32 = jnp.float32
BF16 = jnp.bfloat16


def dot(a, b, ca, cb):
    return lax.dot_general(a, b, (((ca,), (cb,)), ((), ())), preferred_element_type=F32)


def iota(shape, dim):
    return lax.broadcasted_iota(jnp.int32, shape, dim)


def sin_cos(angle):
    turns = jnp.floor(angle * np.float32(2.0 / np.pi) + np.float32(0.5))
    rest = angle - turns * np.float32(1.5703125)
    rest = rest - turns * np.float32(4.837512969970703125e-4)
    rest = rest - turns * np.float32(7.54978995489188216e-8)
    sq = rest * rest
    sin_part = np.float32(-1.9515295891e-4) * sq + np.float32(8.3321608736e-3)
    sin_part = (sin_part * sq + np.float32(-1.6666654611e-1)) * sq * rest + rest
    cos_part = np.float32(2.443315711809948e-5) * sq + np.float32(-1.388731625493765e-3)
    cos_part = (cos_part * sq + np.float32(4.166664568298827e-2)) * sq * sq
    cos_part = cos_part - np.float32(0.5) * sq + np.float32(1.0)
    quadrant = turns.astype(jnp.int32)
    odd = (quadrant & 1) == 1
    sine = jnp.where(odd, cos_part, sin_part)
    cosine = jnp.where(odd, sin_part, cos_part)
    sine = jnp.where((quadrant & 2) == 2, -sine, sine)
    cosine = jnp.where(((quadrant + 1) & 2) == 2, -cosine, cosine)
    return sine, cosine


def as_column(row):
    return jnp.broadcast_to(row, (row.shape[1], row.shape[1])).T


def load(copies):
    for copy in copies:
        copy.start()
    return copies


def prepare_keys(kv, blocks, keys2, values2, keys_t):
    w = WINDOW
    lanes = 2 * HEADDIM
    own_half = (iota((w, lanes), 1) < HEADDIM) == (kv % 2 == 0)
    cols = slice(kv // 2 * lanes, (kv // 2 + 1) * lanes)
    for b, (k_ref, v_ref, first_row) in enumerate(blocks):
        rows = slice(b * w, (b + 1) * w)
        k_tile = k_ref[first_row : first_row + w, cols].astype(F32) * np.float32(HEADDIM**-0.5)
        v_tile = v_ref[first_row : first_row + w, cols].astype(F32)
        k_tile = jnp.where(own_half, k_tile, np.float32(0.0))
        v_tile = jnp.where(own_half, v_tile, np.float32(0.0))
        keys2[kv, kv % 2, rows, :] = k_tile.astype(BF16)
        values2[kv, kv % 2, rows, :] = v_tile.astype(BF16)
        keys2[kv, 1 - kv % 2, rows, :] = pltpu.roll(k_tile, HEADDIM, 1).astype(BF16)
        values2[kv, 1 - kv % 2, rows, :] = pltpu.roll(v_tile, HEADDIM, 1).astype(BF16)
        half = slice(kv % 2 * HEADDIM, (kv % 2 + 1) * HEADDIM)
        keys_t[kv, :, rows] = k_tile.T[half].astype(BF16)


def attend(
    n_kv, group, row_blocks, wait_kv, done_kv, beside, sinks_ref, query, grad, dq, bias, halves, scratch, add_dk
):
    keys2, values2, keys_t, scores_s, grads_s, ds_s = scratch
    w = WINDOW
    lanes = 2 * HEADDIM
    quads = group // 4
    tri = iota((w, w), 0) <= iota((w, w), 1)
    tri2 = jnp.concatenate([tri, tri], axis=1)
    items = [(b, kv, quad) for kv in range(n_kv) for b in range(row_blocks) for quad in range(quads)]

    def tiles(ref, b, kv, first, count):
        rows = slice(b * w, (b + 1) * w)
        start = kv * group // 2 + first
        return jnp.concatenate(
            [ref[rows, (start + t) * lanes : (start + t + 1) * lanes] for t in range(count)], axis=0
        )

    def to_scores(n):
        b, kv, quad = items[n]
        if b == 0 and quad == 0:
            wait_kv(kv)
        window = slice(b * w, (b + 2) * w)
        q_two = tiles(query, b, kv, 2 * quad, 2)
        g_two = tiles(grad, b, kv, 2 * quad, 2)
        bias2 = jnp.concatenate([bias[b], bias[b]], axis=1)
        for side in range(2):
            scores = dot(keys2[kv, side, window, :], q_two, 1, 1)
            scores_s[n % 2, side] = jnp.where(tri2, scores[w:], scores[:w]) + bias2
        for side in range(2):
            grads = dot(values2[kv, side, window, :], g_two, 1, 1)
            grads_s[n % 2, side] = jnp.where(tri2, grads[w:], grads[:w])

    def to_ds(n):
        b, kv, quad = items[n]
        unit = (n // quads) % 2
        for side in range(2):
            for t in range(2):
                cols = slice(t * w, (t + 1) * w)
                sink = sinks_ref[kv * group + 4 * quad + 2 * t + side]
                scores = scores_s[n % 2, side, :, cols]
                peak = jnp.maximum(jnp.max(scores, axis=0, keepdims=True), sink)
                expo = jnp.exp(scores - peak)
                total = jnp.sum(expo, axis=0, keepdims=True) + jnp.exp(sink - peak)
                probs = expo * (np.float32(1.0) / total)
                grads = grads_s[n % 2, side, :, cols]
                delta = jnp.sum(probs * grads, axis=0, keepdims=True)
                ds = (probs * (grads - delta)).astype(BF16)
                out_cols = slice((2 * quad + t) * w, (2 * quad + t + 1) * w)
                ds_s[unit, side, 0:w, out_cols] = ds * halves[0]
                ds_s[unit, side, w : 2 * w, out_cols] = ds * halves[1]

    def to_grads(n):
        b, kv, quad = items[n]
        unit = (n // quads) % 2
        rows = slice(b * w, (b + 1) * w)
        keyt_win = keys_t[kv, :, b * w : (b + 2) * w]
        for t in range(2):
            tile = 2 * quad + t
            cols = slice(tile * w, (tile + 1) * w)
            dq_t = [dot(keyt_win, ds_s[unit, side, :, cols], 1, 0) for side in range(2)]
            start = kv * group // 2 + tile
            dq[rows, start * lanes : (start + 1) * lanes] = jnp.concatenate(dq_t, axis=0).T.astype(BF16)
        if quad == quads - 1:
            q_all = tiles(query, b, kv, 0, group // 2)
            low = iota((2 * w, lanes), 1) < HEADDIM
            sides = [dot(ds_s[unit, side], q_all, 1, 0) for side in range(2)]
            add_dk(b, kv, jnp.where(low, sides[0], sides[1]))
            if b == row_blocks - 1:
                done_kv(kv)

    for n in range(len(items) + 2):
        if n < len(items):
            to_scores(n)
        if 0 <= n - 1 < len(items):
            to_ds(n - 1)
        if n >= 2:
            to_grads(n - 2)
        if n < len(items):
            beside(n, len(items))


def attend_scratch(n_kv, group, row_blocks):
    w = WINDOW
    lanes = 2 * HEADDIM
    return [
        pltpu.VMEM((n_kv, 2, (row_blocks + 1) * w, lanes), BF16),
        pltpu.VMEM((n_kv, 2, (row_blocks + 1) * w, lanes), BF16),
        pltpu.VMEM((n_kv, HEADDIM, (row_blocks + 1) * w), BF16),
        pltpu.VMEM((2, 2, w, 2 * w), F32),
        pltpu.VMEM((2, 2, w, 2 * w), F32),
        pltpu.VMEM((2, 2, 2 * w, group // 2 * w), BF16),
    ]


def set_halves(halves):
    tri = iota((WINDOW, WINDOW), 0) <= iota((WINDOW, WINDOW), 1)
    halves[0] = jnp.where(tri, np.float32(0.0), np.float32(1.0)).astype(BF16)
    halves[1] = jnp.where(tri, np.float32(1.0), np.float32(0.0)).astype(BF16)


def window_bias(bias, b, prev_segs, own_segs):
    tri = iota((WINDOW, WINDOW), 0) <= iota((WINDOW, WINDOW), 1)
    key_segs = jnp.where(tri, as_column(own_segs), as_column(prev_segs))
    bias[b] = jnp.where(key_segs == own_segs, np.float32(0.0), np.float32(LOW))


def store_dk(dk_part, dk_all, first_block, b, kv, part, seen):
    w = WINDOW
    lanes = 2 * HEADDIM
    if kv % 2 == 0:
        dk_part[b] = part
        return
    even = dk_part[b]
    low = iota(part.shape, 1) < HEADDIM
    both = jnp.where(low, even, part) + pltpu.roll(jnp.where(low, part, even), HEADDIM, 1)
    cols = slice(kv // 2 * lanes, (kv // 2 + 1) * lanes)
    for k in range(2):
        rows = slice((first_block + b + k) * w, (first_block + b + k + 1) * w)
        piece = both[k * w : (k + 1) * w]
        if (first_block + b + k, kv) in seen:
            piece = piece + dk_all[rows, cols]
        seen.add((first_block + b + k, kv))
        dk_all[rows, cols] = piece


def rotate(dk, sine, cosine):
    half = HEADDIM // 2
    lanes = dk.shape[1]
    low = (iota(dk.shape, 1) % HEADDIM) < half
    other = jnp.where(low, pltpu.roll(dk, lanes - half, 1), pltpu.roll(dk, half, 1))
    return (dk * cosine + other * sine) * np.float32(HEADDIM**-0.5)


def turn_table(pos):
    half = HEADDIM // 2
    index = iota((1, 2 * HEADDIM), 1) % half
    rates = (THETA ** (-2.0 * np.arange(half) / HEADDIM)).astype(np.float32)
    freq = jnp.zeros((1, 2 * HEADDIM), F32)
    for t in range(half):
        freq = jnp.where(index == t, rates[t], freq)
    sine, cosine = sin_cos(as_column(pos.astype(F32)) * freq)
    low = (iota(sine.shape, 1) % HEADDIM) < HEADDIM // 2
    return jnp.where(low, sine, -sine), cosine


def local_kernel(
    n_kv, group, sinks_hbm, segs_hbm, pos_hbm, query_hbm, grad_hbm, keys_hbm, values_hbm,
    dq_hbm, dk_ref, own_ref, table_ref,
    query, grad, dq, sinks_ref, segs_ref, pos_ref, keys, values, bias, halves, dk_part, dk_all,
    key_sem, in_sem, out_sem, *scratch,
):
    w = WINDOW
    lanes = 2 * HEADDIM
    rows = keys.shape[0]
    row_blocks = rows // w - 1
    step = group * HEADDIM
    ids = load(
        [
            pltpu.make_async_copy(segs_hbm, segs_ref, key_sem.at[2]),
            pltpu.make_async_copy(pos_hbm, pos_ref, key_sem.at[3]),
            pltpu.make_async_copy(sinks_hbm, sinks_ref, key_sem.at[4]),
        ]
    )
    key_copies = load(
        [
            pltpu.make_async_copy(keys_hbm, keys, key_sem.at[0]),
            pltpu.make_async_copy(values_hbm, values, key_sem.at[1]),
        ]
    )

    def ins(kv):
        cols = slice(kv * step, (kv + 1) * step)
        return [
            pltpu.make_async_copy(query_hbm.at[w:, cols], query.at[:, cols], in_sem.at[0, kv]),
            pltpu.make_async_copy(grad_hbm.at[w:, cols], grad.at[:, cols], in_sem.at[1, kv]),
        ]

    def out(kv):
        cols = slice(kv * step, (kv + 1) * step)
        return pltpu.make_async_copy(dq.at[:, cols], dq_hbm.at[w:, cols], out_sem.at[kv])

    in_copies = [load(ins(kv)) for kv in range(n_kv)]
    for copy in ids:
        copy.wait()
    segs = [segs_ref[0:1, b * w : (b + 1) * w].astype(F32) for b in range(row_blocks + 1)]
    set_halves(halves)
    for b in range(row_blocks):
        window_bias(bias, b, segs[b], segs[b + 1])
    for b in range(row_blocks + 1):
        sine, cosine = turn_table(pos_ref[0:1, b * w : (b + 1) * w])
        table_ref[2 * b] = sine
        table_ref[2 * b + 1] = cosine
    for copy in key_copies:
        copy.wait()
    seen = set()

    def wait_kv(kv):
        prepare_keys(kv, [(keys, values, b * w) for b in range(row_blocks + 1)], *scratch[:3])
        for copy in in_copies[kv]:
            copy.wait()

    attend(
        n_kv, group, row_blocks, wait_kv, lambda kv: out(kv).start(), lambda n, count: None,
        sinks_ref, query, grad, dq, bias, halves, scratch,
        lambda b, kv, part: store_dk(dk_part, dk_all, 0, b, kv, part, seen),
    )
    for b in range(row_blocks + 1):
        for tile in range(n_kv // 2):
            cols = slice(tile * lanes, (tile + 1) * lanes)
            turned = rotate(dk_all[b * w : (b + 1) * w, cols], table_ref[2 * b], table_ref[2 * b + 1])
            if b == 0:
                own_ref[:, cols] = turned
            else:
                dk_ref[(b - 1) * w : b * w, cols] = turned.astype(BF16)
    for kv in range(n_kv):
        out(kv).wait()


def rim_kernel(
    n_kv, group, n_dp, dk_ref, own_ref, table_ref, sinks_hbm, segs_hbm,
    query_hbm, grad_hbm, keys_hbm, values_hbm, inputs_hbm, rim_hbm, dq_in,
    dq_hbm, send_ref, keep_ref,
    query, grad, dq, sinks_ref, segs_ref, keys, values, inputs, rim, bias, halves, dk_part, dk_all, dk16, inputs_t, sums,
    key_sem, in_sem, out_sem, *scratch,
):
    w = WINDOW
    lanes = 2 * HEADDIM
    step = group * HEADDIM
    features = inputs.shape[1]
    kv_width = n_kv * HEADDIM
    rows = inputs.shape[0]
    key_copies = load(
        [
            pltpu.make_async_copy(keys_hbm.at[0:w], keys, key_sem.at[0]),
            pltpu.make_async_copy(values_hbm.at[0:w], values, key_sem.at[1]),
            pltpu.make_async_copy(rim_hbm, rim, key_sem.at[2]),
            pltpu.make_async_copy(sinks_hbm, sinks_ref, key_sem.at[4]),
            pltpu.make_async_copy(segs_hbm, segs_ref, key_sem.at[5]),
        ]
    )

    def ins(kv):
        cols = slice(kv * step, (kv + 1) * step)
        return [
            pltpu.make_async_copy(query_hbm.at[0:w, cols], query.at[:, cols], in_sem.at[0, kv]),
            pltpu.make_async_copy(grad_hbm.at[0:w, cols], grad.at[:, cols], in_sem.at[1, kv]),
        ]

    def out(kv):
        cols = slice(kv * step, (kv + 1) * step)
        return pltpu.make_async_copy(dq.at[:, cols], dq_hbm.at[0:w, cols], out_sem.at[kv])

    in_copies = [load(ins(kv)) for kv in range(n_kv)]
    inputs_copy = pltpu.make_async_copy(inputs_hbm, inputs, key_sem.at[3])
    inputs_copy.start()
    for copy in key_copies:
        copy.wait()
    rim_keys = rim.at[:, features : features + kv_width]
    rim_values = rim.at[:, features + kv_width : features + 2 * kv_width]
    aux = rim[0:16, features + 2 * kv_width :].astype(F32)
    rim_segs = jnp.where(lax.axis_index("seq") == 0, np.float32(-1.0), aux[0:1])
    window_bias(bias, 0, rim_segs, segs_ref[0:1, 0:w].astype(F32))
    set_halves(halves)
    rim_sine, rim_cosine = turn_table(aux[1:2] * np.float32(256.0) + aux[2:3])
    seen = set()

    def wait_kv(kv):
        prepare_keys(kv, [(rim_keys, rim_values, 0), (keys, values, 0)], *scratch[:3])
        for copy in in_copies[kv]:
            copy.wait()

    blocks = rows // w + 1
    pieces = [(f, t) for f in range(features // w) for t in range(blocks)]

    def turn_inputs(n, count):
        if n == 0:
            inputs_copy.wait()
        for f, t in pieces[n * len(pieces) // count : (n + 1) * len(pieces) // count]:
            cols = slice(f * w, (f + 1) * w)
            tile = rim[:, cols] if t == 0 else inputs[(t - 1) * w : t * w, cols]
            inputs_t[cols, t * w : (t + 1) * w] = tile.T

    attend(
        n_kv, group, 1, wait_kv, lambda kv: out(kv).start(), turn_inputs,
        sinks_ref, query, grad, dq, bias, halves, scratch,
        lambda b, kv, part: store_dk(dk_part, dk_all, 0, b, kv, part, seen),
    )
    for tile in range(n_kv // 2):
        cols = slice(tile * lanes, (tile + 1) * lanes)
        dk16[0:w, cols] = rotate(dk_all[0:w, cols], rim_sine, rim_cosine).astype(BF16)
        own = rotate(dk_all[w : 2 * w, cols], table_ref[0], table_ref[1]) + own_ref[:, cols]
        dk16[w : 2 * w, cols] = own.astype(BF16)
    if rows > w:
        dk16[2 * w :, :] = dk_ref[...]
    sums[...] = dot(inputs_t[...], dk16[...], 1, 0)
    piece = features // (2 * n_dp)
    dp_index = lax.axis_index("dp")
    core = lax.axis_index("seq") & 1
    for half, ref in enumerate([keep_ref, send_ref]):
        for j, relative in enumerate(bit_reversed(n_dp)):
            if piece % 16 == 0:
                block = (dp_index ^ relative) * 2 + (core ^ half)
                start = pl.multiple_of(block * piece, piece)
                ref[j * piece : (j + 1) * piece, :] = sums[pl.ds(start, piece), :].astype(BF16)
    if piece % 16:
        keep_ref[...] = sums[0 : features // 2, :].astype(BF16)
        send_ref[...] = sums[features // 2 :, :].astype(BF16)
    for kv in range(n_kv):
        out(kv).wait()


ANY = pl.BlockSpec(memory_space=pl.ANY)
HBM = pl.BlockSpec(memory_space=pltpu.HBM)
VMEM = pl.BlockSpec(memory_space=pltpu.VMEM)
SMEM = pl.BlockSpec(memory_space=pltpu.SMEM)
LIMIT = 24 * 2**20


def shared_scratch(n_kv, group, row_blocks):
    w = WINDOW
    width = n_kv * group * HEADDIM
    lanes = 2 * HEADDIM
    wide = pltpu.VMEM((row_blocks * w, width), BF16)
    return [wide, wide, wide]


def estimate(row_blocks, width, extra_flops, extra_bytes):
    w = WINDOW
    return pl.CostEstimate(
        flops=10 * row_blocks * w * 2 * w * width + extra_flops,
        bytes_accessed=6 * row_blocks * w * width + extra_bytes,
        transcendentals=row_blocks * w * w * width // HEADDIM,
    )


def local_grads(query, grad_out, keys, values, segments, positions, sinks):
    rows, width = query.shape
    kv_width = keys.shape[1]
    n_kv = kv_width // HEADDIM
    group = width // kv_width
    w = WINDOW
    lanes = 2 * HEADDIM
    row_blocks = rows // w - 1
    return pl.pallas_call(
        lambda *refs: local_kernel(n_kv, group, *refs),
        name="local_grads",
        in_specs=[HBM] * 7,
        out_specs=[HBM, VMEM, VMEM, VMEM],
        out_shape=[
            jax.ShapeDtypeStruct((rows, width), BF16),
            jax.ShapeDtypeStruct((rows - w, kv_width), BF16),
            jax.ShapeDtypeStruct((w, kv_width), F32),
            jax.ShapeDtypeStruct((2 * (row_blocks + 1), w, lanes), F32),
        ],
        scratch_shapes=shared_scratch(n_kv, group, row_blocks)
        + [
            pltpu.SMEM(sinks.shape, F32),
            pltpu.VMEM(segments.shape, jnp.int32),
            pltpu.VMEM(segments.shape, jnp.int32),
            pltpu.VMEM((rows, kv_width), BF16),
            pltpu.VMEM((rows, kv_width), BF16),
            pltpu.VMEM((row_blocks, w, w), F32),
            pltpu.VMEM((2, w, w), BF16),
            pltpu.VMEM((row_blocks, 2 * w, lanes), F32),
            pltpu.VMEM((rows, kv_width), F32),
            pltpu.SemaphoreType.DMA((5,)),
            pltpu.SemaphoreType.DMA((2, n_kv)),
            pltpu.SemaphoreType.DMA((n_kv,)),
        ]
        + attend_scratch(n_kv, group, row_blocks),
        compiler_params=pltpu.CompilerParams(vmem_limit_bytes=LIMIT),
        cost_estimate=estimate(row_blocks, width, 0, 0),
    )(sinks, segments, positions, query, grad_out, keys, values)


def rim_grads(local, query, grad_out, keys, values, layer_input, rim, segments, sinks, n_dp):
    dq, dk, own, table = local
    rows, width = query.shape
    kv_width = keys.shape[1]
    features = layer_input.shape[1]
    n_kv = kv_width // HEADDIM
    group = width // kv_width
    w = WINDOW
    lanes = 2 * HEADDIM
    return pl.pallas_call(
        lambda *refs: rim_kernel(n_kv, group, n_dp, *refs),
        name="rim_grads",
        in_specs=[VMEM] * 3 + [HBM] * 7 + [ANY, HBM],
        out_specs=[HBM, VMEM, VMEM],
        out_shape=[
            jax.ShapeDtypeStruct((rows, width), BF16),
            jax.ShapeDtypeStruct((features // 2, kv_width), BF16),
            jax.ShapeDtypeStruct((features // 2, kv_width), BF16),
        ],
        input_output_aliases={11: 0},
        scratch_shapes=shared_scratch(n_kv, group, 1)
        + [
            pltpu.SMEM(sinks.shape, F32),
            pltpu.VMEM(segments.shape, jnp.int32),
            pltpu.VMEM((w, kv_width), BF16),
            pltpu.VMEM((w, kv_width), BF16),
            pltpu.VMEM((rows, features), BF16),
            pltpu.VMEM(rim.shape, BF16),
            pltpu.VMEM((1, w, w), F32),
            pltpu.VMEM((2, w, w), BF16),
            pltpu.VMEM((1, 2 * w, lanes), F32),
            pltpu.VMEM((2 * w, kv_width), F32),
            pltpu.VMEM((rows + w, kv_width), BF16),
            pltpu.VMEM((features, rows + w), BF16),
            pltpu.VMEM((features, kv_width), F32),
            pltpu.SemaphoreType.DMA((6,)),
            pltpu.SemaphoreType.DMA((2, n_kv)),
            pltpu.SemaphoreType.DMA((n_kv,)),
        ]
        + attend_scratch(n_kv, group, 1),
        compiler_params=pltpu.CompilerParams(vmem_limit_bytes=LIMIT),
        cost_estimate=estimate(1, width, 2 * features * kv_width * (rows + w), 8 * features * kv_width),
    )(dk, own, table, sinks, segments, query, grad_out, keys, values, layer_input, rim, dq)


def tail_kernel(segs_hbm, pos_hbm, inputs_hbm, keys_hbm, values_hbm, out_ref, segs_ref, pos_ref, sem):
    w = WINDOW
    ids = load(
        [
            pltpu.make_async_copy(segs_hbm, segs_ref, sem.at[3]),
            pltpu.make_async_copy(pos_hbm, pos_ref, sem.at[4]),
        ]
    )
    rows, features = inputs_hbm.shape
    kv_width = keys_hbm.shape[1]
    copies = load(
        [
            pltpu.make_async_copy(inputs_hbm.at[rows - w :], out_ref.at[:, 0:features], sem.at[0]),
            pltpu.make_async_copy(
                keys_hbm.at[rows - w :], out_ref.at[:, features : features + kv_width], sem.at[1]
            ),
            pltpu.make_async_copy(
                values_hbm.at[rows - w :],
                out_ref.at[:, features + kv_width : features + 2 * kv_width],
                sem.at[2],
            ),
        ]
    )
    for copy in ids:
        copy.wait()
    line = iota((16, w), 0)
    segs = segs_ref[0:1, rows - w :]
    pos = pos_ref[0:1, rows - w :]
    aux = jnp.where(line == 0, segs, jnp.where(line == 1, pos >> 8, pos & 255))
    out_ref[0:16, features + 2 * kv_width :] = aux.astype(F32).astype(BF16)
    out_ref[16:, features + 2 * kv_width :] = jnp.zeros((w - 16, w), BF16)
    for copy in copies:
        copy.wait()


def last_tokens(layer_input, keys, values, segments, positions):
    width = layer_input.shape[1] + 2 * keys.shape[1] + WINDOW
    return pl.pallas_call(
        tail_kernel,
        name="last_tokens",
        in_specs=[HBM] * 5,
        out_specs=VMEM,
        out_shape=jax.ShapeDtypeStruct((WINDOW, width), BF16),
        scratch_shapes=[
            pltpu.VMEM(segments.shape, jnp.int32),
            pltpu.VMEM(segments.shape, jnp.int32),
            pltpu.SemaphoreType.DMA((5,)),
        ],
        compiler_params=pltpu.CompilerParams(vmem_limit_bytes=LIMIT),
    )(segments, positions, layer_input, keys, values)


def bit_reversed(n):
    bits = n.bit_length() - 1
    return [int(format(i, "b").zfill(bits)[::-1], 2) if bits else 0 for i in range(n)]


def exchange(part, axis, by):
    count = lax.axis_size(axis)
    return lax.ppermute(part, axis, [(i, i ^ by) for i in range(count)])


def share(total, axis, by, ways):
    rows = total.shape[0] // ways
    parts = [total[k * rows : (k + 1) * rows] for k in range(ways)]
    sends = [part.astype(BF16) for part in parts[1:]]
    got = {}
    for k in reversed(range(1, ways)):
        relative = bit_reversed(ways)[k] * by
        got[k] = exchange(sends[k - 1], axis, relative)
    total = parts[0]
    for k in range(1, ways):
        total = total + got[k].astype(F32)
    return total


def forward_one(part, axis):
    count = lax.axis_size(axis)
    return lax.ppermute(part, axis, [(i, i + 1) for i in range(count - 1)])


def body(query, keys, values, grad_out, layer_input, sinks, segments, positions):
    n_dp = lax.axis_size("dp")
    n_seq = lax.axis_size("seq")
    dp_index = lax.axis_index("dp")
    seq_index = lax.axis_index("seq")
    core = seq_index & 1
    kv_width = keys.shape[2]
    features = layer_input.shape[2]
    piece = features // (2 * n_dp)
    query, grad_out, layer_input, keys, values = [
        pltpu.with_memory_space_constraint(x[0], pltpu.HBM) for x in (query, grad_out, layer_input, keys, values)
    ]
    sinks, segments, positions = [
        pltpu.with_memory_space_constraint(x, pltpu.HBM) for x in (sinks, segments, positions)
    ]
    tail = last_tokens(layer_input, keys, values, segments, positions)
    rim = forward_one(tail, "seq")
    local = local_grads(query, grad_out, keys, values, segments, positions, sinks)
    dq, send, keep = rim_grads(
        local, query, grad_out, keys, values, layer_input, rim, segments, sinks, n_dp
    )
    if piece % 16:
        plain = jnp.concatenate([keep, send], axis=0).reshape(n_dp, 2, piece, kv_width)
        plain = jnp.take(plain, jnp.asarray(bit_reversed(n_dp), jnp.int32) ^ dp_index, axis=0)
        keep = jnp.take(plain, core, axis=1).reshape(-1, kv_width)
        send = jnp.take(plain, core ^ 1, axis=1).reshape(-1, kv_width)
    total = keep.astype(F32) + exchange(send, "seq", 1).astype(F32)
    by = 1
    while by < n_dp:
        ways = 4 if 4 * by <= n_dp else 2
        total = share(total, "dp", by, ways)
        by *= ways
    by = 2
    while by < n_seq:
        mine = total.astype(BF16)
        total = mine.astype(F32) + exchange(mine, "seq", by).astype(F32)
        by *= 2
    other = exchange(total, "seq", 1)
    pair = jnp.where(core == 0, jnp.stack([total, other]), jnp.stack([other, total]))
    return (dq[None], pair.reshape(-1, kv_width))


def solution(mesh):
    return jax.shard_map(
        body,
        mesh=mesh,
        in_specs=(
            P("dp", "seq", None),
            P("dp", "seq", None),
            P("dp", "seq", None),
            P("dp", "seq", None),
            P("dp", "seq", None),
            P(),
            P("dp", "seq"),
            P("dp", "seq"),
        ),
        out_specs=(P("dp", "seq", None), P("dp", None)),
        check_vma=False,
    )
```

```python
import jax
import jax.numpy as jnp
import numpy as np
from jax import lax
from jax.experimental import pallas as pl
from jax.experimental.pallas import tpu as pltpu
from jax.sharding import PartitionSpec as P

HEADDIM = 64
WINDOW = 128
THETA = 150000.0
LOW = -1e30

F32 = jnp.float32
BF16 = jnp.bfloat16


def dot(a, b, ca, cb):
    return lax.dot_general(a, b, (((ca,), (cb,)), ((), ())), preferred_element_type=F32)


def iota(shape, dim):
    return lax.broadcasted_iota(jnp.int32, shape, dim)


def sin_cos(angle):
    turns = jnp.floor(angle * np.float32(2.0 / np.pi) + np.float32(0.5))
    rest = angle - turns * np.float32(1.5703125)
    rest = rest - turns * np.float32(4.837512969970703125e-4)
    rest = rest - turns * np.float32(7.54978995489188216e-8)
    sq = rest * rest
    sin_part = np.float32(-1.9515295891e-4) * sq + np.float32(8.3321608736e-3)
    sin_part = (sin_part * sq + np.float32(-1.6666654611e-1)) * sq * rest + rest
    cos_part = np.float32(2.443315711809948e-5) * sq + np.float32(-1.388731625493765e-3)
    cos_part = (cos_part * sq + np.float32(4.166664568298827e-2)) * sq * sq
    cos_part = cos_part - np.float32(0.5) * sq + np.float32(1.0)
    quadrant = turns.astype(jnp.int32)
    odd = (quadrant & 1) == 1
    sine = jnp.where(odd, cos_part, sin_part)
    cosine = jnp.where(odd, sin_part, cos_part)
    sine = jnp.where((quadrant & 2) == 2, -sine, sine)
    cosine = jnp.where(((quadrant + 1) & 2) == 2, -cosine, cosine)
    return sine, cosine


def as_column(row):
    return jnp.broadcast_to(row, (row.shape[1], row.shape[1])).T


def load(copies):
    for copy in copies:
        copy.start()
    return copies


def prepare_keys(kv, blocks, keys2, values2, keys_t):
    w = WINDOW
    lanes = 2 * HEADDIM
    own_half = (iota((w, lanes), 1) < HEADDIM) == (kv % 2 == 0)
    cols = slice(kv // 2 * lanes, (kv // 2 + 1) * lanes)
    for b, (k_ref, v_ref, first_row) in enumerate(blocks):
        rows = slice(b * w, (b + 1) * w)
        k_tile = k_ref[first_row : first_row + w, cols].astype(F32) * np.float32(HEADDIM**-0.5)
        v_tile = v_ref[first_row : first_row + w, cols].astype(F32)
        k_tile = jnp.where(own_half, k_tile, np.float32(0.0))
        v_tile = jnp.where(own_half, v_tile, np.float32(0.0))
        keys2[kv, kv % 2, rows, :] = k_tile.astype(BF16)
        values2[kv, kv % 2, rows, :] = v_tile.astype(BF16)
        keys2[kv, 1 - kv % 2, rows, :] = pltpu.roll(k_tile, HEADDIM, 1).astype(BF16)
        values2[kv, 1 - kv % 2, rows, :] = pltpu.roll(v_tile, HEADDIM, 1).astype(BF16)
        half = slice(kv % 2 * HEADDIM, (kv % 2 + 1) * HEADDIM)
        keys_t[kv, :, rows] = k_tile.T[half].astype(BF16)


def attend(
    n_kv, group, row_blocks, wait_kv, beside, sinks_ref, query, grad, ds_s, bias, halves, scratch, add_dk
):
    keys2, values2, scores_s, grads_s = scratch
    w = WINDOW
    lanes = 2 * HEADDIM
    quads = group // 4
    tri = iota((w, w), 0) <= iota((w, w), 1)
    tri2 = jnp.concatenate([tri, tri], axis=1)
    items = [(b, kv, quad) for kv in range(n_kv) for b in range(row_blocks) for quad in range(quads)]

    def tiles(ref, b, kv, first, count):
        rows = slice(b * w, (b + 1) * w)
        start = kv * group // 2 + first
        return jnp.concatenate(
            [ref[rows, (start + t) * lanes : (start + t + 1) * lanes] for t in range(count)], axis=0
        )

    def to_scores(n):
        b, kv, quad = items[n]
        if b == 0 and quad == 0:
            wait_kv(kv)
        window = slice(b * w, (b + 2) * w)
        q_two = tiles(query, b, kv, 2 * quad, 2)
        g_two = tiles(grad, b, kv, 2 * quad, 2)
        bias2 = jnp.concatenate([bias[b], bias[b]], axis=1)
        for side in range(2):
            scores = dot(keys2[kv, side, window, :], q_two, 1, 1)
            scores_s[n % 2, side] = jnp.where(tri2, scores[w:], scores[:w]) + bias2
        for side in range(2):
            grads = dot(values2[kv, side, window, :], g_two, 1, 1)
            grads_s[n % 2, side] = jnp.where(tri2, grads[w:], grads[:w])

    def to_ds(n):
        b, kv, quad = items[n]
        unit = n // quads
        for side in range(2):
            for t in range(2):
                cols = slice(t * w, (t + 1) * w)
                sink = sinks_ref[kv * group + 4 * quad + 2 * t + side]
                scores = scores_s[n % 2, side, :, cols]
                peak = jnp.maximum(jnp.max(scores, axis=0, keepdims=True), sink)
                expo = jnp.exp(scores - peak)
                total = jnp.sum(expo, axis=0, keepdims=True) + jnp.exp(sink - peak)
                probs = expo * (np.float32(1.0) / total)
                grads = grads_s[n % 2, side, :, cols]
                delta = jnp.sum(probs * grads, axis=0, keepdims=True)
                ds = (probs * (grads - delta)).astype(BF16)
                out_cols = slice((2 * quad + t) * w, (2 * quad + t + 1) * w)
                ds_s[unit, side, 0:w, out_cols] = ds * halves[0]
                ds_s[unit, side, w : 2 * w, out_cols] = ds * halves[1]

    def to_grads(n):
        b, kv, quad = items[n]
        if quad == quads - 1:
            q_all = tiles(query, b, kv, 0, group // 2)
            low = iota((2 * w, lanes), 1) < HEADDIM
            sides = [dot(ds_s[n // quads, side], q_all, 1, 0) for side in range(2)]
            add_dk(b, kv, jnp.where(low, sides[0], sides[1]))

    for n in range(len(items) + 2):
        if n < len(items):
            to_scores(n)
        if 0 <= n - 1 < len(items):
            to_ds(n - 1)
        if n >= 2:
            to_grads(n - 2)
        if n < len(items):
            beside(n, len(items))


def attend_scratch(n_kv, group, row_blocks):
    w = WINDOW
    lanes = 2 * HEADDIM
    return [
        pltpu.VMEM((n_kv, 2, (row_blocks + 1) * w, lanes), BF16),
        pltpu.VMEM((n_kv, 2, (row_blocks + 1) * w, lanes), BF16),
        pltpu.VMEM((2, 2, w, 2 * w), F32),
        pltpu.VMEM((2, 2, w, 2 * w), F32),
    ]


def set_halves(halves):
    tri = iota((WINDOW, WINDOW), 0) <= iota((WINDOW, WINDOW), 1)
    halves[0] = jnp.where(tri, np.float32(0.0), np.float32(1.0)).astype(BF16)
    halves[1] = jnp.where(tri, np.float32(1.0), np.float32(0.0)).astype(BF16)


def window_bias(bias, b, prev_segs, own_segs):
    tri = iota((WINDOW, WINDOW), 0) <= iota((WINDOW, WINDOW), 1)
    key_segs = jnp.where(tri, as_column(own_segs), as_column(prev_segs))
    bias[b] = jnp.where(key_segs == own_segs, np.float32(0.0), np.float32(LOW))


def store_dk(dk_part, dk_all, first_block, b, kv, part, seen):
    w = WINDOW
    lanes = 2 * HEADDIM
    if kv % 2 == 0:
        dk_part[b] = part
        return
    even = dk_part[b]
    low = iota(part.shape, 1) < HEADDIM
    both = jnp.where(low, even, part) + pltpu.roll(jnp.where(low, part, even), HEADDIM, 1)
    cols = slice(kv // 2 * lanes, (kv // 2 + 1) * lanes)
    for k in range(2):
        rows = slice((first_block + b + k) * w, (first_block + b + k + 1) * w)
        piece = both[k * w : (k + 1) * w]
        if (first_block + b + k, kv) in seen:
            piece = piece + dk_all[rows, cols]
        seen.add((first_block + b + k, kv))
        dk_all[rows, cols] = piece


def rotate(dk, sine, cosine):
    half = HEADDIM // 2
    lanes = dk.shape[1]
    low = (iota(dk.shape, 1) % HEADDIM) < half
    other = jnp.where(low, pltpu.roll(dk, lanes - half, 1), pltpu.roll(dk, half, 1))
    return (dk * cosine + other * sine) * np.float32(HEADDIM**-0.5)


def turn_table(pos):
    half = HEADDIM // 2
    index = iota((1, 2 * HEADDIM), 1) % half
    rates = (THETA ** (-2.0 * np.arange(half) / HEADDIM)).astype(np.float32)
    freq = jnp.zeros((1, 2 * HEADDIM), F32)
    for t in range(half):
        freq = jnp.where(index == t, rates[t], freq)
    sine, cosine = sin_cos(as_column(pos.astype(F32)) * freq)
    low = (iota(sine.shape, 1) % HEADDIM) < HEADDIM // 2
    return jnp.where(low, sine, -sine), cosine


def local_kernel(
    n_kv, group, sinks_hbm, segs_hbm, pos_hbm, query_hbm, grad_hbm, keys_hbm, values_hbm, inputs_hbm,
    dk_ref, own_ref, table_ref, ds_ref, keys_t, segs0_ref, query0, grad0, keys, values, inputs,
    query, grad, sinks_ref, segs_ref, pos_ref, bias, halves, dk_part, dk_all, id_sem, in_sem, next_sem,
    *scratch,
):
    w = WINDOW
    lanes = 2 * HEADDIM
    rows = keys.shape[0]
    row_blocks = rows // w - 1
    step = group * HEADDIM
    ids = load(
        [
            pltpu.make_async_copy(pos_hbm, pos_ref, id_sem.at[3]),
            pltpu.make_async_copy(segs_hbm, segs_ref, id_sem.at[2]),
            pltpu.make_async_copy(sinks_hbm, sinks_ref, id_sem.at[4]),
        ]
    )
    key_copies = load(
        [
            pltpu.make_async_copy(keys_hbm, keys, id_sem.at[0]),
            pltpu.make_async_copy(values_hbm, values, id_sem.at[1]),
        ]
    )

    def ins(kv):
        cols = slice(kv * step, (kv + 1) * step)
        return [
            pltpu.make_async_copy(query_hbm.at[w:, cols], query.at[:, cols], in_sem.at[0, kv]),
            pltpu.make_async_copy(grad_hbm.at[w:, cols], grad.at[:, cols], in_sem.at[1, kv]),
        ]

    in_copies = [load(ins(kv)) for kv in range(n_kv)]
    next_copies = load(
        [
            pltpu.make_async_copy(query_hbm.at[0:w], query0, next_sem.at[0]),
            pltpu.make_async_copy(grad_hbm.at[0:w], grad0, next_sem.at[1]),
            pltpu.make_async_copy(inputs_hbm, inputs, next_sem.at[2]),
        ]
    )
    set_halves(halves)
    for copy in ids:
        copy.wait()
    segs = [segs_ref[0:1, b * w : (b + 1) * w].astype(F32) for b in range(row_blocks + 1)]
    segs0_ref[...] = segs[0]
    for b in range(row_blocks):
        window_bias(bias, b, segs[b], segs[b + 1])
    for b in range(row_blocks + 1):
        sine, cosine = turn_table(pos_ref[0:1, b * w : (b + 1) * w])
        table_ref[2 * b] = sine
        table_ref[2 * b + 1] = cosine
    for copy in key_copies:
        copy.wait()
    seen = set()

    def wait_kv(kv):
        blocks = [(keys, values, b * w) for b in range(row_blocks + 1)]
        prepare_keys(kv, blocks, scratch[0], scratch[1], keys_t)
        for copy in in_copies[kv]:
            copy.wait()

    attend(
        n_kv, group, row_blocks, wait_kv, lambda n, count: None,
        sinks_ref, query, grad, ds_ref, bias, halves, scratch,
        lambda b, kv, part: store_dk(dk_part, dk_all, 0, b, kv, part, seen),
    )
    for b in range(row_blocks + 1):
        for tile in range(n_kv // 2):
            cols = slice(tile * lanes, (tile + 1) * lanes)
            turned = rotate(dk_all[b * w : (b + 1) * w, cols], table_ref[2 * b], table_ref[2 * b + 1])
            if b == 0:
                own_ref[:, cols] = turned
            else:
                dk_ref[(b - 1) * w : b * w, cols] = turned.astype(BF16)
    for copy in next_copies:
        copy.wait()


def rim_kernel(
    n_kv, group, n_dp, dk_ref, own_ref, table_ref, segs0_ref, query, grad, keys, values, inputs, rim, sinks_hbm,
    send_ref, keep_ref, ds_ref, keys_t,
    sinks_ref, bias, halves, dk_part, dk_all, dk16, inputs_t, sums, sink_sem, *scratch,
):
    w = WINDOW
    lanes = 2 * HEADDIM
    rows, features = inputs.shape
    kv_width = n_kv * HEADDIM
    sink_copy = pltpu.make_async_copy(sinks_hbm, sinks_ref, sink_sem)
    sink_copy.start()
    set_halves(halves)
    rim_keys = rim.at[:, features : features + kv_width]
    rim_values = rim.at[:, features + kv_width : features + 2 * kv_width]
    aux = rim[0:16, features + 2 * kv_width :].astype(F32)
    rim_segs = jnp.where(lax.axis_index("seq") == 0, np.float32(-1.0), aux[0:1])
    window_bias(bias, 0, rim_segs, segs0_ref[...])
    rim_sine, rim_cosine = turn_table(aux[1:2] * np.float32(256.0) + aux[2:3])
    seen = set()

    def wait_kv(kv):
        blocks = [(rim_keys, rim_values, 0), (keys, values, 0)]
        prepare_keys(kv, blocks, scratch[0], scratch[1], keys_t)

    blocks = rows // w + 1
    pieces = [(f, t) for f in range(features // w) for t in range(blocks)]

    def turn_inputs(n, count):
        if n == 0:
            sink_copy.wait()
        for f, t in pieces[n * len(pieces) // count : (n + 1) * len(pieces) // count]:
            cols = slice(f * w, (f + 1) * w)
            tile = rim[:, cols] if t == 0 else inputs[(t - 1) * w : t * w, cols]
            inputs_t[cols, t * w : (t + 1) * w] = tile.T

    attend(
        n_kv, group, 1, wait_kv, turn_inputs,
        sinks_ref, query, grad, ds_ref, bias, halves, scratch,
        lambda b, kv, part: store_dk(dk_part, dk_all, 0, b, kv, part, seen),
    )
    for tile in range(n_kv // 2):
        cols = slice(tile * lanes, (tile + 1) * lanes)
        dk16[0:w, cols] = rotate(dk_all[0:w, cols], rim_sine, rim_cosine).astype(BF16)
        own = rotate(dk_all[w : 2 * w, cols], table_ref[0], table_ref[1]) + own_ref[:, cols]
        dk16[w : 2 * w, cols] = own.astype(BF16)
    if rows > w:
        dk16[2 * w :, :] = dk_ref[...]
    sums[...] = dot(inputs_t[...], dk16[...], 1, 0)
    piece = features // (2 * n_dp)
    dp_index = lax.axis_index("dp")
    core = lax.axis_index("seq") & 1
    for half, ref in enumerate([keep_ref, send_ref]):
        for j, relative in enumerate(bit_reversed(n_dp)):
            if piece % 16 == 0:
                block = (dp_index ^ relative) * 2 + (core ^ half)
                start = pl.multiple_of(block * piece, piece)
                ref[j * piece : (j + 1) * piece, :] = sums[pl.ds(start, piece), :].astype(BF16)
    if piece % 16:
        keep_ref[...] = sums[0 : features // 2, :].astype(BF16)
        send_ref[...] = sums[features // 2 :, :].astype(BF16)


def query_kernel(n_kv, group, local_ds, local_keys, rim_ds, rim_keys, dq_hbm, dq, out_sem):
    w = WINDOW
    lanes = 2 * HEADDIM
    step = group * HEADDIM
    row_blocks = local_ds.shape[0] // n_kv
    outs = []
    for block in range(row_blocks + 1):
        rows = slice(block * w, (block + 1) * w)
        for kv in range(n_kv):
            for tile in range(group // 2):
                cols = slice(tile * w, (tile + 1) * w)
                if block == 0:
                    keyt_win, ds_ref, unit = rim_keys[kv], rim_ds, kv
                else:
                    keyt_win = local_keys[kv, :, (block - 1) * w : (block + 1) * w]
                    ds_ref, unit = local_ds, kv * row_blocks + block - 1
                dq_t = [dot(keyt_win, ds_ref[unit, side, :, cols], 1, 0) for side in range(2)]
                start = kv * group // 2 + tile
                dq[rows, start * lanes : (start + 1) * lanes] = jnp.concatenate(dq_t, axis=0).T.astype(BF16)
            cols = slice(kv * step, (kv + 1) * step)
            outs += load([pltpu.make_async_copy(dq.at[rows, cols], dq_hbm.at[rows, cols], out_sem.at[block, kv])])
    for copy in outs:
        copy.wait()


ANY = pl.BlockSpec(memory_space=pl.ANY)
HBM = pl.BlockSpec(memory_space=pltpu.HBM)
VMEM = pl.BlockSpec(memory_space=pltpu.VMEM)
SMEM = pl.BlockSpec(memory_space=pltpu.SMEM)
LIMIT = 24 * 2**20


def estimate(row_blocks, width, extra_flops, extra_bytes):
    w = WINDOW
    return pl.CostEstimate(
        flops=10 * row_blocks * w * 2 * w * width + extra_flops,
        bytes_accessed=6 * row_blocks * w * width + extra_bytes,
        transcendentals=row_blocks * w * w * width // HEADDIM,
    )


def sizes(query, keys):
    width, kv_width = query.shape[-1], keys.shape[-1]
    return width, kv_width, kv_width // HEADDIM, width // kv_width


def shape(*dims, kind=BF16):
    return jax.ShapeDtypeStruct(dims, kind)


def local_grads(query, grad_out, keys, values, layer_input, segments, positions, sinks):
    rows = query.shape[0]
    width, kv_width, n_kv, group = sizes(query, keys)
    w = WINDOW
    lanes = 2 * HEADDIM
    row_blocks = rows // w - 1
    return pl.pallas_call(
        lambda *refs: local_kernel(n_kv, group, *refs),
        name="local_grads",
        in_specs=[HBM] * 8,
        out_specs=[VMEM] * 11,
        out_shape=[
            shape(rows - w, kv_width),
            shape(w, kv_width, kind=F32),
            shape(2 * (row_blocks + 1), w, lanes, kind=F32),
            shape(row_blocks * n_kv, 2, 2 * w, group // 2 * w),
            shape(n_kv, HEADDIM, rows),
            shape(1, w, kind=F32),
            shape(w, width),
            shape(w, width),
            shape(rows, kv_width),
            shape(rows, kv_width),
            shape(*layer_input.shape),
        ],
        scratch_shapes=[
            pltpu.VMEM((row_blocks * w, width), BF16),
            pltpu.VMEM((row_blocks * w, width), BF16),
            pltpu.SMEM(sinks.shape, F32),
            pltpu.VMEM(segments.shape, jnp.int32),
            pltpu.VMEM(segments.shape, jnp.int32),
            pltpu.VMEM((row_blocks, w, w), F32),
            pltpu.VMEM((2, w, w), BF16),
            pltpu.VMEM((row_blocks, 2 * w, lanes), F32),
            pltpu.VMEM((rows, kv_width), F32),
            pltpu.SemaphoreType.DMA((5,)),
            pltpu.SemaphoreType.DMA((2, n_kv)),
            pltpu.SemaphoreType.DMA((3,)),
        ]
        + attend_scratch(n_kv, group, row_blocks),
        compiler_params=pltpu.CompilerParams(vmem_limit_bytes=LIMIT),
        cost_estimate=estimate(row_blocks, width, 0, 0),
    )(sinks, segments, positions, query, grad_out, keys, values, layer_input)


def rim_grads(local, rim, sinks, n_dp):
    dk, own, table, _, _, segs0, query0, grad0, keys, values, inputs = local
    rows, features = inputs.shape
    width, kv_width, n_kv, group = sizes(query0, keys)
    w = WINDOW
    lanes = 2 * HEADDIM
    return pl.pallas_call(
        lambda *refs: rim_kernel(n_kv, group, n_dp, *refs),
        name="rim_grads",
        in_specs=[VMEM] * 10 + [HBM],
        out_specs=[VMEM] * 4,
        out_shape=[
            shape(features // 2, kv_width),
            shape(features // 2, kv_width),
            shape(n_kv, 2, 2 * w, group // 2 * w),
            shape(n_kv, HEADDIM, 2 * w),
        ],
        scratch_shapes=[
            pltpu.SMEM(sinks.shape, F32),
            pltpu.VMEM((1, w, w), F32),
            pltpu.VMEM((2, w, w), BF16),
            pltpu.VMEM((1, 2 * w, lanes), F32),
            pltpu.VMEM((2 * w, kv_width), F32),
            pltpu.VMEM((rows + w, kv_width), BF16),
            pltpu.VMEM((features, rows + w), BF16),
            pltpu.VMEM((features, kv_width), F32),
            pltpu.SemaphoreType.DMA(()),
        ]
        + attend_scratch(n_kv, group, 1),
        compiler_params=pltpu.CompilerParams(vmem_limit_bytes=LIMIT),
        cost_estimate=estimate(1, width, 2 * features * kv_width * (rows + w), 8 * features * kv_width),
    )(dk, own, table, segs0, query0, grad0, keys, values, inputs, rim, sinks)


def query_grads(local_ds, local_keys, rim_ds, rim_keys, group):
    n_kv, _, rows = local_keys.shape
    width = n_kv * group * HEADDIM
    w = WINDOW
    return pl.pallas_call(
        lambda *refs: query_kernel(n_kv, group, *refs),
        name="query_grads",
        in_specs=[VMEM] * 4,
        out_specs=HBM,
        out_shape=shape(rows, width),
        scratch_shapes=[pltpu.VMEM((rows, width), BF16), pltpu.SemaphoreType.DMA((rows // w, n_kv))],
        compiler_params=pltpu.CompilerParams(vmem_limit_bytes=LIMIT),
        cost_estimate=pl.CostEstimate(
            flops=4 * rows * w * width, bytes_accessed=2 * rows * width + 4 * rows * w * width // HEADDIM, transcendentals=0
        ),
    )(local_ds, local_keys, rim_ds, rim_keys)


def tail_kernel(segs_hbm, pos_hbm, inputs_hbm, keys_hbm, values_hbm, out_ref, segs_ref, pos_ref, sem):
    w = WINDOW
    ids = load(
        [
            pltpu.make_async_copy(segs_hbm, segs_ref, sem.at[3]),
            pltpu.make_async_copy(pos_hbm, pos_ref, sem.at[4]),
        ]
    )
    rows, features = inputs_hbm.shape
    kv_width = keys_hbm.shape[1]
    copies = load(
        [
            pltpu.make_async_copy(inputs_hbm.at[rows - w :], out_ref.at[:, 0:features], sem.at[0]),
            pltpu.make_async_copy(
                keys_hbm.at[rows - w :], out_ref.at[:, features : features + kv_width], sem.at[1]
            ),
            pltpu.make_async_copy(
                values_hbm.at[rows - w :],
                out_ref.at[:, features + kv_width : features + 2 * kv_width],
                sem.at[2],
            ),
        ]
    )
    for copy in ids:
        copy.wait()
    line = iota((16, w), 0)
    segs = segs_ref[0:1, rows - w :]
    pos = pos_ref[0:1, rows - w :]
    aux = jnp.where(line == 0, segs, jnp.where(line == 1, pos >> 8, pos & 255))
    out_ref[0:16, features + 2 * kv_width :] = aux.astype(F32).astype(BF16)
    out_ref[16:, features + 2 * kv_width :] = jnp.zeros((w - 16, w), BF16)
    for copy in copies:
        copy.wait()


def last_tokens(layer_input, keys, values, segments, positions):
    width = layer_input.shape[1] + 2 * keys.shape[1] + WINDOW
    return pl.pallas_call(
        tail_kernel,
        name="last_tokens",
        in_specs=[HBM] * 5,
        out_specs=VMEM,
        out_shape=jax.ShapeDtypeStruct((WINDOW, width), BF16),
        scratch_shapes=[
            pltpu.VMEM(segments.shape, jnp.int32),
            pltpu.VMEM(segments.shape, jnp.int32),
            pltpu.SemaphoreType.DMA((5,)),
        ],
        compiler_params=pltpu.CompilerParams(vmem_limit_bytes=LIMIT),
    )(segments, positions, layer_input, keys, values)


def bit_reversed(n):
    bits = n.bit_length() - 1
    return [int(format(i, "b").zfill(bits)[::-1], 2) if bits else 0 for i in range(n)]


def exchange(part, axis, by):
    count = lax.axis_size(axis)
    return lax.ppermute(part, axis, [(i, i ^ by) for i in range(count)])


def share(total, axis, by, ways, beside=None, held=None):
    rows = total.shape[0] // ways
    parts = [total[k * rows : (k + 1) * rows] for k in range(ways)]
    sends = [part.astype(BF16) for part in parts[1:]]
    if beside is not None:
        sends, held = lax.optimization_barrier((sends, held))
        extra = beside(held)
    got = {}
    for k in reversed(range(1, ways)):
        relative = bit_reversed(ways)[k] * by
        got[k] = exchange(sends[k - 1], axis, relative)
    if beside is not None:
        got, extra = lax.optimization_barrier((got, extra))
    total = parts[0]
    for k in range(1, ways):
        total = total + got[k].astype(F32)
    return total if beside is None else (total, extra)


def forward_one(part, axis):
    count = lax.axis_size(axis)
    return lax.ppermute(part, axis, [(i, i + 1) for i in range(count - 1)])


def body(query, keys, values, grad_out, layer_input, sinks, segments, positions):
    n_dp = lax.axis_size("dp")
    n_seq = lax.axis_size("seq")
    dp_index = lax.axis_index("dp")
    seq_index = lax.axis_index("seq")
    core = seq_index & 1
    kv_width = keys.shape[2]
    features = layer_input.shape[2]
    piece = features // (2 * n_dp)
    query, grad_out, layer_input, keys, values = [
        pltpu.with_memory_space_constraint(x[0], pltpu.HBM) for x in (query, grad_out, layer_input, keys, values)
    ]
    sinks, segments, positions = [
        pltpu.with_memory_space_constraint(x, pltpu.HBM) for x in (sinks, segments, positions)
    ]
    tail = last_tokens(layer_input, keys, values, segments, positions)
    rim = forward_one(tail, "seq")
    local = local_grads(query, grad_out, keys, values, layer_input, segments, positions, sinks)
    send, keep, rim_ds, rim_keys = rim_grads(local, rim, sinks, n_dp)
    if piece % 16:
        plain = jnp.concatenate([keep, send], axis=0).reshape(n_dp, 2, piece, kv_width)
        plain = jnp.take(plain, jnp.asarray(bit_reversed(n_dp), jnp.int32) ^ dp_index, axis=0)
        keep = jnp.take(plain, core, axis=1).reshape(-1, kv_width)
        send = jnp.take(plain, core ^ 1, axis=1).reshape(-1, kv_width)
    total = keep.astype(F32) + exchange(send, "seq", 1).astype(F32)
    group = query.shape[1] // kv_width

    def beside(held):
        return query_grads(*held, group)

    held = (local[3], local[4], rim_ds, rim_keys)
    dq = None if n_dp > 1 else beside(held)
    by = 1
    while by < n_dp:
        ways = 4 if 4 * by <= n_dp else 2
        if by == 1:
            total, dq = share(total, "dp", by, ways, beside, held)
        else:
            total = share(total, "dp", by, ways)
        by *= ways
    by = 2
    while by < n_seq:
        mine = total.astype(BF16)
        total = mine.astype(F32) + exchange(mine, "seq", by).astype(F32)
        by *= 2
    other = exchange(total, "seq", 1)
    pair = jnp.where(core == 0, jnp.stack([total, other]), jnp.stack([other, total]))
    return (dq[None], pair.reshape(-1, kv_width))


def solution(mesh):
    return jax.shard_map(
        body,
        mesh=mesh,
        in_specs=(
            P("dp", "seq", None),
            P("dp", "seq", None),
            P("dp", "seq", None),
            P("dp", "seq", None),
            P("dp", "seq", None),
            P(),
            P("dp", "seq"),
            P("dp", "seq"),
        ),
        out_specs=(P("dp", "seq", None), P("dp", None)),
        check_vma=False,
    )
```

```python
import jax
import jax.numpy as jnp
import numpy as np
from jax import lax
from jax.experimental import pallas as pl
from jax.experimental.pallas import tpu as pltpu
from jax.sharding import PartitionSpec as P

HEADDIM = 64
WINDOW = 128
THETA = 150000.0
LOW = -1e30

F32 = jnp.float32
BF16 = jnp.bfloat16


def dot(a, b, ca, cb):
    return lax.dot_general(a, b, (((ca,), (cb,)), ((), ())), preferred_element_type=F32)


def iota(shape, dim):
    return lax.broadcasted_iota(jnp.int32, shape, dim)


def sin_cos(angle):
    turns = jnp.floor(angle * np.float32(2.0 / np.pi) + np.float32(0.5))
    rest = angle - turns * np.float32(1.5703125)
    rest = rest - turns * np.float32(4.837512969970703125e-4)
    rest = rest - turns * np.float32(7.54978995489188216e-8)
    sq = rest * rest
    sin_part = np.float32(-1.9515295891e-4) * sq + np.float32(8.3321608736e-3)
    sin_part = (sin_part * sq + np.float32(-1.6666654611e-1)) * sq * rest + rest
    cos_part = np.float32(2.443315711809948e-5) * sq + np.float32(-1.388731625493765e-3)
    cos_part = (cos_part * sq + np.float32(4.166664568298827e-2)) * sq * sq
    cos_part = cos_part - np.float32(0.5) * sq + np.float32(1.0)
    quadrant = turns.astype(jnp.int32)
    odd = (quadrant & 1) == 1
    sine = jnp.where(odd, cos_part, sin_part)
    cosine = jnp.where(odd, sin_part, cos_part)
    sine = jnp.where((quadrant & 2) == 2, -sine, sine)
    cosine = jnp.where(((quadrant + 1) & 2) == 2, -cosine, cosine)
    return sine, cosine


def as_column(row):
    return jnp.broadcast_to(row, (row.shape[1], row.shape[1])).T


def load(copies):
    for copy in copies:
        copy.start()
    return copies


def prepare_keys(kv, blocks, keys2, values2, keys_t):
    w = WINDOW
    lanes = 2 * HEADDIM
    own_half = (iota((w, lanes), 1) < HEADDIM) == (kv % 2 == 0)
    cols = slice(kv // 2 * lanes, (kv // 2 + 1) * lanes)
    for b, (k_ref, v_ref, first_row) in enumerate(blocks):
        rows = slice(b * w, (b + 1) * w)
        k_tile = k_ref[first_row : first_row + w, cols].astype(F32) * np.float32(HEADDIM**-0.5)
        v_tile = v_ref[first_row : first_row + w, cols].astype(F32)
        k_tile = jnp.where(own_half, k_tile, np.float32(0.0))
        v_tile = jnp.where(own_half, v_tile, np.float32(0.0))
        keys2[kv, kv % 2, rows, :] = k_tile.astype(BF16)
        values2[kv, kv % 2, rows, :] = v_tile.astype(BF16)
        keys2[kv, 1 - kv % 2, rows, :] = pltpu.roll(k_tile, HEADDIM, 1).astype(BF16)
        values2[kv, 1 - kv % 2, rows, :] = pltpu.roll(v_tile, HEADDIM, 1).astype(BF16)
        half = slice(kv % 2 * HEADDIM, (kv % 2 + 1) * HEADDIM)
        keys_t[kv, :, rows] = k_tile.T[half].astype(BF16)


def attend(
    n_kv, group, row_blocks, window_of, beside, sink_rows, query, grad, ds_s, bias, halves, scratch, add_dk
):
    scores_s, grads_s = scratch
    w = WINDOW
    lanes = 2 * HEADDIM
    quads = group // 4
    tri = iota((w, w), 0) <= iota((w, w), 1)
    tri2 = jnp.concatenate([tri, tri], axis=1)
    items = [(b, kv, quad) for kv in range(n_kv) for b in range(row_blocks) for quad in range(quads)]

    def tiles(ref, b, kv, first, count):
        rows = slice(b * w, (b + 1) * w)
        start = kv * group // 2 + first
        return jnp.concatenate(
            [ref[rows, (start + t) * lanes : (start + t + 1) * lanes] for t in range(count)], axis=0
        )

    def to_scores(n):
        b, kv, quad = items[n]
        key_win, value_win = window_of(b, kv, quad == 0)
        q_two = tiles(query, b, kv, 2 * quad, 2)
        g_two = tiles(grad, b, kv, 2 * quad, 2)
        bias2 = jnp.concatenate([bias[b], bias[b]], axis=1)
        for side in range(2):
            scores = dot(key_win[side], q_two, 1, 1)
            scores_s[n % 2, side] = jnp.where(tri2, scores[w:], scores[:w]) + bias2
        for side in range(2):
            grads = dot(value_win[side], g_two, 1, 1)
            grads_s[n % 2, side] = jnp.where(tri2, grads[w:], grads[:w])

    def to_ds(n):
        b, kv, quad = items[n]
        unit = n // quads
        for side in range(2):
            for t in range(2):
                cols = slice(t * w, (t + 1) * w)
                head = kv * group + 4 * quad + 2 * t + side
                sink = sink_rows[head : head + 1, :]
                scores = scores_s[n % 2, side, :, cols]
                peak = jnp.maximum(jnp.max(scores, axis=0, keepdims=True), sink)
                expo = jnp.exp(scores - peak)
                total = jnp.sum(expo, axis=0, keepdims=True) + jnp.exp(sink - peak)
                probs = expo * (np.float32(1.0) / total)
                grads = grads_s[n % 2, side, :, cols]
                delta = jnp.sum(probs * grads, axis=0, keepdims=True)
                ds = (probs * (grads - delta)).astype(BF16)
                out_cols = slice((2 * quad + t) * w, (2 * quad + t + 1) * w)
                ds_s[unit, side, 0:w, out_cols] = ds * halves[0]
                ds_s[unit, side, w : 2 * w, out_cols] = ds * halves[1]

    def to_grads(n):
        b, kv, quad = items[n]
        if quad == quads - 1:
            q_all = tiles(query, b, kv, 0, group // 2)
            low = iota((2 * w, lanes), 1) < HEADDIM
            sides = [dot(ds_s[n // quads, side], q_all, 1, 0) for side in range(2)]
            add_dk(b, kv, jnp.where(low, sides[0], sides[1]))

    for n in range(len(items) + 2):
        if n < len(items):
            to_scores(n)
        if 0 <= n - 1 < len(items):
            to_ds(n - 1)
        if n >= 2:
            to_grads(n - 2)
        if n < len(items):
            beside(n, len(items))


def attend_scratch():
    w = WINDOW
    return [
        pltpu.VMEM((2, 2, w, 2 * w), F32),
        pltpu.VMEM((2, 2, w, 2 * w), F32),
    ]


def set_halves(halves):
    tri = iota((WINDOW, WINDOW), 0) <= iota((WINDOW, WINDOW), 1)
    halves[0] = jnp.where(tri, np.float32(0.0), np.float32(1.0)).astype(BF16)
    halves[1] = jnp.where(tri, np.float32(1.0), np.float32(0.0)).astype(BF16)


def window_bias(bias, b, prev_segs, own_segs):
    tri = iota((WINDOW, WINDOW), 0) <= iota((WINDOW, WINDOW), 1)
    key_segs = jnp.where(tri, as_column(own_segs), as_column(prev_segs))
    bias[b] = jnp.where(key_segs == own_segs, np.float32(0.0), np.float32(LOW))


def store_dk(dk_part, dk_all, first_block, b, kv, part, seen):
    w = WINDOW
    lanes = 2 * HEADDIM
    if kv % 2 == 0:
        dk_part[b] = part
        return
    even = dk_part[b]
    low = iota(part.shape, 1) < HEADDIM
    both = jnp.where(low, even, part) + pltpu.roll(jnp.where(low, part, even), HEADDIM, 1)
    cols = slice(kv // 2 * lanes, (kv // 2 + 1) * lanes)
    for k in range(2):
        rows = slice((first_block + b + k) * w, (first_block + b + k + 1) * w)
        piece = both[k * w : (k + 1) * w]
        if (first_block + b + k, kv) in seen:
            piece = piece + dk_all[rows, cols]
        seen.add((first_block + b + k, kv))
        dk_all[rows, cols] = piece


def rotate(dk, sine, cosine):
    half = HEADDIM // 2
    lanes = dk.shape[1]
    low = (iota(dk.shape, 1) % HEADDIM) < half
    other = jnp.where(low, pltpu.roll(dk, lanes - half, 1), pltpu.roll(dk, half, 1))
    return (dk * cosine + other * sine) * np.float32(HEADDIM**-0.5)


def turn_table(pos):
    half = HEADDIM // 2
    index = iota((1, 2 * HEADDIM), 1) % half
    rates = (THETA ** (-2.0 * np.arange(half) / HEADDIM)).astype(np.float32)
    freq = jnp.zeros((1, 2 * HEADDIM), F32)
    for t in range(half):
        freq = jnp.where(index == t, rates[t], freq)
    sine, cosine = sin_cos(as_column(pos.astype(F32)) * freq)
    low = (iota(sine.shape, 1) % HEADDIM) < HEADDIM // 2
    return jnp.where(low, sine, -sine), cosine


def local_kernel(
    n_kv, group, sinks_hbm, segs_hbm, pos_hbm, query_hbm, grad_hbm, keys_hbm, values_hbm, inputs_hbm,
    own_ref, table_ref, ds_ref, keys_t, segs0_ref, query0, grad0, keys2, values2, inputs_t, later_ref, sink_rows,
    query, grad, keys, values, inputs, dk_ref, sinks_ref, segs_ref, pos_ref, bias, halves, dk_part, dk_all, id_sem, in_sem, next_sem,
    *scratch,
):
    w = WINDOW
    lanes = 2 * HEADDIM
    rows = keys.shape[0]
    row_blocks = rows // w - 1
    step = group * HEADDIM
    ids = load(
        [
            pltpu.make_async_copy(pos_hbm, pos_ref, id_sem.at[3]),
            pltpu.make_async_copy(segs_hbm, segs_ref, id_sem.at[2]),
            pltpu.make_async_copy(sinks_hbm, sinks_ref, id_sem.at[4]),
        ]
    )
    key_copies = load(
        [
            pltpu.make_async_copy(keys_hbm, keys, id_sem.at[0]),
            pltpu.make_async_copy(values_hbm, values, id_sem.at[1]),
        ]
    )

    def ins(kv):
        cols = slice(kv * step, (kv + 1) * step)
        return [
            pltpu.make_async_copy(query_hbm.at[w:, cols], query.at[:, cols], in_sem.at[0, kv]),
            pltpu.make_async_copy(grad_hbm.at[w:, cols], grad.at[:, cols], in_sem.at[1, kv]),
        ]

    in_copies = [load(ins(kv)) for kv in range(n_kv)]
    next_copies = load(
        [
            pltpu.make_async_copy(query_hbm.at[0:w], query0, next_sem.at[0]),
            pltpu.make_async_copy(grad_hbm.at[0:w], grad0, next_sem.at[1]),
            pltpu.make_async_copy(inputs_hbm, inputs, next_sem.at[2]),
        ]
    )
    set_halves(halves)
    for copy in ids:
        copy.wait()
    for head in range(n_kv * group):
        sink_rows[head : head + 1, :] = jnp.full((1, w), sinks_ref[head], F32)
    segs = [segs_ref[0:1, b * w : (b + 1) * w].astype(F32) for b in range(row_blocks + 1)]
    segs0_ref[...] = segs[0]
    for b in range(row_blocks):
        window_bias(bias, b, segs[b], segs[b + 1])
    for b in range(row_blocks + 1):
        sine, cosine = turn_table(pos_ref[0:1, b * w : (b + 1) * w])
        table_ref[2 * b] = sine
        table_ref[2 * b + 1] = cosine
    for copy in key_copies:
        copy.wait()
    seen = set()

    def window_of(b, kv, first):
        if b == 0 and first:
            prepare_keys(kv, [(keys, values, b * w) for b in range(row_blocks + 1)], keys2, values2, keys_t)
            for copy in in_copies[kv]:
                copy.wait()
        window = slice(b * w, (b + 2) * w)
        return [keys2[kv, side, window, :] for side in range(2)], [values2[kv, side, window, :] for side in range(2)]

    features = inputs.shape[1]
    pieces = [(f, t) for f in range(features // w) for t in range(row_blocks + 1)]

    def turn_inputs(n, count):
        if n == 1:
            next_copies[2].wait()
        n, count = n - 1, count - 1
        for f, t in pieces[n * len(pieces) // count : (n + 1) * len(pieces) // count] if n >= 0 else []:
            cols = slice(f * w, (f + 1) * w)
            inputs_t[cols, t * w : (t + 1) * w] = inputs[t * w : (t + 1) * w, cols].T

    attend(
        n_kv, group, row_blocks, window_of, turn_inputs,
        sink_rows, query, grad, ds_ref, bias, halves, scratch,
        lambda b, kv, part: store_dk(dk_part, dk_all, 0, b, kv, part, seen),
    )
    for b in range(row_blocks + 1):
        for tile in range(n_kv // 2):
            cols = slice(tile * lanes, (tile + 1) * lanes)
            turned = rotate(dk_all[b * w : (b + 1) * w, cols], table_ref[2 * b], table_ref[2 * b + 1])
            if b == 0:
                own_ref[:, cols] = turned
            else:
                dk_ref[(b - 1) * w : b * w, cols] = turned.astype(BF16)
    later_ref[...] = dot(inputs_t[:, w:], dk_ref[...], 1, 0)
    for copy in next_copies[:2]:
        copy.wait()


def rim_kernel(
    n_kv, group, n_dp, own_ref, table_ref, segs0_ref, query, grad, own_keys2, own_values2, own_inputs_t, later_ref,
    sink_rows, rim,
    send_ref, keep_ref, ds_ref, keys_t,
    keys2, values2, bias, halves, dk_part, dk_all, dk16, inputs_t, sums, *scratch,
):
    w = WINDOW
    lanes = 2 * HEADDIM
    features = own_inputs_t.shape[0]
    kv_width = n_kv * HEADDIM
    set_halves(halves)
    rim_keys = rim.at[:, features : features + kv_width]
    rim_values = rim.at[:, features + kv_width : features + 2 * kv_width]
    aux = rim[0:16, features + 2 * kv_width :].astype(F32)
    rim_segs = jnp.where(lax.axis_index("seq") == 0, np.float32(-1.0), aux[0:1])
    window_bias(bias, 0, rim_segs, segs0_ref[...])
    rim_sine, rim_cosine = turn_table(aux[1:2] * np.float32(256.0) + aux[2:3])
    seen = set()

    def window_of(b, kv, first):
        if first:
            prepare_keys(kv, [(rim_keys, rim_values, 0)], keys2, values2, keys_t)
        both = [(keys2, own_keys2), (values2, own_values2)]
        return [
            [jnp.concatenate([rim2[kv, side], own2[kv, side, 0:w]], axis=0) for side in range(2)]
            for rim2, own2 in both
        ]

    tiles = features // w

    def turn_inputs(n, count):
        for f in range(n * tiles // count, (n + 1) * tiles // count):
            cols = slice(f * w, (f + 1) * w)
            inputs_t[cols, 0:w] = rim[:, cols].T
            inputs_t[cols, w : 2 * w] = own_inputs_t[cols, 0:w]

    attend(
        n_kv, group, 1, window_of, turn_inputs,
        sink_rows, query, grad, ds_ref, bias, halves, scratch,
        lambda b, kv, part: store_dk(dk_part, dk_all, 0, b, kv, part, seen),
    )
    for tile in range(n_kv // 2):
        cols = slice(tile * lanes, (tile + 1) * lanes)
        dk16[0:w, cols] = rotate(dk_all[0:w, cols], rim_sine, rim_cosine).astype(BF16)
        own = rotate(dk_all[w : 2 * w, cols], table_ref[0], table_ref[1]) + own_ref[:, cols]
        dk16[w : 2 * w, cols] = own.astype(BF16)
    sums[...] = dot(inputs_t[...], dk16[...], 1, 0) + later_ref[...]
    piece = features // (2 * n_dp)
    dp_index = lax.axis_index("dp")
    core = lax.axis_index("seq") & 1
    for half, ref in enumerate([keep_ref, send_ref]):
        for j, relative in enumerate(bit_reversed(n_dp)):
            if piece % 16 == 0:
                side = core ^ half
                block = (dp_index ^ (relative + side * (swapped(relative, n_dp) - relative))) * 2 + side
                start = pl.multiple_of(block * piece, piece)
                ref[j * piece : (j + 1) * piece, :] = sums[pl.ds(start, piece), :].astype(BF16)
    if piece % 16:
        keep_ref[...] = sums[0 : features // 2, :].astype(BF16)
        send_ref[...] = sums[features // 2 :, :].astype(BF16)


def query_kernel(n_kv, group, local_ds, local_keys, rim_ds, rim_keys, dq_hbm, dq, out_sem):
    w = WINDOW
    lanes = 2 * HEADDIM
    step = group * HEADDIM
    row_blocks = local_ds.shape[0] // n_kv
    outs = []
    for block in range(row_blocks + 1):
        rows = slice(block * w, (block + 1) * w)
        for kv in range(n_kv):
            for tile in range(group // 2):
                cols = slice(tile * w, (tile + 1) * w)
                if block == 0:
                    keyt_win = jnp.concatenate([rim_keys[kv], local_keys[kv, :, 0:w]], axis=1)
                    ds_ref, unit = rim_ds, kv
                else:
                    keyt_win = local_keys[kv, :, (block - 1) * w : (block + 1) * w]
                    ds_ref, unit = local_ds, kv * row_blocks + block - 1
                dq_t = [dot(keyt_win, ds_ref[unit, side, :, cols], 1, 0) for side in range(2)]
                start = kv * group // 2 + tile
                dq[rows, start * lanes : (start + 1) * lanes] = jnp.concatenate(dq_t, axis=0).T.astype(BF16)
            cols = slice(kv * step, (kv + 1) * step)
            outs += load([pltpu.make_async_copy(dq.at[rows, cols], dq_hbm.at[rows, cols], out_sem.at[block, kv])])
    for copy in outs:
        copy.wait()


ANY = pl.BlockSpec(memory_space=pl.ANY)
HBM = pl.BlockSpec(memory_space=pltpu.HBM)
VMEM = pl.BlockSpec(memory_space=pltpu.VMEM)
SMEM = pl.BlockSpec(memory_space=pltpu.SMEM)
LIMIT = 24 * 2**20


def estimate(row_blocks, width, extra_flops, extra_bytes):
    w = WINDOW
    return pl.CostEstimate(
        flops=10 * row_blocks * w * 2 * w * width + extra_flops,
        bytes_accessed=6 * row_blocks * w * width + extra_bytes,
        transcendentals=row_blocks * w * w * width // HEADDIM,
    )


def sizes(query, keys):
    width, kv_width = query.shape[-1], keys.shape[-1]
    return width, kv_width, kv_width // HEADDIM, width // kv_width


def shape(*dims, kind=BF16):
    return jax.ShapeDtypeStruct(dims, kind)


def local_grads(query, grad_out, keys, values, layer_input, segments, positions, sinks):
    rows, features = layer_input.shape
    width, kv_width, n_kv, group = sizes(query, keys)
    w = WINDOW
    lanes = 2 * HEADDIM
    row_blocks = rows // w - 1
    return pl.pallas_call(
        lambda *refs: local_kernel(n_kv, group, *refs),
        name="local_grads",
        in_specs=[HBM] * 8,
        out_specs=[VMEM] * 12,
        out_shape=[
            shape(w, kv_width, kind=F32),
            shape(2 * (row_blocks + 1), w, lanes, kind=F32),
            shape(row_blocks * n_kv, 2, 2 * w, group // 2 * w),
            shape(n_kv, HEADDIM, rows),
            shape(1, w, kind=F32),
            shape(w, width),
            shape(w, width),
            shape(n_kv, 2, rows, lanes),
            shape(n_kv, 2, rows, lanes),
            shape(features, rows),
            shape(features, kv_width, kind=F32),
            shape(n_kv * group, w, kind=F32),
        ],
        scratch_shapes=[
            pltpu.VMEM((row_blocks * w, width), BF16),
            pltpu.VMEM((row_blocks * w, width), BF16),
            pltpu.VMEM((rows, kv_width), BF16),
            pltpu.VMEM((rows, kv_width), BF16),
            pltpu.VMEM(layer_input.shape, BF16),
            pltpu.VMEM((rows - w, kv_width), BF16),
            pltpu.SMEM(sinks.shape, F32),
            pltpu.VMEM(segments.shape, jnp.int32),
            pltpu.VMEM(segments.shape, jnp.int32),
            pltpu.VMEM((row_blocks, w, w), F32),
            pltpu.VMEM((2, w, w), BF16),
            pltpu.VMEM((row_blocks, 2 * w, lanes), F32),
            pltpu.VMEM((rows, kv_width), F32),
            pltpu.SemaphoreType.DMA((5,)),
            pltpu.SemaphoreType.DMA((2, n_kv)),
            pltpu.SemaphoreType.DMA((3,)),
        ]
        + attend_scratch(),
        compiler_params=pltpu.CompilerParams(vmem_limit_bytes=LIMIT),
        cost_estimate=estimate(row_blocks, width, 0, 0),
    )(sinks, segments, positions, query, grad_out, keys, values, layer_input)


def rim_grads(local, rim, kv_width, n_dp):
    own, table, _, _, segs0, query0, grad0, keys2, values2, inputs_t, later, sink_rows = local
    features, rows = inputs_t.shape
    width = query0.shape[1]
    n_kv = kv_width // HEADDIM
    group = width // kv_width
    w = WINDOW
    lanes = 2 * HEADDIM
    return pl.pallas_call(
        lambda *refs: rim_kernel(n_kv, group, n_dp, *refs),
        name="rim_grads",
        in_specs=[VMEM] * 11,
        out_specs=[VMEM] * 4,
        out_shape=[
            shape(features // 2, kv_width),
            shape(features // 2, kv_width),
            shape(n_kv, 2, 2 * w, group // 2 * w),
            shape(n_kv, HEADDIM, w),
        ],
        scratch_shapes=[
            pltpu.VMEM((n_kv, 2, w, lanes), BF16),
            pltpu.VMEM((n_kv, 2, w, lanes), BF16),
            pltpu.VMEM((1, w, w), F32),
            pltpu.VMEM((2, w, w), BF16),
            pltpu.VMEM((1, 2 * w, lanes), F32),
            pltpu.VMEM((2 * w, kv_width), F32),
            pltpu.VMEM((2 * w, kv_width), BF16),
            pltpu.VMEM((features, 2 * w), BF16),
            pltpu.VMEM((features, kv_width), F32),
        ]
        + attend_scratch(),
        compiler_params=pltpu.CompilerParams(vmem_limit_bytes=LIMIT),
        cost_estimate=estimate(1, width, 2 * features * kv_width * 2 * w, 8 * features * kv_width),
    )(own, table, segs0, query0, grad0, keys2, values2, inputs_t, later, sink_rows, rim)


def query_grads(local_ds, local_keys, rim_ds, rim_keys, group):
    n_kv, _, rows = local_keys.shape
    width = n_kv * group * HEADDIM
    w = WINDOW
    return pl.pallas_call(
        lambda *refs: query_kernel(n_kv, group, *refs),
        name="query_grads",
        in_specs=[VMEM] * 4,
        out_specs=HBM,
        out_shape=shape(rows, width),
        scratch_shapes=[pltpu.VMEM((rows, width), BF16), pltpu.SemaphoreType.DMA((rows // w, n_kv))],
        compiler_params=pltpu.CompilerParams(vmem_limit_bytes=LIMIT),
        cost_estimate=pl.CostEstimate(
            flops=4 * rows * w * width, bytes_accessed=2 * rows * width + 4 * rows * w * width // HEADDIM, transcendentals=0
        ),
    )(local_ds, local_keys, rim_ds, rim_keys)


def tail_kernel(segs_hbm, pos_hbm, inputs_hbm, keys_hbm, values_hbm, out_ref, segs_ref, pos_ref, sem):
    w = WINDOW
    ids = load(
        [
            pltpu.make_async_copy(segs_hbm, segs_ref, sem.at[3]),
            pltpu.make_async_copy(pos_hbm, pos_ref, sem.at[4]),
        ]
    )
    rows, features = inputs_hbm.shape
    kv_width = keys_hbm.shape[1]
    copies = load(
        [
            pltpu.make_async_copy(inputs_hbm.at[rows - w :], out_ref.at[:, 0:features], sem.at[0]),
            pltpu.make_async_copy(
                keys_hbm.at[rows - w :], out_ref.at[:, features : features + kv_width], sem.at[1]
            ),
            pltpu.make_async_copy(
                values_hbm.at[rows - w :],
                out_ref.at[:, features + kv_width : features + 2 * kv_width],
                sem.at[2],
            ),
        ]
    )
    for copy in ids:
        copy.wait()
    line = iota((16, w), 0)
    segs = segs_ref[0:1, rows - w :]
    pos = pos_ref[0:1, rows - w :]
    aux = jnp.where(line == 0, segs, jnp.where(line == 1, pos >> 8, pos & 255))
    out_ref[0:16, features + 2 * kv_width :] = aux.astype(F32).astype(BF16)
    out_ref[16:, features + 2 * kv_width :] = jnp.zeros((w - 16, w), BF16)
    for copy in copies:
        copy.wait()


def last_tokens(layer_input, keys, values, segments, positions):
    width = layer_input.shape[1] + 2 * keys.shape[1] + WINDOW
    return pl.pallas_call(
        tail_kernel,
        name="last_tokens",
        in_specs=[HBM] * 5,
        out_specs=VMEM,
        out_shape=jax.ShapeDtypeStruct((WINDOW, width), BF16),
        scratch_shapes=[
            pltpu.VMEM(segments.shape, jnp.int32),
            pltpu.VMEM(segments.shape, jnp.int32),
            pltpu.SemaphoreType.DMA((5,)),
        ],
        compiler_params=pltpu.CompilerParams(vmem_limit_bytes=LIMIT),
    )(segments, positions, layer_input, keys, values)


def swapped(relative, n):
    return relative if n < 4 else (relative & ~3) | (relative & 1) << 1 | (relative & 2) >> 1


def bit_reversed(n):
    bits = n.bit_length() - 1
    return [int(format(i, "b").zfill(bits)[::-1], 2) if bits else 0 for i in range(n)]


def exchange(part, axis, by):
    count = lax.axis_size(axis)
    return lax.ppermute(part, axis, [(i, i ^ by) for i in range(count)])


def exchange_by_core(part, relative):
    n_dp, n_seq = lax.axis_size("dp"), lax.axis_size("seq")
    pairs = []
    for d in range(n_dp):
        for q in range(n_seq):
            other = d ^ (swapped(relative, n_dp) if q % 2 else relative)
            pairs.append((d * n_seq + q, other * n_seq + q))
    return lax.ppermute(part, ("dp", "seq"), pairs)


def share(total, by, ways, beside=None, held=None):
    rows = total.shape[0] // ways
    parts = [total[k * rows : (k + 1) * rows] for k in range(ways)]
    sends = [part.astype(BF16) for part in parts[1:]]
    if beside is not None:
        sends, held = lax.optimization_barrier((sends, held))
        extra = beside(held)
    got = {}
    for k in reversed(range(1, ways)):
        relative = bit_reversed(ways)[k] * by
        got[k] = exchange_by_core(sends[k - 1], relative)
    if beside is not None:
        got, extra = lax.optimization_barrier((got, extra))
    total = parts[0]
    for k in range(1, ways):
        total = total + got[k].astype(F32)
    return total if beside is None else (total, extra)


def forward_one(part, axis):
    count = lax.axis_size(axis)
    return lax.ppermute(part, axis, [(i, i + 1) for i in range(count - 1)])


def body(query, keys, values, grad_out, layer_input, sinks, segments, positions):
    n_dp = lax.axis_size("dp")
    n_seq = lax.axis_size("seq")
    dp_index = lax.axis_index("dp")
    seq_index = lax.axis_index("seq")
    core = seq_index & 1
    kv_width = keys.shape[2]
    features = layer_input.shape[2]
    piece = features // (2 * n_dp)
    query, grad_out, layer_input, keys, values = [
        pltpu.with_memory_space_constraint(x[0], pltpu.HBM) for x in (query, grad_out, layer_input, keys, values)
    ]
    sinks, segments, positions = [
        pltpu.with_memory_space_constraint(x, pltpu.HBM) for x in (sinks, segments, positions)
    ]
    tail = last_tokens(layer_input, keys, values, segments, positions)
    rim = forward_one(tail, "seq")
    local = local_grads(query, grad_out, keys, values, layer_input, segments, positions, sinks)
    send, keep, rim_ds, rim_keys = rim_grads(local, rim, kv_width, n_dp)
    if piece % 16:
        plain = jnp.concatenate([keep, send], axis=0).reshape(n_dp, 2, piece, kv_width)
        order = bit_reversed(n_dp)
        orders = jnp.asarray([order, [swapped(relative, n_dp) for relative in order]], jnp.int32) ^ dp_index
        keep, send = [
            jnp.take(plain[:, side], orders[side], axis=0).reshape(-1, kv_width) for side in (core, core ^ 1)
        ]
    total = keep.astype(F32) + exchange(send, "seq", 1).astype(F32)
    group = query.shape[1] // kv_width

    def beside(held):
        return query_grads(*held, group)

    held = (local[2], local[3], rim_ds, rim_keys)
    dq = None if n_dp > 1 else beside(held)
    by = 1
    while by < n_dp:
        ways = 4 if 4 * by <= n_dp else 2
        if by == 1:
            total, dq = share(total, by, ways, beside, held)
        else:
            total = share(total, by, ways)
        by *= ways
    by = 2
    while by < n_seq:
        mine = total.astype(BF16)
        total = mine.astype(F32) + exchange(mine, "seq", by).astype(F32)
        by *= 2
    other = exchange(total, "seq", 1)
    pair = jnp.where(core == 0, jnp.stack([total, other]), jnp.stack([other, total]))
    return (dq[None], pair.reshape(-1, kv_width))


def solution(mesh):
    return jax.shard_map(
        body,
        mesh=mesh,
        in_specs=(
            P("dp", "seq", None),
            P("dp", "seq", None),
            P("dp", "seq", None),
            P("dp", "seq", None),
            P("dp", "seq", None),
            P(),
            P("dp", "seq"),
            P("dp", "seq"),
        ),
        out_specs=(P("dp", "seq", None), P("dp", None)),
        check_vma=False,
    )
```

```python
import jax
import jax.numpy as jnp
import numpy as np
from jax import lax
from jax.experimental import pallas as pl
from jax.experimental.pallas import tpu as pltpu
from jax.sharding import PartitionSpec as P

HEADDIM = 64
WINDOW = 128
THETA = 150000.0
LOW = -1e30

F32 = jnp.float32
BF16 = jnp.bfloat16


def dot(a, b, ca, cb):
    return lax.dot_general(a, b, (((ca,), (cb,)), ((), ())), preferred_element_type=F32)


def iota(shape, dim):
    return lax.broadcasted_iota(jnp.int32, shape, dim)


def sin_cos(angle):
    turns = jnp.floor(angle * np.float32(2.0 / np.pi) + np.float32(0.5))
    rest = angle - turns * np.float32(1.5703125)
    rest = rest - turns * np.float32(4.837512969970703125e-4)
    rest = rest - turns * np.float32(7.54978995489188216e-8)
    sq = rest * rest
    sin_part = np.float32(-1.9515295891e-4) * sq + np.float32(8.3321608736e-3)
    sin_part = (sin_part * sq + np.float32(-1.6666654611e-1)) * sq * rest + rest
    cos_part = np.float32(2.443315711809948e-5) * sq + np.float32(-1.388731625493765e-3)
    cos_part = (cos_part * sq + np.float32(4.166664568298827e-2)) * sq * sq
    cos_part = cos_part - np.float32(0.5) * sq + np.float32(1.0)
    quadrant = turns.astype(jnp.int32)
    odd = (quadrant & 1) == 1
    sine = jnp.where(odd, cos_part, sin_part)
    cosine = jnp.where(odd, sin_part, cos_part)
    sine = jnp.where((quadrant & 2) == 2, -sine, sine)
    cosine = jnp.where(((quadrant + 1) & 2) == 2, -cosine, cosine)
    return sine, cosine


def as_column(row):
    return jnp.broadcast_to(row, (row.shape[1], row.shape[1])).T


def load(copies):
    for copy in copies:
        copy.start()
    return copies


def prepare_keys(kv, blocks, keys2, values2, keys_t):
    w = WINDOW
    lanes = 2 * HEADDIM
    own_half = (iota((w, lanes), 1) < HEADDIM) == (kv % 2 == 0)
    cols = slice(kv // 2 * lanes, (kv // 2 + 1) * lanes)
    for b, (k_ref, v_ref, first_row) in enumerate(blocks):
        rows = slice(b * w, (b + 1) * w)
        k_tile = k_ref[first_row : first_row + w, cols].astype(F32) * np.float32(HEADDIM**-0.5)
        v_tile = v_ref[first_row : first_row + w, cols].astype(F32)
        k_tile = jnp.where(own_half, k_tile, np.float32(0.0))
        v_tile = jnp.where(own_half, v_tile, np.float32(0.0))
        keys2[kv, kv % 2, rows, :] = k_tile.astype(BF16)
        values2[kv, kv % 2, rows, :] = v_tile.astype(BF16)
        keys2[kv, 1 - kv % 2, rows, :] = pltpu.roll(k_tile, HEADDIM, 1).astype(BF16)
        values2[kv, 1 - kv % 2, rows, :] = pltpu.roll(v_tile, HEADDIM, 1).astype(BF16)
        half = slice(kv % 2 * HEADDIM, (kv % 2 + 1) * HEADDIM)
        keys_t[kv, :, rows] = k_tile.T[half].astype(BF16)


def attend(
    n_kv, group, row_blocks, window_of, beside, sink_rows, query, grad, ds_s, bias, halves, scratch, add_dk
):
    scores_s, grads_s = scratch
    w = WINDOW
    lanes = 2 * HEADDIM
    quads = group // 4
    tri = iota((w, w), 0) <= iota((w, w), 1)
    tri2 = jnp.concatenate([tri, tri], axis=1)
    items = [(b, kv, quad) for kv in range(n_kv) for b in range(row_blocks) for quad in range(quads)]

    def tiles(tile_of, b, kv, first, count):
        return jnp.concatenate([tile_of(b, kv, first + t) for t in range(count)], axis=0)

    def to_scores(n):
        b, kv, quad = items[n]
        key_win, value_win = window_of(b, kv, quad == 0)
        q_two = tiles(query, b, kv, 2 * quad, 2)
        g_two = tiles(grad, b, kv, 2 * quad, 2)
        bias2 = jnp.concatenate([bias[b], bias[b]], axis=1)
        for side in range(2):
            scores = dot(key_win[side], q_two, 1, 1)
            scores_s[n % 2, side] = jnp.where(tri2, scores[w:], scores[:w]) + bias2
        for side in range(2):
            grads = dot(value_win[side], g_two, 1, 1)
            grads_s[n % 2, side] = jnp.where(tri2, grads[w:], grads[:w])

    def to_ds(n):
        b, kv, quad = items[n]
        unit = n // quads
        for side in range(2):
            for t in range(2):
                cols = slice(t * w, (t + 1) * w)
                head = kv * group + 4 * quad + 2 * t + side
                sink = sink_rows[head : head + 1, :]
                scores = scores_s[n % 2, side, :, cols]
                peak = jnp.maximum(jnp.max(scores, axis=0, keepdims=True), sink)
                expo = jnp.exp(scores - peak)
                total = jnp.sum(expo, axis=0, keepdims=True) + jnp.exp(sink - peak)
                probs = expo * (np.float32(1.0) / total)
                grads = grads_s[n % 2, side, :, cols]
                delta = jnp.sum(probs * grads, axis=0, keepdims=True)
                ds = (probs * (grads - delta)).astype(BF16)
                out_cols = slice((2 * quad + t) * w, (2 * quad + t + 1) * w)
                ds_s[unit, side, 0:w, out_cols] = ds * halves[0]
                ds_s[unit, side, w : 2 * w, out_cols] = ds * halves[1]

    def to_grads(n):
        b, kv, quad = items[n]
        if quad == quads - 1:
            q_all = tiles(query, b, kv, 0, group // 2)
            low = iota((2 * w, lanes), 1) < HEADDIM
            sides = [dot(ds_s[n // quads, side], q_all, 1, 0) for side in range(2)]
            add_dk(b, kv, jnp.where(low, sides[0], sides[1]))

    for n in range(len(items) + 2):
        if n < len(items):
            to_scores(n)
        if 0 <= n - 1 < len(items):
            to_ds(n - 1)
        if n >= 2:
            to_grads(n - 2)
        if n < len(items):
            beside(n, len(items))


def attend_scratch():
    w = WINDOW
    return [
        pltpu.VMEM((2, 2, w, 2 * w), F32),
        pltpu.VMEM((2, 2, w, 2 * w), F32),
    ]


def set_halves(halves):
    tri = iota((WINDOW, WINDOW), 0) <= iota((WINDOW, WINDOW), 1)
    halves[0] = jnp.where(tri, np.float32(0.0), np.float32(1.0)).astype(BF16)
    halves[1] = jnp.where(tri, np.float32(1.0), np.float32(0.0)).astype(BF16)


def window_bias(bias, b, prev_segs, own_segs):
    tri = iota((WINDOW, WINDOW), 0) <= iota((WINDOW, WINDOW), 1)
    key_segs = jnp.where(tri, as_column(own_segs), as_column(prev_segs))
    bias[b] = jnp.where(key_segs == own_segs, np.float32(0.0), np.float32(LOW))


def store_dk(dk_part, dk_all, first_block, b, kv, part, seen):
    w = WINDOW
    lanes = 2 * HEADDIM
    if kv % 2 == 0:
        dk_part[b] = part
        return
    even = dk_part[b]
    low = iota(part.shape, 1) < HEADDIM
    both = jnp.where(low, even, part) + pltpu.roll(jnp.where(low, part, even), HEADDIM, 1)
    cols = slice(kv // 2 * lanes, (kv // 2 + 1) * lanes)
    for k in range(2):
        rows = slice((first_block + b + k) * w, (first_block + b + k + 1) * w)
        piece = both[k * w : (k + 1) * w]
        if (first_block + b + k, kv) in seen:
            piece = piece + dk_all[rows, cols]
        seen.add((first_block + b + k, kv))
        dk_all[rows, cols] = piece


def rotate(dk, sine, cosine):
    half = HEADDIM // 2
    lanes = dk.shape[1]
    low = (iota(dk.shape, 1) % HEADDIM) < half
    other = jnp.where(low, pltpu.roll(dk, lanes - half, 1), pltpu.roll(dk, half, 1))
    return (dk * cosine + other * sine) * np.float32(HEADDIM**-0.5)


def turn_table(pos):
    half = HEADDIM // 2
    index = iota((1, 2 * HEADDIM), 1) % half
    rates = (THETA ** (-2.0 * np.arange(half) / HEADDIM)).astype(np.float32)
    freq = jnp.zeros((1, 2 * HEADDIM), F32)
    for t in range(half):
        freq = jnp.where(index == t, rates[t], freq)
    sine, cosine = sin_cos(as_column(pos.astype(F32)) * freq)
    low = (iota(sine.shape, 1) % HEADDIM) < HEADDIM // 2
    return jnp.where(low, sine, -sine), cosine


def local_kernel(
    n_kv, group, sink_rows, segs_ref, pos_ref, keys, values, first_query, first_grad, query_hbm, grad_hbm, inputs_hbm,
    own_ref, table_ref, ds_ref, keys_t, query0, grad0, keys2, values2, inputs_t, later_ref,
    query, grad, inputs, dk_ref, bias, halves, dk_part, dk_all, in_sem, next_sem, *scratch,
):
    w = WINDOW
    lanes = 2 * HEADDIM
    rows = keys.shape[0]
    row_blocks = rows // w - 1
    step = group * HEADDIM
    def ins(kv):
        cols = slice(kv * step, (kv + 1) * step)
        return [
            pltpu.make_async_copy(query_hbm.at[w:, cols], query.at[:, cols], in_sem.at[0, kv]),
            pltpu.make_async_copy(grad_hbm.at[w:, cols], grad.at[:, cols], in_sem.at[1, kv]),
        ]

    in_copies = [[]] + [load(ins(kv)) for kv in range(1, n_kv)]
    next_copies = load(
        [
            pltpu.make_async_copy(query_hbm.at[0:w], query0, next_sem.at[0]),
            pltpu.make_async_copy(grad_hbm.at[0:w], grad0, next_sem.at[1]),
            pltpu.make_async_copy(inputs_hbm, inputs, next_sem.at[2]),
        ]
    )
    set_halves(halves)
    segs = [segs_ref[0:1, b * w : (b + 1) * w].astype(F32) for b in range(row_blocks + 1)]
    for b in range(row_blocks):
        window_bias(bias, b, segs[b], segs[b + 1])
    for b in range(row_blocks + 1):
        sine, cosine = turn_table(pos_ref[0:1, b * w : (b + 1) * w])
        table_ref[2 * b] = sine
        table_ref[2 * b + 1] = cosine
    seen = set()

    def tile_in(first, rest):
        def tile_of(b, kv, tile):
            ref, start = (first, tile) if kv == 0 else (rest, kv * group // 2 + tile)
            return ref[b * w : (b + 1) * w, start * lanes : (start + 1) * lanes]

        return tile_of

    def window_of(b, kv, first):
        if b == 0 and first:
            prepare_keys(kv, [(keys, values, b * w) for b in range(row_blocks + 1)], keys2, values2, keys_t)
            for copy in in_copies[kv]:
                copy.wait()
        window = slice(b * w, (b + 2) * w)
        return [keys2[kv, side, window, :] for side in range(2)], [values2[kv, side, window, :] for side in range(2)]

    features = inputs.shape[1]
    pieces = [(f, t) for f in range(features // w) for t in range(row_blocks + 1)]

    def turn_inputs(n, count):
        if n == 1:
            next_copies[2].wait()
        n, count = n - 1, count - 1
        for f, t in pieces[n * len(pieces) // count : (n + 1) * len(pieces) // count] if n >= 0 else []:
            cols = slice(f * w, (f + 1) * w)
            inputs_t[cols, t * w : (t + 1) * w] = inputs[t * w : (t + 1) * w, cols].T

    attend(
        n_kv, group, row_blocks, window_of, turn_inputs,
        sink_rows, tile_in(first_query, query), tile_in(first_grad, grad), ds_ref, bias, halves, scratch,
        lambda b, kv, part: store_dk(dk_part, dk_all, 0, b, kv, part, seen),
    )
    for b in range(row_blocks + 1):
        for tile in range(n_kv // 2):
            cols = slice(tile * lanes, (tile + 1) * lanes)
            turned = rotate(dk_all[b * w : (b + 1) * w, cols], table_ref[2 * b], table_ref[2 * b + 1])
            if b == 0:
                own_ref[:, cols] = turned
            else:
                dk_ref[(b - 1) * w : b * w, cols] = turned.astype(BF16)
    later_ref[...] = dot(inputs_t[:, w:], dk_ref[...], 1, 0)
    for copy in next_copies[:2]:
        copy.wait()


def rim_kernel(
    n_kv, group, n_dp, own_ref, table_ref, segs_ref, query, grad, own_keys2, own_values2, own_inputs_t, later_ref,
    sink_rows, rim,
    send_ref, keep_ref, ds_ref, keys_t,
    keys2, values2, bias, halves, dk_part, dk_all, dk16, inputs_t, sums, *scratch,
):
    w = WINDOW
    lanes = 2 * HEADDIM
    features = own_inputs_t.shape[0]
    kv_width = n_kv * HEADDIM
    set_halves(halves)
    rim_keys = rim.at[:, features : features + kv_width]
    rim_values = rim.at[:, features + kv_width : features + 2 * kv_width]
    aux = rim[0:16, features + 2 * kv_width :].astype(F32)
    rim_segs = jnp.where(lax.axis_index("seq") == 0, np.float32(-1.0), aux[0:1])
    window_bias(bias, 0, rim_segs, segs_ref[0:1, 0:w].astype(F32))
    rim_sine, rim_cosine = turn_table(aux[1:2] * np.float32(256.0) + aux[2:3])
    seen = set()

    def window_of(b, kv, first):
        if first:
            prepare_keys(kv, [(rim_keys, rim_values, 0)], keys2, values2, keys_t)
        both = [(keys2, own_keys2), (values2, own_values2)]
        return [
            [jnp.concatenate([rim2[kv, side], own2[kv, side, 0:w]], axis=0) for side in range(2)]
            for rim2, own2 in both
        ]

    tiles = features // w

    def turn_inputs(n, count):
        for f in range(n * tiles // count, (n + 1) * tiles // count):
            cols = slice(f * w, (f + 1) * w)
            inputs_t[cols, 0:w] = rim[:, cols].T
            inputs_t[cols, w : 2 * w] = own_inputs_t[cols, 0:w]

    def tile_in(ref):
        def tile_of(b, kv, tile):
            start = kv * group // 2 + tile
            return ref[:, start * lanes : (start + 1) * lanes]

        return tile_of

    attend(
        n_kv, group, 1, window_of, turn_inputs,
        sink_rows, tile_in(query), tile_in(grad), ds_ref, bias, halves, scratch,
        lambda b, kv, part: store_dk(dk_part, dk_all, 0, b, kv, part, seen),
    )
    for tile in range(n_kv // 2):
        cols = slice(tile * lanes, (tile + 1) * lanes)
        dk16[0:w, cols] = rotate(dk_all[0:w, cols], rim_sine, rim_cosine).astype(BF16)
        own = rotate(dk_all[w : 2 * w, cols], table_ref[0], table_ref[1]) + own_ref[:, cols]
        dk16[w : 2 * w, cols] = own.astype(BF16)
    sums[...] = dot(inputs_t[...], dk16[...], 1, 0) + later_ref[...]
    piece = features // (2 * n_dp)
    dp_index = lax.axis_index("dp")
    core = lax.axis_index("seq") & 1
    for half, ref in enumerate([keep_ref, send_ref]):
        for j, relative in enumerate(bit_reversed(n_dp)):
            if piece % 16 == 0:
                side = core ^ half
                block = (dp_index ^ (relative + side * (swapped(relative, n_dp) - relative))) * 2 + side
                start = pl.multiple_of(block * piece, piece)
                ref[j * piece : (j + 1) * piece, :] = sums[pl.ds(start, piece), :].astype(BF16)
    if piece % 16:
        keep_ref[...] = sums[0 : features // 2, :].astype(BF16)
        send_ref[...] = sums[features // 2 :, :].astype(BF16)


def query_kernel(n_kv, group, local_ds, local_keys, rim_ds, rim_keys, dq_hbm, dq, out_sem):
    w = WINDOW
    lanes = 2 * HEADDIM
    step = group * HEADDIM
    row_blocks = local_ds.shape[0] // n_kv
    outs = []
    for block in range(row_blocks + 1):
        rows = slice(block * w, (block + 1) * w)
        for kv in range(n_kv):
            for tile in range(group // 2):
                cols = slice(tile * w, (tile + 1) * w)
                if block == 0:
                    keyt_win = jnp.concatenate([rim_keys[kv], local_keys[kv, :, 0:w]], axis=1)
                    ds_ref, unit = rim_ds, kv
                else:
                    keyt_win = local_keys[kv, :, (block - 1) * w : (block + 1) * w]
                    ds_ref, unit = local_ds, kv * row_blocks + block - 1
                dq_t = [dot(keyt_win, ds_ref[unit, side, :, cols], 1, 0) for side in range(2)]
                start = kv * group // 2 + tile
                dq[rows, start * lanes : (start + 1) * lanes] = jnp.concatenate(dq_t, axis=0).T.astype(BF16)
            cols = slice(kv * step, (kv + 1) * step)
            outs += load([pltpu.make_async_copy(dq.at[rows, cols], dq_hbm.at[rows, cols], out_sem.at[block, kv])])
    for copy in outs:
        copy.wait()


ANY = pl.BlockSpec(memory_space=pl.ANY)
HBM = pl.BlockSpec(memory_space=pltpu.HBM)
VMEM = pl.BlockSpec(memory_space=pltpu.VMEM)
SMEM = pl.BlockSpec(memory_space=pltpu.SMEM)
LIMIT = 24 * 2**20


def estimate(row_blocks, width, extra_flops, extra_bytes):
    w = WINDOW
    return pl.CostEstimate(
        flops=10 * row_blocks * w * 2 * w * width + extra_flops,
        bytes_accessed=6 * row_blocks * w * width + extra_bytes,
        transcendentals=row_blocks * w * w * width // HEADDIM,
    )


def sizes(query, keys):
    width, kv_width = query.shape[-1], keys.shape[-1]
    return width, kv_width, kv_width // HEADDIM, width // kv_width


def shape(*dims, kind=BF16):
    return jax.ShapeDtypeStruct(dims, kind)


def local_grads(first, query, grad_out, layer_input):
    sink_rows, segments, positions, keys, values, first_query, first_grad = first
    rows, features = layer_input.shape
    width, kv_width, n_kv, group = sizes(query, keys)
    w = WINDOW
    lanes = 2 * HEADDIM
    row_blocks = rows // w - 1
    return pl.pallas_call(
        lambda *refs: local_kernel(n_kv, group, *refs),
        name="local_grads",
        in_specs=[VMEM] * 7 + [HBM] * 3,
        out_specs=[VMEM] * 10,
        out_shape=[
            shape(w, kv_width, kind=F32),
            shape(2 * (row_blocks + 1), w, lanes, kind=F32),
            shape(row_blocks * n_kv, 2, 2 * w, group // 2 * w),
            shape(n_kv, HEADDIM, rows),
            shape(w, width),
            shape(w, width),
            shape(n_kv, 2, rows, lanes),
            shape(n_kv, 2, rows, lanes),
            shape(features, rows),
            shape(features, kv_width, kind=F32),
        ],
        scratch_shapes=[
            pltpu.VMEM((row_blocks * w, width), BF16),
            pltpu.VMEM((row_blocks * w, width), BF16),
            pltpu.VMEM(layer_input.shape, BF16),
            pltpu.VMEM((rows - w, kv_width), BF16),
            pltpu.VMEM((row_blocks, w, w), F32),
            pltpu.VMEM((2, w, w), BF16),
            pltpu.VMEM((row_blocks, 2 * w, lanes), F32),
            pltpu.VMEM((rows, kv_width), F32),
            pltpu.SemaphoreType.DMA((2, n_kv)),
            pltpu.SemaphoreType.DMA((3,)),
        ]
        + attend_scratch(),
        compiler_params=pltpu.CompilerParams(vmem_limit_bytes=LIMIT),
        cost_estimate=estimate(row_blocks, width, 0, 0),
    )(sink_rows, segments, positions, keys, values, first_query, first_grad, query, grad_out, layer_input)


def rim_grads(first, local, rim, kv_width, n_dp):
    sink_rows, segments = first[:2]
    own, table, _, _, query0, grad0, keys2, values2, inputs_t, later = local
    features, rows = inputs_t.shape
    width = query0.shape[1]
    n_kv = kv_width // HEADDIM
    group = width // kv_width
    w = WINDOW
    lanes = 2 * HEADDIM
    return pl.pallas_call(
        lambda *refs: rim_kernel(n_kv, group, n_dp, *refs),
        name="rim_grads",
        in_specs=[VMEM] * 11,
        out_specs=[VMEM] * 4,
        out_shape=[
            shape(features // 2, kv_width),
            shape(features // 2, kv_width),
            shape(n_kv, 2, 2 * w, group // 2 * w),
            shape(n_kv, HEADDIM, w),
        ],
        scratch_shapes=[
            pltpu.VMEM((n_kv, 2, w, lanes), BF16),
            pltpu.VMEM((n_kv, 2, w, lanes), BF16),
            pltpu.VMEM((1, w, w), F32),
            pltpu.VMEM((2, w, w), BF16),
            pltpu.VMEM((1, 2 * w, lanes), F32),
            pltpu.VMEM((2 * w, kv_width), F32),
            pltpu.VMEM((2 * w, kv_width), BF16),
            pltpu.VMEM((features, 2 * w), BF16),
            pltpu.VMEM((features, kv_width), F32),
        ]
        + attend_scratch(),
        compiler_params=pltpu.CompilerParams(vmem_limit_bytes=LIMIT),
        cost_estimate=estimate(1, width, 2 * features * kv_width * 2 * w, 8 * features * kv_width),
    )(own, table, segments, query0, grad0, keys2, values2, inputs_t, later, sink_rows, rim)


def query_grads(local_ds, local_keys, rim_ds, rim_keys, group):
    n_kv, _, rows = local_keys.shape
    width = n_kv * group * HEADDIM
    w = WINDOW
    return pl.pallas_call(
        lambda *refs: query_kernel(n_kv, group, *refs),
        name="query_grads",
        in_specs=[VMEM] * 4,
        out_specs=HBM,
        out_shape=shape(rows, width),
        scratch_shapes=[pltpu.VMEM((rows, width), BF16), pltpu.SemaphoreType.DMA((rows // w, n_kv))],
        compiler_params=pltpu.CompilerParams(vmem_limit_bytes=LIMIT),
        cost_estimate=pl.CostEstimate(
            flops=4 * rows * w * width, bytes_accessed=2 * rows * width + 4 * rows * w * width // HEADDIM, transcendentals=0
        ),
    )(local_ds, local_keys, rim_ds, rim_keys)


def first_kernel(
    sinks_hbm, segs_hbm, pos_hbm, inputs_hbm, keys_hbm, values_hbm, query_hbm, grad_hbm,
    out_ref, sink_rows, segs_ref, pos_ref, keys, values, first_query, first_grad, sinks_ref, sem,
):
    w = WINDOW
    rows, features = inputs_hbm.shape
    kv_width = keys.shape[1]
    step = first_query.shape[1]
    ids = load(
        [
            pltpu.make_async_copy(segs_hbm, segs_ref, sem.at[0]),
            pltpu.make_async_copy(pos_hbm, pos_ref, sem.at[1]),
            pltpu.make_async_copy(sinks_hbm, sinks_ref, sem.at[2]),
        ]
    )
    at = [features, features + kv_width, features + 2 * kv_width]
    copies = load(
        [
            pltpu.make_async_copy(inputs_hbm.at[rows - w :], out_ref.at[:, 0 : at[0]], sem.at[3]),
            pltpu.make_async_copy(keys_hbm.at[rows - w :], out_ref.at[:, at[0] : at[1]], sem.at[4]),
            pltpu.make_async_copy(values_hbm.at[rows - w :], out_ref.at[:, at[1] : at[2]], sem.at[5]),
            pltpu.make_async_copy(keys_hbm, keys, sem.at[6]),
            pltpu.make_async_copy(values_hbm, values, sem.at[7]),
            pltpu.make_async_copy(query_hbm.at[w:, 0:step], first_query, sem.at[8]),
            pltpu.make_async_copy(grad_hbm.at[w:, 0:step], first_grad, sem.at[9]),
        ]
    )
    for copy in ids:
        copy.wait()
    line = iota((16, w), 0)
    segs = segs_ref[0:1, rows - w :]
    pos = pos_ref[0:1, rows - w :]
    aux = jnp.where(line == 0, segs, jnp.where(line == 1, pos >> 8, pos & 255))
    out_ref[0:16, at[2] :] = aux.astype(F32).astype(BF16)
    out_ref[16:, at[2] :] = jnp.zeros((w - 16, w), BF16)
    for head in range(sink_rows.shape[0]):
        sink_rows[head : head + 1, :] = jnp.full((1, w), sinks_ref[head], F32)
    for copy in copies:
        copy.wait()


def first_copies(layer_input, keys, values, segments, positions, sinks, query, grad_out):
    rows, kv_width = keys.shape
    width = layer_input.shape[1] + 2 * kv_width + WINDOW
    step = query.shape[1] * HEADDIM // kv_width
    return pl.pallas_call(
        first_kernel,
        name="first_copies",
        in_specs=[HBM] * 8,
        out_specs=[VMEM] * 8,
        out_shape=[
            shape(WINDOW, width),
            shape(sinks.shape[0], WINDOW, kind=F32),
            shape(*segments.shape, kind=jnp.int32),
            shape(*segments.shape, kind=jnp.int32),
            shape(rows, kv_width),
            shape(rows, kv_width),
            shape(rows - WINDOW, step),
            shape(rows - WINDOW, step),
        ],
        scratch_shapes=[pltpu.SMEM(sinks.shape, F32), pltpu.SemaphoreType.DMA((10,))],
        compiler_params=pltpu.CompilerParams(vmem_limit_bytes=LIMIT),
    )(sinks, segments, positions, layer_input, keys, values, query, grad_out)


def swapped(relative, n):
    return relative if n < 4 else (relative & ~3) | (relative & 1) << 1 | (relative & 2) >> 1


def bit_reversed(n):
    bits = n.bit_length() - 1
    return [int(format(i, "b").zfill(bits)[::-1], 2) if bits else 0 for i in range(n)]


def exchange(part, axis, by):
    count = lax.axis_size(axis)
    return lax.ppermute(part, axis, [(i, i ^ by) for i in range(count)])


def bits(n):
    return n.bit_length() - 1


def share_and_sum(total, by):
    n_dp, n_seq = lax.axis_size("dp"), lax.axis_size("seq")
    half = total.shape[0] // 2
    mine, theirs = total[:half].astype(BF16), total[half:].astype(BF16)

    def swap(part, dp_bits, seq_bits):
        pairs = [
            (d * n_seq + q, (d ^ dp_bits) * n_seq + (q ^ seq_bits)) for d in range(n_dp) for q in range(n_seq)
        ]
        return lax.ppermute(part, ("dp", "seq"), pairs).astype(F32)

    far = swap(theirs, by, 2)
    near = swap(theirs, by, 0)
    beside = swap(mine, 0, 2)
    return (mine.astype(F32) + beside) + (near + far)


def exchange_by_core(part, relative):
    n_dp, n_seq = lax.axis_size("dp"), lax.axis_size("seq")
    pairs = []
    for d in range(n_dp):
        for q in range(n_seq):
            other = d ^ (swapped(relative, n_dp) if q % 2 else relative)
            pairs.append((d * n_seq + q, other * n_seq + q))
    return lax.ppermute(part, ("dp", "seq"), pairs)


def share(total, by, ways, beside=None, held=None):
    rows = total.shape[0] // ways
    parts = [total[k * rows : (k + 1) * rows] for k in range(ways)]
    sends = [part.astype(BF16) for part in parts[1:]]
    if beside is not None:
        sends, held = lax.optimization_barrier((sends, held))
        extra = beside(held)
    got = {}
    for k in reversed(range(1, ways)):
        relative = bit_reversed(ways)[k] * by
        got[k] = exchange_by_core(sends[k - 1], relative)
    if beside is not None:
        got, extra = lax.optimization_barrier((got, extra))
    total = parts[0]
    for k in range(1, ways):
        total = total + got[k].astype(F32)
    return total if beside is None else (total, extra)


def forward_one(part, axis):
    count = lax.axis_size(axis)
    return lax.ppermute(part, axis, [(i, i + 1) for i in range(count - 1)])


def body(query, keys, values, grad_out, layer_input, sinks, segments, positions):
    n_dp = lax.axis_size("dp")
    n_seq = lax.axis_size("seq")
    dp_index = lax.axis_index("dp")
    seq_index = lax.axis_index("seq")
    core = seq_index & 1
    kv_width = keys.shape[2]
    features = layer_input.shape[2]
    piece = features // (2 * n_dp)
    query, grad_out, layer_input, keys, values = [
        pltpu.with_memory_space_constraint(x[0], pltpu.HBM) for x in (query, grad_out, layer_input, keys, values)
    ]
    sinks, segments, positions = [
        pltpu.with_memory_space_constraint(x, pltpu.HBM) for x in (sinks, segments, positions)
    ]
    tail, *first = first_copies(layer_input, keys, values, segments, positions, sinks, query, grad_out)
    rim = forward_one(tail, "seq")
    local = local_grads(first, query, grad_out, layer_input)
    send, keep, rim_ds, rim_keys = rim_grads(first, local, rim, kv_width, n_dp)
    if piece % 16:
        plain = jnp.concatenate([keep, send], axis=0).reshape(n_dp, 2, piece, kv_width)
        order = bit_reversed(n_dp)
        orders = jnp.asarray([order, [swapped(relative, n_dp) for relative in order]], jnp.int32) ^ dp_index
        keep, send = [
            jnp.take(plain[:, side], orders[side], axis=0).reshape(-1, kv_width) for side in (core, core ^ 1)
        ]
    total = keep.astype(F32) + exchange(send, "seq", 1).astype(F32)
    group = query.shape[1] // kv_width

    def beside(held):
        return query_grads(*held, group)

    held = (local[2], local[3], rim_ds, rim_keys)
    dq = None
    by = 1
    last = n_dp // 2 if n_seq == 4 and bits(n_dp) % 2 else n_dp
    while by < last:
        ways = 4 if 4 * by <= last else 2
        if dq is None:
            total, dq = share(total, by, ways, beside, held)
        else:
            total = share(total, by, ways)
        by *= ways
    if dq is None:
        dq = beside(held)
    if last < n_dp:
        total = share_and_sum(total, last)
    else:
        by = 2
        while by < n_seq:
            mine = total.astype(BF16)
            total = mine.astype(F32) + exchange(mine, "seq", by).astype(F32)
            by *= 2
    other = exchange(total, "seq", 1)
    pair = jnp.where(core == 0, jnp.stack([total, other]), jnp.stack([other, total]))
    return (dq[None], pair.reshape(-1, kv_width))


def solution(mesh):
    return jax.shard_map(
        body,
        mesh=mesh,
        in_specs=(
            P("dp", "seq", None),
            P("dp", "seq", None),
            P("dp", "seq", None),
            P("dp", "seq", None),
            P("dp", "seq", None),
            P(),
            P("dp", "seq"),
            P("dp", "seq"),
        ),
        out_specs=(P("dp", "seq", None), P("dp", None)),
        check_vma=False,
    )
```

```python
import jax
import jax.numpy as jnp
import numpy as np
from jax import lax
from jax.experimental import pallas as pl
from jax.experimental.pallas import tpu as pltpu
from jax.sharding import PartitionSpec as P

HEADDIM = 64
WINDOW = 128
THETA = 150000.0
LOW = -1e30

F32 = jnp.float32
BF16 = jnp.bfloat16


def dot(a, b, ca, cb):
    return lax.dot_general(a, b, (((ca,), (cb,)), ((), ())), preferred_element_type=F32)


def iota(shape, dim):
    return lax.broadcasted_iota(jnp.int32, shape, dim)


def sin_cos(angle):
    turns = jnp.floor(angle * np.float32(2.0 / np.pi) + np.float32(0.5))
    rest = angle - turns * np.float32(1.5703125)
    rest = rest - turns * np.float32(4.837512969970703125e-4)
    rest = rest - turns * np.float32(7.54978995489188216e-8)
    sq = rest * rest
    sin_part = np.float32(-1.9515295891e-4) * sq + np.float32(8.3321608736e-3)
    sin_part = (sin_part * sq + np.float32(-1.6666654611e-1)) * sq * rest + rest
    cos_part = np.float32(2.443315711809948e-5) * sq + np.float32(-1.388731625493765e-3)
    cos_part = (cos_part * sq + np.float32(4.166664568298827e-2)) * sq * sq
    cos_part = cos_part - np.float32(0.5) * sq + np.float32(1.0)
    quadrant = turns.astype(jnp.int32)
    odd = (quadrant & 1) == 1
    sine = jnp.where(odd, cos_part, sin_part)
    cosine = jnp.where(odd, sin_part, cos_part)
    sine = jnp.where((quadrant & 2) == 2, -sine, sine)
    cosine = jnp.where(((quadrant + 1) & 2) == 2, -cosine, cosine)
    return sine, cosine


def as_column(row):
    return jnp.broadcast_to(row, (row.shape[1], row.shape[1])).T


def load(copies):
    for copy in copies:
        copy.start()
    return copies


def prepare_keys(kv, blocks, keys2, values2, keys_t):
    w = WINDOW
    lanes = 2 * HEADDIM
    own_half = (iota((w, lanes), 1) < HEADDIM) == (kv % 2 == 0)
    cols = slice(kv // 2 * lanes, (kv // 2 + 1) * lanes)
    for b, (k_ref, v_ref, first_row) in enumerate(blocks):
        rows = slice(b * w, (b + 1) * w)
        k_tile = k_ref[first_row : first_row + w, cols].astype(F32) * np.float32(HEADDIM**-0.5)
        v_tile = v_ref[first_row : first_row + w, cols].astype(F32)
        k_tile = jnp.where(own_half, k_tile, np.float32(0.0))
        v_tile = jnp.where(own_half, v_tile, np.float32(0.0))
        keys2[kv, kv % 2, rows, :] = k_tile.astype(BF16)
        values2[kv, kv % 2, rows, :] = v_tile.astype(BF16)
        keys2[kv, 1 - kv % 2, rows, :] = pltpu.roll(k_tile, HEADDIM, 1).astype(BF16)
        values2[kv, 1 - kv % 2, rows, :] = pltpu.roll(v_tile, HEADDIM, 1).astype(BF16)
        half = slice(kv % 2 * HEADDIM, (kv % 2 + 1) * HEADDIM)
        keys_t[kv, :, rows] = k_tile.T[half].astype(BF16)


def attend(
    n_kv, group, row_blocks, window_of, beside, sink_rows, query, grad, ds_s, bias, halves, scratch, add_dk
):
    scores_s, grads_s = scratch
    w = WINDOW
    lanes = 2 * HEADDIM
    quads = group // 4
    tri = iota((w, w), 0) <= iota((w, w), 1)
    tri2 = jnp.concatenate([tri, tri], axis=1)
    items = [(b, kv, quad) for kv in range(n_kv) for b in range(row_blocks) for quad in range(quads)]

    def tiles(tile_of, b, kv, first, count):
        return jnp.concatenate([tile_of(b, kv, first + t) for t in range(count)], axis=0)

    def to_scores(n):
        b, kv, quad = items[n]
        key_win, value_win = window_of(b, kv, quad == 0)
        q_two = tiles(query, b, kv, 2 * quad, 2)
        g_two = tiles(grad, b, kv, 2 * quad, 2)
        bias2 = jnp.concatenate([bias[b], bias[b]], axis=1)
        for side in range(2):
            scores = dot(key_win[side], q_two, 1, 1)
            scores_s[n % 2, side] = jnp.where(tri2, scores[w:], scores[:w]) + bias2
        for side in range(2):
            grads = dot(value_win[side], g_two, 1, 1)
            grads_s[n % 2, side] = jnp.where(tri2, grads[w:], grads[:w])

    def to_ds(n):
        b, kv, quad = items[n]
        unit = n // quads
        for side in range(2):
            for t in range(2):
                cols = slice(t * w, (t + 1) * w)
                head = kv * group + 4 * quad + 2 * t + side
                sink = sink_rows[head : head + 1, :]
                scores = scores_s[n % 2, side, :, cols]
                peak = jnp.maximum(jnp.max(scores, axis=0, keepdims=True), sink)
                expo = jnp.exp(scores - peak)
                total = jnp.sum(expo, axis=0, keepdims=True) + jnp.exp(sink - peak)
                probs = expo * (np.float32(1.0) / total)
                grads = grads_s[n % 2, side, :, cols]
                delta = jnp.sum(probs * grads, axis=0, keepdims=True)
                ds = (probs * (grads - delta)).astype(BF16)
                out_cols = slice((2 * quad + t) * w, (2 * quad + t + 1) * w)
                ds_s[unit, side, 0:w, out_cols] = ds * halves[0]
                ds_s[unit, side, w : 2 * w, out_cols] = ds * halves[1]

    def to_grads(n):
        b, kv, quad = items[n]
        if quad == quads - 1:
            q_all = tiles(query, b, kv, 0, group // 2)
            low = iota((2 * w, lanes), 1) < HEADDIM
            sides = [dot(ds_s[n // quads, side], q_all, 1, 0) for side in range(2)]
            add_dk(b, kv, jnp.where(low, sides[0], sides[1]))

    for n in range(len(items) + 2):
        if n < len(items):
            to_scores(n)
        if 0 <= n - 1 < len(items):
            to_ds(n - 1)
        if n >= 2:
            to_grads(n - 2)
        if n < len(items):
            beside(n, len(items))


def attend_scratch():
    w = WINDOW
    return [
        pltpu.VMEM((2, 2, w, 2 * w), F32),
        pltpu.VMEM((2, 2, w, 2 * w), F32),
    ]


def set_halves(halves):
    tri = iota((WINDOW, WINDOW), 0) <= iota((WINDOW, WINDOW), 1)
    halves[0] = jnp.where(tri, np.float32(0.0), np.float32(1.0)).astype(BF16)
    halves[1] = jnp.where(tri, np.float32(1.0), np.float32(0.0)).astype(BF16)


def window_bias(bias, b, prev_segs, own_segs):
    tri = iota((WINDOW, WINDOW), 0) <= iota((WINDOW, WINDOW), 1)
    key_segs = jnp.where(tri, as_column(own_segs), as_column(prev_segs))
    bias[b] = jnp.where(key_segs == own_segs, np.float32(0.0), np.float32(LOW))


def store_dk(dk_part, dk_all, first_block, b, kv, part, seen):
    w = WINDOW
    lanes = 2 * HEADDIM
    if kv % 2 == 0:
        dk_part[b] = part
        return
    even = dk_part[b]
    low = iota(part.shape, 1) < HEADDIM
    both = jnp.where(low, even, part) + pltpu.roll(jnp.where(low, part, even), HEADDIM, 1)
    cols = slice(kv // 2 * lanes, (kv // 2 + 1) * lanes)
    for k in range(2):
        rows = slice((first_block + b + k) * w, (first_block + b + k + 1) * w)
        piece = both[k * w : (k + 1) * w]
        if (first_block + b + k, kv) in seen:
            piece = piece + dk_all[rows, cols]
        seen.add((first_block + b + k, kv))
        dk_all[rows, cols] = piece


def rotate(dk, sine, cosine):
    half = HEADDIM // 2
    lanes = dk.shape[1]
    low = (iota(dk.shape, 1) % HEADDIM) < half
    other = jnp.where(low, pltpu.roll(dk, lanes - half, 1), pltpu.roll(dk, half, 1))
    return (dk * cosine + other * sine) * np.float32(HEADDIM**-0.5)


def turn_table(pos):
    half = HEADDIM // 2
    index = iota((1, 2 * HEADDIM), 1) % half
    rates = (THETA ** (-2.0 * np.arange(half) / HEADDIM)).astype(np.float32)
    freq = jnp.zeros((1, 2 * HEADDIM), F32)
    for t in range(half):
        freq = jnp.where(index == t, rates[t], freq)
    sine, cosine = sin_cos(as_column(pos.astype(F32)) * freq)
    low = (iota(sine.shape, 1) % HEADDIM) < HEADDIM // 2
    return jnp.where(low, sine, -sine), cosine


def local_kernel(
    n_kv, group, sink_rows, segs_ref, pos_ref, keys, values, first_query, first_grad, query_hbm, grad_hbm, inputs_hbm,
    own_ref, table_ref, ds_ref, keys_t, query0, grad0, keys2, values2, inputs_t, later_ref,
    query, grad, inputs, dk_ref, bias, halves, dk_part, dk_all, in_sem, next_sem, *scratch,
):
    w = WINDOW
    lanes = 2 * HEADDIM
    rows = keys.shape[0]
    row_blocks = rows // w - 1
    step = group * HEADDIM
    def ins(kv):
        cols = slice(kv * step, (kv + 1) * step)
        return [
            pltpu.make_async_copy(query_hbm.at[w:, cols], query.at[:, cols], in_sem.at[0, kv]),
            pltpu.make_async_copy(grad_hbm.at[w:, cols], grad.at[:, cols], in_sem.at[1, kv]),
        ]

    in_copies = [[]] + [load(ins(kv)) for kv in range(1, n_kv)]
    next_copies = load(
        [
            pltpu.make_async_copy(query_hbm.at[0:w], query0, next_sem.at[0]),
            pltpu.make_async_copy(grad_hbm.at[0:w], grad0, next_sem.at[1]),
            pltpu.make_async_copy(inputs_hbm, inputs, next_sem.at[2]),
        ]
    )
    set_halves(halves)
    segs = [segs_ref[0:1, b * w : (b + 1) * w].astype(F32) for b in range(row_blocks + 1)]
    for b in range(row_blocks):
        window_bias(bias, b, segs[b], segs[b + 1])
    for b in range(row_blocks + 1):
        sine, cosine = turn_table(pos_ref[0:1, b * w : (b + 1) * w])
        table_ref[2 * b] = sine
        table_ref[2 * b + 1] = cosine
    seen = set()

    def tile_in(first, rest):
        def tile_of(b, kv, tile):
            ref, start = (first, tile) if kv == 0 else (rest, kv * group // 2 + tile)
            return ref[b * w : (b + 1) * w, start * lanes : (start + 1) * lanes]

        return tile_of

    def window_of(b, kv, first):
        if b == 0 and first:
            prepare_keys(kv, [(keys, values, b * w) for b in range(row_blocks + 1)], keys2, values2, keys_t)
            for copy in in_copies[kv]:
                copy.wait()
        window = slice(b * w, (b + 2) * w)
        return [keys2[kv, side, window, :] for side in range(2)], [values2[kv, side, window, :] for side in range(2)]

    features = inputs.shape[1]
    pieces = [(f, t) for f in range(features // w) for t in range(row_blocks + 1)]

    def turn_inputs(n, count):
        if n == 1:
            next_copies[2].wait()
        n, count = n - 1, count - 1
        for f, t in pieces[n * len(pieces) // count : (n + 1) * len(pieces) // count] if n >= 0 else []:
            cols = slice(f * w, (f + 1) * w)
            inputs_t[cols, t * w : (t + 1) * w] = inputs[t * w : (t + 1) * w, cols].T

    attend(
        n_kv, group, row_blocks, window_of, turn_inputs,
        sink_rows, tile_in(first_query, query), tile_in(first_grad, grad), ds_ref, bias, halves, scratch,
        lambda b, kv, part: store_dk(dk_part, dk_all, 0, b, kv, part, seen),
    )
    for b in range(row_blocks + 1):
        for tile in range(n_kv // 2):
            cols = slice(tile * lanes, (tile + 1) * lanes)
            turned = rotate(dk_all[b * w : (b + 1) * w, cols], table_ref[2 * b], table_ref[2 * b + 1])
            if b == 0:
                own_ref[:, cols] = turned
            else:
                dk_ref[(b - 1) * w : b * w, cols] = turned.astype(BF16)
    later_ref[...] = dot(inputs_t[:, w:], dk_ref[...], 1, 0)
    for copy in next_copies[:2]:
        copy.wait()


def rim_kernel(
    n_kv, group, n_dp, own_ref, table_ref, segs_ref, query, grad, own_keys2, own_values2, own_inputs_t, later_ref,
    sink_rows, rim,
    send_ref, keep_ref, ds_ref, keys_t,
    keys2, values2, bias, halves, dk_part, dk_all, dk16, inputs_t, sums, *scratch,
):
    w = WINDOW
    lanes = 2 * HEADDIM
    features = own_inputs_t.shape[0]
    kv_width = n_kv * HEADDIM
    set_halves(halves)
    rim_keys = rim.at[:, features : features + kv_width]
    rim_values = rim.at[:, features + kv_width : features + 2 * kv_width]
    aux = rim[0:16, features + 2 * kv_width :].astype(F32)
    rim_segs = jnp.where(lax.axis_index("seq") == 0, np.float32(-1.0), aux[0:1])
    window_bias(bias, 0, rim_segs, segs_ref[0:1, 0:w].astype(F32))
    rim_sine, rim_cosine = turn_table(aux[1:2] * np.float32(256.0) + aux[2:3])
    seen = set()

    def window_of(b, kv, first):
        if first:
            prepare_keys(kv, [(rim_keys, rim_values, 0)], keys2, values2, keys_t)
        both = [(keys2, own_keys2), (values2, own_values2)]
        return [
            [jnp.concatenate([rim2[kv, side], own2[kv, side, 0:w]], axis=0) for side in range(2)]
            for rim2, own2 in both
        ]

    tiles = features // w

    def turn_inputs(n, count):
        for f in range(n * tiles // count, (n + 1) * tiles // count):
            cols = slice(f * w, (f + 1) * w)
            inputs_t[cols, 0:w] = rim[:, cols].T
            inputs_t[cols, w : 2 * w] = own_inputs_t[cols, 0:w]

    def tile_in(ref):
        def tile_of(b, kv, tile):
            start = kv * group // 2 + tile
            return ref[:, start * lanes : (start + 1) * lanes]

        return tile_of

    attend(
        n_kv, group, 1, window_of, turn_inputs,
        sink_rows, tile_in(query), tile_in(grad), ds_ref, bias, halves, scratch,
        lambda b, kv, part: store_dk(dk_part, dk_all, 0, b, kv, part, seen),
    )
    for tile in range(n_kv // 2):
        cols = slice(tile * lanes, (tile + 1) * lanes)
        dk16[0:w, cols] = rotate(dk_all[0:w, cols], rim_sine, rim_cosine).astype(BF16)
        own = rotate(dk_all[w : 2 * w, cols], table_ref[0], table_ref[1]) + own_ref[:, cols]
        dk16[w : 2 * w, cols] = own.astype(BF16)
    sums[...] = dot(inputs_t[...], dk16[...], 1, 0) + later_ref[...]
    piece = features // (2 * n_dp)
    dp_index = lax.axis_index("dp")
    core = lax.axis_index("seq") & 1
    for half, ref in enumerate([keep_ref, send_ref]):
        for j, relative in enumerate(bit_reversed(n_dp)):
            if piece % 16 == 0:
                side = core ^ half
                block = (dp_index ^ (relative + side * (swapped(relative, n_dp) - relative))) * 2 + side
                start = pl.multiple_of(block * piece, piece)
                ref[j * piece : (j + 1) * piece, :] = sums[pl.ds(start, piece), :].astype(BF16)
    if piece % 16:
        keep_ref[...] = sums[0 : features // 2, :].astype(BF16)
        send_ref[...] = sums[features // 2 :, :].astype(BF16)


def query_kernel(n_kv, group, local_ds, local_keys, rim_ds, rim_keys, dq_hbm, dq, out_sem):
    w = WINDOW
    lanes = 2 * HEADDIM
    step = group * HEADDIM
    row_blocks = local_ds.shape[0] // n_kv
    outs = []
    for block in range(row_blocks + 1):
        rows = slice(block * w, (block + 1) * w)
        for kv in range(n_kv):
            for tile in range(group // 2):
                cols = slice(tile * w, (tile + 1) * w)
                if block == 0:
                    keyt_win = jnp.concatenate([rim_keys[kv], local_keys[kv, :, 0:w]], axis=1)
                    ds_ref, unit = rim_ds, kv
                else:
                    keyt_win = local_keys[kv, :, (block - 1) * w : (block + 1) * w]
                    ds_ref, unit = local_ds, kv * row_blocks + block - 1
                dq_t = [dot(keyt_win, ds_ref[unit, side, :, cols], 1, 0) for side in range(2)]
                start = kv * group // 2 + tile
                dq[rows, start * lanes : (start + 1) * lanes] = jnp.concatenate(dq_t, axis=0).T.astype(BF16)
            cols = slice(kv * step, (kv + 1) * step)
            outs += load([pltpu.make_async_copy(dq.at[rows, cols], dq_hbm.at[rows, cols], out_sem.at[block, kv])])
    for copy in outs:
        copy.wait()


ANY = pl.BlockSpec(memory_space=pl.ANY)
HBM = pl.BlockSpec(memory_space=pltpu.HBM)
VMEM = pl.BlockSpec(memory_space=pltpu.VMEM)
SMEM = pl.BlockSpec(memory_space=pltpu.SMEM)
LIMIT = 24 * 2**20


def estimate(row_blocks, width, extra_flops, extra_bytes):
    w = WINDOW
    return pl.CostEstimate(
        flops=10 * row_blocks * w * 2 * w * width + extra_flops,
        bytes_accessed=6 * row_blocks * w * width + extra_bytes,
        transcendentals=row_blocks * w * w * width // HEADDIM,
    )


def sizes(query, keys):
    width, kv_width = query.shape[-1], keys.shape[-1]
    return width, kv_width, kv_width // HEADDIM, width // kv_width


def shape(*dims, kind=BF16):
    return jax.ShapeDtypeStruct(dims, kind)


def local_grads(first, query, grad_out, layer_input):
    sink_rows, segments, positions, keys, values, first_query, first_grad = first
    rows, features = layer_input.shape
    width, kv_width, n_kv, group = sizes(query, keys)
    w = WINDOW
    lanes = 2 * HEADDIM
    row_blocks = rows // w - 1
    return pl.pallas_call(
        lambda *refs: local_kernel(n_kv, group, *refs),
        name="local_grads",
        in_specs=[VMEM] * 7 + [HBM] * 3,
        out_specs=[VMEM] * 10,
        out_shape=[
            shape(w, kv_width, kind=F32),
            shape(2 * (row_blocks + 1), w, lanes, kind=F32),
            shape(row_blocks * n_kv, 2, 2 * w, group // 2 * w),
            shape(n_kv, HEADDIM, rows),
            shape(w, width),
            shape(w, width),
            shape(n_kv, 2, rows, lanes),
            shape(n_kv, 2, rows, lanes),
            shape(features, rows),
            shape(features, kv_width, kind=F32),
        ],
        scratch_shapes=[
            pltpu.VMEM((row_blocks * w, width), BF16),
            pltpu.VMEM((row_blocks * w, width), BF16),
            pltpu.VMEM(layer_input.shape, BF16),
            pltpu.VMEM((rows - w, kv_width), BF16),
            pltpu.VMEM((row_blocks, w, w), F32),
            pltpu.VMEM((2, w, w), BF16),
            pltpu.VMEM((row_blocks, 2 * w, lanes), F32),
            pltpu.VMEM((rows, kv_width), F32),
            pltpu.SemaphoreType.DMA((2, n_kv)),
            pltpu.SemaphoreType.DMA((3,)),
        ]
        + attend_scratch(),
        compiler_params=pltpu.CompilerParams(vmem_limit_bytes=LIMIT),
        cost_estimate=estimate(row_blocks, width, 0, 0),
    )(sink_rows, segments, positions, keys, values, first_query, first_grad, query, grad_out, layer_input)


def rim_grads(first, local, rim, kv_width, n_dp):
    sink_rows, segments = first[:2]
    own, table, _, _, query0, grad0, keys2, values2, inputs_t, later = local
    features, rows = inputs_t.shape
    width = query0.shape[1]
    n_kv = kv_width // HEADDIM
    group = width // kv_width
    w = WINDOW
    lanes = 2 * HEADDIM
    return pl.pallas_call(
        lambda *refs: rim_kernel(n_kv, group, n_dp, *refs),
        name="rim_grads",
        in_specs=[VMEM] * 11,
        out_specs=[VMEM] * 4,
        out_shape=[
            shape(features // 2, kv_width),
            shape(features // 2, kv_width),
            shape(n_kv, 2, 2 * w, group // 2 * w),
            shape(n_kv, HEADDIM, w),
        ],
        scratch_shapes=[
            pltpu.VMEM((n_kv, 2, w, lanes), BF16),
            pltpu.VMEM((n_kv, 2, w, lanes), BF16),
            pltpu.VMEM((1, w, w), F32),
            pltpu.VMEM((2, w, w), BF16),
            pltpu.VMEM((1, 2 * w, lanes), F32),
            pltpu.VMEM((2 * w, kv_width), F32),
            pltpu.VMEM((2 * w, kv_width), BF16),
            pltpu.VMEM((features, 2 * w), BF16),
            pltpu.VMEM((features, kv_width), F32),
        ]
        + attend_scratch(),
        compiler_params=pltpu.CompilerParams(vmem_limit_bytes=LIMIT),
        cost_estimate=estimate(1, width, 2 * features * kv_width * 2 * w, 8 * features * kv_width),
    )(own, table, segments, query0, grad0, keys2, values2, inputs_t, later, sink_rows, rim)


def query_grads(local_ds, local_keys, rim_ds, rim_keys, group):
    n_kv, _, rows = local_keys.shape
    width = n_kv * group * HEADDIM
    w = WINDOW
    return pl.pallas_call(
        lambda *refs: query_kernel(n_kv, group, *refs),
        name="query_grads",
        in_specs=[VMEM] * 4,
        out_specs=HBM,
        out_shape=shape(rows, width),
        scratch_shapes=[pltpu.VMEM((rows, width), BF16), pltpu.SemaphoreType.DMA((rows // w, n_kv))],
        compiler_params=pltpu.CompilerParams(vmem_limit_bytes=LIMIT),
        cost_estimate=pl.CostEstimate(
            flops=4 * rows * w * width, bytes_accessed=2 * rows * width + 4 * rows * w * width // HEADDIM, transcendentals=0
        ),
    )(local_ds, local_keys, rim_ds, rim_keys)


def first_kernel(
    sinks_hbm, segs_hbm, pos_hbm, inputs_hbm, keys_hbm, values_hbm, query_hbm, grad_hbm,
    out_ref, sink_rows, segs_ref, pos_ref, keys, values, first_query, first_grad, sinks_ref, sem,
):
    w = WINDOW
    rows, features = inputs_hbm.shape
    kv_width = keys.shape[1]
    step = first_query.shape[1]
    ids = load(
        [
            pltpu.make_async_copy(segs_hbm, segs_ref, sem.at[0]),
            pltpu.make_async_copy(pos_hbm, pos_ref, sem.at[1]),
            pltpu.make_async_copy(sinks_hbm, sinks_ref, sem.at[2]),
        ]
    )
    at = [features, features + kv_width, features + 2 * kv_width]
    copies = load(
        [
            pltpu.make_async_copy(inputs_hbm.at[rows - w :], out_ref.at[:, 0 : at[0]], sem.at[3]),
            pltpu.make_async_copy(keys_hbm.at[rows - w :], out_ref.at[:, at[0] : at[1]], sem.at[4]),
            pltpu.make_async_copy(values_hbm.at[rows - w :], out_ref.at[:, at[1] : at[2]], sem.at[5]),
            pltpu.make_async_copy(keys_hbm, keys, sem.at[6]),
            pltpu.make_async_copy(values_hbm, values, sem.at[7]),
            pltpu.make_async_copy(query_hbm.at[w:, 0:step], first_query, sem.at[8]),
            pltpu.make_async_copy(grad_hbm.at[w:, 0:step], first_grad, sem.at[9]),
        ]
    )
    for copy in ids:
        copy.wait()
    line = iota((16, w), 0)
    segs = segs_ref[0:1, rows - w :]
    pos = pos_ref[0:1, rows - w :]
    aux = jnp.where(line == 0, segs, jnp.where(line == 1, pos >> 8, pos & 255))
    out_ref[0:16, at[2] :] = aux.astype(F32).astype(BF16)
    out_ref[16:, at[2] :] = jnp.zeros((w - 16, w), BF16)
    for head in range(sink_rows.shape[0]):
        sink_rows[head : head + 1, :] = jnp.full((1, w), sinks_ref[head], F32)
    for copy in copies:
        copy.wait()


def first_copies(layer_input, keys, values, segments, positions, sinks, query, grad_out):
    rows, kv_width = keys.shape
    width = layer_input.shape[1] + 2 * kv_width + WINDOW
    step = query.shape[1] * HEADDIM // kv_width
    return pl.pallas_call(
        first_kernel,
        name="first_copies",
        in_specs=[HBM] * 8,
        out_specs=[VMEM] * 8,
        out_shape=[
            shape(WINDOW, width),
            shape(sinks.shape[0], WINDOW, kind=F32),
            shape(*segments.shape, kind=jnp.int32),
            shape(*segments.shape, kind=jnp.int32),
            shape(rows, kv_width),
            shape(rows, kv_width),
            shape(rows - WINDOW, step),
            shape(rows - WINDOW, step),
        ],
        scratch_shapes=[pltpu.SMEM(sinks.shape, F32), pltpu.SemaphoreType.DMA((10,))],
        compiler_params=pltpu.CompilerParams(vmem_limit_bytes=LIMIT),
    )(sinks, segments, positions, layer_input, keys, values, query, grad_out)


def swapped(relative, n):
    return relative if n < 4 else (relative & ~3) | (relative & 1) << 1 | (relative & 2) >> 1


def bit_reversed(n):
    bits = n.bit_length() - 1
    return [int(format(i, "b").zfill(bits)[::-1], 2) if bits else 0 for i in range(n)]


def exchange(part, axis, by):
    count = lax.axis_size(axis)
    return lax.ppermute(part, axis, [(i, i ^ by) for i in range(count)])


def bits(n):
    return n.bit_length() - 1


def share_and_sum(total, by):
    n_dp, n_seq = lax.axis_size("dp"), lax.axis_size("seq")
    half = total.shape[0] // 2
    mine, theirs = total[:half].astype(BF16), total[half:].astype(BF16)

    def swap(part, dp_bits, seq_bits):
        pairs = [
            (d * n_seq + q, (d ^ dp_bits) * n_seq + (q ^ seq_bits)) for d in range(n_dp) for q in range(n_seq)
        ]
        return lax.ppermute(part, ("dp", "seq"), pairs).astype(F32)

    far = swap(theirs, by, 2)
    near = swap(theirs, by, 0)
    beside = swap(mine, 0, 2)
    return (far + near) + (beside + mine.astype(F32))


def exchange_by_core(part, relative):
    n_dp, n_seq = lax.axis_size("dp"), lax.axis_size("seq")
    pairs = []
    for d in range(n_dp):
        for q in range(n_seq):
            other = d ^ (swapped(relative, n_dp) if q % 2 else relative)
            pairs.append((d * n_seq + q, other * n_seq + q))
    return lax.ppermute(part, ("dp", "seq"), pairs)


def share(total, by, ways, beside=None, held=None):
    rows = total.shape[0] // ways
    parts = [total[k * rows : (k + 1) * rows] for k in range(ways)]
    sends = [part.astype(BF16) for part in parts[1:]]
    if beside is not None:
        sends, held = lax.optimization_barrier((sends, held))
        extra = beside(held)
    got = []
    for k in reversed(range(1, ways)):
        relative = bit_reversed(ways)[k] * by
        got.append(exchange_by_core(sends[k - 1], relative))
    if beside is not None:
        got, extra = lax.optimization_barrier((got, extra))
    total = parts[0]
    for part in got:
        total = total + part.astype(F32)
    return total if beside is None else (total, extra)


def forward_one(part, axis):
    count = lax.axis_size(axis)
    return lax.ppermute(part, axis, [(i, i + 1) for i in range(count - 1)])


def body(query, keys, values, grad_out, layer_input, sinks, segments, positions):
    n_dp = lax.axis_size("dp")
    n_seq = lax.axis_size("seq")
    dp_index = lax.axis_index("dp")
    seq_index = lax.axis_index("seq")
    core = seq_index & 1
    kv_width = keys.shape[2]
    features = layer_input.shape[2]
    piece = features // (2 * n_dp)
    query, grad_out, layer_input, keys, values = [
        pltpu.with_memory_space_constraint(x[0], pltpu.HBM) for x in (query, grad_out, layer_input, keys, values)
    ]
    sinks, segments, positions = [
        pltpu.with_memory_space_constraint(x, pltpu.HBM) for x in (sinks, segments, positions)
    ]
    tail, *first = first_copies(layer_input, keys, values, segments, positions, sinks, query, grad_out)
    rim = forward_one(tail, "seq")
    local = local_grads(first, query, grad_out, layer_input)
    send, keep, rim_ds, rim_keys = rim_grads(first, local, rim, kv_width, n_dp)
    if piece % 16:
        plain = jnp.concatenate([keep, send], axis=0).reshape(n_dp, 2, piece, kv_width)
        order = bit_reversed(n_dp)
        orders = jnp.asarray([order, [swapped(relative, n_dp) for relative in order]], jnp.int32) ^ dp_index
        keep, send = [
            jnp.take(plain[:, side], orders[side], axis=0).reshape(-1, kv_width) for side in (core, core ^ 1)
        ]
    total = keep.astype(F32) + exchange(send, "seq", 1).astype(F32)
    group = query.shape[1] // kv_width

    def beside(held):
        return query_grads(*held, group)

    held = (local[2], local[3], rim_ds, rim_keys)
    dq = None
    by = 1
    last = n_dp // 2 if n_seq == 4 and bits(n_dp) % 2 else n_dp
    while by < last:
        ways = 4 if 4 * by <= last else 2
        if dq is None:
            total, dq = share(total, by, ways, beside, held)
        else:
            total = share(total, by, ways)
        by *= ways
    if dq is None:
        dq = beside(held)
    if last < n_dp:
        total = share_and_sum(total, last)
    else:
        by = 2
        while by < n_seq:
            mine = total.astype(BF16)
            total = mine.astype(F32) + exchange(mine, "seq", by).astype(F32)
            by *= 2
    other = exchange(total, "seq", 1)
    pair = jnp.where(core == 0, jnp.stack([total, other]), jnp.stack([other, total]))
    return (dq[None], pair.reshape(-1, kv_width))


def solution(mesh):
    return jax.shard_map(
        body,
        mesh=mesh,
        in_specs=(
            P("dp", "seq", None),
            P("dp", "seq", None),
            P("dp", "seq", None),
            P("dp", "seq", None),
            P("dp", "seq", None),
            P(),
            P("dp", "seq"),
            P("dp", "seq"),
        ),
        out_specs=(P("dp", "seq", None), P("dp", None)),
        check_vma=False,
    )
```

```python
import jax
import jax.numpy as jnp
import numpy as np
from jax import lax
from jax.experimental import pallas as pl
from jax.experimental.pallas import tpu as pltpu
from jax.sharding import PartitionSpec as P

HEADDIM = 64
WINDOW = 128
THETA = 150000.0
LOW = -1e30

F32 = jnp.float32
BF16 = jnp.bfloat16


def dot(a, b, ca, cb):
    return lax.dot_general(a, b, (((ca,), (cb,)), ((), ())), preferred_element_type=F32)


def iota(shape, dim):
    return lax.broadcasted_iota(jnp.int32, shape, dim)


def sin_cos(angle):
    turns = jnp.floor(angle * np.float32(2.0 / np.pi) + np.float32(0.5))
    rest = angle - turns * np.float32(1.5703125)
    rest = rest - turns * np.float32(4.837512969970703125e-4)
    rest = rest - turns * np.float32(7.54978995489188216e-8)
    sq = rest * rest
    sin_part = np.float32(-1.9515295891e-4) * sq + np.float32(8.3321608736e-3)
    sin_part = (sin_part * sq + np.float32(-1.6666654611e-1)) * sq * rest + rest
    cos_part = np.float32(2.443315711809948e-5) * sq + np.float32(-1.388731625493765e-3)
    cos_part = (cos_part * sq + np.float32(4.166664568298827e-2)) * sq * sq
    cos_part = cos_part - np.float32(0.5) * sq + np.float32(1.0)
    quadrant = turns.astype(jnp.int32)
    odd = (quadrant & 1) == 1
    sine = jnp.where(odd, cos_part, sin_part)
    cosine = jnp.where(odd, sin_part, cos_part)
    sine = jnp.where((quadrant & 2) == 2, -sine, sine)
    cosine = jnp.where(((quadrant + 1) & 2) == 2, -cosine, cosine)
    return sine, cosine


def as_column(row):
    return jnp.broadcast_to(row, (row.shape[1], row.shape[1])).T


def load(copies):
    for copy in copies:
        copy.start()
    return copies


def prepare_keys(kv, blocks, keys2, values2, keys_t):
    w = WINDOW
    lanes = 2 * HEADDIM
    own_half = (iota((w, lanes), 1) < HEADDIM) == (kv % 2 == 0)
    cols = slice(kv // 2 * lanes, (kv // 2 + 1) * lanes)
    for b, (k_ref, v_ref, first_row) in enumerate(blocks):
        rows = slice(b * w, (b + 1) * w)
        k_tile = k_ref[first_row : first_row + w, cols].astype(F32) * np.float32(HEADDIM**-0.5)
        v_tile = v_ref[first_row : first_row + w, cols].astype(F32)
        k_tile = jnp.where(own_half, k_tile, np.float32(0.0))
        v_tile = jnp.where(own_half, v_tile, np.float32(0.0))
        keys2[kv, kv % 2, rows, :] = k_tile.astype(BF16)
        values2[kv, kv % 2, rows, :] = v_tile.astype(BF16)
        keys2[kv, 1 - kv % 2, rows, :] = pltpu.roll(k_tile, HEADDIM, 1).astype(BF16)
        values2[kv, 1 - kv % 2, rows, :] = pltpu.roll(v_tile, HEADDIM, 1).astype(BF16)
        half = slice(kv % 2 * HEADDIM, (kv % 2 + 1) * HEADDIM)
        keys_t[kv, :, rows] = k_tile.T[half].astype(BF16)


def attend(
    n_kv, group, row_blocks, window_of, beside, sink_rows, query, grad, ds_s, bias, halves, scratch, add_dk
):
    scores_s, grads_s = scratch
    w = WINDOW
    lanes = 2 * HEADDIM
    quads = group // 4
    tri = iota((w, w), 0) <= iota((w, w), 1)
    tri2 = jnp.concatenate([tri, tri], axis=1)
    items = [(b, kv, quad) for kv in range(n_kv) for b in range(row_blocks) for quad in range(quads)]

    def tiles(tile_of, b, kv, first, count):
        return jnp.concatenate([tile_of(b, kv, first + t) for t in range(count)], axis=0)

    def to_scores(n):
        b, kv, quad = items[n]
        key_win, value_win = window_of(b, kv, quad == 0)
        q_two = tiles(query, b, kv, 2 * quad, 2)
        g_two = tiles(grad, b, kv, 2 * quad, 2)
        bias2 = jnp.concatenate([bias[b], bias[b]], axis=1)
        for side in range(2):
            scores = dot(key_win[side], q_two, 1, 1)
            scores_s[n % 2, side] = jnp.where(tri2, scores[w:], scores[:w]) + bias2
        for side in range(2):
            grads = dot(value_win[side], g_two, 1, 1)
            grads_s[n % 2, side] = jnp.where(tri2, grads[w:], grads[:w])

    def to_ds(n):
        _, kv, quad = items[n]
        unit = n // quads
        for side in range(2):
            for t in range(2):
                cols = slice(t * w, (t + 1) * w)
                head = kv * group + 4 * quad + 2 * t + side
                sink = sink_rows[head : head + 1, :]
                scores = scores_s[n % 2, side, :, cols]
                peak = jnp.maximum(jnp.max(scores, axis=0, keepdims=True), sink)
                expo = jnp.exp(scores - peak)
                total = jnp.sum(expo, axis=0, keepdims=True) + jnp.exp(sink - peak)
                probs = expo * (np.float32(1.0) / total)
                grads = grads_s[n % 2, side, :, cols]
                delta = jnp.sum(probs * grads, axis=0, keepdims=True)
                ds = (probs * (grads - delta)).astype(BF16)
                out_cols = slice((2 * quad + t) * w, (2 * quad + t + 1) * w)
                ds_s[unit, side, 0:w, out_cols] = ds * halves[0]
                ds_s[unit, side, w : 2 * w, out_cols] = ds * halves[1]

    def to_grads(n):
        b, kv, quad = items[n]
        if quad == quads - 1:
            q_all = tiles(query, b, kv, 0, group // 2)
            low = iota((2 * w, lanes), 1) < HEADDIM
            sides = [dot(ds_s[n // quads, side], q_all, 1, 0) for side in range(2)]
            add_dk(b, kv, jnp.where(low, sides[0], sides[1]))

    for n in range(len(items) + 2):
        if n < len(items):
            to_scores(n)
        if 0 <= n - 1 < len(items):
            to_ds(n - 1)
        if n >= 2:
            to_grads(n - 2)
        if n < len(items):
            beside(n, len(items))


def attend_scratch():
    w = WINDOW
    return [
        pltpu.VMEM((2, 2, w, 2 * w), F32),
        pltpu.VMEM((2, 2, w, 2 * w), F32),
    ]


def set_halves(halves):
    tri = iota((WINDOW, WINDOW), 0) <= iota((WINDOW, WINDOW), 1)
    halves[0] = jnp.where(tri, np.float32(0.0), np.float32(1.0)).astype(BF16)
    halves[1] = jnp.where(tri, np.float32(1.0), np.float32(0.0)).astype(BF16)


def window_bias(bias, b, prev_segs, own_segs):
    tri = iota((WINDOW, WINDOW), 0) <= iota((WINDOW, WINDOW), 1)
    key_segs = jnp.where(tri, as_column(own_segs), as_column(prev_segs))
    bias[b] = jnp.where(key_segs == own_segs, np.float32(0.0), np.float32(LOW))


def store_dk(dk_part, dk_all, first_block, b, kv, part, seen):
    w = WINDOW
    lanes = 2 * HEADDIM
    if kv % 2 == 0:
        dk_part[b] = part
        return
    even = dk_part[b]
    low = iota(part.shape, 1) < HEADDIM
    both = jnp.where(low, even, part) + pltpu.roll(jnp.where(low, part, even), HEADDIM, 1)
    cols = slice(kv // 2 * lanes, (kv // 2 + 1) * lanes)
    for k in range(2):
        rows = slice((first_block + b + k) * w, (first_block + b + k + 1) * w)
        piece = both[k * w : (k + 1) * w]
        if (first_block + b + k, kv) in seen:
            piece = piece + dk_all[rows, cols]
        seen.add((first_block + b + k, kv))
        dk_all[rows, cols] = piece


def rotate(dk, sine, cosine):
    half = HEADDIM // 2
    lanes = dk.shape[1]
    low = (iota(dk.shape, 1) % HEADDIM) < half
    other = jnp.where(low, pltpu.roll(dk, lanes - half, 1), pltpu.roll(dk, half, 1))
    return (dk * cosine + other * sine) * np.float32(HEADDIM**-0.5)


def turn_table(pos):
    half = HEADDIM // 2
    index = iota((1, 2 * HEADDIM), 1) % half
    rates = (THETA ** (-2.0 * np.arange(half) / HEADDIM)).astype(np.float32)
    freq = jnp.zeros((1, 2 * HEADDIM), F32)
    for t in range(half):
        freq = jnp.where(index == t, rates[t], freq)
    sine, cosine = sin_cos(as_column(pos.astype(F32)) * freq)
    low = (iota(sine.shape, 1) % HEADDIM) < HEADDIM // 2
    return jnp.where(low, sine, -sine), cosine


def local_kernel(
    n_kv, group, sink_rows, segs_ref, pos_ref, keys, values, first_query, first_grad, query_hbm, grad_hbm, inputs_hbm,
    own_ref, table_ref, ds_ref, keys_t, query0, grad0, keys2, values2, inputs_t, later_ref,
    query, grad, inputs, dk_ref, bias, halves, dk_part, dk_all, in_sem, next_sem, *scratch,
):
    w = WINDOW
    lanes = 2 * HEADDIM
    rows = keys.shape[0]
    row_blocks = rows // w - 1
    step = group * HEADDIM

    def ins(kv):
        cols = slice(kv * step, (kv + 1) * step)
        return [
            pltpu.make_async_copy(query_hbm.at[w:, cols], query.at[:, cols], in_sem.at[0, kv]),
            pltpu.make_async_copy(grad_hbm.at[w:, cols], grad.at[:, cols], in_sem.at[1, kv]),
        ]

    in_copies = [[]] + [load(ins(kv)) for kv in range(1, n_kv)]
    next_copies = load(
        [
            pltpu.make_async_copy(query_hbm.at[0:w], query0, next_sem.at[0]),
            pltpu.make_async_copy(grad_hbm.at[0:w], grad0, next_sem.at[1]),
            pltpu.make_async_copy(inputs_hbm, inputs, next_sem.at[2]),
        ]
    )
    set_halves(halves)
    segs = [segs_ref[0:1, b * w : (b + 1) * w].astype(F32) for b in range(row_blocks + 1)]
    for b in range(row_blocks):
        window_bias(bias, b, segs[b], segs[b + 1])
    for b in range(row_blocks + 1):
        sine, cosine = turn_table(pos_ref[0:1, b * w : (b + 1) * w])
        table_ref[2 * b] = sine
        table_ref[2 * b + 1] = cosine
    seen = set()

    def tile_in(first, rest):
        def tile_of(b, kv, tile):
            ref, start = (first, tile) if kv == 0 else (rest, kv * group // 2 + tile)
            return ref[b * w : (b + 1) * w, start * lanes : (start + 1) * lanes]

        return tile_of

    def window_of(b, kv, first):
        if b == 0 and first:
            prepare_keys(kv, [(keys, values, b * w) for b in range(row_blocks + 1)], keys2, values2, keys_t)
            for copy in in_copies[kv]:
                copy.wait()
        window = slice(b * w, (b + 2) * w)
        return [keys2[kv, side, window, :] for side in range(2)], [values2[kv, side, window, :] for side in range(2)]

    features = inputs.shape[1]
    pieces = [(f, t) for f in range(features // w) for t in range(row_blocks + 1)]

    def turn_inputs(n, count):
        if n == 1:
            next_copies[2].wait()
        n, count = n - 1, count - 1
        for f, t in pieces[n * len(pieces) // count : (n + 1) * len(pieces) // count] if n >= 0 else []:
            cols = slice(f * w, (f + 1) * w)
            inputs_t[cols, t * w : (t + 1) * w] = inputs[t * w : (t + 1) * w, cols].T

    attend(
        n_kv, group, row_blocks, window_of, turn_inputs,
        sink_rows, tile_in(first_query, query), tile_in(first_grad, grad), ds_ref, bias, halves, scratch,
        lambda b, kv, part: store_dk(dk_part, dk_all, 0, b, kv, part, seen),
    )
    for b in range(row_blocks + 1):
        for tile in range(n_kv // 2):
            cols = slice(tile * lanes, (tile + 1) * lanes)
            turned = rotate(dk_all[b * w : (b + 1) * w, cols], table_ref[2 * b], table_ref[2 * b + 1])
            if b == 0:
                own_ref[:, cols] = turned
            else:
                dk_ref[(b - 1) * w : b * w, cols] = turned.astype(BF16)
    later_ref[...] = dot(inputs_t[:, w:], dk_ref[...], 1, 0)
    for copy in next_copies[:2]:
        copy.wait()


def rim_kernel(
    n_kv, group, own_ref, table_ref, segs_ref, query, grad, own_keys2, own_values2, sink_rows, rim,
    dk16, ds_ref, keys_t,
    keys2, values2, bias, halves, dk_part, dk_all, *scratch,
):
    w = WINDOW
    lanes = 2 * HEADDIM
    kv_width = n_kv * HEADDIM
    set_halves(halves)
    rim_keys = rim.at[:, 0:kv_width]
    rim_values = rim.at[:, kv_width : 2 * kv_width]
    aux = rim[0:16, 2 * kv_width :].astype(F32)
    rim_segs = jnp.where(lax.axis_index("seq") == 0, np.float32(-1.0), aux[0:1])
    window_bias(bias, 0, rim_segs, segs_ref[0:1, 0:w].astype(F32))
    rim_sine, rim_cosine = turn_table(aux[1:2] * np.float32(256.0) + aux[2:3])
    seen = set()

    def window_of(b, kv, first):
        if first:
            prepare_keys(kv, [(rim_keys, rim_values, 0)], keys2, values2, keys_t)
        both = [(keys2, own_keys2), (values2, own_values2)]
        return [
            [jnp.concatenate([rim2[kv, side], own2[kv, side, 0:w]], axis=0) for side in range(2)]
            for rim2, own2 in both
        ]

    def tile_in(ref):
        def tile_of(b, kv, tile):
            start = kv * group // 2 + tile
            return ref[:, start * lanes : (start + 1) * lanes]

        return tile_of

    attend(
        n_kv, group, 1, window_of, lambda n, count: None,
        sink_rows, tile_in(query), tile_in(grad), ds_ref, bias, halves, scratch,
        lambda b, kv, part: store_dk(dk_part, dk_all, 0, b, kv, part, seen),
    )
    for tile in range(n_kv // 2):
        cols = slice(tile * lanes, (tile + 1) * lanes)
        dk16[0:w, cols] = rotate(dk_all[0:w, cols], rim_sine, rim_cosine).astype(BF16)
        own = rotate(dk_all[w : 2 * w, cols], table_ref[0], table_ref[1]) + own_ref[:, cols]
        dk16[w : 2 * w, cols] = own.astype(BF16)


def weight_kernel(n_dp, inputs, own_inputs_t, later_ref, dk16, send_ref, keep_ref, inputs_t, sums):
    w, features = inputs.shape
    for f in range(features // w):
        cols = slice(f * w, (f + 1) * w)
        inputs_t[cols, 0:w] = inputs[:, cols].T
        inputs_t[cols, w : 2 * w] = own_inputs_t[cols, 0:w]
    sums[...] = dot(inputs_t[...], dk16[...], 1, 0) + later_ref[...]
    piece = features // (2 * n_dp)
    dp_index = lax.axis_index("dp")
    core = lax.axis_index("seq") & 1
    for half, ref in enumerate([keep_ref, send_ref]):
        for j, relative in enumerate(bit_reversed(n_dp)):
            if piece % 16 == 0:
                side = core ^ half
                block = (dp_index ^ (relative + side * (swapped(relative, n_dp) - relative))) * 2 + side
                start = pl.multiple_of(block * piece, piece)
                ref[j * piece : (j + 1) * piece, :] = sums[pl.ds(start, piece), :].astype(BF16)
    if piece % 16:
        keep_ref[...] = sums[0 : features // 2, :].astype(BF16)
        send_ref[...] = sums[features // 2 :, :].astype(BF16)


def query_kernel(n_kv, group, local_ds, local_keys, rim_ds, rim_keys, dq_hbm, dq, out_sem):
    w = WINDOW
    lanes = 2 * HEADDIM
    step = group * HEADDIM
    row_blocks = local_ds.shape[0] // n_kv
    outs = []
    for block in range(row_blocks + 1):
        rows = slice(block * w, (block + 1) * w)
        for kv in range(n_kv):
            for tile in range(group // 2):
                cols = slice(tile * w, (tile + 1) * w)
                if block == 0:
                    keyt_win = jnp.concatenate([rim_keys[kv], local_keys[kv, :, 0:w]], axis=1)
                    ds_ref, unit = rim_ds, kv
                else:
                    keyt_win = local_keys[kv, :, (block - 1) * w : (block + 1) * w]
                    ds_ref, unit = local_ds, kv * row_blocks + block - 1
                dq_t = [dot(keyt_win, ds_ref[unit, side, :, cols], 1, 0) for side in range(2)]
                start = kv * group // 2 + tile
                dq[rows, start * lanes : (start + 1) * lanes] = jnp.concatenate(dq_t, axis=0).T.astype(BF16)
            cols = slice(kv * step, (kv + 1) * step)
            outs += load([pltpu.make_async_copy(dq.at[rows, cols], dq_hbm.at[rows, cols], out_sem.at[block, kv])])
    for copy in outs:
        copy.wait()


ANY = pl.BlockSpec(memory_space=pl.ANY)
HBM = pl.BlockSpec(memory_space=pltpu.HBM)
VMEM = pl.BlockSpec(memory_space=pltpu.VMEM)
SMEM = pl.BlockSpec(memory_space=pltpu.SMEM)
LIMIT = 24 * 2**20


def estimate(row_blocks, width, extra_flops, extra_bytes):
    w = WINDOW
    return pl.CostEstimate(
        flops=10 * row_blocks * w * 2 * w * width + extra_flops,
        bytes_accessed=6 * row_blocks * w * width + extra_bytes,
        transcendentals=row_blocks * w * w * width // HEADDIM,
    )


def sizes(query, keys):
    width, kv_width = query.shape[-1], keys.shape[-1]
    return width, kv_width, kv_width // HEADDIM, width // kv_width


def shape(*dims, kind=BF16):
    return jax.ShapeDtypeStruct(dims, kind)


def local_grads(first, query, grad_out, layer_input):
    sink_rows, segments, positions, keys, values, first_query, first_grad = first
    rows, features = layer_input.shape
    width, kv_width, n_kv, group = sizes(query, keys)
    w = WINDOW
    lanes = 2 * HEADDIM
    row_blocks = rows // w - 1
    return pl.pallas_call(
        lambda *refs: local_kernel(n_kv, group, *refs),
        name="local_grads",
        in_specs=[VMEM] * 7 + [HBM] * 3,
        out_specs=[VMEM] * 10,
        out_shape=[
            shape(w, kv_width, kind=F32),
            shape(2 * (row_blocks + 1), w, lanes, kind=F32),
            shape(row_blocks * n_kv, 2, 2 * w, group // 2 * w),
            shape(n_kv, HEADDIM, rows),
            shape(w, width),
            shape(w, width),
            shape(n_kv, 2, rows, lanes),
            shape(n_kv, 2, rows, lanes),
            shape(features, rows),
            shape(features, kv_width, kind=F32),
        ],
        scratch_shapes=[
            pltpu.VMEM((row_blocks * w, width), BF16),
            pltpu.VMEM((row_blocks * w, width), BF16),
            pltpu.VMEM(layer_input.shape, BF16),
            pltpu.VMEM((rows - w, kv_width), BF16),
            pltpu.VMEM((row_blocks, w, w), F32),
            pltpu.VMEM((2, w, w), BF16),
            pltpu.VMEM((row_blocks, 2 * w, lanes), F32),
            pltpu.VMEM((rows, kv_width), F32),
            pltpu.SemaphoreType.DMA((2, n_kv)),
            pltpu.SemaphoreType.DMA((3,)),
        ]
        + attend_scratch(),
        compiler_params=pltpu.CompilerParams(vmem_limit_bytes=LIMIT),
        cost_estimate=estimate(row_blocks, width, 0, 0),
    )(sink_rows, segments, positions, keys, values, first_query, first_grad, query, grad_out, layer_input)


def rim_grads(first, local, rim, kv_width):
    sink_rows, segments = first[:2]
    own, table, _, _, query0, grad0, keys2, values2, _, _ = local
    width = query0.shape[1]
    n_kv = kv_width // HEADDIM
    group = width // kv_width
    w = WINDOW
    lanes = 2 * HEADDIM
    return pl.pallas_call(
        lambda *refs: rim_kernel(n_kv, group, *refs),
        name="rim_grads",
        in_specs=[VMEM] * 9,
        out_specs=[VMEM] * 3,
        out_shape=[
            shape(2 * w, kv_width),
            shape(n_kv, 2, 2 * w, group // 2 * w),
            shape(n_kv, HEADDIM, w),
        ],
        scratch_shapes=[
            pltpu.VMEM((n_kv, 2, w, lanes), BF16),
            pltpu.VMEM((n_kv, 2, w, lanes), BF16),
            pltpu.VMEM((1, w, w), F32),
            pltpu.VMEM((2, w, w), BF16),
            pltpu.VMEM((1, 2 * w, lanes), F32),
            pltpu.VMEM((2 * w, kv_width), F32),
        ]
        + attend_scratch(),
        compiler_params=pltpu.CompilerParams(vmem_limit_bytes=LIMIT),
        cost_estimate=estimate(1, width, 0, 0),
    )(own, table, segments, query0, grad0, keys2, values2, sink_rows, rim)


def weight_parts(rim_inputs, local, dk16, n_dp):
    inputs_t, later = local[-2:]
    features, kv_width = later.shape
    w = WINDOW
    return pl.pallas_call(
        lambda *refs: weight_kernel(n_dp, *refs),
        name="weight_parts",
        in_specs=[VMEM] * 4,
        out_specs=[VMEM] * 2,
        out_shape=[shape(features // 2, kv_width), shape(features // 2, kv_width)],
        scratch_shapes=[pltpu.VMEM((features, 2 * w), BF16), pltpu.VMEM((features, kv_width), F32)],
        compiler_params=pltpu.CompilerParams(vmem_limit_bytes=LIMIT),
        cost_estimate=pl.CostEstimate(
            flops=4 * features * kv_width * w, bytes_accessed=8 * features * kv_width, transcendentals=0
        ),
    )(rim_inputs, inputs_t, later, dk16)


def query_grads(local_ds, local_keys, rim_ds, rim_keys, group):
    n_kv, _, rows = local_keys.shape
    width = n_kv * group * HEADDIM
    w = WINDOW
    return pl.pallas_call(
        lambda *refs: query_kernel(n_kv, group, *refs),
        name="query_grads",
        in_specs=[VMEM] * 4,
        out_specs=HBM,
        out_shape=shape(rows, width),
        scratch_shapes=[pltpu.VMEM((rows, width), BF16), pltpu.SemaphoreType.DMA((rows // w, n_kv))],
        compiler_params=pltpu.CompilerParams(vmem_limit_bytes=LIMIT),
        cost_estimate=pl.CostEstimate(
            flops=4 * rows * w * width, bytes_accessed=2 * rows * width + 4 * rows * w * width // HEADDIM, transcendentals=0
        ),
    )(local_ds, local_keys, rim_ds, rim_keys)


def first_kernel(
    sinks_hbm, segs_hbm, pos_hbm, inputs_hbm, keys_hbm, values_hbm, query_hbm, grad_hbm,
    out_ref, inputs_ref, sink_rows, segs_ref, pos_ref, keys, values, first_query, first_grad, sinks_ref, sem,
):
    w = WINDOW
    rows = inputs_hbm.shape[0]
    kv_width = keys.shape[1]
    step = first_query.shape[1]
    ids = load(
        [
            pltpu.make_async_copy(segs_hbm, segs_ref, sem.at[0]),
            pltpu.make_async_copy(pos_hbm, pos_ref, sem.at[1]),
            pltpu.make_async_copy(sinks_hbm, sinks_ref, sem.at[2]),
        ]
    )
    copies = load(
        [
            pltpu.make_async_copy(inputs_hbm.at[rows - w :], inputs_ref, sem.at[3]),
            pltpu.make_async_copy(keys_hbm.at[rows - w :], out_ref.at[:, 0:kv_width], sem.at[4]),
            pltpu.make_async_copy(values_hbm.at[rows - w :], out_ref.at[:, kv_width : 2 * kv_width], sem.at[5]),
            pltpu.make_async_copy(keys_hbm, keys, sem.at[6]),
            pltpu.make_async_copy(values_hbm, values, sem.at[7]),
            pltpu.make_async_copy(query_hbm.at[w:, 0:step], first_query, sem.at[8]),
            pltpu.make_async_copy(grad_hbm.at[w:, 0:step], first_grad, sem.at[9]),
        ]
    )
    for copy in ids:
        copy.wait()
    line = iota((16, w), 0)
    segs = segs_ref[0:1, rows - w :]
    pos = pos_ref[0:1, rows - w :]
    aux = jnp.where(line == 0, segs, jnp.where(line == 1, pos >> 8, pos & 255))
    out_ref[0:16, 2 * kv_width :] = aux.astype(F32).astype(BF16)
    out_ref[16:, 2 * kv_width :] = jnp.zeros((w - 16, w), BF16)
    for head in range(sink_rows.shape[0]):
        sink_rows[head : head + 1, :] = jnp.full((1, w), sinks_ref[head], F32)
    for copy in copies:
        copy.wait()


def first_copies(layer_input, keys, values, segments, positions, sinks, query, grad_out):
    rows, kv_width = keys.shape
    step = query.shape[1] * HEADDIM // kv_width
    return pl.pallas_call(
        first_kernel,
        name="first_copies",
        in_specs=[HBM] * 8,
        out_specs=[VMEM] * 9,
        out_shape=[
            shape(WINDOW, 2 * kv_width + WINDOW),
            shape(WINDOW, layer_input.shape[1]),
            shape(sinks.shape[0], WINDOW, kind=F32),
            shape(*segments.shape, kind=jnp.int32),
            shape(*segments.shape, kind=jnp.int32),
            shape(rows, kv_width),
            shape(rows, kv_width),
            shape(rows - WINDOW, step),
            shape(rows - WINDOW, step),
        ],
        scratch_shapes=[pltpu.SMEM(sinks.shape, F32), pltpu.SemaphoreType.DMA((10,))],
        compiler_params=pltpu.CompilerParams(vmem_limit_bytes=LIMIT),
    )(sinks, segments, positions, layer_input, keys, values, query, grad_out)


def swapped(relative, n):
    return relative if n < 4 else (relative & ~3) | (relative & 1) << 1 | (relative & 2) >> 1


def bit_reversed(n):
    bits = n.bit_length() - 1
    return [int(format(i, "b").zfill(bits)[::-1], 2) if bits else 0 for i in range(n)]


def exchange(part, axis, by):
    count = lax.axis_size(axis)
    return lax.ppermute(part, axis, [(i, i ^ by) for i in range(count)])


def bits(n):
    return n.bit_length() - 1


def share_and_sum(total, by):
    n_dp, n_seq = lax.axis_size("dp"), lax.axis_size("seq")
    half = total.shape[0] // 2
    mine, theirs = total[:half].astype(BF16), total[half:].astype(BF16)

    def swap(part, dp_bits, seq_bits):
        pairs = [
            (d * n_seq + q, (d ^ dp_bits) * n_seq + (q ^ seq_bits)) for d in range(n_dp) for q in range(n_seq)
        ]
        return lax.ppermute(part, ("dp", "seq"), pairs).astype(F32)

    far = swap(theirs, by, 2)
    near = swap(theirs, by, 0)
    beside = swap(mine, 0, 2)
    return (far + near) + (beside + mine.astype(F32))


def exchange_by_core(part, relative):
    n_dp, n_seq = lax.axis_size("dp"), lax.axis_size("seq")
    pairs = []
    for d in range(n_dp):
        for q in range(n_seq):
            other = d ^ (swapped(relative, n_dp) if q % 2 else relative)
            pairs.append((d * n_seq + q, other * n_seq + q))
    return lax.ppermute(part, ("dp", "seq"), pairs)


def share(total, by, ways, beside=None, held=None):
    rows = total.shape[0] // ways
    parts = [total[k * rows : (k + 1) * rows] for k in range(ways)]
    sends = [part.astype(BF16) for part in parts[1:]]
    if beside is not None:
        sends, held = lax.optimization_barrier((sends, held))
        extra = beside(held)
    got = []
    for k in reversed(range(1, ways)):
        relative = bit_reversed(ways)[k] * by
        got.append(exchange_by_core(sends[k - 1], relative))
    if beside is not None:
        got, extra = lax.optimization_barrier((got, extra))
    total = parts[0]
    for part in got:
        total = total + part.astype(F32)
    return total if beside is None else (total, extra)


def forward_one(part, axis):
    count = lax.axis_size(axis)
    return lax.ppermute(part, axis, [(i, i + 1) for i in range(count - 1)])


def body(query, keys, values, grad_out, layer_input, sinks, segments, positions):
    n_dp = lax.axis_size("dp")
    n_seq = lax.axis_size("seq")
    dp_index = lax.axis_index("dp")
    seq_index = lax.axis_index("seq")
    core = seq_index & 1
    kv_width = keys.shape[2]
    features = layer_input.shape[2]
    piece = features // (2 * n_dp)
    query, grad_out, layer_input, keys, values = [
        pltpu.with_memory_space_constraint(x[0], pltpu.HBM) for x in (query, grad_out, layer_input, keys, values)
    ]
    sinks, segments, positions = [
        pltpu.with_memory_space_constraint(x, pltpu.HBM) for x in (sinks, segments, positions)
    ]
    tail, tail_inputs, *first = first_copies(layer_input, keys, values, segments, positions, sinks, query, grad_out)
    rim = forward_one(tail, "seq")
    rim_inputs = forward_one(tail_inputs, "seq")
    local = local_grads(first, query, grad_out, layer_input)
    dk16, rim_ds, rim_keys = rim_grads(first, local, rim, kv_width)
    send, keep = weight_parts(rim_inputs, local, dk16, n_dp)
    if piece % 16:
        plain = jnp.concatenate([keep, send], axis=0).reshape(n_dp, 2, piece, kv_width)
        order = bit_reversed(n_dp)
        orders = jnp.asarray([order, [swapped(relative, n_dp) for relative in order]], jnp.int32) ^ dp_index
        keep, send = [
            jnp.take(plain[:, side], orders[side], axis=0).reshape(-1, kv_width) for side in (core, core ^ 1)
        ]
    total = keep.astype(F32) + exchange(send, "seq", 1).astype(F32)
    group = query.shape[1] // kv_width

    def beside(held):
        return query_grads(*held, group)

    held = (local[2], local[3], rim_ds, rim_keys)
    dq = None
    by = 1
    last = n_dp // 2 if n_seq == 4 and bits(n_dp) % 2 else n_dp
    while by < last:
        ways = 4 if 4 * by <= last else 2
        if dq is None:
            total, dq = share(total, by, ways, beside, held)
        else:
            total = share(total, by, ways)
        by *= ways
    if dq is None:
        dq = beside(held)
    if last < n_dp:
        total = share_and_sum(total, last)
    else:
        by = 2
        while by < n_seq:
            mine = total.astype(BF16)
            total = mine.astype(F32) + exchange(mine, "seq", by).astype(F32)
            by *= 2
    other = exchange(total, "seq", 1)
    pair = jnp.where(core == 0, jnp.stack([total, other]), jnp.stack([other, total]))
    return (dq[None], pair.reshape(-1, kv_width))


def solution(mesh):
    return jax.shard_map(
        body,
        mesh=mesh,
        in_specs=(
            P("dp", "seq", None),
            P("dp", "seq", None),
            P("dp", "seq", None),
            P("dp", "seq", None),
            P("dp", "seq", None),
            P(),
            P("dp", "seq"),
            P("dp", "seq"),
        ),
        out_specs=(P("dp", "seq", None), P("dp", None)),
        check_vma=False,
    )
```

```python
import jax
import jax.numpy as jnp
import numpy as np
from jax import lax
from jax.experimental import pallas as pl
from jax.experimental.pallas import tpu as pltpu
from jax.sharding import PartitionSpec as P

HEADDIM = 64
WINDOW = 128
THETA = 150000.0
LOW = -1e30

F32 = jnp.float32
BF16 = jnp.bfloat16


def dot(a, b, ca, cb):
    return lax.dot_general(a, b, (((ca,), (cb,)), ((), ())), preferred_element_type=F32)


def iota(shape, dim):
    return lax.broadcasted_iota(jnp.int32, shape, dim)


def sin_cos(angle):
    turns = jnp.floor(angle * np.float32(2.0 / np.pi) + np.float32(0.5))
    rest = angle - turns * np.float32(1.5703125)
    rest = rest - turns * np.float32(4.837512969970703125e-4)
    rest = rest - turns * np.float32(7.54978995489188216e-8)
    sq = rest * rest
    sin_part = np.float32(-1.9515295891e-4) * sq + np.float32(8.3321608736e-3)
    sin_part = (sin_part * sq + np.float32(-1.6666654611e-1)) * sq * rest + rest
    cos_part = np.float32(2.443315711809948e-5) * sq + np.float32(-1.388731625493765e-3)
    cos_part = (cos_part * sq + np.float32(4.166664568298827e-2)) * sq * sq
    cos_part = cos_part - np.float32(0.5) * sq + np.float32(1.0)
    quadrant = turns.astype(jnp.int32)
    odd = (quadrant & 1) == 1
    sine = jnp.where(odd, cos_part, sin_part)
    cosine = jnp.where(odd, sin_part, cos_part)
    sine = jnp.where((quadrant & 2) == 2, -sine, sine)
    cosine = jnp.where(((quadrant + 1) & 2) == 2, -cosine, cosine)
    return sine, cosine


def as_column(row):
    return jnp.broadcast_to(row, (row.shape[1], row.shape[1])).T


def load(copies):
    for copy in copies:
        copy.start()
    return copies


def prepare_keys(kv, blocks, keys2, values2, keys_t):
    w = WINDOW
    lanes = 2 * HEADDIM
    own_half = (iota((w, lanes), 1) < HEADDIM) == (kv % 2 == 0)
    for b, (k_ref, v_ref, first_row) in enumerate(blocks):
        rows = slice(b * w, (b + 1) * w)
        if first_row is None:
            at = (slice(kv // 2 * w, (kv // 2 + 1) * w), slice(None))
        else:
            at = (slice(first_row, first_row + w), slice(kv // 2 * lanes, (kv // 2 + 1) * lanes))
        k_tile = k_ref[at].astype(F32) * np.float32(HEADDIM**-0.5)
        v_tile = v_ref[at].astype(F32)
        k_tile = jnp.where(own_half, k_tile, np.float32(0.0))
        v_tile = jnp.where(own_half, v_tile, np.float32(0.0))
        keys2[kv, kv % 2, rows, :] = k_tile.astype(BF16)
        values2[kv, kv % 2, rows, :] = v_tile.astype(BF16)
        keys2[kv, 1 - kv % 2, rows, :] = pltpu.roll(k_tile, HEADDIM, 1).astype(BF16)
        values2[kv, 1 - kv % 2, rows, :] = pltpu.roll(v_tile, HEADDIM, 1).astype(BF16)
        half = slice(kv % 2 * HEADDIM, (kv % 2 + 1) * HEADDIM)
        keys_t[kv, :, rows] = k_tile.T[half].astype(BF16)


def attend(
    n_kv, group, row_blocks, window_of, beside, sink_rows, query, grad, ds_s, bias, halves, scratch, add_dk
):
    scores_s, grads_s = scratch
    w = WINDOW
    lanes = 2 * HEADDIM
    quads = group // 4
    tri = iota((w, w), 0) <= iota((w, w), 1)
    tri2 = jnp.concatenate([tri, tri], axis=1)
    items = [(b, kv, quad) for kv in range(n_kv) for b in range(row_blocks) for quad in range(quads)]

    def tiles(ref, b, kv, first, count):
        rows = slice(b * w, (b + 1) * w)
        start = kv * group // 2 + first
        return jnp.concatenate(
            [ref[rows, (start + t) * lanes : (start + t + 1) * lanes] for t in range(count)], axis=0
        )

    def to_scores(n):
        b, kv, quad = items[n]
        key_win, value_win = window_of(b, kv, quad == 0)
        q_two = tiles(query, b, kv, 2 * quad, 2)
        g_two = tiles(grad, b, kv, 2 * quad, 2)
        bias2 = jnp.concatenate([bias[b], bias[b]], axis=1)
        for side in range(2):
            scores = dot(key_win[side], q_two, 1, 1)
            scores_s[n % 2, side] = jnp.where(tri2, scores[w:], scores[:w]) + bias2
        for side in range(2):
            grads = dot(value_win[side], g_two, 1, 1)
            grads_s[n % 2, side] = jnp.where(tri2, grads[w:], grads[:w])

    def to_ds(n):
        b, kv, quad = items[n]
        unit = n // quads
        for side in range(2):
            for t in range(2):
                cols = slice(t * w, (t + 1) * w)
                head = kv * group + 4 * quad + 2 * t + side
                sink = sink_rows[head : head + 1, :]
                scores = scores_s[n % 2, side, :, cols]
                peak = jnp.maximum(jnp.max(scores, axis=0, keepdims=True), sink)
                expo = jnp.exp(scores - peak)
                total = jnp.sum(expo, axis=0, keepdims=True) + jnp.exp(sink - peak)
                probs = expo * (np.float32(1.0) / total)
                grads = grads_s[n % 2, side, :, cols]
                delta = jnp.sum(probs * grads, axis=0, keepdims=True)
                ds = (probs * (grads - delta)).astype(BF16)
                out_cols = slice((2 * quad + t) * w, (2 * quad + t + 1) * w)
                ds_s[unit, side, 0:w, out_cols] = ds * halves[0]
                ds_s[unit, side, w : 2 * w, out_cols] = ds * halves[1]

    def to_grads(n):
        b, kv, quad = items[n]
        if quad == quads - 1:
            q_all = tiles(query, b, kv, 0, group // 2)
            low = iota((2 * w, lanes), 1) < HEADDIM
            sides = [dot(ds_s[n // quads, side], q_all, 1, 0) for side in range(2)]
            add_dk(b, kv, jnp.where(low, sides[0], sides[1]))

    for n in range(len(items) + 2):
        if n < len(items):
            to_scores(n)
        if 0 <= n - 1 < len(items):
            to_ds(n - 1)
        if n >= 2:
            to_grads(n - 2)
        if n < len(items):
            beside(n, len(items))


def attend_scratch():
    w = WINDOW
    return [
        pltpu.VMEM((2, 2, w, 2 * w), F32),
        pltpu.VMEM((2, 2, w, 2 * w), F32),
    ]


def set_halves(halves):
    tri = iota((WINDOW, WINDOW), 0) <= iota((WINDOW, WINDOW), 1)
    halves[0] = jnp.where(tri, np.float32(0.0), np.float32(1.0)).astype(BF16)
    halves[1] = jnp.where(tri, np.float32(1.0), np.float32(0.0)).astype(BF16)


def window_bias(bias, b, prev_segs, own_segs):
    tri = iota((WINDOW, WINDOW), 0) <= iota((WINDOW, WINDOW), 1)
    key_segs = jnp.where(tri, as_column(own_segs), as_column(prev_segs))
    bias[b] = jnp.where(key_segs == own_segs, np.float32(0.0), np.float32(LOW))


def store_dk(dk_part, dk_all, first_block, b, kv, part, seen):
    w = WINDOW
    lanes = 2 * HEADDIM
    if kv % 2 == 0:
        dk_part[b] = part
        return
    even = dk_part[b]
    low = iota(part.shape, 1) < HEADDIM
    both = jnp.where(low, even, part) + pltpu.roll(jnp.where(low, part, even), HEADDIM, 1)
    cols = slice(kv // 2 * lanes, (kv // 2 + 1) * lanes)
    for k in range(2):
        rows = slice((first_block + b + k) * w, (first_block + b + k + 1) * w)
        piece = both[k * w : (k + 1) * w]
        if (first_block + b + k, kv) in seen:
            piece = piece + dk_all[rows, cols]
        seen.add((first_block + b + k, kv))
        dk_all[rows, cols] = piece


def rotate(dk, sine, cosine):
    half = HEADDIM // 2
    lanes = dk.shape[1]
    low = (iota(dk.shape, 1) % HEADDIM) < half
    other = jnp.where(low, pltpu.roll(dk, lanes - half, 1), pltpu.roll(dk, half, 1))
    return (dk * cosine + other * sine) * np.float32(HEADDIM**-0.5)


def turn_table(pos):
    half = HEADDIM // 2
    index = iota((1, 2 * HEADDIM), 1) % half
    rates = (THETA ** (-2.0 * np.arange(half) / HEADDIM)).astype(np.float32)
    freq = jnp.zeros((1, 2 * HEADDIM), F32)
    for t in range(half):
        freq = jnp.where(index == t, rates[t], freq)
    sine, cosine = sin_cos(as_column(pos.astype(F32)) * freq)
    low = (iota(sine.shape, 1) % HEADDIM) < HEADDIM // 2
    return jnp.where(low, sine, -sine), cosine


def local_kernel(
    n_kv, group, sinks_hbm, segs_hbm, pos_hbm, query_hbm, grad_hbm, keys_hbm, values_hbm, inputs_hbm,
    own_ref, table_ref, ds_ref, keys_t, segs0_ref, query0, grad0, keys2, values2, inputs_t, later_ref, sink_rows,
    query, grad, keys, values, inputs, dk_ref, sinks_ref, segs_ref, pos_ref, bias, halves, dk_part, dk_all, id_sem, in_sem, next_sem,
    *scratch,
):
    w = WINDOW
    lanes = 2 * HEADDIM
    rows = keys.shape[0]
    row_blocks = rows // w - 1
    step = group * HEADDIM
    ids = load(
        [
            pltpu.make_async_copy(pos_hbm, pos_ref, id_sem.at[3]),
            pltpu.make_async_copy(segs_hbm, segs_ref, id_sem.at[2]),
            pltpu.make_async_copy(sinks_hbm, sinks_ref, id_sem.at[4]),
        ]
    )
    key_copies = load(
        [
            pltpu.make_async_copy(keys_hbm, keys, id_sem.at[0]),
            pltpu.make_async_copy(values_hbm, values, id_sem.at[1]),
        ]
    )

    def ins(kv):
        cols = slice(kv * step, (kv + 1) * step)
        return [
            pltpu.make_async_copy(query_hbm.at[w:, cols], query.at[:, cols], in_sem.at[0, kv]),
            pltpu.make_async_copy(grad_hbm.at[w:, cols], grad.at[:, cols], in_sem.at[1, kv]),
        ]

    in_copies = [load(ins(kv)) for kv in range(n_kv)]
    next_copies = load(
        [
            pltpu.make_async_copy(query_hbm.at[0:w], query0, next_sem.at[0]),
            pltpu.make_async_copy(grad_hbm.at[0:w], grad0, next_sem.at[1]),
            pltpu.make_async_copy(inputs_hbm, inputs, next_sem.at[2]),
        ]
    )
    set_halves(halves)
    for copy in ids:
        copy.wait()
    for head in range(n_kv * group):
        sink_rows[head : head + 1, :] = jnp.full((1, w), sinks_ref[head], F32)
    segs = [segs_ref[0:1, b * w : (b + 1) * w].astype(F32) for b in range(row_blocks + 1)]
    segs0_ref[...] = segs[0]
    for b in range(row_blocks):
        window_bias(bias, b, segs[b], segs[b + 1])
    for b in range(row_blocks + 1):
        sine, cosine = turn_table(pos_ref[0:1, b * w : (b + 1) * w])
        table_ref[2 * b] = sine
        table_ref[2 * b + 1] = cosine
    for copy in key_copies:
        copy.wait()
    seen = set()

    def window_of(b, kv, first):
        if b == 0 and first:
            prepare_keys(kv, [(keys, values, b * w) for b in range(row_blocks + 1)], keys2, values2, keys_t)
            for copy in in_copies[kv]:
                copy.wait()
        window = slice(b * w, (b + 2) * w)
        return [keys2[kv, side, window, :] for side in range(2)], [values2[kv, side, window, :] for side in range(2)]

    features = inputs.shape[1]
    pieces = [(f, t) for f in range(features // w) for t in range(row_blocks + 1)]

    def turn_inputs(n, count):
        if n == 1:
            next_copies[2].wait()
        n, count = n - 1, count - 1
        for f, t in pieces[n * len(pieces) // count : (n + 1) * len(pieces) // count] if n >= 0 else []:
            cols = slice(f * w, (f + 1) * w)
            inputs_t[cols, t * w : (t + 1) * w] = inputs[t * w : (t + 1) * w, cols].T

    attend(
        n_kv, group, row_blocks, window_of, turn_inputs,
        sink_rows, query, grad, ds_ref, bias, halves, scratch,
        lambda b, kv, part: store_dk(dk_part, dk_all, 0, b, kv, part, seen),
    )
    for b in range(row_blocks + 1):
        for tile in range(n_kv // 2):
            cols = slice(tile * lanes, (tile + 1) * lanes)
            turned = rotate(dk_all[b * w : (b + 1) * w, cols], table_ref[2 * b], table_ref[2 * b + 1])
            if b == 0:
                own_ref[:, cols] = turned
            else:
                dk_ref[(b - 1) * w : b * w, cols] = turned.astype(BF16)
    later_ref[...] = dot(inputs_t[:, w:], dk_ref[...], 1, 0)
    for copy in next_copies[:2]:
        copy.wait()


def rim_kernel(
    n_kv, group, n_dp, own_ref, table_ref, segs0_ref, query, grad, own_keys2, own_values2, own_inputs_t, later_ref,
    sink_rows, rim,
    send_ref, keep_ref, ds_ref, keys_t,
    keys2, values2, bias, halves, dk_part, dk_all, dk16, inputs_t, sums, *scratch,
):
    w = WINDOW
    lanes = 2 * HEADDIM
    features = own_inputs_t.shape[0]
    kv_width = n_kv * HEADDIM
    set_halves(halves)
    rim_keys = rim.at[features : features + kv_width]
    rim_values = rim.at[features + kv_width : features + 2 * kv_width]
    aux = rim[features + 2 * kv_width :, :].astype(F32)
    rim_segs = jnp.where(lax.axis_index("seq") == 0, np.float32(-1.0), aux[0:1])
    window_bias(bias, 0, rim_segs, segs0_ref[...])
    rim_sine, rim_cosine = turn_table(aux[1:2] * np.float32(256.0) + aux[2:3])
    seen = set()

    def window_of(b, kv, first):
        if first:
            prepare_keys(kv, [(rim_keys, rim_values, None)], keys2, values2, keys_t)
        both = [(keys2, own_keys2), (values2, own_values2)]
        return [
            [jnp.concatenate([rim2[kv, side], own2[kv, side, 0:w]], axis=0) for side in range(2)]
            for rim2, own2 in both
        ]

    tiles = features // w

    def turn_inputs(n, count):
        for f in range(n * tiles // count, (n + 1) * tiles // count):
            cols = slice(f * w, (f + 1) * w)
            inputs_t[cols, 0:w] = rim[cols, :].T
            inputs_t[cols, w : 2 * w] = own_inputs_t[cols, 0:w]

    attend(
        n_kv, group, 1, window_of, turn_inputs,
        sink_rows, query, grad, ds_ref, bias, halves, scratch,
        lambda b, kv, part: store_dk(dk_part, dk_all, 0, b, kv, part, seen),
    )
    for tile in range(n_kv // 2):
        cols = slice(tile * lanes, (tile + 1) * lanes)
        dk16[0:w, cols] = rotate(dk_all[0:w, cols], rim_sine, rim_cosine).astype(BF16)
        own = rotate(dk_all[w : 2 * w, cols], table_ref[0], table_ref[1]) + own_ref[:, cols]
        dk16[w : 2 * w, cols] = own.astype(BF16)
    sums[...] = dot(inputs_t[...], dk16[...], 1, 0) + later_ref[...]
    piece = features // (2 * n_dp)
    dp_index = lax.axis_index("dp")
    core = lax.axis_index("seq") & 1
    for half, ref in enumerate([keep_ref, send_ref]):
        for j, relative in enumerate(bit_reversed(n_dp)):
            if piece % 16 == 0:
                side = core ^ half
                block = (dp_index ^ (relative + side * (swapped(relative, n_dp) - relative))) * 2 + side
                start = pl.multiple_of(block * piece, piece)
                ref[j * piece : (j + 1) * piece, :] = sums[pl.ds(start, piece), :].astype(BF16)
    if piece % 16:
        keep_ref[...] = sums[0 : features // 2, :].astype(BF16)
        send_ref[...] = sums[features // 2 :, :].astype(BF16)


def query_kernel(n_kv, group, local_ds, local_keys, rim_ds, rim_keys, dq_hbm, dq, out_sem):
    w = WINDOW
    lanes = 2 * HEADDIM
    step = group * HEADDIM
    row_blocks = local_ds.shape[0] // n_kv
    outs = []
    for block in range(row_blocks + 1):
        rows = slice(block * w, (block + 1) * w)
        for kv in range(n_kv):
            for tile in range(group // 2):
                cols = slice(tile * w, (tile + 1) * w)
                if block == 0:
                    keyt_win = jnp.concatenate([rim_keys[kv], local_keys[kv, :, 0:w]], axis=1)
                    ds_ref, unit = rim_ds, kv
                else:
                    keyt_win = local_keys[kv, :, (block - 1) * w : (block + 1) * w]
                    ds_ref, unit = local_ds, kv * row_blocks + block - 1
                dq_t = [dot(keyt_win, ds_ref[unit, side, :, cols], 1, 0) for side in range(2)]
                start = kv * group // 2 + tile
                dq[rows, start * lanes : (start + 1) * lanes] = jnp.concatenate(dq_t, axis=0).T.astype(BF16)
            cols = slice(kv * step, (kv + 1) * step)
            outs += load([pltpu.make_async_copy(dq.at[rows, cols], dq_hbm.at[rows, cols], out_sem.at[block, kv])])
    for copy in outs:
        copy.wait()


ANY = pl.BlockSpec(memory_space=pl.ANY)
HBM = pl.BlockSpec(memory_space=pltpu.HBM)
VMEM = pl.BlockSpec(memory_space=pltpu.VMEM)
SMEM = pl.BlockSpec(memory_space=pltpu.SMEM)
LIMIT = 24 * 2**20


def estimate(row_blocks, width, extra_flops, extra_bytes):
    w = WINDOW
    return pl.CostEstimate(
        flops=10 * row_blocks * w * 2 * w * width + extra_flops,
        bytes_accessed=6 * row_blocks * w * width + extra_bytes,
        transcendentals=row_blocks * w * w * width // HEADDIM,
    )


def sizes(query, keys):
    width, kv_width = query.shape[-1], keys.shape[-1]
    return width, kv_width, kv_width // HEADDIM, width // kv_width


def shape(*dims, kind=BF16):
    return jax.ShapeDtypeStruct(dims, kind)


def local_grads(query, grad_out, keys, values, layer_input, segments, positions, sinks):
    rows, features = layer_input.shape
    width, kv_width, n_kv, group = sizes(query, keys)
    w = WINDOW
    lanes = 2 * HEADDIM
    row_blocks = rows // w - 1
    return pl.pallas_call(
        lambda *refs: local_kernel(n_kv, group, *refs),
        name="local_grads",
        in_specs=[HBM] * 8,
        out_specs=[VMEM] * 12,
        out_shape=[
            shape(w, kv_width, kind=F32),
            shape(2 * (row_blocks + 1), w, lanes, kind=F32),
            shape(row_blocks * n_kv, 2, 2 * w, group // 2 * w),
            shape(n_kv, HEADDIM, rows),
            shape(1, w, kind=F32),
            shape(w, width),
            shape(w, width),
            shape(n_kv, 2, rows, lanes),
            shape(n_kv, 2, rows, lanes),
            shape(features, rows),
            shape(features, kv_width, kind=F32),
            shape(n_kv * group, w, kind=F32),
        ],
        scratch_shapes=[
            pltpu.VMEM((row_blocks * w, width), BF16),
            pltpu.VMEM((row_blocks * w, width), BF16),
            pltpu.VMEM((rows, kv_width), BF16),
            pltpu.VMEM((rows, kv_width), BF16),
            pltpu.VMEM(layer_input.shape, BF16),
            pltpu.VMEM((rows - w, kv_width), BF16),
            pltpu.SMEM(sinks.shape, F32),
            pltpu.VMEM(segments.shape, jnp.int32),
            pltpu.VMEM(segments.shape, jnp.int32),
            pltpu.VMEM((row_blocks, w, w), F32),
            pltpu.VMEM((2, w, w), BF16),
            pltpu.VMEM((row_blocks, 2 * w, lanes), F32),
            pltpu.VMEM((rows, kv_width), F32),
            pltpu.SemaphoreType.DMA((5,)),
            pltpu.SemaphoreType.DMA((2, n_kv)),
            pltpu.SemaphoreType.DMA((3,)),
        ]
        + attend_scratch(),
        compiler_params=pltpu.CompilerParams(vmem_limit_bytes=LIMIT),
        cost_estimate=estimate(row_blocks, width, 0, 0),
    )(sinks, segments, positions, query, grad_out, keys, values, layer_input)


def rim_grads(local, rim, kv_width, n_dp):
    own, table, _, _, segs0, query0, grad0, keys2, values2, inputs_t, later, sink_rows = local
    features, rows = inputs_t.shape
    width = query0.shape[1]
    n_kv = kv_width // HEADDIM
    group = width // kv_width
    w = WINDOW
    lanes = 2 * HEADDIM
    return pl.pallas_call(
        lambda *refs: rim_kernel(n_kv, group, n_dp, *refs),
        name="rim_grads",
        in_specs=[VMEM] * 11,
        out_specs=[VMEM] * 4,
        out_shape=[
            shape(features // 2, kv_width),
            shape(features // 2, kv_width),
            shape(n_kv, 2, 2 * w, group // 2 * w),
            shape(n_kv, HEADDIM, w),
        ],
        scratch_shapes=[
            pltpu.VMEM((n_kv, 2, w, lanes), BF16),
            pltpu.VMEM((n_kv, 2, w, lanes), BF16),
            pltpu.VMEM((1, w, w), F32),
            pltpu.VMEM((2, w, w), BF16),
            pltpu.VMEM((1, 2 * w, lanes), F32),
            pltpu.VMEM((2 * w, kv_width), F32),
            pltpu.VMEM((2 * w, kv_width), BF16),
            pltpu.VMEM((features, 2 * w), BF16),
            pltpu.VMEM((features, kv_width), F32),
        ]
        + attend_scratch(),
        compiler_params=pltpu.CompilerParams(vmem_limit_bytes=LIMIT),
        cost_estimate=estimate(1, width, 2 * features * kv_width * 2 * w, 8 * features * kv_width),
    )(own, table, segs0, query0, grad0, keys2, values2, inputs_t, later, sink_rows, rim)


def query_grads(local_ds, local_keys, rim_ds, rim_keys, group):
    n_kv, _, rows = local_keys.shape
    width = n_kv * group * HEADDIM
    w = WINDOW
    return pl.pallas_call(
        lambda *refs: query_kernel(n_kv, group, *refs),
        name="query_grads",
        in_specs=[VMEM] * 4,
        out_specs=HBM,
        out_shape=shape(rows, width),
        scratch_shapes=[pltpu.VMEM((rows, width), BF16), pltpu.SemaphoreType.DMA((rows // w, n_kv))],
        compiler_params=pltpu.CompilerParams(vmem_limit_bytes=LIMIT),
        cost_estimate=pl.CostEstimate(
            flops=4 * rows * w * width, bytes_accessed=2 * rows * width + 4 * rows * w * width // HEADDIM, transcendentals=0
        ),
    )(local_ds, local_keys, rim_ds, rim_keys)


def tail_kernel(segs_hbm, pos_hbm, inputs_hbm, keys_hbm, values_hbm, out_ref, segs_ref, pos_ref, sem):
    w = WINDOW
    rows = inputs_hbm.shape[0]
    ids = load(
        [
            pltpu.make_async_copy(segs_hbm, segs_ref, sem.at[0]),
            pltpu.make_async_copy(pos_hbm, pos_ref, sem.at[1]),
        ]
    )
    copies = []
    for hbm in (inputs_hbm, keys_hbm, values_hbm):
        for start in range(0, hbm.shape[1], w):
            n = len(copies)
            source = hbm.at[rows - w :, start : start + w]
            copies += load([pltpu.make_async_copy(source, out_ref.at[n * w : (n + 1) * w], sem.at[n + 2])])
    for copy in ids:
        copy.wait()
    line = iota((16, w), 0)
    segs = segs_ref[0:1, rows - w :]
    pos = pos_ref[0:1, rows - w :]
    aux = jnp.where(line == 0, segs, jnp.where(line == 1, pos >> 8, pos & 255))
    out_ref[len(copies) * w :, :] = aux.astype(F32).astype(BF16)
    for copy in copies:
        copy.wait()


def last_tokens(layer_input, keys, values, segments, positions):
    tiles = (layer_input.shape[1] + 2 * keys.shape[1]) // WINDOW
    return pl.pallas_call(
        tail_kernel,
        name="last_tokens",
        in_specs=[HBM] * 5,
        out_specs=VMEM,
        out_shape=shape(tiles * WINDOW + 16, WINDOW),
        scratch_shapes=[
            pltpu.VMEM(segments.shape, jnp.int32),
            pltpu.VMEM(segments.shape, jnp.int32),
            pltpu.SemaphoreType.DMA((tiles + 2,)),
        ],
        compiler_params=pltpu.CompilerParams(vmem_limit_bytes=LIMIT),
    )(segments, positions, layer_input, keys, values)


def swapped(relative, n):
    return relative if n < 4 else (relative & ~3) | (relative & 1) << 1 | (relative & 2) >> 1


def bit_reversed(n):
    bits = n.bit_length() - 1
    return [int(format(i, "b").zfill(bits)[::-1], 2) if bits else 0 for i in range(n)]


def exchange(part, axis, by):
    count = lax.axis_size(axis)
    return lax.ppermute(part, axis, [(i, i ^ by) for i in range(count)])


def bits(n):
    return n.bit_length() - 1


def share_and_sum(total, by):
    n_dp, n_seq = lax.axis_size("dp"), lax.axis_size("seq")
    half = total.shape[0] // 2
    mine, theirs = total[:half].astype(BF16), total[half:].astype(BF16)

    def swap(part, dp_bits, seq_bits):
        pairs = [
            (d * n_seq + q, (d ^ dp_bits) * n_seq + (q ^ seq_bits)) for d in range(n_dp) for q in range(n_seq)
        ]
        return lax.ppermute(part, ("dp", "seq"), pairs).astype(F32)

    far = swap(theirs, by, 2)
    near = swap(theirs, by, 0)
    beside = swap(mine, 0, 2)
    return (far + near) + (beside + mine.astype(F32))


def exchange_by_core(part, relative):
    n_dp, n_seq = lax.axis_size("dp"), lax.axis_size("seq")
    pairs = []
    for d in range(n_dp):
        for q in range(n_seq):
            other = d ^ (swapped(relative, n_dp) if q % 2 else relative)
            pairs.append((d * n_seq + q, other * n_seq + q))
    return lax.ppermute(part, ("dp", "seq"), pairs)


def share(total, by, ways, beside=None, held=None):
    rows = total.shape[0] // ways
    parts = [total[k * rows : (k + 1) * rows] for k in range(ways)]
    sends = [part.astype(BF16) for part in parts[1:]]
    if beside is not None:
        sends, held = lax.optimization_barrier((sends, held))
        extra = beside(held)
    got = []
    for k in reversed(range(1, ways)):
        relative = bit_reversed(ways)[k] * by
        got.append(exchange_by_core(sends[k - 1], relative))
    if beside is not None:
        got, extra = lax.optimization_barrier((got, extra))
    total = parts[0]
    for part in got:
        total = total + part.astype(F32)
    return total if beside is None else (total, extra)


def forward_one(part, axis):
    count = lax.axis_size(axis)
    return lax.ppermute(part, axis, [(i, i + 1) for i in range(count - 1)])


def body(query, keys, values, grad_out, layer_input, sinks, segments, positions):
    n_dp = lax.axis_size("dp")
    n_seq = lax.axis_size("seq")
    dp_index = lax.axis_index("dp")
    seq_index = lax.axis_index("seq")
    core = seq_index & 1
    kv_width = keys.shape[2]
    features = layer_input.shape[2]
    piece = features // (2 * n_dp)
    query, grad_out, layer_input, keys, values = [
        pltpu.with_memory_space_constraint(x[0], pltpu.HBM) for x in (query, grad_out, layer_input, keys, values)
    ]
    sinks, segments, positions = [
        pltpu.with_memory_space_constraint(x, pltpu.HBM) for x in (sinks, segments, positions)
    ]
    tail = last_tokens(layer_input, keys, values, segments, positions)
    rim = forward_one(tail, "seq")
    local = local_grads(query, grad_out, keys, values, layer_input, segments, positions, sinks)
    send, keep, rim_ds, rim_keys = rim_grads(local, rim, kv_width, n_dp)
    if piece % 16:
        plain = jnp.concatenate([keep, send], axis=0).reshape(n_dp, 2, piece, kv_width)
        order = bit_reversed(n_dp)
        orders = jnp.asarray([order, [swapped(relative, n_dp) for relative in order]], jnp.int32) ^ dp_index
        keep, send = [
            jnp.take(plain[:, side], orders[side], axis=0).reshape(-1, kv_width) for side in (core, core ^ 1)
        ]
    total = keep.astype(F32) + exchange(send, "seq", 1).astype(F32)
    group = query.shape[1] // kv_width

    def beside(held):
        return query_grads(*held, group)

    held = (local[2], local[3], rim_ds, rim_keys)
    dq = None
    by = 1
    last = n_dp // 2 if n_seq == 4 and bits(n_dp) % 2 else n_dp
    while by < last:
        ways = 4 if 4 * by <= last else 2
        if dq is None:
            total, dq = share(total, by, ways, beside, held)
        else:
            total = share(total, by, ways)
        by *= ways
    if dq is None:
        dq = beside(held)
    if last < n_dp:
        total = share_and_sum(total, last)
    else:
        by = 2
        while by < n_seq:
            mine = total.astype(BF16)
            total = mine.astype(F32) + exchange(mine, "seq", by).astype(F32)
            by *= 2
    other = exchange(total, "seq", 1)
    pair = jnp.where(core == 0, jnp.stack([total, other]), jnp.stack([other, total]))
    return (dq[None], pair.reshape(-1, kv_width))


def solution(mesh):
    return jax.shard_map(
        body,
        mesh=mesh,
        in_specs=(
            P("dp", "seq", None),
            P("dp", "seq", None),
            P("dp", "seq", None),
            P("dp", "seq", None),
            P("dp", "seq", None),
            P(),
            P("dp", "seq"),
            P("dp", "seq"),
        ),
        out_specs=(P("dp", "seq", None), P("dp", None)),
        check_vma=False,
    )
```

```python
import jax
import jax.numpy as jnp
import numpy as np
from jax import lax
from jax.experimental import pallas as pl
from jax.experimental.pallas import tpu as pltpu
from jax.sharding import PartitionSpec as P

HEADDIM = 64
WINDOW = 128
THETA = 150000.0
LOW = -1e30

F32 = jnp.float32
BF16 = jnp.bfloat16


def dot(a, b, ca, cb):
    return lax.dot_general(a, b, (((ca,), (cb,)), ((), ())), preferred_element_type=F32)


def iota(shape, dim):
    return lax.broadcasted_iota(jnp.int32, shape, dim)


def sin_cos(angle):
    turns = jnp.floor(angle * np.float32(2.0 / np.pi) + np.float32(0.5))
    rest = angle - turns * np.float32(1.5703125)
    rest = rest - turns * np.float32(4.837512969970703125e-4)
    rest = rest - turns * np.float32(7.54978995489188216e-8)
    sq = rest * rest
    sin_part = np.float32(-1.9515295891e-4) * sq + np.float32(8.3321608736e-3)
    sin_part = (sin_part * sq + np.float32(-1.6666654611e-1)) * sq * rest + rest
    cos_part = np.float32(2.443315711809948e-5) * sq + np.float32(-1.388731625493765e-3)
    cos_part = (cos_part * sq + np.float32(4.166664568298827e-2)) * sq * sq
    cos_part = cos_part - np.float32(0.5) * sq + np.float32(1.0)
    quadrant = turns.astype(jnp.int32)
    odd = (quadrant & 1) == 1
    sine = jnp.where(odd, cos_part, sin_part)
    cosine = jnp.where(odd, sin_part, cos_part)
    sine = jnp.where((quadrant & 2) == 2, -sine, sine)
    cosine = jnp.where(((quadrant + 1) & 2) == 2, -cosine, cosine)
    return sine, cosine


def as_column(row):
    return jnp.broadcast_to(row, (row.shape[1], row.shape[1])).T


def load(copies):
    for copy in copies:
        copy.start()
    return copies


def prepare_keys(kv, blocks, keys2, values2, keys_t):
    w = WINDOW
    lanes = 2 * HEADDIM
    own_half = (iota((w, lanes), 1) < HEADDIM) == (kv % 2 == 0)
    for b, (k_ref, v_ref, first_row) in enumerate(blocks):
        rows = slice(b * w, (b + 1) * w)
        if first_row is None:
            at = (slice(kv // 2 * w, (kv // 2 + 1) * w), slice(None))
        else:
            at = (slice(first_row, first_row + w), slice(kv // 2 * lanes, (kv // 2 + 1) * lanes))
        k_tile = k_ref[at].astype(F32) * np.float32(HEADDIM**-0.5)
        v_tile = v_ref[at].astype(F32)
        k_tile = jnp.where(own_half, k_tile, np.float32(0.0))
        v_tile = jnp.where(own_half, v_tile, np.float32(0.0))
        keys2[kv, kv % 2, rows, :] = k_tile.astype(BF16)
        values2[kv, kv % 2, rows, :] = v_tile.astype(BF16)
        keys2[kv, 1 - kv % 2, rows, :] = pltpu.roll(k_tile, HEADDIM, 1).astype(BF16)
        values2[kv, 1 - kv % 2, rows, :] = pltpu.roll(v_tile, HEADDIM, 1).astype(BF16)
        half = slice(kv % 2 * HEADDIM, (kv % 2 + 1) * HEADDIM)
        keys_t[kv, :, rows] = k_tile.T[half].astype(BF16)


def attend(
    n_kv, group, row_blocks, window_of, beside, sink_rows, query, grad, ds_s, bias, halves, scratch, add_dk
):
    scores_s, grads_s = scratch
    w = WINDOW
    lanes = 2 * HEADDIM
    quads = group // 4
    tri = iota((w, w), 0) <= iota((w, w), 1)
    tri2 = jnp.concatenate([tri, tri], axis=1)
    items = [(b, kv, quad) for kv in range(n_kv) for b in range(row_blocks) for quad in range(quads)]

    def tiles(ref, b, kv, first, count):
        rows = slice(b * w, (b + 1) * w)
        start = kv * group // 2 + first
        return jnp.concatenate(
            [ref[rows, (start + t) * lanes : (start + t + 1) * lanes] for t in range(count)], axis=0
        )

    def to_scores(n):
        b, kv, quad = items[n]
        key_win, value_win = window_of(b, kv, quad == 0)
        q_two = tiles(query, b, kv, 2 * quad, 2)
        g_two = tiles(grad, b, kv, 2 * quad, 2)
        bias2 = jnp.concatenate([bias[b], bias[b]], axis=1)
        for side in range(2):
            scores = dot(key_win[side], q_two, 1, 1)
            scores_s[n % 2, side] = jnp.where(tri2, scores[w:], scores[:w]) + bias2
        for side in range(2):
            grads = dot(value_win[side], g_two, 1, 1)
            grads_s[n % 2, side] = jnp.where(tri2, grads[w:], grads[:w])

    def to_ds(n):
        b, kv, quad = items[n]
        unit = n // quads
        for side in range(2):
            for t in range(2):
                cols = slice(t * w, (t + 1) * w)
                head = kv * group + 4 * quad + 2 * t + side
                sink = sink_rows[head : head + 1, :]
                scores = scores_s[n % 2, side, :, cols]
                peak = jnp.maximum(jnp.max(scores, axis=0, keepdims=True), sink)
                expo = jnp.exp(scores - peak)
                total = jnp.sum(expo, axis=0, keepdims=True) + jnp.exp(sink - peak)
                probs = expo * (np.float32(1.0) / total)
                grads = grads_s[n % 2, side, :, cols]
                delta = jnp.sum(probs * grads, axis=0, keepdims=True)
                ds = (probs * (grads - delta)).astype(BF16)
                out_cols = slice((2 * quad + t) * w, (2 * quad + t + 1) * w)
                ds_s[unit, side, 0:w, out_cols] = ds * halves[0]
                ds_s[unit, side, w : 2 * w, out_cols] = ds * halves[1]

    def to_grads(n):
        b, kv, quad = items[n]
        if quad == quads - 1:
            q_all = tiles(query, b, kv, 0, group // 2)
            low = iota((2 * w, lanes), 1) < HEADDIM
            sides = [dot(ds_s[n // quads, side], q_all, 1, 0) for side in range(2)]
            add_dk(b, kv, jnp.where(low, sides[0], sides[1]))

    for n in range(len(items) + 2):
        if n < len(items):
            to_scores(n)
        if 0 <= n - 1 < len(items):
            to_ds(n - 1)
        if n >= 2:
            to_grads(n - 2)
        if n < len(items):
            beside(n, len(items))


def attend_scratch():
    w = WINDOW
    return [
        pltpu.VMEM((2, 2, w, 2 * w), F32),
        pltpu.VMEM((2, 2, w, 2 * w), F32),
    ]


def set_halves(halves):
    tri = iota((WINDOW, WINDOW), 0) <= iota((WINDOW, WINDOW), 1)
    halves[0] = jnp.where(tri, np.float32(0.0), np.float32(1.0)).astype(BF16)
    halves[1] = jnp.where(tri, np.float32(1.0), np.float32(0.0)).astype(BF16)


def tile_ready(tile, count, n_kv):
    n = (2 * tile + 2) * count // n_kv + 2
    return n if n < count else None


def window_bias(bias, b, prev_segs, own_segs):
    tri = iota((WINDOW, WINDOW), 0) <= iota((WINDOW, WINDOW), 1)
    key_segs = jnp.where(tri, as_column(own_segs), as_column(prev_segs))
    bias[b] = jnp.where(key_segs == own_segs, np.float32(0.0), np.float32(LOW))


def store_dk(dk_part, dk_all, first_block, b, kv, part, seen):
    w = WINDOW
    lanes = 2 * HEADDIM
    if kv % 2 == 0:
        dk_part[b] = part
        return
    even = dk_part[b]
    low = iota(part.shape, 1) < HEADDIM
    both = jnp.where(low, even, part) + pltpu.roll(jnp.where(low, part, even), HEADDIM, 1)
    cols = slice(kv // 2 * lanes, (kv // 2 + 1) * lanes)
    for k in range(2):
        rows = slice((first_block + b + k) * w, (first_block + b + k + 1) * w)
        piece = both[k * w : (k + 1) * w]
        if (first_block + b + k, kv) in seen:
            piece = piece + dk_all[rows, cols]
        seen.add((first_block + b + k, kv))
        dk_all[rows, cols] = piece


def rotate(dk, sine, cosine):
    half = HEADDIM // 2
    lanes = dk.shape[1]
    low = (iota(dk.shape, 1) % HEADDIM) < half
    other = jnp.where(low, pltpu.roll(dk, lanes - half, 1), pltpu.roll(dk, half, 1))
    return (dk * cosine + other * sine) * np.float32(HEADDIM**-0.5)


def turn_table(pos):
    half = HEADDIM // 2
    index = iota((1, 2 * HEADDIM), 1) % half
    rates = (THETA ** (-2.0 * np.arange(half) / HEADDIM)).astype(np.float32)
    freq = jnp.zeros((1, 2 * HEADDIM), F32)
    for t in range(half):
        freq = jnp.where(index == t, rates[t], freq)
    sine, cosine = sin_cos(as_column(pos.astype(F32)) * freq)
    low = (iota(sine.shape, 1) % HEADDIM) < HEADDIM // 2
    return jnp.where(low, sine, -sine), cosine


def local_kernel(
    n_kv, group, sinks_hbm, segs_hbm, pos_hbm, query_hbm, grad_hbm, keys_hbm, values_hbm, inputs_hbm,
    own_ref, table_ref, ds_ref, keys_t, segs0_ref, query0, grad0, keys2, values2, inputs_t, later_ref, sink_rows,
    query, grad, keys, values, inputs, dk_ref, sinks_ref, segs_ref, pos_ref, bias, halves, dk_part, dk_all, id_sem, in_sem, next_sem,
    *scratch,
):
    w = WINDOW
    lanes = 2 * HEADDIM
    rows = keys.shape[0]
    row_blocks = rows // w - 1
    step = group * HEADDIM
    ids = load(
        [
            pltpu.make_async_copy(pos_hbm, pos_ref, id_sem.at[3]),
            pltpu.make_async_copy(segs_hbm, segs_ref, id_sem.at[2]),
            pltpu.make_async_copy(sinks_hbm, sinks_ref, id_sem.at[4]),
        ]
    )
    key_copies = load(
        [
            pltpu.make_async_copy(keys_hbm, keys, id_sem.at[0]),
            pltpu.make_async_copy(values_hbm, values, id_sem.at[1]),
        ]
    )

    def ins(kv):
        cols = slice(kv * step, (kv + 1) * step)
        return [
            pltpu.make_async_copy(query_hbm.at[w:, cols], query.at[:, cols], in_sem.at[0, kv]),
            pltpu.make_async_copy(grad_hbm.at[w:, cols], grad.at[:, cols], in_sem.at[1, kv]),
        ]

    in_copies = [load(ins(kv)) for kv in range(n_kv)]
    next_copies = load(
        [
            pltpu.make_async_copy(query_hbm.at[0:w], query0, next_sem.at[0]),
            pltpu.make_async_copy(grad_hbm.at[0:w], grad0, next_sem.at[1]),
            pltpu.make_async_copy(inputs_hbm, inputs, next_sem.at[2]),
        ]
    )
    set_halves(halves)
    for copy in ids:
        copy.wait()
    for head in range(n_kv * group):
        sink_rows[head : head + 1, :] = jnp.full((1, w), sinks_ref[head], F32)
    segs = [segs_ref[0:1, b * w : (b + 1) * w].astype(F32) for b in range(row_blocks + 1)]
    segs0_ref[...] = segs[0]
    for b in range(row_blocks):
        window_bias(bias, b, segs[b], segs[b + 1])
    for b in range(row_blocks + 1):
        sine, cosine = turn_table(pos_ref[0:1, b * w : (b + 1) * w])
        table_ref[2 * b] = sine
        table_ref[2 * b + 1] = cosine
    for copy in key_copies:
        copy.wait()
    seen = set()

    def window_of(b, kv, first):
        if b == 0 and first:
            prepare_keys(kv, [(keys, values, b * w) for b in range(row_blocks + 1)], keys2, values2, keys_t)
            waits = [in_copies[0], sum(in_copies[1:], []) + next_copies[2:]] + [[]] * n_kv
            for copy in waits[kv]:
                copy.wait()
        window = slice(b * w, (b + 2) * w)
        return [keys2[kv, side, window, :] for side in range(2)], [values2[kv, side, window, :] for side in range(2)]

    features = inputs.shape[1]
    pieces = [(f, t) for f in range(features // w) for t in range(row_blocks + 1)]

    def turn_inputs(n, count):
        begin, end = count // n_kv, 2 * count // n_kv + 2
        if n == tile_ready(0, count, n_kv):
            finish(0)
        if begin <= n < end:
            for f, t in pieces[(n - begin) * len(pieces) // (end - begin) : (n + 1 - begin) * len(pieces) // (end - begin)]:
                cols = slice(f * w, (f + 1) * w)
                inputs_t[cols, t * w : (t + 1) * w] = inputs[t * w : (t + 1) * w, cols].T

    def finish(tile):
        cols = slice(tile * lanes, (tile + 1) * lanes)
        for b in range(row_blocks + 1):
            turned = rotate(dk_all[b * w : (b + 1) * w, cols], table_ref[2 * b], table_ref[2 * b + 1])
            if b == 0:
                own_ref[:, cols] = turned
            else:
                dk_ref[(b - 1) * w : b * w, cols] = turned.astype(BF16)
        later_ref[:, cols] = dot(inputs_t[:, w:], dk_ref[:, cols], 1, 0)

    attend(
        n_kv, group, row_blocks, window_of, turn_inputs,
        sink_rows, query, grad, ds_ref, bias, halves, scratch,
        lambda b, kv, part: store_dk(dk_part, dk_all, 0, b, kv, part, seen),
    )
    for tile in range(1 if tile_ready(0, n_kv * row_blocks * group // 4, n_kv) else 0, n_kv // 2):
        finish(tile)
    for copy in next_copies[:2]:
        copy.wait()


def rim_kernel(
    n_kv, group, n_dp, own_ref, table_ref, segs0_ref, query, grad, own_keys2, own_values2, own_inputs_t, later_ref,
    sink_rows, rim,
    send_ref, keep_ref, ds_ref, keys_t,
    keys2, values2, bias, halves, dk_part, dk_all, dk16, inputs_t, sums, *scratch,
):
    w = WINDOW
    lanes = 2 * HEADDIM
    features = own_inputs_t.shape[0]
    kv_width = n_kv * HEADDIM
    set_halves(halves)
    rim_keys = rim.at[features : features + kv_width]
    rim_values = rim.at[features + kv_width : features + 2 * kv_width]
    aux = rim[features + 2 * kv_width :, :].astype(F32)
    rim_segs = jnp.where(lax.axis_index("seq") == 0, np.float32(-1.0), aux[0:1])
    window_bias(bias, 0, rim_segs, segs0_ref[...])
    rim_sine, rim_cosine = turn_table(aux[1:2] * np.float32(256.0) + aux[2:3])
    seen = set()

    def window_of(b, kv, first):
        if first:
            prepare_keys(kv, [(rim_keys, rim_values, None)], keys2, values2, keys_t)
        both = [(keys2, own_keys2), (values2, own_values2)]
        return [
            [jnp.concatenate([rim2[kv, side], own2[kv, side, 0:w]], axis=0) for side in range(2)]
            for rim2, own2 in both
        ]

    tiles = features // w

    def turn_inputs(n, count):
        end = 2 * count // n_kv + 2
        if n == tile_ready(0, count, n_kv):
            finish(0)
        if n < end:
            for f in range(n * tiles // end, (n + 1) * tiles // end):
                cols = slice(f * w, (f + 1) * w)
                inputs_t[cols, 0:w] = rim[cols, :].T
                inputs_t[cols, w : 2 * w] = own_inputs_t[cols, 0:w]

    piece = features // (2 * n_dp)
    dp_index = lax.axis_index("dp")
    core = lax.axis_index("seq") & 1

    def finish(tile):
        cols = slice(tile * lanes, (tile + 1) * lanes)
        dk16[0:w, cols] = rotate(dk_all[0:w, cols], rim_sine, rim_cosine).astype(BF16)
        own = rotate(dk_all[w : 2 * w, cols], table_ref[0], table_ref[1]) + own_ref[:, cols]
        dk16[w : 2 * w, cols] = own.astype(BF16)
        sums[:, cols] = dot(inputs_t[...], dk16[:, cols], 1, 0) + later_ref[:, cols]
        for half, ref in enumerate([keep_ref, send_ref]):
            for j, relative in enumerate(bit_reversed(n_dp)):
                if piece % 16 == 0:
                    side = core ^ half
                    block = (dp_index ^ (relative + side * (swapped(relative, n_dp) - relative))) * 2 + side
                    start = pl.multiple_of(block * piece, piece)
                    ref[j * piece : (j + 1) * piece, cols] = sums[pl.ds(start, piece), cols].astype(BF16)
            if piece % 16:
                ref[:, cols] = sums[half * features // 2 : (half + 1) * features // 2, cols].astype(BF16)

    attend(
        n_kv, group, 1, window_of, turn_inputs,
        sink_rows, query, grad, ds_ref, bias, halves, scratch,
        lambda b, kv, part: store_dk(dk_part, dk_all, 0, b, kv, part, seen),
    )
    for tile in range(1 if tile_ready(0, n_kv * group // 4, n_kv) else 0, n_kv // 2):
        finish(tile)


def query_kernel(n_kv, group, local_ds, local_keys, rim_ds, rim_keys, dq_hbm, dq, out_sem):
    w = WINDOW
    lanes = 2 * HEADDIM
    step = group * HEADDIM
    row_blocks = local_ds.shape[0] // n_kv
    outs = []
    for block in range(row_blocks + 1):
        rows = slice(block * w, (block + 1) * w)
        for kv in range(n_kv):
            for tile in range(group // 2):
                cols = slice(tile * w, (tile + 1) * w)
                if block == 0:
                    keyt_win = jnp.concatenate([rim_keys[kv], local_keys[kv, :, 0:w]], axis=1)
                    ds_ref, unit = rim_ds, kv
                else:
                    keyt_win = local_keys[kv, :, (block - 1) * w : (block + 1) * w]
                    ds_ref, unit = local_ds, kv * row_blocks + block - 1
                dq_t = [dot(keyt_win, ds_ref[unit, side, :, cols], 1, 0) for side in range(2)]
                start = kv * group // 2 + tile
                dq[rows, start * lanes : (start + 1) * lanes] = jnp.concatenate(dq_t, axis=0).T.astype(BF16)
            cols = slice(kv * step, (kv + 1) * step)
            outs += load([pltpu.make_async_copy(dq.at[rows, cols], dq_hbm.at[rows, cols], out_sem.at[block, kv])])
    for copy in outs:
        copy.wait()


ANY = pl.BlockSpec(memory_space=pl.ANY)
HBM = pl.BlockSpec(memory_space=pltpu.HBM)
VMEM = pl.BlockSpec(memory_space=pltpu.VMEM)
SMEM = pl.BlockSpec(memory_space=pltpu.SMEM)
LIMIT = 24 * 2**20


def estimate(row_blocks, width, extra_flops, extra_bytes):
    w = WINDOW
    return pl.CostEstimate(
        flops=10 * row_blocks * w * 2 * w * width + extra_flops,
        bytes_accessed=6 * row_blocks * w * width + extra_bytes,
        transcendentals=row_blocks * w * w * width // HEADDIM,
    )


def sizes(query, keys):
    width, kv_width = query.shape[-1], keys.shape[-1]
    return width, kv_width, kv_width // HEADDIM, width // kv_width


def shape(*dims, kind=BF16):
    return jax.ShapeDtypeStruct(dims, kind)


def local_grads(query, grad_out, keys, values, layer_input, segments, positions, sinks):
    rows, features = layer_input.shape
    width, kv_width, n_kv, group = sizes(query, keys)
    w = WINDOW
    lanes = 2 * HEADDIM
    row_blocks = rows // w - 1
    return pl.pallas_call(
        lambda *refs: local_kernel(n_kv, group, *refs),
        name="local_grads",
        in_specs=[HBM] * 8,
        out_specs=[VMEM] * 12,
        out_shape=[
            shape(w, kv_width, kind=F32),
            shape(2 * (row_blocks + 1), w, lanes, kind=F32),
            shape(row_blocks * n_kv, 2, 2 * w, group // 2 * w),
            shape(n_kv, HEADDIM, rows),
            shape(1, w, kind=F32),
            shape(w, width),
            shape(w, width),
            shape(n_kv, 2, rows, lanes),
            shape(n_kv, 2, rows, lanes),
            shape(features, rows),
            shape(features, kv_width, kind=F32),
            shape(n_kv * group, w, kind=F32),
        ],
        scratch_shapes=[
            pltpu.VMEM((row_blocks * w, width), BF16),
            pltpu.VMEM((row_blocks * w, width), BF16),
            pltpu.VMEM((rows, kv_width), BF16),
            pltpu.VMEM((rows, kv_width), BF16),
            pltpu.VMEM(layer_input.shape, BF16),
            pltpu.VMEM((rows - w, kv_width), BF16),
            pltpu.SMEM(sinks.shape, F32),
            pltpu.VMEM(segments.shape, jnp.int32),
            pltpu.VMEM(segments.shape, jnp.int32),
            pltpu.VMEM((row_blocks, w, w), F32),
            pltpu.VMEM((2, w, w), BF16),
            pltpu.VMEM((row_blocks, 2 * w, lanes), F32),
            pltpu.VMEM((rows, kv_width), F32),
            pltpu.SemaphoreType.DMA((5,)),
            pltpu.SemaphoreType.DMA((2, n_kv)),
            pltpu.SemaphoreType.DMA((3,)),
        ]
        + attend_scratch(),
        compiler_params=pltpu.CompilerParams(vmem_limit_bytes=LIMIT),
        cost_estimate=estimate(row_blocks, width, 0, 0),
    )(sinks, segments, positions, query, grad_out, keys, values, layer_input)


def rim_grads(local, rim, kv_width, n_dp):
    own, table, _, _, segs0, query0, grad0, keys2, values2, inputs_t, later, sink_rows = local
    features, rows = inputs_t.shape
    width = query0.shape[1]
    n_kv = kv_width // HEADDIM
    group = width // kv_width
    w = WINDOW
    lanes = 2 * HEADDIM
    return pl.pallas_call(
        lambda *refs: rim_kernel(n_kv, group, n_dp, *refs),
        name="rim_grads",
        in_specs=[VMEM] * 11,
        out_specs=[VMEM] * 4,
        out_shape=[
            shape(features // 2, kv_width),
            shape(features // 2, kv_width),
            shape(n_kv, 2, 2 * w, group // 2 * w),
            shape(n_kv, HEADDIM, w),
        ],
        scratch_shapes=[
            pltpu.VMEM((n_kv, 2, w, lanes), BF16),
            pltpu.VMEM((n_kv, 2, w, lanes), BF16),
            pltpu.VMEM((1, w, w), F32),
            pltpu.VMEM((2, w, w), BF16),
            pltpu.VMEM((1, 2 * w, lanes), F32),
            pltpu.VMEM((2 * w, kv_width), F32),
            pltpu.VMEM((2 * w, kv_width), BF16),
            pltpu.VMEM((features, 2 * w), BF16),
            pltpu.VMEM((features, kv_width), F32),
        ]
        + attend_scratch(),
        compiler_params=pltpu.CompilerParams(vmem_limit_bytes=LIMIT),
        cost_estimate=estimate(1, width, 2 * features * kv_width * 2 * w, 8 * features * kv_width),
    )(own, table, segs0, query0, grad0, keys2, values2, inputs_t, later, sink_rows, rim)


def query_grads(local_ds, local_keys, rim_ds, rim_keys, group):
    n_kv, _, rows = local_keys.shape
    width = n_kv * group * HEADDIM
    w = WINDOW
    return pl.pallas_call(
        lambda *refs: query_kernel(n_kv, group, *refs),
        name="query_grads",
        in_specs=[VMEM] * 4,
        out_specs=HBM,
        out_shape=shape(rows, width),
        scratch_shapes=[pltpu.VMEM((rows, width), BF16), pltpu.SemaphoreType.DMA((rows // w, n_kv))],
        compiler_params=pltpu.CompilerParams(vmem_limit_bytes=LIMIT),
        cost_estimate=pl.CostEstimate(
            flops=4 * rows * w * width, bytes_accessed=2 * rows * width + 4 * rows * w * width // HEADDIM, transcendentals=0
        ),
    )(local_ds, local_keys, rim_ds, rim_keys)


def tail_kernel(segs_hbm, pos_hbm, inputs_hbm, keys_hbm, values_hbm, out_ref, segs_ref, pos_ref, sem):
    w = WINDOW
    rows = inputs_hbm.shape[0]
    ids = load(
        [
            pltpu.make_async_copy(segs_hbm, segs_ref, sem.at[0]),
            pltpu.make_async_copy(pos_hbm, pos_ref, sem.at[1]),
        ]
    )
    copies = []
    for hbm in (inputs_hbm, keys_hbm, values_hbm):
        for start in range(0, hbm.shape[1], w):
            n = len(copies)
            source = hbm.at[rows - w :, start : start + w]
            copies += load([pltpu.make_async_copy(source, out_ref.at[n * w : (n + 1) * w], sem.at[n + 2])])
    for copy in ids:
        copy.wait()
    line = iota((16, w), 0)
    segs = segs_ref[0:1, rows - w :]
    pos = pos_ref[0:1, rows - w :]
    aux = jnp.where(line == 0, segs, jnp.where(line == 1, pos >> 8, pos & 255))
    out_ref[len(copies) * w :, :] = aux.astype(F32).astype(BF16)
    for copy in copies:
        copy.wait()


def last_tokens(layer_input, keys, values, segments, positions):
    tiles = (layer_input.shape[1] + 2 * keys.shape[1]) // WINDOW
    return pl.pallas_call(
        tail_kernel,
        name="last_tokens",
        in_specs=[HBM] * 5,
        out_specs=VMEM,
        out_shape=shape(tiles * WINDOW + 16, WINDOW),
        scratch_shapes=[
            pltpu.VMEM(segments.shape, jnp.int32),
            pltpu.VMEM(segments.shape, jnp.int32),
            pltpu.SemaphoreType.DMA((tiles + 2,)),
        ],
        compiler_params=pltpu.CompilerParams(vmem_limit_bytes=LIMIT),
    )(segments, positions, layer_input, keys, values)


def swapped(relative, n):
    return relative if n < 4 else (relative & ~3) | (relative & 1) << 1 | (relative & 2) >> 1


def bit_reversed(n):
    bits = n.bit_length() - 1
    return [int(format(i, "b").zfill(bits)[::-1], 2) if bits else 0 for i in range(n)]


def exchange(part, axis, by):
    count = lax.axis_size(axis)
    return lax.ppermute(part, axis, [(i, i ^ by) for i in range(count)])


def bits(n):
    return n.bit_length() - 1


def share_and_sum(total, by):
    n_dp, n_seq = lax.axis_size("dp"), lax.axis_size("seq")
    half = total.shape[0] // 2
    mine, theirs = total[:half].astype(BF16), total[half:].astype(BF16)

    def swap(part, dp_bits, seq_bits):
        pairs = [
            (d * n_seq + q, (d ^ dp_bits) * n_seq + (q ^ seq_bits)) for d in range(n_dp) for q in range(n_seq)
        ]
        return lax.ppermute(part, ("dp", "seq"), pairs).astype(F32)

    far = swap(theirs, by, 2)
    near = swap(theirs, by, 0)
    beside = swap(mine, 0, 2)
    return (far + near) + (beside + mine.astype(F32))


def exchange_by_core(part, relative):
    n_dp, n_seq = lax.axis_size("dp"), lax.axis_size("seq")
    pairs = []
    for d in range(n_dp):
        for q in range(n_seq):
            other = d ^ (swapped(relative, n_dp) if q % 2 else relative)
            pairs.append((d * n_seq + q, other * n_seq + q))
    return lax.ppermute(part, ("dp", "seq"), pairs)


def share(total, by, ways, beside=None, held=None):
    rows = total.shape[0] // ways
    parts = [total[k * rows : (k + 1) * rows] for k in range(ways)]
    sends = [part.astype(BF16) for part in parts[1:]]
    if beside is not None:
        sends, held = lax.optimization_barrier((sends, held))
        extra = beside(held)
    got = []
    for k in reversed(range(1, ways)):
        relative = bit_reversed(ways)[k] * by
        got.append(exchange_by_core(sends[k - 1], relative))
    if beside is not None:
        got, extra = lax.optimization_barrier((got, extra))
    total = parts[0]
    for part in got:
        total = total + part.astype(F32)
    return total if beside is None else (total, extra)


def forward_one(part, axis):
    count = lax.axis_size(axis)
    return lax.ppermute(part, axis, [(i, i + 1) for i in range(count - 1)])


def body(query, keys, values, grad_out, layer_input, sinks, segments, positions):
    n_dp = lax.axis_size("dp")
    n_seq = lax.axis_size("seq")
    dp_index = lax.axis_index("dp")
    seq_index = lax.axis_index("seq")
    core = seq_index & 1
    kv_width = keys.shape[2]
    features = layer_input.shape[2]
    piece = features // (2 * n_dp)
    query, grad_out, layer_input, keys, values = [
        pltpu.with_memory_space_constraint(x[0], pltpu.HBM) for x in (query, grad_out, layer_input, keys, values)
    ]
    sinks, segments, positions = [
        pltpu.with_memory_space_constraint(x, pltpu.HBM) for x in (sinks, segments, positions)
    ]
    tail = last_tokens(layer_input, keys, values, segments, positions)
    rim = forward_one(tail, "seq")
    local = local_grads(query, grad_out, keys, values, layer_input, segments, positions, sinks)
    send, keep, rim_ds, rim_keys = rim_grads(local, rim, kv_width, n_dp)
    if piece % 16:
        plain = jnp.concatenate([keep, send], axis=0).reshape(n_dp, 2, piece, kv_width)
        order = bit_reversed(n_dp)
        orders = jnp.asarray([order, [swapped(relative, n_dp) for relative in order]], jnp.int32) ^ dp_index
        keep, send = [
            jnp.take(plain[:, side], orders[side], axis=0).reshape(-1, kv_width) for side in (core, core ^ 1)
        ]
    total = keep.astype(F32) + exchange(send, "seq", 1).astype(F32)
    group = query.shape[1] // kv_width

    def beside(held):
        return query_grads(*held, group)

    held = (local[2], local[3], rim_ds, rim_keys)
    dq = None
    by = 1
    last = n_dp // 2 if n_seq == 4 and bits(n_dp) % 2 else n_dp
    while by < last:
        ways = 4 if 4 * by <= last else 2
        if dq is None:
            total, dq = share(total, by, ways, beside, held)
        else:
            total = share(total, by, ways)
        by *= ways
    if dq is None:
        dq = beside(held)
    if last < n_dp:
        total = share_and_sum(total, last)
    else:
        by = 2
        while by < n_seq:
            mine = total.astype(BF16)
            total = mine.astype(F32) + exchange(mine, "seq", by).astype(F32)
            by *= 2
    other = exchange(total, "seq", 1)
    pair = jnp.where(core == 0, jnp.stack([total, other]), jnp.stack([other, total]))
    return (dq[None], pair.reshape(-1, kv_width))


def solution(mesh):
    return jax.shard_map(
        body,
        mesh=mesh,
        in_specs=(
            P("dp", "seq", None),
            P("dp", "seq", None),
            P("dp", "seq", None),
            P("dp", "seq", None),
            P("dp", "seq", None),
            P(),
            P("dp", "seq"),
            P("dp", "seq"),
        ),
        out_specs=(P("dp", "seq", None), P("dp", None)),
        check_vma=False,
    )
```

```python
import jax
import jax.numpy as jnp
import numpy as np
from jax import lax
from jax.experimental import pallas as pl
from jax.experimental.pallas import tpu as pltpu
from jax.sharding import PartitionSpec as P

HEADDIM = 64
WINDOW = 128
THETA = 150000.0
LOW = -1e30

F32 = jnp.float32
BF16 = jnp.bfloat16


def dot(a, b, ca, cb):
    return lax.dot_general(a, b, (((ca,), (cb,)), ((), ())), preferred_element_type=F32)


def iota(shape, dim):
    return lax.broadcasted_iota(jnp.int32, shape, dim)


def sin_cos(angle):
    turns = jnp.floor(angle * np.float32(2.0 / np.pi) + np.float32(0.5))
    rest = angle - turns * np.float32(1.5703125)
    rest = rest - turns * np.float32(4.837512969970703125e-4)
    rest = rest - turns * np.float32(7.54978995489188216e-8)
    sq = rest * rest
    sin_part = np.float32(-1.9515295891e-4) * sq + np.float32(8.3321608736e-3)
    sin_part = (sin_part * sq + np.float32(-1.6666654611e-1)) * sq * rest + rest
    cos_part = np.float32(2.443315711809948e-5) * sq + np.float32(-1.388731625493765e-3)
    cos_part = (cos_part * sq + np.float32(4.166664568298827e-2)) * sq * sq
    cos_part = cos_part - np.float32(0.5) * sq + np.float32(1.0)
    quadrant = turns.astype(jnp.int32)
    odd = (quadrant & 1) == 1
    sine = jnp.where(odd, cos_part, sin_part)
    cosine = jnp.where(odd, sin_part, cos_part)
    sine = jnp.where((quadrant & 2) == 2, -sine, sine)
    cosine = jnp.where(((quadrant + 1) & 2) == 2, -cosine, cosine)
    return sine, cosine


def as_column(row):
    return jnp.broadcast_to(row, (row.shape[1], row.shape[1])).T


def load(copies):
    for copy in copies:
        copy.start()
    return copies


def prepare_keys(kv, blocks, keys2, values2, keys_t):
    w = WINDOW
    lanes = 2 * HEADDIM
    own_half = (iota((w, lanes), 1) < HEADDIM) == (kv % 2 == 0)
    for b, (k_ref, v_ref, first_row) in enumerate(blocks):
        rows = slice(b * w, (b + 1) * w)
        if first_row is None:
            at = (slice(kv // 2 * w, (kv // 2 + 1) * w), slice(None))
        else:
            at = (slice(first_row, first_row + w), slice(kv // 2 * lanes, (kv // 2 + 1) * lanes))
        k_tile = k_ref[at].astype(F32) * np.float32(HEADDIM**-0.5)
        v_tile = v_ref[at].astype(F32)
        k_tile = jnp.where(own_half, k_tile, np.float32(0.0))
        v_tile = jnp.where(own_half, v_tile, np.float32(0.0))
        keys2[kv, kv % 2, rows, :] = k_tile.astype(BF16)
        values2[kv, kv % 2, rows, :] = v_tile.astype(BF16)
        keys2[kv, 1 - kv % 2, rows, :] = pltpu.roll(k_tile, HEADDIM, 1).astype(BF16)
        values2[kv, 1 - kv % 2, rows, :] = pltpu.roll(v_tile, HEADDIM, 1).astype(BF16)
        half = slice(kv % 2 * HEADDIM, (kv % 2 + 1) * HEADDIM)
        keys_t[kv, :, rows] = k_tile.T[half].astype(BF16)


def attend(
    n_kv, group, row_blocks, window_of, beside, sink_rows, query, grad, ds_s, bias, halves, scratch, add_dk
):
    scores_s, grads_s = scratch
    w = WINDOW
    lanes = 2 * HEADDIM
    quads = group // 4
    tri = iota((w, w), 0) <= iota((w, w), 1)
    tri2 = jnp.concatenate([tri, tri], axis=1)
    items = [(b, kv, quad) for kv in range(n_kv) for b in range(row_blocks) for quad in range(quads)]

    def tiles(ref, b, kv, first, count):
        rows = slice(b * w, (b + 1) * w)
        start = kv * group // 2 + first
        return jnp.concatenate(
            [ref[rows, (start + t) * lanes : (start + t + 1) * lanes] for t in range(count)], axis=0
        )

    def to_scores(n):
        b, kv, quad = items[n]
        key_win, value_win = window_of(b, kv, quad == 0)
        q_two = tiles(query, b, kv, 2 * quad, 2)
        g_two = tiles(grad, b, kv, 2 * quad, 2)
        bias2 = jnp.concatenate([bias[b], bias[b]], axis=1)
        for side in range(2):
            scores = dot(key_win[side], q_two, 1, 1)
            scores_s[n % 2, side] = jnp.where(tri2, scores[w:], scores[:w]) + bias2
        for side in range(2):
            grads = dot(value_win[side], g_two, 1, 1)
            grads_s[n % 2, side] = jnp.where(tri2, grads[w:], grads[:w])

    def to_ds(n):
        b, kv, quad = items[n]
        unit = n // quads
        for side in range(2):
            for t in range(2):
                cols = slice(t * w, (t + 1) * w)
                head = kv * group + 4 * quad + 2 * t + side
                sink = sink_rows[head : head + 1, :]
                scores = scores_s[n % 2, side, :, cols]
                peak = jnp.maximum(jnp.max(scores, axis=0, keepdims=True), sink)
                expo = jnp.exp(scores - peak)
                total = jnp.sum(expo, axis=0, keepdims=True) + jnp.exp(sink - peak)
                probs = expo * (np.float32(1.0) / total)
                grads = grads_s[n % 2, side, :, cols]
                delta = jnp.sum(probs * grads, axis=0, keepdims=True)
                ds = (probs * (grads - delta)).astype(BF16)
                out_cols = slice((2 * quad + t) * w, (2 * quad + t + 1) * w)
                ds_s[unit, side, 0:w, out_cols] = ds * halves[0]
                ds_s[unit, side, w : 2 * w, out_cols] = ds * halves[1]

    def to_grads(n):
        b, kv, quad = items[n]
        if quad == quads - 1:
            q_all = tiles(query, b, kv, 0, group // 2)
            low = iota((2 * w, lanes), 1) < HEADDIM
            sides = [dot(ds_s[n // quads, side], q_all, 1, 0) for side in range(2)]
            add_dk(b, kv, jnp.where(low, sides[0], sides[1]))

    for n in range(len(items) + 2):
        if n < len(items):
            to_scores(n)
        if 0 <= n - 1 < len(items):
            to_ds(n - 1)
        if n >= 2:
            to_grads(n - 2)
        if n < len(items):
            beside(n, len(items))


def attend_scratch():
    w = WINDOW
    return [
        pltpu.VMEM((2, 2, w, 2 * w), F32),
        pltpu.VMEM((2, 2, w, 2 * w), F32),
    ]


def set_halves(halves):
    tri = iota((WINDOW, WINDOW), 0) <= iota((WINDOW, WINDOW), 1)
    halves[0] = jnp.where(tri, np.float32(0.0), np.float32(1.0)).astype(BF16)
    halves[1] = jnp.where(tri, np.float32(1.0), np.float32(0.0)).astype(BF16)


def tile_ready(tile, count, n_kv):
    n = (2 * tile + 2) * count // n_kv + 2
    return n if n < count else None


def window_bias(bias, b, prev_segs, own_segs):
    tri = iota((WINDOW, WINDOW), 0) <= iota((WINDOW, WINDOW), 1)
    key_segs = jnp.where(tri, as_column(own_segs), as_column(prev_segs))
    bias[b] = jnp.where(key_segs == own_segs, np.float32(0.0), np.float32(LOW))


def store_dk(dk_part, dk_all, first_block, b, kv, part, seen):
    w = WINDOW
    lanes = 2 * HEADDIM
    if kv % 2 == 0:
        dk_part[b] = part
        return
    even = dk_part[b]
    low = iota(part.shape, 1) < HEADDIM
    both = jnp.where(low, even, part) + pltpu.roll(jnp.where(low, part, even), HEADDIM, 1)
    cols = slice(kv // 2 * lanes, (kv // 2 + 1) * lanes)
    for k in range(2):
        rows = slice((first_block + b + k) * w, (first_block + b + k + 1) * w)
        piece = both[k * w : (k + 1) * w]
        if (first_block + b + k, kv) in seen:
            piece = piece + dk_all[rows, cols]
        seen.add((first_block + b + k, kv))
        dk_all[rows, cols] = piece


def rotate(dk, sine, cosine):
    half = HEADDIM // 2
    lanes = dk.shape[1]
    low = (iota(dk.shape, 1) % HEADDIM) < half
    other = jnp.where(low, pltpu.roll(dk, lanes - half, 1), pltpu.roll(dk, half, 1))
    return (dk * cosine + other * sine) * np.float32(HEADDIM**-0.5)


def turn_table(pos):
    half = HEADDIM // 2
    index = iota((1, 2 * HEADDIM), 1) % half
    rates = (THETA ** (-2.0 * np.arange(half) / HEADDIM)).astype(np.float32)
    freq = jnp.zeros((1, 2 * HEADDIM), F32)
    for t in range(half):
        freq = jnp.where(index == t, rates[t], freq)
    sine, cosine = sin_cos(as_column(pos.astype(F32)) * freq)
    low = (iota(sine.shape, 1) % HEADDIM) < HEADDIM // 2
    return jnp.where(low, sine, -sine), cosine


def local_kernel(
    n_kv, group, sinks_hbm, segs_hbm, pos_hbm, query_hbm, grad_hbm, keys_hbm, values_hbm, inputs_hbm,
    own_ref, table_ref, ds_ref, keys_t, segs0_ref, query0, grad0, keys2, values2, inputs_t, later_ref, sink_rows,
    query, grad, keys, values, inputs, dk_ref, sinks_ref, segs_ref, pos_ref, bias, halves, dk_part, dk_all, id_sem, in_sem, next_sem,
    *scratch,
):
    w = WINDOW
    lanes = 2 * HEADDIM
    rows = keys.shape[0]
    row_blocks = rows // w - 1
    step = group * HEADDIM
    ids = load(
        [
            pltpu.make_async_copy(pos_hbm, pos_ref, id_sem.at[3]),
            pltpu.make_async_copy(segs_hbm, segs_ref, id_sem.at[2]),
            pltpu.make_async_copy(sinks_hbm, sinks_ref, id_sem.at[4]),
        ]
    )
    key_copies = load(
        [
            pltpu.make_async_copy(keys_hbm, keys, id_sem.at[0]),
            pltpu.make_async_copy(values_hbm, values, id_sem.at[1]),
        ]
    )

    def ins(kv):
        cols = slice(kv * step, (kv + 1) * step)
        return [
            pltpu.make_async_copy(query_hbm.at[w:, cols], query.at[:, cols], in_sem.at[0, kv]),
            pltpu.make_async_copy(grad_hbm.at[w:, cols], grad.at[:, cols], in_sem.at[1, kv]),
        ]

    in_copies = [load(ins(kv)) for kv in range(n_kv)]
    next_copies = load(
        [
            pltpu.make_async_copy(query_hbm.at[0:w], query0, next_sem.at[0]),
            pltpu.make_async_copy(grad_hbm.at[0:w], grad0, next_sem.at[1]),
            pltpu.make_async_copy(inputs_hbm, inputs, next_sem.at[2]),
        ]
    )
    set_halves(halves)
    for copy in ids:
        copy.wait()
    for head in range(n_kv * group):
        sink_rows[head : head + 1, :] = jnp.full((1, w), sinks_ref[head], F32)
    segs = [segs_ref[0:1, b * w : (b + 1) * w].astype(F32) for b in range(row_blocks + 1)]
    segs0_ref[...] = segs[0]
    for b in range(row_blocks):
        window_bias(bias, b, segs[b], segs[b + 1])
    for b in range(row_blocks + 1):
        sine, cosine = turn_table(pos_ref[0:1, b * w : (b + 1) * w])
        table_ref[2 * b] = sine
        table_ref[2 * b + 1] = cosine
    for copy in key_copies:
        copy.wait()
    seen = set()

    def window_of(b, kv, first):
        if b == 0 and first:
            prepare_keys(kv, [(keys, values, b * w) for b in range(row_blocks + 1)], keys2, values2, keys_t)
            waits = [in_copies[0], sum(in_copies[1:], []) + next_copies[2:]] + [[]] * n_kv
            for copy in waits[kv]:
                copy.wait()
        window = slice(b * w, (b + 2) * w)
        return [keys2[kv, side, window, :] for side in range(2)], [values2[kv, side, window, :] for side in range(2)]

    features = inputs.shape[1]
    pieces = [(f, t) for f in range(features // w) for t in range(row_blocks + 1)]

    def turn_inputs(n, count):
        begin, end = count // n_kv, 2 * count // n_kv + 2
        if n == tile_ready(0, count, n_kv):
            finish(0)
        if begin <= n < end:
            for f, t in pieces[(n - begin) * len(pieces) // (end - begin) : (n + 1 - begin) * len(pieces) // (end - begin)]:
                cols = slice(f * w, (f + 1) * w)
                inputs_t[cols, t * w : (t + 1) * w] = inputs[t * w : (t + 1) * w, cols].T

    def finish(tile):
        cols = slice(tile * lanes, (tile + 1) * lanes)
        for b in range(row_blocks + 1):
            turned = rotate(dk_all[b * w : (b + 1) * w, cols], table_ref[2 * b], table_ref[2 * b + 1])
            if b == 0:
                own_ref[:, cols] = turned
            else:
                dk_ref[(b - 1) * w : b * w, cols] = turned.astype(BF16)
        later_ref[:, cols] = dot(inputs_t[:, w:], dk_ref[:, cols], 1, 0)

    attend(
        n_kv, group, row_blocks, window_of, turn_inputs,
        sink_rows, query, grad, ds_ref, bias, halves, scratch,
        lambda b, kv, part: store_dk(dk_part, dk_all, 0, b, kv, part, seen),
    )
    for tile in range(1 if tile_ready(0, n_kv * row_blocks * group // 4, n_kv) else 0, n_kv // 2):
        finish(tile)
    for copy in next_copies[:2]:
        copy.wait()


def rim_kernel(
    n_kv, group, n_dp, own_ref, table_ref, segs0_ref, query, grad, own_keys2, own_values2, own_inputs_t, later_ref,
    sink_rows, rim,
    send_ref, keep_ref, ds_ref, keys_t,
    keys2, values2, bias, halves, dk_part, dk_all, dk16, inputs_t, sums, *scratch,
):
    w = WINDOW
    lanes = 2 * HEADDIM
    features = own_inputs_t.shape[0]
    kv_width = n_kv * HEADDIM
    set_halves(halves)
    rim_keys = rim.at[features : features + kv_width]
    rim_values = rim.at[features + kv_width : features + 2 * kv_width]
    aux = rim[features + 2 * kv_width :, :].astype(F32)
    rim_segs = jnp.where(lax.axis_index("seq") == 0, np.float32(-1.0), aux[0:1])
    window_bias(bias, 0, rim_segs, segs0_ref[...])
    rim_sine, rim_cosine = turn_table(aux[1:2] * np.float32(256.0) + aux[2:3])
    seen = set()

    def window_of(b, kv, first):
        if first:
            prepare_keys(kv, [(rim_keys, rim_values, None)], keys2, values2, keys_t)
        both = [(keys2, own_keys2), (values2, own_values2)]
        return [
            [jnp.concatenate([rim2[kv, side], own2[kv, side, 0:w]], axis=0) for side in range(2)]
            for rim2, own2 in both
        ]

    tiles = features // w

    def turn_inputs(n, count):
        for f in range(n * tiles // count, (n + 1) * tiles // count):
            cols = slice(f * w, (f + 1) * w)
            inputs_t[cols, 0:w] = rim[cols, :].T
            inputs_t[cols, w : 2 * w] = own_inputs_t[cols, 0:w]

    attend(
        n_kv, group, 1, window_of, turn_inputs,
        sink_rows, query, grad, ds_ref, bias, halves, scratch,
        lambda b, kv, part: store_dk(dk_part, dk_all, 0, b, kv, part, seen),
    )
    for tile in range(n_kv // 2):
        cols = slice(tile * lanes, (tile + 1) * lanes)
        dk16[0:w, cols] = rotate(dk_all[0:w, cols], rim_sine, rim_cosine).astype(BF16)
        own = rotate(dk_all[w : 2 * w, cols], table_ref[0], table_ref[1]) + own_ref[:, cols]
        dk16[w : 2 * w, cols] = own.astype(BF16)
    sums[...] = dot(inputs_t[...], dk16[...], 1, 0) + later_ref[...]
    piece = features // (2 * n_dp)
    dp_index = lax.axis_index("dp")
    core = lax.axis_index("seq") & 1
    for half, ref in enumerate([keep_ref, send_ref]):
        for j, relative in enumerate(bit_reversed(n_dp)):
            if piece % 16 == 0:
                side = core ^ half
                block = (dp_index ^ (relative + side * (swapped(relative, n_dp) - relative))) * 2 + side
                start = pl.multiple_of(block * piece, piece)
                ref[j * piece : (j + 1) * piece, :] = sums[pl.ds(start, piece), :].astype(BF16)
    if piece % 16:
        keep_ref[...] = sums[0 : features // 2, :].astype(BF16)
        send_ref[...] = sums[features // 2 :, :].astype(BF16)


def query_kernel(n_kv, group, local_ds, local_keys, rim_ds, rim_keys, dq_hbm, dq, out_sem):
    w = WINDOW
    lanes = 2 * HEADDIM
    step = group * HEADDIM
    row_blocks = local_ds.shape[0] // n_kv
    outs = []
    for block in range(row_blocks + 1):
        rows = slice(block * w, (block + 1) * w)
        for kv in range(n_kv):
            for tile in range(group // 2):
                cols = slice(tile * w, (tile + 1) * w)
                if block == 0:
                    keyt_win = jnp.concatenate([rim_keys[kv], local_keys[kv, :, 0:w]], axis=1)
                    ds_ref, unit = rim_ds, kv
                else:
                    keyt_win = local_keys[kv, :, (block - 1) * w : (block + 1) * w]
                    ds_ref, unit = local_ds, kv * row_blocks + block - 1
                dq_t = [dot(keyt_win, ds_ref[unit, side, :, cols], 1, 0) for side in range(2)]
                start = kv * group // 2 + tile
                dq[rows, start * lanes : (start + 1) * lanes] = jnp.concatenate(dq_t, axis=0).T.astype(BF16)
            cols = slice(kv * step, (kv + 1) * step)
            outs += load([pltpu.make_async_copy(dq.at[rows, cols], dq_hbm.at[rows, cols], out_sem.at[block, kv])])
    for copy in outs:
        copy.wait()


ANY = pl.BlockSpec(memory_space=pl.ANY)
HBM = pl.BlockSpec(memory_space=pltpu.HBM)
VMEM = pl.BlockSpec(memory_space=pltpu.VMEM)
SMEM = pl.BlockSpec(memory_space=pltpu.SMEM)
LIMIT = 24 * 2**20


def estimate(row_blocks, width, extra_flops, extra_bytes):
    w = WINDOW
    return pl.CostEstimate(
        flops=10 * row_blocks * w * 2 * w * width + extra_flops,
        bytes_accessed=6 * row_blocks * w * width + extra_bytes,
        transcendentals=row_blocks * w * w * width // HEADDIM,
    )


def sizes(query, keys):
    width, kv_width = query.shape[-1], keys.shape[-1]
    return width, kv_width, kv_width // HEADDIM, width // kv_width


def shape(*dims, kind=BF16):
    return jax.ShapeDtypeStruct(dims, kind)


def local_grads(query, grad_out, keys, values, layer_input, segments, positions, sinks):
    rows, features = layer_input.shape
    width, kv_width, n_kv, group = sizes(query, keys)
    w = WINDOW
    lanes = 2 * HEADDIM
    row_blocks = rows // w - 1
    return pl.pallas_call(
        lambda *refs: local_kernel(n_kv, group, *refs),
        name="local_grads",
        in_specs=[HBM] * 8,
        out_specs=[VMEM] * 12,
        out_shape=[
            shape(w, kv_width, kind=F32),
            shape(2 * (row_blocks + 1), w, lanes, kind=F32),
            shape(row_blocks * n_kv, 2, 2 * w, group // 2 * w),
            shape(n_kv, HEADDIM, rows),
            shape(1, w, kind=F32),
            shape(w, width),
            shape(w, width),
            shape(n_kv, 2, rows, lanes),
            shape(n_kv, 2, rows, lanes),
            shape(features, rows),
            shape(features, kv_width, kind=F32),
            shape(n_kv * group, w, kind=F32),
        ],
        scratch_shapes=[
            pltpu.VMEM((row_blocks * w, width), BF16),
            pltpu.VMEM((row_blocks * w, width), BF16),
            pltpu.VMEM((rows, kv_width), BF16),
            pltpu.VMEM((rows, kv_width), BF16),
            pltpu.VMEM(layer_input.shape, BF16),
            pltpu.VMEM((rows - w, kv_width), BF16),
            pltpu.SMEM(sinks.shape, F32),
            pltpu.VMEM(segments.shape, jnp.int32),
            pltpu.VMEM(segments.shape, jnp.int32),
            pltpu.VMEM((row_blocks, w, w), F32),
            pltpu.VMEM((2, w, w), BF16),
            pltpu.VMEM((row_blocks, 2 * w, lanes), F32),
            pltpu.VMEM((rows, kv_width), F32),
            pltpu.SemaphoreType.DMA((5,)),
            pltpu.SemaphoreType.DMA((2, n_kv)),
            pltpu.SemaphoreType.DMA((3,)),
        ]
        + attend_scratch(),
        compiler_params=pltpu.CompilerParams(vmem_limit_bytes=LIMIT),
        cost_estimate=estimate(row_blocks, width, 0, 0),
    )(sinks, segments, positions, query, grad_out, keys, values, layer_input)


def rim_grads(local, rim, kv_width, n_dp):
    own, table, _, _, segs0, query0, grad0, keys2, values2, inputs_t, later, sink_rows = local
    features, rows = inputs_t.shape
    width = query0.shape[1]
    n_kv = kv_width // HEADDIM
    group = width // kv_width
    w = WINDOW
    lanes = 2 * HEADDIM
    return pl.pallas_call(
        lambda *refs: rim_kernel(n_kv, group, n_dp, *refs),
        name="rim_grads",
        in_specs=[VMEM] * 11,
        out_specs=[VMEM] * 4,
        out_shape=[
            shape(features // 2, kv_width),
            shape(features // 2, kv_width),
            shape(n_kv, 2, 2 * w, group // 2 * w),
            shape(n_kv, HEADDIM, w),
        ],
        scratch_shapes=[
            pltpu.VMEM((n_kv, 2, w, lanes), BF16),
            pltpu.VMEM((n_kv, 2, w, lanes), BF16),
            pltpu.VMEM((1, w, w), F32),
            pltpu.VMEM((2, w, w), BF16),
            pltpu.VMEM((1, 2 * w, lanes), F32),
            pltpu.VMEM((2 * w, kv_width), F32),
            pltpu.VMEM((2 * w, kv_width), BF16),
            pltpu.VMEM((features, 2 * w), BF16),
            pltpu.VMEM((features, kv_width), F32),
        ]
        + attend_scratch(),
        compiler_params=pltpu.CompilerParams(vmem_limit_bytes=LIMIT),
        cost_estimate=estimate(1, width, 2 * features * kv_width * 2 * w, 8 * features * kv_width),
    )(own, table, segs0, query0, grad0, keys2, values2, inputs_t, later, sink_rows, rim)


def query_grads(local_ds, local_keys, rim_ds, rim_keys, group):
    n_kv, _, rows = local_keys.shape
    width = n_kv * group * HEADDIM
    w = WINDOW
    return pl.pallas_call(
        lambda *refs: query_kernel(n_kv, group, *refs),
        name="query_grads",
        in_specs=[VMEM] * 4,
        out_specs=HBM,
        out_shape=shape(rows, width),
        scratch_shapes=[pltpu.VMEM((rows, width), BF16), pltpu.SemaphoreType.DMA((rows // w, n_kv))],
        compiler_params=pltpu.CompilerParams(vmem_limit_bytes=LIMIT),
        cost_estimate=pl.CostEstimate(
            flops=4 * rows * w * width, bytes_accessed=2 * rows * width + 4 * rows * w * width // HEADDIM, transcendentals=0
        ),
    )(local_ds, local_keys, rim_ds, rim_keys)


def tail_kernel(segs_hbm, pos_hbm, inputs_hbm, keys_hbm, values_hbm, out_ref, segs_ref, pos_ref, sem):
    w = WINDOW
    rows = inputs_hbm.shape[0]
    ids = load(
        [
            pltpu.make_async_copy(segs_hbm, segs_ref, sem.at[0]),
            pltpu.make_async_copy(pos_hbm, pos_ref, sem.at[1]),
        ]
    )
    copies = []
    for hbm in (inputs_hbm, keys_hbm, values_hbm):
        for start in range(0, hbm.shape[1], w):
            n = len(copies)
            source = hbm.at[rows - w :, start : start + w]
            copies += load([pltpu.make_async_copy(source, out_ref.at[n * w : (n + 1) * w], sem.at[n + 2])])
    for copy in ids:
        copy.wait()
    line = iota((16, w), 0)
    segs = segs_ref[0:1, rows - w :]
    pos = pos_ref[0:1, rows - w :]
    aux = jnp.where(line == 0, segs, jnp.where(line == 1, pos >> 8, pos & 255))
    out_ref[len(copies) * w :, :] = aux.astype(F32).astype(BF16)
    for copy in copies:
        copy.wait()


def last_tokens(layer_input, keys, values, segments, positions):
    tiles = (layer_input.shape[1] + 2 * keys.shape[1]) // WINDOW
    return pl.pallas_call(
        tail_kernel,
        name="last_tokens",
        in_specs=[HBM] * 5,
        out_specs=VMEM,
        out_shape=shape(tiles * WINDOW + 16, WINDOW),
        scratch_shapes=[
            pltpu.VMEM(segments.shape, jnp.int32),
            pltpu.VMEM(segments.shape, jnp.int32),
            pltpu.SemaphoreType.DMA((tiles + 2,)),
        ],
        compiler_params=pltpu.CompilerParams(vmem_limit_bytes=LIMIT),
    )(segments, positions, layer_input, keys, values)


def swapped(relative, n):
    return relative if n < 4 else (relative & ~3) | (relative & 1) << 1 | (relative & 2) >> 1


def bit_reversed(n):
    bits = n.bit_length() - 1
    return [int(format(i, "b").zfill(bits)[::-1], 2) if bits else 0 for i in range(n)]


def exchange(part, axis, by):
    count = lax.axis_size(axis)
    return lax.ppermute(part, axis, [(i, i ^ by) for i in range(count)])


def bits(n):
    return n.bit_length() - 1


def share_and_sum(total, by):
    n_dp, n_seq = lax.axis_size("dp"), lax.axis_size("seq")
    half = total.shape[0] // 2
    mine, theirs = total[:half].astype(BF16), total[half:].astype(BF16)

    def swap(part, dp_bits, seq_bits):
        pairs = [
            (d * n_seq + q, (d ^ dp_bits) * n_seq + (q ^ seq_bits)) for d in range(n_dp) for q in range(n_seq)
        ]
        return lax.ppermute(part, ("dp", "seq"), pairs).astype(F32)

    far = swap(theirs, by, 2)
    near = swap(theirs, by, 0)
    beside = swap(mine, 0, 2)
    return (far + near) + (beside + mine.astype(F32))


def exchange_by_core(part, relative):
    n_dp, n_seq = lax.axis_size("dp"), lax.axis_size("seq")
    pairs = []
    for d in range(n_dp):
        for q in range(n_seq):
            other = d ^ (swapped(relative, n_dp) if q % 2 else relative)
            pairs.append((d * n_seq + q, other * n_seq + q))
    return lax.ppermute(part, ("dp", "seq"), pairs)


def share(total, by, ways, beside=None, held=None):
    rows = total.shape[0] // ways
    parts = [total[k * rows : (k + 1) * rows] for k in range(ways)]
    sends = [part.astype(BF16) for part in parts[1:]]
    if beside is not None:
        sends, held = lax.optimization_barrier((sends, held))
        extra = beside(held)
    got = []
    for k in reversed(range(1, ways)):
        relative = bit_reversed(ways)[k] * by
        got.append(exchange_by_core(sends[k - 1], relative))
    if beside is not None:
        got, extra = lax.optimization_barrier((got, extra))
    total = parts[0]
    for part in got:
        total = total + part.astype(F32)
    return total if beside is None else (total, extra)


def forward_one(part, axis):
    count = lax.axis_size(axis)
    return lax.ppermute(part, axis, [(i, i + 1) for i in range(count - 1)])


def body(query, keys, values, grad_out, layer_input, sinks, segments, positions):
    n_dp = lax.axis_size("dp")
    n_seq = lax.axis_size("seq")
    dp_index = lax.axis_index("dp")
    seq_index = lax.axis_index("seq")
    core = seq_index & 1
    kv_width = keys.shape[2]
    features = layer_input.shape[2]
    piece = features // (2 * n_dp)
    query, grad_out, layer_input, keys, values = [
        pltpu.with_memory_space_constraint(x[0], pltpu.HBM) for x in (query, grad_out, layer_input, keys, values)
    ]
    sinks, segments, positions = [
        pltpu.with_memory_space_constraint(x, pltpu.HBM) for x in (sinks, segments, positions)
    ]
    tail = last_tokens(layer_input, keys, values, segments, positions)
    rim = forward_one(tail, "seq")
    local = local_grads(query, grad_out, keys, values, layer_input, segments, positions, sinks)
    send, keep, rim_ds, rim_keys = rim_grads(local, rim, kv_width, n_dp)
    if piece % 16:
        plain = jnp.concatenate([keep, send], axis=0).reshape(n_dp, 2, piece, kv_width)
        order = bit_reversed(n_dp)
        orders = jnp.asarray([order, [swapped(relative, n_dp) for relative in order]], jnp.int32) ^ dp_index
        keep, send = [
            jnp.take(plain[:, side], orders[side], axis=0).reshape(-1, kv_width) for side in (core, core ^ 1)
        ]
    total = keep.astype(F32) + exchange(send, "seq", 1).astype(F32)
    group = query.shape[1] // kv_width

    def beside(held):
        return query_grads(*held, group)

    held = (local[2], local[3], rim_ds, rim_keys)
    dq = None
    by = 1
    last = n_dp // 2 if n_seq == 4 and bits(n_dp) % 2 else n_dp
    while by < last:
        ways = 4 if 4 * by <= last else 2
        if dq is None:
            total, dq = share(total, by, ways, beside, held)
        else:
            total = share(total, by, ways)
        by *= ways
    if dq is None:
        dq = beside(held)
    if last < n_dp:
        total = share_and_sum(total, last)
    else:
        by = 2
        while by < n_seq:
            mine = total.astype(BF16)
            total = mine.astype(F32) + exchange(mine, "seq", by).astype(F32)
            by *= 2
    other = exchange(total, "seq", 1)
    pair = jnp.where(core == 0, jnp.stack([total, other]), jnp.stack([other, total]))
    return (dq[None], pair.reshape(-1, kv_width))


def solution(mesh):
    return jax.shard_map(
        body,
        mesh=mesh,
        in_specs=(
            P("dp", "seq", None),
            P("dp", "seq", None),
            P("dp", "seq", None),
            P("dp", "seq", None),
            P("dp", "seq", None),
            P(),
            P("dp", "seq"),
            P("dp", "seq"),
        ),
        out_specs=(P("dp", "seq", None), P("dp", None)),
        check_vma=False,
    )
```

```python
import jax
import jax.numpy as jnp
import numpy as np
from jax import lax
from jax.experimental import pallas as pl
from jax.experimental.pallas import tpu as pltpu
from jax.sharding import PartitionSpec as P

HEADDIM = 64
WINDOW = 128
THETA = 150000.0
LOW = -1e30

F32 = jnp.float32
BF16 = jnp.bfloat16


def dot(a, b, ca, cb):
    return lax.dot_general(a, b, (((ca,), (cb,)), ((), ())), preferred_element_type=F32)


def iota(shape, dim):
    return lax.broadcasted_iota(jnp.int32, shape, dim)


def sin_cos(angle):
    turns = jnp.floor(angle * np.float32(2.0 / np.pi) + np.float32(0.5))
    rest = angle - turns * np.float32(1.5703125)
    rest = rest - turns * np.float32(4.837512969970703125e-4)
    rest = rest - turns * np.float32(7.54978995489188216e-8)
    sq = rest * rest
    sin_part = np.float32(-1.9515295891e-4) * sq + np.float32(8.3321608736e-3)
    sin_part = (sin_part * sq + np.float32(-1.6666654611e-1)) * sq * rest + rest
    cos_part = np.float32(2.443315711809948e-5) * sq + np.float32(-1.388731625493765e-3)
    cos_part = (cos_part * sq + np.float32(4.166664568298827e-2)) * sq * sq
    cos_part = cos_part - np.float32(0.5) * sq + np.float32(1.0)
    quadrant = turns.astype(jnp.int32)
    odd = (quadrant & 1) == 1
    sine = jnp.where(odd, cos_part, sin_part)
    cosine = jnp.where(odd, sin_part, cos_part)
    sine = jnp.where((quadrant & 2) == 2, -sine, sine)
    cosine = jnp.where(((quadrant + 1) & 2) == 2, -cosine, cosine)
    return sine, cosine


def as_column(row):
    return jnp.broadcast_to(row, (row.shape[1], row.shape[1])).T


def load(copies):
    for copy in copies:
        copy.start()
    return copies


def prepare_keys(kv, blocks, keys2, values2, keys_t):
    w = WINDOW
    lanes = 2 * HEADDIM
    own_half = (iota((w, lanes), 1) < HEADDIM) == (kv % 2 == 0)
    for b, (k_ref, v_ref, first_row) in enumerate(blocks):
        rows = slice(b * w, (b + 1) * w)
        if first_row is None:
            at = (slice(kv // 2 * w, (kv // 2 + 1) * w), slice(None))
        else:
            at = (slice(first_row, first_row + w), slice(kv // 2 * lanes, (kv // 2 + 1) * lanes))
        k_tile = k_ref[at].astype(F32) * np.float32(HEADDIM**-0.5)
        v_tile = v_ref[at].astype(F32)
        k_tile = jnp.where(own_half, k_tile, np.float32(0.0))
        v_tile = jnp.where(own_half, v_tile, np.float32(0.0))
        keys2[kv, kv % 2, rows, :] = k_tile.astype(BF16)
        values2[kv, kv % 2, rows, :] = v_tile.astype(BF16)
        keys2[kv, 1 - kv % 2, rows, :] = pltpu.roll(k_tile, HEADDIM, 1).astype(BF16)
        values2[kv, 1 - kv % 2, rows, :] = pltpu.roll(v_tile, HEADDIM, 1).astype(BF16)
        half = slice(kv % 2 * HEADDIM, (kv % 2 + 1) * HEADDIM)
        keys_t[kv, :, rows] = k_tile.T[half].astype(BF16)


def attend(
    n_kv, group, row_blocks, window_of, beside, sink_rows, query, grad, ds_s, bias, halves, scratch, add_dk,
    own_scores=None, own_grads=None,
):
    scores_s, grads_s = scratch
    w = WINDOW
    lanes = 2 * HEADDIM
    quads = group // 4
    tri = iota((w, w), 0) <= iota((w, w), 1)
    tri2 = jnp.concatenate([tri, tri], axis=1)
    items = [(b, kv, quad) for kv in range(n_kv) for b in range(row_blocks) for quad in range(quads)]

    def tiles(ref, b, kv, first, count):
        rows = slice(b * w, (b + 1) * w)
        start = kv * group // 2 + first
        return jnp.concatenate(
            [ref[rows, (start + t) * lanes : (start + t + 1) * lanes] for t in range(count)], axis=0
        )

    def to_scores(n):
        b, kv, quad = items[n]
        key_win, value_win = window_of(b, kv, quad == 0)
        q_two = tiles(query, b, kv, 2 * quad, 2)
        g_two = tiles(grad, b, kv, 2 * quad, 2)
        bias2 = jnp.concatenate([bias[b], bias[b]], axis=1)
        for side in range(2):
            scores = dot(key_win[side], q_two, 1, 1)
            own = scores[w:] if own_scores is None else own_scores[n, side]
            scores_s[n % 2, side] = jnp.where(tri2, own, scores[:w]) + bias2
        for side in range(2):
            grads = dot(value_win[side], g_two, 1, 1)
            own = grads[w:] if own_grads is None else own_grads[n, side]
            grads_s[n % 2, side] = jnp.where(tri2, own, grads[:w])

    def to_ds(n):
        b, kv, quad = items[n]
        unit = n // quads
        for side in range(2):
            for t in range(2):
                cols = slice(t * w, (t + 1) * w)
                head = kv * group + 4 * quad + 2 * t + side
                sink = sink_rows[head : head + 1, :]
                scores = scores_s[n % 2, side, :, cols]
                peak = jnp.maximum(jnp.max(scores, axis=0, keepdims=True), sink)
                expo = jnp.exp(scores - peak)
                total = jnp.sum(expo, axis=0, keepdims=True) + jnp.exp(sink - peak)
                probs = expo * (np.float32(1.0) / total)
                grads = grads_s[n % 2, side, :, cols]
                delta = jnp.sum(probs * grads, axis=0, keepdims=True)
                ds = (probs * (grads - delta)).astype(BF16)
                out_cols = slice((2 * quad + t) * w, (2 * quad + t + 1) * w)
                ds_s[unit, side, 0:w, out_cols] = ds * halves[0]
                ds_s[unit, side, w : 2 * w, out_cols] = ds * halves[1]

    def to_grads(n):
        b, kv, quad = items[n]
        if quad == quads - 1:
            q_all = tiles(query, b, kv, 0, group // 2)
            low = iota((2 * w, lanes), 1) < HEADDIM
            sides = [dot(ds_s[n // quads, side], q_all, 1, 0) for side in range(2)]
            add_dk(b, kv, jnp.where(low, sides[0], sides[1]))

    for n in range(len(items) + 2):
        if n < len(items):
            to_scores(n)
        if 0 <= n - 1 < len(items):
            to_ds(n - 1)
        if n >= 2:
            to_grads(n - 2)
        if n < len(items):
            beside(n, len(items))


def attend_scratch():
    w = WINDOW
    return [
        pltpu.VMEM((2, 2, w, 2 * w), F32),
        pltpu.VMEM((2, 2, w, 2 * w), F32),
    ]


def set_halves(halves):
    tri = iota((WINDOW, WINDOW), 0) <= iota((WINDOW, WINDOW), 1)
    halves[0] = jnp.where(tri, np.float32(0.0), np.float32(1.0)).astype(BF16)
    halves[1] = jnp.where(tri, np.float32(1.0), np.float32(0.0)).astype(BF16)


def tile_ready(tile, count, n_kv):
    n = (2 * tile + 2) * count // n_kv + 2
    return n if n < count else None


def window_bias(bias, b, prev_segs, own_segs):
    tri = iota((WINDOW, WINDOW), 0) <= iota((WINDOW, WINDOW), 1)
    key_segs = jnp.where(tri, as_column(own_segs), as_column(prev_segs))
    bias[b] = jnp.where(key_segs == own_segs, np.float32(0.0), np.float32(LOW))


def store_dk(dk_part, dk_all, first_block, b, kv, part, seen):
    w = WINDOW
    lanes = 2 * HEADDIM
    if kv % 2 == 0:
        dk_part[b] = part
        return
    even = dk_part[b]
    low = iota(part.shape, 1) < HEADDIM
    both = jnp.where(low, even, part) + pltpu.roll(jnp.where(low, part, even), HEADDIM, 1)
    cols = slice(kv // 2 * lanes, (kv // 2 + 1) * lanes)
    for k in range(2):
        rows = slice((first_block + b + k) * w, (first_block + b + k + 1) * w)
        piece = both[k * w : (k + 1) * w]
        if (first_block + b + k, kv) in seen:
            piece = piece + dk_all[rows, cols]
        seen.add((first_block + b + k, kv))
        dk_all[rows, cols] = piece


def rotate(dk, sine, cosine):
    half = HEADDIM // 2
    lanes = dk.shape[1]
    low = (iota(dk.shape, 1) % HEADDIM) < half
    other = jnp.where(low, pltpu.roll(dk, lanes - half, 1), pltpu.roll(dk, half, 1))
    return (dk * cosine + other * sine) * np.float32(HEADDIM**-0.5)


def turn_table(pos):
    half = HEADDIM // 2
    index = iota((1, 2 * HEADDIM), 1) % half
    rates = (THETA ** (-2.0 * np.arange(half) / HEADDIM)).astype(np.float32)
    freq = jnp.zeros((1, 2 * HEADDIM), F32)
    for t in range(half):
        freq = jnp.where(index == t, rates[t], freq)
    sine, cosine = sin_cos(as_column(pos.astype(F32)) * freq)
    low = (iota(sine.shape, 1) % HEADDIM) < HEADDIM // 2
    return jnp.where(low, sine, -sine), cosine


def local_kernel(
    n_kv, group, sinks_hbm, segs_hbm, pos_hbm, query_hbm, grad_hbm, keys_hbm, values_hbm, inputs_hbm,
    own_ref, table_ref, ds_ref, keys_t, segs0_ref, query0, grad0, keys2, inputs_t, later_ref, sink_rows,
    own_scores, own_grads,
    values2, query, grad, keys, values, inputs, dk_ref, sinks_ref, segs_ref, pos_ref, bias, halves, dk_part, dk_all, id_sem, in_sem, next_sem,
    *scratch,
):
    w = WINDOW
    lanes = 2 * HEADDIM
    rows = keys.shape[0]
    row_blocks = rows // w - 1
    step = group * HEADDIM
    ids = load(
        [
            pltpu.make_async_copy(pos_hbm, pos_ref, id_sem.at[3]),
            pltpu.make_async_copy(segs_hbm, segs_ref, id_sem.at[2]),
            pltpu.make_async_copy(sinks_hbm, sinks_ref, id_sem.at[4]),
        ]
    )
    key_copies = load(
        [
            pltpu.make_async_copy(keys_hbm, keys, id_sem.at[0]),
            pltpu.make_async_copy(values_hbm, values, id_sem.at[1]),
        ]
    )

    def ins(kv):
        cols = slice(kv * step, (kv + 1) * step)
        return [
            pltpu.make_async_copy(query_hbm.at[w:, cols], query.at[:, cols], in_sem.at[0, kv]),
            pltpu.make_async_copy(grad_hbm.at[w:, cols], grad.at[:, cols], in_sem.at[1, kv]),
        ]

    in_copies = [load(ins(kv)) for kv in range(n_kv)]
    next_copies = load(
        [
            pltpu.make_async_copy(query_hbm.at[0:w], query0, next_sem.at[0]),
            pltpu.make_async_copy(grad_hbm.at[0:w], grad0, next_sem.at[1]),
            pltpu.make_async_copy(inputs_hbm, inputs, next_sem.at[2]),
        ]
    )
    set_halves(halves)
    for copy in ids:
        copy.wait()
    for head in range(n_kv * group):
        sink_rows[head : head + 1, :] = jnp.full((1, w), sinks_ref[head], F32)
    segs = [segs_ref[0:1, b * w : (b + 1) * w].astype(F32) for b in range(row_blocks + 1)]
    segs0_ref[...] = segs[0]
    for b in range(row_blocks):
        window_bias(bias, b, segs[b], segs[b + 1])
    for b in range(row_blocks + 1):
        sine, cosine = turn_table(pos_ref[0:1, b * w : (b + 1) * w])
        table_ref[2 * b] = sine
        table_ref[2 * b + 1] = cosine
    for copy in key_copies:
        copy.wait()
    seen = set()
    prepared = [-1]

    def window_of(b, kv, first):
        if b == 0 and first:
            if kv > prepared[0]:
                prepare_keys(kv, [(keys, values, b * w) for b in range(row_blocks + 1)], keys2, values2, keys_t)
            prepared[0] = max(kv, prepared[0])
            waits = [in_copies[0], sum(in_copies[1:], []) + next_copies] + [[]] * n_kv
            for copy in waits[kv]:
                copy.wait()
        window = slice(b * w, (b + 2) * w)
        return [keys2[kv, side, window, :] for side in range(2)], [values2[kv, side, window, :] for side in range(2)]

    features = inputs.shape[1]
    pieces = [(f, t) for f in range(features // w) for t in range(row_blocks + 1)]
    quads = group // 4
    units = n_kv * quads

    def first_block_scores(unit):
        kv, quad = unit // quads, unit % quads
        if kv > prepared[0]:
            prepare_keys(kv, [(keys, values, b * w) for b in range(row_blocks + 1)], keys2, values2, keys_t)
        prepared[0] = max(kv, prepared[0])
        for ref, keys_of, out in [(query0, keys2, own_scores), (grad0, values2, own_grads)]:
            start = kv * group // 2 + 2 * quad
            two = jnp.concatenate([ref[:, (start + t) * lanes : (start + t + 1) * lanes] for t in range(2)], axis=0)
            for side in range(2):
                out[unit, side] = dot(keys_of[kv, side, 0:w, :], two, 1, 1)

    def turn_inputs(n, count):
        begin, end = count // n_kv, 2 * count // n_kv + 2
        if n >= begin:
            done = (n - begin) * units // (count - begin), (n + 1 - begin) * units // (count - begin)
            for unit in range(*done):
                first_block_scores(unit)
        if n == tile_ready(0, count, n_kv):
            finish(0)
        if begin <= n < end:
            for f, t in pieces[(n - begin) * len(pieces) // (end - begin) : (n + 1 - begin) * len(pieces) // (end - begin)]:
                cols = slice(f * w, (f + 1) * w)
                inputs_t[cols, t * w : (t + 1) * w] = inputs[t * w : (t + 1) * w, cols].T

    def finish(tile):
        cols = slice(tile * lanes, (tile + 1) * lanes)
        for b in range(row_blocks + 1):
            turned = rotate(dk_all[b * w : (b + 1) * w, cols], table_ref[2 * b], table_ref[2 * b + 1])
            if b == 0:
                own_ref[:, cols] = turned
            else:
                dk_ref[(b - 1) * w : b * w, cols] = turned.astype(BF16)
        later_ref[:, cols] = dot(inputs_t[:, w:], dk_ref[:, cols], 1, 0)

    attend(
        n_kv, group, row_blocks, window_of, turn_inputs,
        sink_rows, query, grad, ds_ref, bias, halves, scratch,
        lambda b, kv, part: store_dk(dk_part, dk_all, 0, b, kv, part, seen),
    )
    for tile in range(1 if tile_ready(0, n_kv * row_blocks * group // 4, n_kv) else 0, n_kv // 2):
        finish(tile)


def rim_kernel(
    n_kv, group, n_dp, own_ref, table_ref, segs0_ref, query, grad, own_inputs_t, later_ref,
    sink_rows, own_scores, own_grads, rim,
    send_ref, keep_ref, ds_ref, keys_t,
    keys2, values2, bias, halves, dk_part, dk_all, dk16, inputs_t, sums, *scratch,
):
    w = WINDOW
    lanes = 2 * HEADDIM
    features = own_inputs_t.shape[0]
    kv_width = n_kv * HEADDIM
    set_halves(halves)
    rim_keys = rim.at[features : features + kv_width]
    rim_values = rim.at[features + kv_width : features + 2 * kv_width]
    aux = rim[features + 2 * kv_width :, :].astype(F32)
    rim_segs = jnp.where(lax.axis_index("seq") == 0, np.float32(-1.0), aux[0:1])
    window_bias(bias, 0, rim_segs, segs0_ref[...])
    rim_sine, rim_cosine = turn_table(aux[1:2] * np.float32(256.0) + aux[2:3])
    seen = set()

    def window_of(b, kv, first):
        if first:
            prepare_keys(kv, [(rim_keys, rim_values, None)], keys2, values2, keys_t)
        return [[ref[kv, side] for side in range(2)] for ref in (keys2, values2)]

    tiles = features // w

    def turn_inputs(n, count):
        for f in range(n * tiles // count, (n + 1) * tiles // count):
            cols = slice(f * w, (f + 1) * w)
            inputs_t[cols, 0:w] = rim[cols, :].T
            inputs_t[cols, w : 2 * w] = own_inputs_t[cols, 0:w]

    attend(
        n_kv, group, 1, window_of, turn_inputs,
        sink_rows, query, grad, ds_ref, bias, halves, scratch,
        lambda b, kv, part: store_dk(dk_part, dk_all, 0, b, kv, part, seen),
        own_scores, own_grads,
    )
    for tile in range(n_kv // 2):
        cols = slice(tile * lanes, (tile + 1) * lanes)
        dk16[0:w, cols] = rotate(dk_all[0:w, cols], rim_sine, rim_cosine).astype(BF16)
        own = rotate(dk_all[w : 2 * w, cols], table_ref[0], table_ref[1]) + own_ref[:, cols]
        dk16[w : 2 * w, cols] = own.astype(BF16)
    sums[...] = dot(inputs_t[...], dk16[...], 1, 0) + later_ref[...]
    piece = features // (2 * n_dp)
    dp_index = lax.axis_index("dp")
    core = lax.axis_index("seq") & 1
    for half, ref in enumerate([keep_ref, send_ref]):
        for j, relative in enumerate(bit_reversed(n_dp)):
            if piece % 16 == 0:
                side = core ^ half
                block = (dp_index ^ (relative + side * (swapped(relative, n_dp) - relative))) * 2 + side
                start = pl.multiple_of(block * piece, piece)
                ref[j * piece : (j + 1) * piece, :] = sums[pl.ds(start, piece), :].astype(BF16)
    if piece % 16:
        keep_ref[...] = sums[0 : features // 2, :].astype(BF16)
        send_ref[...] = sums[features // 2 :, :].astype(BF16)


def query_kernel(n_kv, group, local_ds, local_keys, rim_ds, rim_keys, dq_hbm, dq, out_sem):
    w = WINDOW
    lanes = 2 * HEADDIM
    step = group * HEADDIM
    row_blocks = local_ds.shape[0] // n_kv
    outs = []
    for block in range(row_blocks + 1):
        rows = slice(block * w, (block + 1) * w)
        for kv in range(n_kv):
            for tile in range(group // 2):
                cols = slice(tile * w, (tile + 1) * w)
                if block == 0:
                    keyt_win = jnp.concatenate([rim_keys[kv], local_keys[kv, :, 0:w]], axis=1)
                    ds_ref, unit = rim_ds, kv
                else:
                    keyt_win = local_keys[kv, :, (block - 1) * w : (block + 1) * w]
                    ds_ref, unit = local_ds, kv * row_blocks + block - 1
                dq_t = [dot(keyt_win, ds_ref[unit, side, :, cols], 1, 0) for side in range(2)]
                start = kv * group // 2 + tile
                dq[rows, start * lanes : (start + 1) * lanes] = jnp.concatenate(dq_t, axis=0).T.astype(BF16)
            cols = slice(kv * step, (kv + 1) * step)
            outs += load([pltpu.make_async_copy(dq.at[rows, cols], dq_hbm.at[rows, cols], out_sem.at[block, kv])])
    for copy in outs:
        copy.wait()


ANY = pl.BlockSpec(memory_space=pl.ANY)
HBM = pl.BlockSpec(memory_space=pltpu.HBM)
VMEM = pl.BlockSpec(memory_space=pltpu.VMEM)
SMEM = pl.BlockSpec(memory_space=pltpu.SMEM)
LIMIT = 24 * 2**20


def estimate(row_blocks, width, extra_flops, extra_bytes):
    w = WINDOW
    return pl.CostEstimate(
        flops=10 * row_blocks * w * 2 * w * width + extra_flops,
        bytes_accessed=6 * row_blocks * w * width + extra_bytes,
        transcendentals=row_blocks * w * w * width // HEADDIM,
    )


def sizes(query, keys):
    width, kv_width = query.shape[-1], keys.shape[-1]
    return width, kv_width, kv_width // HEADDIM, width // kv_width


def shape(*dims, kind=BF16):
    return jax.ShapeDtypeStruct(dims, kind)


def local_grads(query, grad_out, keys, values, layer_input, segments, positions, sinks):
    rows, features = layer_input.shape
    width, kv_width, n_kv, group = sizes(query, keys)
    w = WINDOW
    lanes = 2 * HEADDIM
    row_blocks = rows // w - 1
    return pl.pallas_call(
        lambda *refs: local_kernel(n_kv, group, *refs),
        name="local_grads",
        in_specs=[HBM] * 8,
        out_specs=[VMEM] * 13,
        out_shape=[
            shape(w, kv_width, kind=F32),
            shape(2 * (row_blocks + 1), w, lanes, kind=F32),
            shape(row_blocks * n_kv, 2, 2 * w, group // 2 * w),
            shape(n_kv, HEADDIM, rows),
            shape(1, w, kind=F32),
            shape(w, width),
            shape(w, width),
            shape(n_kv, 2, rows, lanes),
            shape(features, rows),
            shape(features, kv_width, kind=F32),
            shape(n_kv * group, w, kind=F32),
            shape(n_kv * group // 4, 2, w, 2 * w, kind=F32),
            shape(n_kv * group // 4, 2, w, 2 * w, kind=F32),
        ],
        scratch_shapes=[
            pltpu.VMEM((n_kv, 2, rows, lanes), BF16),
            pltpu.VMEM((row_blocks * w, width), BF16),
            pltpu.VMEM((row_blocks * w, width), BF16),
            pltpu.VMEM((rows, kv_width), BF16),
            pltpu.VMEM((rows, kv_width), BF16),
            pltpu.VMEM(layer_input.shape, BF16),
            pltpu.VMEM((rows - w, kv_width), BF16),
            pltpu.SMEM(sinks.shape, F32),
            pltpu.VMEM(segments.shape, jnp.int32),
            pltpu.VMEM(segments.shape, jnp.int32),
            pltpu.VMEM((row_blocks, w, w), F32),
            pltpu.VMEM((2, w, w), BF16),
            pltpu.VMEM((row_blocks, 2 * w, lanes), F32),
            pltpu.VMEM((rows, kv_width), F32),
            pltpu.SemaphoreType.DMA((5,)),
            pltpu.SemaphoreType.DMA((2, n_kv)),
            pltpu.SemaphoreType.DMA((3,)),
        ]
        + attend_scratch(),
        compiler_params=pltpu.CompilerParams(vmem_limit_bytes=LIMIT),
        cost_estimate=estimate(row_blocks, width, 0, 0),
    )(sinks, segments, positions, query, grad_out, keys, values, layer_input)


def rim_grads(local, rim, kv_width, n_dp):
    own, table, _, _, segs0, query0, grad0, _, inputs_t, later, sink_rows, own_scores, own_grads = local
    features, rows = inputs_t.shape
    width = query0.shape[1]
    n_kv = kv_width // HEADDIM
    group = width // kv_width
    w = WINDOW
    lanes = 2 * HEADDIM
    return pl.pallas_call(
        lambda *refs: rim_kernel(n_kv, group, n_dp, *refs),
        name="rim_grads",
        in_specs=[VMEM] * 11,
        out_specs=[VMEM] * 4,
        out_shape=[
            shape(features // 2, kv_width),
            shape(features // 2, kv_width),
            shape(n_kv, 2, 2 * w, group // 2 * w),
            shape(n_kv, HEADDIM, w),
        ],
        scratch_shapes=[
            pltpu.VMEM((n_kv, 2, w, lanes), BF16),
            pltpu.VMEM((n_kv, 2, w, lanes), BF16),
            pltpu.VMEM((1, w, w), F32),
            pltpu.VMEM((2, w, w), BF16),
            pltpu.VMEM((1, 2 * w, lanes), F32),
            pltpu.VMEM((2 * w, kv_width), F32),
            pltpu.VMEM((2 * w, kv_width), BF16),
            pltpu.VMEM((features, 2 * w), BF16),
            pltpu.VMEM((features, kv_width), F32),
        ]
        + attend_scratch(),
        compiler_params=pltpu.CompilerParams(vmem_limit_bytes=LIMIT),
        cost_estimate=estimate(1, width, 2 * features * kv_width * 2 * w, 8 * features * kv_width),
    )(own, table, segs0, query0, grad0, inputs_t, later, sink_rows, own_scores, own_grads, rim)


def query_grads(local_ds, local_keys, rim_ds, rim_keys, group):
    n_kv, _, rows = local_keys.shape
    width = n_kv * group * HEADDIM
    w = WINDOW
    return pl.pallas_call(
        lambda *refs: query_kernel(n_kv, group, *refs),
        name="query_grads",
        in_specs=[VMEM] * 4,
        out_specs=HBM,
        out_shape=shape(rows, width),
        scratch_shapes=[pltpu.VMEM((rows, width), BF16), pltpu.SemaphoreType.DMA((rows // w, n_kv))],
        compiler_params=pltpu.CompilerParams(vmem_limit_bytes=LIMIT),
        cost_estimate=pl.CostEstimate(
            flops=4 * rows * w * width, bytes_accessed=2 * rows * width + 4 * rows * w * width // HEADDIM, transcendentals=0
        ),
    )(local_ds, local_keys, rim_ds, rim_keys)


def tail_kernel(segs_hbm, pos_hbm, inputs_hbm, keys_hbm, values_hbm, out_ref, segs_ref, pos_ref, sem):
    w = WINDOW
    rows = inputs_hbm.shape[0]
    ids = load(
        [
            pltpu.make_async_copy(segs_hbm, segs_ref, sem.at[0]),
            pltpu.make_async_copy(pos_hbm, pos_ref, sem.at[1]),
        ]
    )
    copies = []
    for hbm in (inputs_hbm, keys_hbm, values_hbm):
        for start in range(0, hbm.shape[1], w):
            n = len(copies)
            source = hbm.at[rows - w :, start : start + w]
            copies += load([pltpu.make_async_copy(source, out_ref.at[n * w : (n + 1) * w], sem.at[n + 2])])
    for copy in ids:
        copy.wait()
    line = iota((16, w), 0)
    segs = segs_ref[0:1, rows - w :]
    pos = pos_ref[0:1, rows - w :]
    aux = jnp.where(line == 0, segs, jnp.where(line == 1, pos >> 8, pos & 255))
    out_ref[len(copies) * w :, :] = aux.astype(F32).astype(BF16)
    for copy in copies:
        copy.wait()


def last_tokens(layer_input, keys, values, segments, positions):
    tiles = (layer_input.shape[1] + 2 * keys.shape[1]) // WINDOW
    return pl.pallas_call(
        tail_kernel,
        name="last_tokens",
        in_specs=[HBM] * 5,
        out_specs=VMEM,
        out_shape=shape(tiles * WINDOW + 16, WINDOW),
        scratch_shapes=[
            pltpu.VMEM(segments.shape, jnp.int32),
            pltpu.VMEM(segments.shape, jnp.int32),
            pltpu.SemaphoreType.DMA((tiles + 2,)),
        ],
        compiler_params=pltpu.CompilerParams(vmem_limit_bytes=LIMIT),
    )(segments, positions, layer_input, keys, values)


def swapped(relative, n):
    return relative if n < 4 else (relative & ~3) | (relative & 1) << 1 | (relative & 2) >> 1


def bit_reversed(n):
    bits = n.bit_length() - 1
    return [int(format(i, "b").zfill(bits)[::-1], 2) if bits else 0 for i in range(n)]


def exchange(part, axis, by):
    count = lax.axis_size(axis)
    return lax.ppermute(part, axis, [(i, i ^ by) for i in range(count)])


def bits(n):
    return n.bit_length() - 1


def share_and_sum(total, by):
    n_dp, n_seq = lax.axis_size("dp"), lax.axis_size("seq")
    half = total.shape[0] // 2
    mine, theirs = total[:half].astype(BF16), total[half:].astype(BF16)

    def swap(part, dp_bits, seq_bits):
        pairs = [
            (d * n_seq + q, (d ^ dp_bits) * n_seq + (q ^ seq_bits)) for d in range(n_dp) for q in range(n_seq)
        ]
        return lax.ppermute(part, ("dp", "seq"), pairs).astype(F32)

    far = swap(theirs, by, 2)
    near = swap(theirs, by, 0)
    beside = swap(mine, 0, 2)
    return (far + near) + (beside + mine.astype(F32))


def exchange_by_core(part, relative):
    n_dp, n_seq = lax.axis_size("dp"), lax.axis_size("seq")
    pairs = []
    for d in range(n_dp):
        for q in range(n_seq):
            other = d ^ (swapped(relative, n_dp) if q % 2 else relative)
            pairs.append((d * n_seq + q, other * n_seq + q))
    return lax.ppermute(part, ("dp", "seq"), pairs)


def share(total, by, ways, beside=None, held=None):
    rows = total.shape[0] // ways
    parts = [total[k * rows : (k + 1) * rows] for k in range(ways)]
    sends = [part.astype(BF16) for part in parts[1:]]
    if beside is not None:
        sends, held = lax.optimization_barrier((sends, held))
        extra = beside(held)
    got = []
    for k in reversed(range(1, ways)):
        relative = bit_reversed(ways)[k] * by
        got.append(exchange_by_core(sends[k - 1], relative))
    if beside is not None:
        got, extra = lax.optimization_barrier((got, extra))
    total = parts[0]
    for part in got:
        total = total + part.astype(F32)
    return total if beside is None else (total, extra)


def forward_one(part, axis):
    count = lax.axis_size(axis)
    return lax.ppermute(part, axis, [(i, i + 1) for i in range(count - 1)])


def body(query, keys, values, grad_out, layer_input, sinks, segments, positions):
    n_dp = lax.axis_size("dp")
    n_seq = lax.axis_size("seq")
    dp_index = lax.axis_index("dp")
    seq_index = lax.axis_index("seq")
    core = seq_index & 1
    kv_width = keys.shape[2]
    features = layer_input.shape[2]
    piece = features // (2 * n_dp)
    query, grad_out, layer_input, keys, values = [
        pltpu.with_memory_space_constraint(x[0], pltpu.HBM) for x in (query, grad_out, layer_input, keys, values)
    ]
    sinks, segments, positions = [
        pltpu.with_memory_space_constraint(x, pltpu.HBM) for x in (sinks, segments, positions)
    ]
    tail = last_tokens(layer_input, keys, values, segments, positions)
    rim = forward_one(tail, "seq")
    local = local_grads(query, grad_out, keys, values, layer_input, segments, positions, sinks)
    send, keep, rim_ds, rim_keys = rim_grads(local, rim, kv_width, n_dp)
    if piece % 16:
        plain = jnp.concatenate([keep, send], axis=0).reshape(n_dp, 2, piece, kv_width)
        order = bit_reversed(n_dp)
        orders = jnp.asarray([order, [swapped(relative, n_dp) for relative in order]], jnp.int32) ^ dp_index
        keep, send = [
            jnp.take(plain[:, side], orders[side], axis=0).reshape(-1, kv_width) for side in (core, core ^ 1)
        ]
    total = keep.astype(F32) + exchange(send, "seq", 1).astype(F32)
    group = query.shape[1] // kv_width

    def beside(held):
        return query_grads(*held, group)

    held = (local[2], local[3], rim_ds, rim_keys)
    dq = None
    by = 1
    last = n_dp // 2 if n_seq == 4 and bits(n_dp) % 2 else n_dp
    while by < last:
        ways = 4 if 4 * by <= last else 2
        if dq is None:
            total, dq = share(total, by, ways, beside, held)
        else:
            total = share(total, by, ways)
        by *= ways
    if dq is None:
        dq = beside(held)
    if last < n_dp:
        total = share_and_sum(total, last)
    else:
        by = 2
        while by < n_seq:
            mine = total.astype(BF16)
            total = mine.astype(F32) + exchange(mine, "seq", by).astype(F32)
            by *= 2
    other = exchange(total, "seq", 1)
    pair = jnp.where(core == 0, jnp.stack([total, other]), jnp.stack([other, total]))
    return (dq[None], pair.reshape(-1, kv_width))


def solution(mesh):
    return jax.shard_map(
        body,
        mesh=mesh,
        in_specs=(
            P("dp", "seq", None),
            P("dp", "seq", None),
            P("dp", "seq", None),
            P("dp", "seq", None),
            P("dp", "seq", None),
            P(),
            P("dp", "seq"),
            P("dp", "seq"),
        ),
        out_specs=(P("dp", "seq", None), P("dp", None)),
        check_vma=False,
    )
```

```python
import jax
import jax.numpy as jnp
import numpy as np
from jax import lax
from jax.experimental import pallas as pl
from jax.experimental.pallas import tpu as pltpu
from jax.sharding import PartitionSpec as P

HEADDIM = 64
WINDOW = 128
THETA = 150000.0
LOW = -1e30

F32 = jnp.float32
BF16 = jnp.bfloat16


def dot(a, b, ca, cb):
    return lax.dot_general(a, b, (((ca,), (cb,)), ((), ())), preferred_element_type=F32)


def iota(shape, dim):
    return lax.broadcasted_iota(jnp.int32, shape, dim)


def sin_cos(angle):
    turns = jnp.floor(angle * np.float32(2.0 / np.pi) + np.float32(0.5))
    rest = angle - turns * np.float32(1.5703125)
    rest = rest - turns * np.float32(4.837512969970703125e-4)
    rest = rest - turns * np.float32(7.54978995489188216e-8)
    sq = rest * rest
    sin_part = np.float32(-1.9515295891e-4) * sq + np.float32(8.3321608736e-3)
    sin_part = (sin_part * sq + np.float32(-1.6666654611e-1)) * sq * rest + rest
    cos_part = np.float32(2.443315711809948e-5) * sq + np.float32(-1.388731625493765e-3)
    cos_part = (cos_part * sq + np.float32(4.166664568298827e-2)) * sq * sq
    cos_part = cos_part - np.float32(0.5) * sq + np.float32(1.0)
    quadrant = turns.astype(jnp.int32)
    odd = (quadrant & 1) == 1
    sine = jnp.where(odd, cos_part, sin_part)
    cosine = jnp.where(odd, sin_part, cos_part)
    sine = jnp.where((quadrant & 2) == 2, -sine, sine)
    cosine = jnp.where(((quadrant + 1) & 2) == 2, -cosine, cosine)
    return sine, cosine


def as_column(row):
    return jnp.broadcast_to(row, (row.shape[1], row.shape[1])).T


def load(copies):
    for copy in copies:
        copy.start()
    return copies


def prepare_keys(kv, blocks, keys2, values2, keys_t):
    w = WINDOW
    lanes = 2 * HEADDIM
    own_half = (iota((w, lanes), 1) < HEADDIM) == (kv % 2 == 0)
    for b, (k_ref, v_ref, first_row) in enumerate(blocks):
        rows = slice(b * w, (b + 1) * w)
        if first_row is None:
            at = (slice(kv // 2 * w, (kv // 2 + 1) * w), slice(None))
        else:
            at = (slice(first_row, first_row + w), slice(kv // 2 * lanes, (kv // 2 + 1) * lanes))
        k_tile = k_ref[at].astype(F32) * np.float32(HEADDIM**-0.5)
        v_tile = v_ref[at].astype(F32)
        k_tile = jnp.where(own_half, k_tile, np.float32(0.0))
        v_tile = jnp.where(own_half, v_tile, np.float32(0.0))
        keys2[kv, kv % 2, rows, :] = k_tile.astype(BF16)
        values2[kv, kv % 2, rows, :] = v_tile.astype(BF16)
        keys2[kv, 1 - kv % 2, rows, :] = pltpu.roll(k_tile, HEADDIM, 1).astype(BF16)
        values2[kv, 1 - kv % 2, rows, :] = pltpu.roll(v_tile, HEADDIM, 1).astype(BF16)
        half = slice(kv % 2 * HEADDIM, (kv % 2 + 1) * HEADDIM)
        keys_t[kv, :, rows] = k_tile.T[half].astype(BF16)


def attend(
    n_kv, group, row_blocks, window_of, beside, sink_rows, query, grad, ds_s, bias, halves, scratch, add_dk
):
    scores_s, grads_s = scratch
    w = WINDOW
    lanes = 2 * HEADDIM
    quads = group // 4
    tri = iota((w, w), 0) <= iota((w, w), 1)
    tri2 = jnp.concatenate([tri, tri], axis=1)
    items = [(b, kv, quad) for kv in range(n_kv) for b in range(row_blocks) for quad in range(quads)]

    def tiles(ref, b, kv, first, count):
        rows = slice(b * w, (b + 1) * w)
        start = kv * group // 2 + first
        return jnp.concatenate(
            [ref[rows, (start + t) * lanes : (start + t + 1) * lanes] for t in range(count)], axis=0
        )

    def to_scores(n):
        b, kv, quad = items[n]
        key_win, value_win = window_of(b, kv, quad == 0)
        q_two = tiles(query, b, kv, 2 * quad, 2)
        g_two = tiles(grad, b, kv, 2 * quad, 2)
        bias2 = jnp.concatenate([bias[b], bias[b]], axis=1)
        for side in range(2):
            scores = dot(key_win[side], q_two, 1, 1)
            scores_s[n % 2, side] = jnp.where(tri2, scores[w:], scores[:w]) + bias2
        for side in range(2):
            grads = dot(value_win[side], g_two, 1, 1)
            grads_s[n % 2, side] = jnp.where(tri2, grads[w:], grads[:w])

    def to_ds(n):
        b, kv, quad = items[n]
        unit = n // quads
        for side in range(2):
            for t in range(2):
                cols = slice(t * w, (t + 1) * w)
                head = kv * group + 4 * quad + 2 * t + side
                sink = sink_rows[head : head + 1, :]
                scores = scores_s[n % 2, side, :, cols]
                peak = jnp.maximum(jnp.max(scores, axis=0, keepdims=True), sink)
                expo = jnp.exp(scores - peak)
                total = jnp.sum(expo, axis=0, keepdims=True) + jnp.exp(sink - peak)
                probs = expo * (np.float32(1.0) / total)
                grads = grads_s[n % 2, side, :, cols]
                delta = jnp.sum(probs * grads, axis=0, keepdims=True)
                ds = (probs * (grads - delta)).astype(BF16)
                out_cols = slice((2 * quad + t) * w, (2 * quad + t + 1) * w)
                ds_s[unit, side, 0:w, out_cols] = ds * halves[0]
                ds_s[unit, side, w : 2 * w, out_cols] = ds * halves[1]

    def to_grads(n):
        b, kv, quad = items[n]
        if quad == quads - 1:
            q_all = tiles(query, b, kv, 0, group // 2)
            low = iota((2 * w, lanes), 1) < HEADDIM
            sides = [dot(ds_s[n // quads, side], q_all, 1, 0) for side in range(2)]
            add_dk(b, kv, jnp.where(low, sides[0], sides[1]))

    for n in range(len(items) + 2):
        if n < len(items):
            to_scores(n)
        if 0 <= n - 1 < len(items):
            to_ds(n - 1)
        if n >= 2:
            to_grads(n - 2)
        if n < len(items):
            beside(n, len(items))


def attend_scratch():
    w = WINDOW
    return [
        pltpu.VMEM((2, 2, w, 2 * w), F32),
        pltpu.VMEM((2, 2, w, 2 * w), F32),
    ]


def set_halves(halves):
    tri = iota((WINDOW, WINDOW), 0) <= iota((WINDOW, WINDOW), 1)
    halves[0] = jnp.where(tri, np.float32(0.0), np.float32(1.0)).astype(BF16)
    halves[1] = jnp.where(tri, np.float32(1.0), np.float32(0.0)).astype(BF16)


def tile_ready(tile, count, n_kv):
    n = (2 * tile + 2) * count // n_kv + 2
    return n if n < count else None


def window_bias(bias, b, prev_segs, own_segs):
    tri = iota((WINDOW, WINDOW), 0) <= iota((WINDOW, WINDOW), 1)
    key_segs = jnp.where(tri, as_column(own_segs), as_column(prev_segs))
    bias[b] = jnp.where(key_segs == own_segs, np.float32(0.0), np.float32(LOW))


def store_dk(dk_part, dk_all, first_block, b, kv, part, seen):
    w = WINDOW
    lanes = 2 * HEADDIM
    if kv % 2 == 0:
        dk_part[b] = part
        return
    even = dk_part[b]
    low = iota(part.shape, 1) < HEADDIM
    both = jnp.where(low, even, part) + pltpu.roll(jnp.where(low, part, even), HEADDIM, 1)
    cols = slice(kv // 2 * lanes, (kv // 2 + 1) * lanes)
    for k in range(2):
        rows = slice((first_block + b + k) * w, (first_block + b + k + 1) * w)
        piece = both[k * w : (k + 1) * w]
        if (first_block + b + k, kv) in seen:
            piece = piece + dk_all[rows, cols]
        seen.add((first_block + b + k, kv))
        dk_all[rows, cols] = piece


def rotate(dk, sine, cosine):
    half = HEADDIM // 2
    lanes = dk.shape[1]
    low = (iota(dk.shape, 1) % HEADDIM) < half
    other = jnp.where(low, pltpu.roll(dk, lanes - half, 1), pltpu.roll(dk, half, 1))
    return (dk * cosine + other * sine) * np.float32(HEADDIM**-0.5)


def turn_table(pos):
    half = HEADDIM // 2
    index = iota((1, 2 * HEADDIM), 1) % half
    rates = (THETA ** (-2.0 * np.arange(half) / HEADDIM)).astype(np.float32)
    freq = jnp.zeros((1, 2 * HEADDIM), F32)
    for t in range(half):
        freq = jnp.where(index == t, rates[t], freq)
    sine, cosine = sin_cos(as_column(pos.astype(F32)) * freq)
    low = (iota(sine.shape, 1) % HEADDIM) < HEADDIM // 2
    return jnp.where(low, sine, -sine), cosine


def local_kernel(
    n_kv, group, sinks_hbm, segs_hbm, pos_hbm, query_hbm, grad_hbm, keys_hbm, values_hbm, inputs_hbm,
    own_ref, table_ref, ds_ref, keys_t, segs0_ref, query0, grad0, keys2, values2, inputs_t, later_ref, sink_rows,
    query, grad, keys, values, inputs, dk_ref, sinks_ref, segs_ref, pos_ref, bias, halves, dk_part, dk_all, id_sem, in_sem, next_sem,
    *scratch,
):
    w = WINDOW
    lanes = 2 * HEADDIM
    rows = keys.shape[0]
    row_blocks = rows // w - 1
    step = group * HEADDIM
    ids = load(
        [
            pltpu.make_async_copy(pos_hbm, pos_ref, id_sem.at[3]),
            pltpu.make_async_copy(segs_hbm, segs_ref, id_sem.at[2]),
            pltpu.make_async_copy(sinks_hbm, sinks_ref, id_sem.at[4]),
        ]
    )
    key_copies = load(
        [
            pltpu.make_async_copy(keys_hbm, keys, id_sem.at[0]),
            pltpu.make_async_copy(values_hbm, values, id_sem.at[1]),
        ]
    )

    def ins(kv):
        cols = slice(kv * step, (kv + 1) * step)
        return [
            pltpu.make_async_copy(query_hbm.at[w:, cols], query.at[:, cols], in_sem.at[0, kv]),
            pltpu.make_async_copy(grad_hbm.at[w:, cols], grad.at[:, cols], in_sem.at[1, kv]),
        ]

    in_copies = [load(ins(kv)) for kv in range(n_kv)]
    next_copies = load(
        [
            pltpu.make_async_copy(query_hbm.at[0:w], query0, next_sem.at[0]),
            pltpu.make_async_copy(grad_hbm.at[0:w], grad0, next_sem.at[1]),
            pltpu.make_async_copy(inputs_hbm, inputs, next_sem.at[2]),
        ]
    )
    set_halves(halves)
    for copy in ids:
        copy.wait()
    for head in range(n_kv * group):
        sink_rows[head : head + 1, :] = jnp.full((1, w), sinks_ref[head], F32)
    segs = [segs_ref[0:1, b * w : (b + 1) * w].astype(F32) for b in range(row_blocks + 1)]
    segs0_ref[...] = segs[0]
    for b in range(row_blocks):
        window_bias(bias, b, segs[b], segs[b + 1])
    for b in range(row_blocks + 1):
        sine, cosine = turn_table(pos_ref[0:1, b * w : (b + 1) * w])
        table_ref[2 * b] = sine
        table_ref[2 * b + 1] = cosine
    for copy in key_copies:
        copy.wait()
    seen = set()

    def window_of(b, kv, first):
        if b == 0 and first:
            prepare_keys(kv, [(keys, values, b * w) for b in range(row_blocks + 1)], keys2, values2, keys_t)
            waits = [in_copies[0], sum(in_copies[1:], []) + next_copies[2:]] + [[]] * n_kv
            for copy in waits[kv]:
                copy.wait()
        window = slice(b * w, (b + 2) * w)
        return [keys2[kv, side, window, :] for side in range(2)], [values2[kv, side, window, :] for side in range(2)]

    features = inputs.shape[1]
    pieces = [(f, t) for f in range(features // w) for t in range(row_blocks + 1)]

    def turn_inputs(n, count):
        begin, end = count // n_kv, 2 * count // n_kv + 2
        if n == tile_ready(0, count, n_kv):
            finish(0)
        if begin <= n < end:
            for f, t in pieces[(n - begin) * len(pieces) // (end - begin) : (n + 1 - begin) * len(pieces) // (end - begin)]:
                cols = slice(f * w, (f + 1) * w)
                inputs_t[cols, t * w : (t + 1) * w] = inputs[t * w : (t + 1) * w, cols].T

    def finish(tile):
        cols = slice(tile * lanes, (tile + 1) * lanes)
        for b in range(row_blocks + 1):
            turned = rotate(dk_all[b * w : (b + 1) * w, cols], table_ref[2 * b], table_ref[2 * b + 1])
            if b == 0:
                own_ref[:, cols] = turned
            else:
                dk_ref[(b - 1) * w : b * w, cols] = turned.astype(BF16)
        later_ref[:, cols] = dot(inputs_t[:, w:], dk_ref[:, cols], 1, 0)

    attend(
        n_kv, group, row_blocks, window_of, turn_inputs,
        sink_rows, query, grad, ds_ref, bias, halves, scratch,
        lambda b, kv, part: store_dk(dk_part, dk_all, 0, b, kv, part, seen),
    )
    for tile in range(1 if tile_ready(0, n_kv * row_blocks * group // 4, n_kv) else 0, n_kv // 2):
        finish(tile)
    for copy in next_copies[:2]:
        copy.wait()


def rim_kernel(
    n_kv, group, n_dp, own_ref, table_ref, segs0_ref, query, grad, own_keys2, own_values2, own_inputs_t, later_ref,
    sink_rows, rim,
    send_ref, keep_ref, ds_ref, keys_t,
    keys2, values2, bias, halves, dk_part, dk_all, dk16, inputs_t, sums, *scratch,
):
    w = WINDOW
    lanes = 2 * HEADDIM
    features = own_inputs_t.shape[0]
    kv_width = n_kv * HEADDIM
    set_halves(halves)
    rim_keys = rim.at[features : features + kv_width]
    rim_values = rim.at[features + kv_width : features + 2 * kv_width]
    aux = rim[features + 2 * kv_width :, :].astype(F32)
    rim_segs = jnp.where(lax.axis_index("seq") == 0, np.float32(-1.0), aux[0:1])
    window_bias(bias, 0, rim_segs, segs0_ref[...])
    rim_sine, rim_cosine = turn_table(aux[1:2] * np.float32(256.0) + aux[2:3])
    seen = set()

    def window_of(b, kv, first):
        if first:
            prepare_keys(kv, [(rim_keys, rim_values, None)], keys2, values2, keys_t)
        both = [(keys2, own_keys2), (values2, own_values2)]
        return [
            [jnp.concatenate([rim2[kv, side], own2[kv, side, 0:w]], axis=0) for side in range(2)]
            for rim2, own2 in both
        ]

    tiles = features // w

    def turn_inputs(n, count):
        for f in range(n * tiles // count, (n + 1) * tiles // count):
            cols = slice(f * w, (f + 1) * w)
            inputs_t[cols, 0:w] = rim[cols, :].T
            inputs_t[cols, w : 2 * w] = own_inputs_t[cols, 0:w]

    attend(
        n_kv, group, 1, window_of, turn_inputs,
        sink_rows, query, grad, ds_ref, bias, halves, scratch,
        lambda b, kv, part: store_dk(dk_part, dk_all, 0, b, kv, part, seen),
    )
    for tile in range(n_kv // 2):
        cols = slice(tile * lanes, (tile + 1) * lanes)
        dk16[0:w, cols] = rotate(dk_all[0:w, cols], rim_sine, rim_cosine).astype(BF16)
        own = rotate(dk_all[w : 2 * w, cols], table_ref[0], table_ref[1]) + own_ref[:, cols]
        dk16[w : 2 * w, cols] = own.astype(BF16)
    sums[...] = dot(inputs_t[...], dk16[...], 1, 0) + later_ref[...]
    piece = features // (2 * n_dp)
    dp_index = lax.axis_index("dp")
    core = lax.axis_index("seq") & 1
    for half, ref in enumerate([keep_ref, send_ref]):
        for j, relative in enumerate(bit_reversed(n_dp)):
            if piece % 16 == 0:
                side = core ^ half
                block = (dp_index ^ (relative + side * (swapped(relative, n_dp) - relative))) * 2 + side
                start = pl.multiple_of(block * piece, piece)
                ref[j * piece : (j + 1) * piece, :] = sums[pl.ds(start, piece), :].astype(BF16)
    if piece % 16:
        keep_ref[...] = sums[0 : features // 2, :].astype(BF16)
        send_ref[...] = sums[features // 2 :, :].astype(BF16)


def query_kernel(n_kv, group, local_ds, local_keys, rim_ds, rim_keys, dq_hbm, dq, out_sem):
    w = WINDOW
    lanes = 2 * HEADDIM
    step = group * HEADDIM
    row_blocks = local_ds.shape[0] // n_kv
    outs = []
    for block in range(row_blocks + 1):
        rows = slice(block * w, (block + 1) * w)
        for kv in range(n_kv):
            for tile in range(group // 2):
                cols = slice(tile * w, (tile + 1) * w)
                if block == 0:
                    keyt_win = jnp.concatenate([rim_keys[kv], local_keys[kv, :, 0:w]], axis=1)
                    ds_ref, unit = rim_ds, kv
                else:
                    keyt_win = local_keys[kv, :, (block - 1) * w : (block + 1) * w]
                    ds_ref, unit = local_ds, kv * row_blocks + block - 1
                dq_t = [dot(keyt_win, ds_ref[unit, side, :, cols], 1, 0) for side in range(2)]
                start = kv * group // 2 + tile
                dq[rows, start * lanes : (start + 1) * lanes] = jnp.concatenate(dq_t, axis=0).T.astype(BF16)
            cols = slice(kv * step, (kv + 1) * step)
            outs += load([pltpu.make_async_copy(dq.at[rows, cols], dq_hbm.at[rows, cols], out_sem.at[block, kv])])
    for copy in outs:
        copy.wait()


ANY = pl.BlockSpec(memory_space=pl.ANY)
HBM = pl.BlockSpec(memory_space=pltpu.HBM)
VMEM = pl.BlockSpec(memory_space=pltpu.VMEM)
SMEM = pl.BlockSpec(memory_space=pltpu.SMEM)
LIMIT = 24 * 2**20


def estimate(row_blocks, width, extra_flops, extra_bytes):
    w = WINDOW
    return pl.CostEstimate(
        flops=10 * row_blocks * w * 2 * w * width + extra_flops,
        bytes_accessed=6 * row_blocks * w * width + extra_bytes,
        transcendentals=row_blocks * w * w * width // HEADDIM,
    )


def sizes(query, keys):
    width, kv_width = query.shape[-1], keys.shape[-1]
    return width, kv_width, kv_width // HEADDIM, width // kv_width


def shape(*dims, kind=BF16):
    return jax.ShapeDtypeStruct(dims, kind)


def local_grads(query, grad_out, keys, values, layer_input, segments, positions, sinks):
    rows, features = layer_input.shape
    width, kv_width, n_kv, group = sizes(query, keys)
    w = WINDOW
    lanes = 2 * HEADDIM
    row_blocks = rows // w - 1
    return pl.pallas_call(
        lambda *refs: local_kernel(n_kv, group, *refs),
        name="local_grads",
        in_specs=[HBM] * 8,
        out_specs=[VMEM] * 12,
        out_shape=[
            shape(w, kv_width, kind=F32),
            shape(2 * (row_blocks + 1), w, lanes, kind=F32),
            shape(row_blocks * n_kv, 2, 2 * w, group // 2 * w),
            shape(n_kv, HEADDIM, rows),
            shape(1, w, kind=F32),
            shape(w, width),
            shape(w, width),
            shape(n_kv, 2, rows, lanes),
            shape(n_kv, 2, rows, lanes),
            shape(features, rows),
            shape(features, kv_width, kind=F32),
            shape(n_kv * group, w, kind=F32),
        ],
        scratch_shapes=[
            pltpu.VMEM((row_blocks * w, width), BF16),
            pltpu.VMEM((row_blocks * w, width), BF16),
            pltpu.VMEM((rows, kv_width), BF16),
            pltpu.VMEM((rows, kv_width), BF16),
            pltpu.VMEM(layer_input.shape, BF16),
            pltpu.VMEM((rows - w, kv_width), BF16),
            pltpu.SMEM(sinks.shape, F32),
            pltpu.VMEM(segments.shape, jnp.int32),
            pltpu.VMEM(segments.shape, jnp.int32),
            pltpu.VMEM((row_blocks, w, w), F32),
            pltpu.VMEM((2, w, w), BF16),
            pltpu.VMEM((row_blocks, 2 * w, lanes), F32),
            pltpu.VMEM((rows, kv_width), F32),
            pltpu.SemaphoreType.DMA((5,)),
            pltpu.SemaphoreType.DMA((2, n_kv)),
            pltpu.SemaphoreType.DMA((3,)),
        ]
        + attend_scratch(),
        compiler_params=pltpu.CompilerParams(vmem_limit_bytes=LIMIT),
        cost_estimate=estimate(row_blocks, width, 0, 0),
    )(sinks, segments, positions, query, grad_out, keys, values, layer_input)


def rim_grads(local, rim, kv_width, n_dp):
    own, table, _, _, segs0, query0, grad0, keys2, values2, inputs_t, later, sink_rows = local
    features, rows = inputs_t.shape
    width = query0.shape[1]
    n_kv = kv_width // HEADDIM
    group = width // kv_width
    w = WINDOW
    lanes = 2 * HEADDIM
    return pl.pallas_call(
        lambda *refs: rim_kernel(n_kv, group, n_dp, *refs),
        name="rim_grads",
        in_specs=[VMEM] * 11,
        out_specs=[VMEM] * 4,
        out_shape=[
            shape(features // 2, kv_width),
            shape(features // 2, kv_width),
            shape(n_kv, 2, 2 * w, group // 2 * w),
            shape(n_kv, HEADDIM, w),
        ],
        scratch_shapes=[
            pltpu.VMEM((n_kv, 2, w, lanes), BF16),
            pltpu.VMEM((n_kv, 2, w, lanes), BF16),
            pltpu.VMEM((1, w, w), F32),
            pltpu.VMEM((2, w, w), BF16),
            pltpu.VMEM((1, 2 * w, lanes), F32),
            pltpu.VMEM((2 * w, kv_width), F32),
            pltpu.VMEM((2 * w, kv_width), BF16),
            pltpu.VMEM((features, 2 * w), BF16),
            pltpu.VMEM((features, kv_width), F32),
        ]
        + attend_scratch(),
        compiler_params=pltpu.CompilerParams(vmem_limit_bytes=LIMIT),
        cost_estimate=estimate(1, width, 2 * features * kv_width * 2 * w, 8 * features * kv_width),
    )(own, table, segs0, query0, grad0, keys2, values2, inputs_t, later, sink_rows, rim)


def query_grads(local_ds, local_keys, rim_ds, rim_keys, group):
    n_kv, _, rows = local_keys.shape
    width = n_kv * group * HEADDIM
    w = WINDOW
    return pl.pallas_call(
        lambda *refs: query_kernel(n_kv, group, *refs),
        name="query_grads",
        in_specs=[VMEM] * 4,
        out_specs=HBM,
        out_shape=shape(rows, width),
        scratch_shapes=[pltpu.VMEM((rows, width), BF16), pltpu.SemaphoreType.DMA((rows // w, n_kv))],
        compiler_params=pltpu.CompilerParams(vmem_limit_bytes=LIMIT),
        cost_estimate=pl.CostEstimate(
            flops=4 * rows * w * width, bytes_accessed=2 * rows * width + 4 * rows * w * width // HEADDIM, transcendentals=0
        ),
    )(local_ds, local_keys, rim_ds, rim_keys)


def tail_kernel(segs_hbm, pos_hbm, inputs_hbm, keys_hbm, values_hbm, out_ref, segs_ref, pos_ref, sem):
    w = WINDOW
    rows = inputs_hbm.shape[0]
    ids = load(
        [
            pltpu.make_async_copy(segs_hbm, segs_ref, sem.at[0]),
            pltpu.make_async_copy(pos_hbm, pos_ref, sem.at[1]),
        ]
    )
    copies = []
    for hbm in (inputs_hbm, keys_hbm, values_hbm):
        for start in range(0, hbm.shape[1], w):
            n = len(copies)
            source = hbm.at[rows - w :, start : start + w]
            copies += load([pltpu.make_async_copy(source, out_ref.at[n * w : (n + 1) * w], sem.at[n + 2])])
    for copy in ids:
        copy.wait()
    line = iota((16, w), 0)
    segs = segs_ref[0:1, rows - w :]
    pos = pos_ref[0:1, rows - w :]
    aux = jnp.where(line == 0, segs, jnp.where(line == 1, pos >> 8, pos & 255))
    out_ref[len(copies) * w :, :] = aux.astype(F32).astype(BF16)
    for copy in copies:
        copy.wait()


def last_tokens(layer_input, keys, values, segments, positions):
    tiles = (layer_input.shape[1] + 2 * keys.shape[1]) // WINDOW
    return pl.pallas_call(
        tail_kernel,
        name="last_tokens",
        in_specs=[HBM] * 5,
        out_specs=VMEM,
        out_shape=shape(tiles * WINDOW + 16, WINDOW),
        scratch_shapes=[
            pltpu.VMEM(segments.shape, jnp.int32),
            pltpu.VMEM(segments.shape, jnp.int32),
            pltpu.SemaphoreType.DMA((tiles + 2,)),
        ],
        compiler_params=pltpu.CompilerParams(vmem_limit_bytes=LIMIT),
    )(segments, positions, layer_input, keys, values)


def swapped(relative, n):
    return relative if n < 4 else (relative & ~3) | (relative & 1) << 1 | (relative & 2) >> 1


def bit_reversed(n):
    bits = n.bit_length() - 1
    return [int(format(i, "b").zfill(bits)[::-1], 2) if bits else 0 for i in range(n)]


def exchange(part, axis, by):
    count = lax.axis_size(axis)
    return lax.ppermute(part, axis, [(i, i ^ by) for i in range(count)])


def bits(n):
    return n.bit_length() - 1


def share_and_sum(total, by):
    n_dp, n_seq = lax.axis_size("dp"), lax.axis_size("seq")
    rows_of, size = total
    mine, theirs = rows_of(0, size // 2).astype(BF16), rows_of(size // 2, size).astype(BF16)

    def swap(part, dp_bits, seq_bits):
        pairs = [
            (d * n_seq + q, (d ^ dp_bits) * n_seq + (q ^ seq_bits)) for d in range(n_dp) for q in range(n_seq)
        ]
        return lax.ppermute(part, ("dp", "seq"), pairs).astype(F32)

    far = swap(theirs, by, 2)
    near = swap(theirs, by, 0)
    beside = swap(mine, 0, 2)
    return (far + near) + (beside + mine.astype(F32))


def exchange_by_core(part, relative):
    n_dp, n_seq = lax.axis_size("dp"), lax.axis_size("seq")
    pairs = []
    for d in range(n_dp):
        for q in range(n_seq):
            other = d ^ (swapped(relative, n_dp) if q % 2 else relative)
            pairs.append((d * n_seq + q, other * n_seq + q))
    return lax.ppermute(part, ("dp", "seq"), pairs)


def share(total, by, ways, beside=None, held=None):
    rows_of, size = total
    rows = size // ways
    sends = [rows_of(k * rows, (k + 1) * rows).astype(BF16) for k in range(1, ways)]
    if beside is not None:
        sends, held = lax.optimization_barrier((sends, held))
        extra = beside(held)
    got = []
    for k in reversed(range(1, ways)):
        relative = bit_reversed(ways)[k] * by
        got.append(exchange_by_core(sends[k - 1], relative))
    if beside is not None:
        got, extra = lax.optimization_barrier((got, extra))

    def sum_of(first, end):
        part = rows_of(first, end)
        for one in got:
            part = part + one[first:end].astype(F32)
        return part

    total = (sum_of, rows)
    return total if beside is None else (total, extra)


def forward_one(part, axis):
    count = lax.axis_size(axis)
    return lax.ppermute(part, axis, [(i, i + 1) for i in range(count - 1)])


def body(query, keys, values, grad_out, layer_input, sinks, segments, positions):
    n_dp = lax.axis_size("dp")
    n_seq = lax.axis_size("seq")
    dp_index = lax.axis_index("dp")
    seq_index = lax.axis_index("seq")
    core = seq_index & 1
    kv_width = keys.shape[2]
    features = layer_input.shape[2]
    piece = features // (2 * n_dp)
    query, grad_out, layer_input, keys, values = [
        pltpu.with_memory_space_constraint(x[0], pltpu.HBM) for x in (query, grad_out, layer_input, keys, values)
    ]
    sinks, segments, positions = [
        pltpu.with_memory_space_constraint(x, pltpu.HBM) for x in (sinks, segments, positions)
    ]
    tail = last_tokens(layer_input, keys, values, segments, positions)
    rim = forward_one(tail, "seq")
    local = local_grads(query, grad_out, keys, values, layer_input, segments, positions, sinks)
    send, keep, rim_ds, rim_keys = rim_grads(local, rim, kv_width, n_dp)
    if piece % 16:
        plain = jnp.concatenate([keep, send], axis=0).reshape(n_dp, 2, piece, kv_width)
        order = bit_reversed(n_dp)
        orders = jnp.asarray([order, [swapped(relative, n_dp) for relative in order]], jnp.int32) ^ dp_index
        keep, send = [
            jnp.take(plain[:, side], orders[side], axis=0).reshape(-1, kv_width) for side in (core, core ^ 1)
        ]
    got = exchange(send, "seq", 1)
    total = (lambda first, end: keep[first:end].astype(F32) + got[first:end].astype(F32), keep.shape[0])
    group = query.shape[1] // kv_width

    def beside(held):
        return query_grads(*held, group)

    held = (local[2], local[3], rim_ds, rim_keys)
    dq = None
    by = 1
    last = n_dp // 2 if n_seq == 4 and bits(n_dp) % 2 else n_dp
    while by < last:
        ways = 4 if 4 * by <= last else 2
        if dq is None:
            total, dq = share(total, by, ways, beside, held)
        else:
            total = share(total, by, ways)
        by *= ways
    if dq is None:
        dq = beside(held)
    if last < n_dp:
        total = share_and_sum(total, last)
    else:
        total = total[0](0, total[1])
        by = 2
        while by < n_seq:
            mine = total.astype(BF16)
            total = mine.astype(F32) + exchange(mine, "seq", by).astype(F32)
            by *= 2
    other = exchange(total, "seq", 1)
    pair = jnp.where(core == 0, jnp.stack([total, other]), jnp.stack([other, total]))
    return (dq[None], pair.reshape(-1, kv_width))


def solution(mesh):
    return jax.shard_map(
        body,
        mesh=mesh,
        in_specs=(
            P("dp", "seq", None),
            P("dp", "seq", None),
            P("dp", "seq", None),
            P("dp", "seq", None),
            P("dp", "seq", None),
            P(),
            P("dp", "seq"),
            P("dp", "seq"),
        ),
        out_specs=(P("dp", "seq", None), P("dp", None)),
        check_vma=False,
    )
```
